32 devices in a mesh: dp: 8 (over y, x, core), stream: 4 (over z).
Axes of the slice: x: 2, y: 2, z: 4, core: 2. Of those that a mesh axis runs over, the one named last changes fastest.
Arguments:
- visual: bfloat16 [8, 8, 256, 1024], P('dp', None, 'stream'), may hold values from -6 to 6
- conditioning: bfloat16 [8, 8, 2, 1024], P('dp', 'stream'), may hold values from -6 to 6
- d_visual: bfloat16 [8, 8, 256, 1024], P('dp', None, 'stream'), may hold values from -6 to 6
- d_conditioning: bfloat16 [8, 8, 2, 1024], P('dp', 'stream'), may hold values from -6 to 6
- episode_frames: int32 [8, 3], P('dp'), may hold values from 1 to 5, 8 in all within a row
- patch_mask: int32 [8, 8, 256], P('dp'), may hold values 0 or 1
- ln1_gain: bfloat16 [1024], replicated, may hold values from 0.5 to 1.5
- ln1_bias: bfloat16 [1024], replicated, may hold values from -1.75 to 1.75
- w_qkv: bfloat16 [1024, 3072], replicated, may hold values from -0.1875 to 0.1875
- b_qkv: bfloat16 [3072], replicated, may hold values from -1.75 to 1.75
- w_proj: bfloat16 [1024, 1024], replicated, may hold values from -0.75 to 0.75
- b_proj: bfloat16 [1024], replicated, may hold values from -1.75 to 1.75
- ln2_gain: bfloat16 [1024], replicated, may hold values from 0.5 to 1.5
- ln2_bias: bfloat16 [1024], replicated, may hold values from -1.75 to 1.75
- w_in: bfloat16 [1024, 4096], replicated, may hold values from -0.1875 to 0.1875
- b_in: bfloat16 [4096], replicated, may hold values from -1.75 to 1.75
- w_out: bfloat16 [4096, 1024], replicated, may hold values from -0.09375 to 0.09375
- b_out: bfloat16 [1024], replicated, may hold values from -1.75 to 1.75
Outputs:
- out_visual: bfloat16 [8, 8, 256, 1024], P('dp', None, 'stream')
- out_conditioning: bfloat16 [8, 8, 2, 1024], P('dp', 'stream')
- grad_visual: float32 [8, 8, 256, 1024], P('dp', None, 'stream')
- grad_conditioning: float32 [8, 8, 2, 1024], P('dp', 'stream')
- grad_ln1_gain: float32 [1024], P(('dp', 'stream'))
- grad_ln1_bias: float32 [1024], P(('dp', 'stream'))
- grad_w_qkv: float32 [1024, 3072], P(('dp', 'stream'))
- grad_b_query_key: float32 [2048], P(('dp', 'stream'))
- grad_b_value: float32 [1024], P(('dp', 'stream'))
- grad_w_proj: float32 [1024, 1024], P(('dp', 'stream'))
- grad_b_proj: float32 [1024], P(('dp', 'stream'))
- grad_ln2_gain: float32 [1024], P(('dp', 'stream'))
- grad_ln2_bias: float32 [1024], P(('dp', 'stream'))
- grad_w_in: float32 [1024, 4096], P(('dp', 'stream'))
- grad_b_in: float32 [4096], P(('dp', 'stream'))
- grad_w_out: float32 [4096, 1024], P(('dp', 'stream'))
- grad_b_out: float32 [1024], P(('dp', 'stream'))
The draws below stay inside these ranges and needn't reach their ends.
Inputs may be any that keep to these rules, and one draw needn't show every extreme that they name: `episode_frames`: each row holds the frame counts of the 3 episodes packed in one sequence; they sum to 8, and the longest holds exactly 5. `patch_mask`: 1 marks a visual row that may be attended to.
All inputs are finite; a program needn't handle non-finite values. No bound on the sum of `patch_mask` on one device may be relied on, other than what follows from the above.
Results may differ from the reference program's by a relative error of at most 0.035.
Values may be sent and summed in bfloat16 or wider, within the bound.
A program may use at most 192 MiB of HBM per device.

```python
import math
import jax
import jax.numpy as jnp
import numpy as np
from jax import lax

D = 1024
FF = 4096
HEADS = 16
HEAD_DIM = 64
GRID = 16
COND = 2
FRAMES = 8
EPIS = 3
MOST = 5
PATCHES = 256
SEQS = 8


def touch_ends(values, key, smallest, high):
    index_at = [jax.random.randint(jax.random.fold_in(key, axis), (), 0, length) for axis, length in enumerate(values.shape)]
    longest = values.shape.index(max(values.shape))
    beside = index_at[:longest] + [(index_at[longest] + 1) % values.shape[longest]] + index_at[longest + 1:]
    return values.at[tuple(index_at)].set(smallest).at[tuple(beside)].set(high)


def shard_levels(key, shape, shards, least, largest):
    loudness, own = 1.0, jax.random.fold_in(key, 6)
    for dim, parts in shards:
        heights = jnp.exp(jax.random.uniform(jax.random.fold_in(own, dim), (parts,), jnp.float32, least / len(shards), largest / len(shards)))
        loudness = loudness * jnp.repeat(heights, shape[dim] // parts).reshape([-1 if axis == dim else 1 for axis in range(len(shape))])
    return loudness


def split_up(number_of, total, bound, lean):
    weights = [(1 << 20) // math.isqrt(grade ** lean) + 1 for grade in range(2, number_of + 1)]
    surplus, given = total - bound - (number_of - 1), [1] * (number_of - 1)
    while surplus > 0:
        candidates = [i for i in range(number_of - 1) if given[i] < bound]
        mass, budget = sum([weights[i] for i in candidates]), surplus
        for i in candidates:
            more = min(bound - given[i], max(1, budget * weights[i] // mass), surplus)
            given[i] = given[i] + more
            surplus = surplus - more
    return np.array([bound] + given)


def uneven_parts(rng, count, total, bound, slope):
    if count == 2:
        one = jax.random.randint(rng, (), max(1, total - bound), min(bound, total - 1) + 1)
        return jnp.stack([one, total - one])
    sizes = jnp.asarray(split_up(count, total, bound, slope), jnp.int32)
    twos = (count - 1) // 2
    giver, taker = sizes[1:1 + 2 * twos:2], sizes[2:2 + 2 * twos:2]
    room = jnp.minimum(giver - 1, bound - taker)
    shifted = jax.random.randint(jax.random.fold_in(rng, 1), (twos,), 0, 1 << 20) % (room + 1)
    sizes = sizes.at[1:1 + 2 * twos:2].set(giver - shifted).at[2:2 + 2 * twos:2].set(taker + shifted)
    return sizes[jax.random.permutation(jax.random.fold_in(rng, 2), count)]


def noise(stream_key, dims, width, reach, split=(), kind=jnp.bfloat16):
    drawn = jax.random.normal(stream_key, dims, jnp.float32) * width
    if len(split) > 0:
        drawn = shard_levels(stream_key, dims, split, -0.22, 0.18) * drawn
    return jnp.clip(drawn, min=-reach, max=reach).astype(kind)


def setup_inputs(seed: int = 0) -> dict:
    key_of = jax.random.split(jax.random.key(seed), 19)
    visual = noise(key_of[0], (SEQS, FRAMES, PATCHES, D), 1.0, 6.0, ((0, 8), (2, 4)))
    conditioning = noise(key_of[1], (SEQS, FRAMES, COND, D), 1.0, 6.0, ((0, 8), (1, 4)))
    d_visual = noise(key_of[2], (SEQS, FRAMES, PATCHES, D), 1.0, 6.0, ((0, 8), (2, 4)))
    d_conditioning = noise(key_of[3], (SEQS, FRAMES, COND, D), 1.0, 6.0, ((0, 8), (1, 4)))
    episode_frames = jax.vmap(lambda own: uneven_parts(own, EPIS, FRAMES, MOST, 2))(jax.random.split(key_of[4], SEQS)).reshape((SEQS, EPIS)).astype(jnp.int32)
    patch_mask = touch_ends((jax.random.randint(key_of[5], (SEQS, FRAMES, PATCHES), 0, 8) < 7).astype(jnp.int32), jax.random.fold_in(key_of[5], 1), 0, 1)
    ln1_gain = jnp.clip(1.0 + 0.1 * jax.random.normal(key_of[6], (D,), jnp.float32), 0.5, 1.5).astype(jnp.bfloat16)
    ln1_bias = noise(key_of[7], (D,), 0.3, 1.75)
    w_qkv = noise(key_of[8], (D, 3 * D), D ** -0.5, 0.1875)
    b_qkv = noise(key_of[9], (3 * D,), 0.3, 1.75)
    w_proj = noise(key_of[10], (D, D), (D // 16) ** -0.5, 0.75)
    b_proj = noise(key_of[11], (D,), 0.3, 1.75)
    ln2_gain = jnp.clip(1.0 + 0.1 * jax.random.normal(key_of[12], (D,), jnp.float32), 0.5, 1.5).astype(jnp.bfloat16)
    ln2_bias = noise(key_of[13], (D,), 0.3, 1.75)
    w_in = noise(key_of[14], (D, FF), D ** -0.5, 0.1875)
    b_in = noise(key_of[15], (FF,), 0.3, 1.75)
    w_out = noise(key_of[16], (FF, D), FF ** -0.5, 0.09375)
    b_out = noise(key_of[17], (D,), 0.3, 1.75)
    return dict(visual=visual, conditioning=conditioning, d_visual=d_visual, d_conditioning=d_conditioning, episode_frames=episode_frames, patch_mask=patch_mask, ln1_gain=ln1_gain, ln1_bias=ln1_bias, w_qkv=w_qkv, b_qkv=b_qkv, w_proj=w_proj, b_proj=b_proj, ln2_gain=ln2_gain, ln2_bias=ln2_bias, w_in=w_in, b_in=b_in, w_out=w_out, b_out=b_out)


@jax.custom_vjp
def low(v):
    return lax.optimization_barrier(v.astype(jnp.bfloat16)).astype(jnp.float32)

@jax.custom_vjp
def low_back(v):
    return v

def low_keep(v):
    return (low(v), None)

def low_pass(kept, grad):
    return (grad,)

def back_keep(v):
    return (v, None)

def back_low(kept, grad):
    return (low(grad),)
low.defvjp(low_keep, low_pass)
low_back.defvjp(back_keep, back_low)
HIGHEST = lax.Precision.HIGHEST

def layer_norm(values, norm_gain, norm_shift):
    centre = values - lax.optimization_barrier(jnp.mean(values, axis=-1, keepdims=True))
    spread = lax.optimization_barrier(jnp.mean(centre * centre, axis=-1, keepdims=True))
    return centre * lax.rsqrt(spread + 1e-06) * norm_gain + norm_shift

def rotary_tables(times, grid_rows, grid_cols, half_dim):
    pair_ids = jnp.arange(half_dim, dtype=jnp.int32)
    exponent = jnp.where(pair_ids < 30, (pair_ids % 10).astype(jnp.float32) / 10.0, 0.0)
    inverse_freq = jnp.exp(-math.log(10000.0) * exponent)
    zeros_pos = jnp.zeros_like(times)
    position = jnp.where(pair_ids[None, :] < 10, times[:, None], jnp.where(pair_ids[None, :] < 20, grid_rows[:, None], jnp.where(pair_ids[None, :] < 30, grid_cols[:, None], zeros_pos[:, None])))
    angles = position * inverse_freq[None, :]
    return (jnp.cos(angles), jnp.sin(angles))

def rotate(values, cosine_table, sine_table):
    shaped = values.reshape(values.shape[0], values.shape[1], -1, 2)
    first_part = shaped[..., 0]
    second_part = shaped[..., 1]
    cosine_rows = cosine_table[:, None, :]
    sine_rows = sine_table[:, None, :]
    turned_first = first_part * cosine_rows - second_part * sine_rows
    turned_second = first_part * sine_rows + second_part * cosine_rows
    return jnp.stack([turned_first, turned_second], axis=-1).reshape(values.shape)

def episode_of(lengths, frame_ids):
    episode_ends = jnp.cumsum(lengths, axis=-1)
    reached = episode_ends[:, None, :] <= frame_ids[None, :, None]
    episode = lax.optimization_barrier(jnp.sum(reached.astype(jnp.int32), axis=-1))
    episode_start = lax.optimization_barrier(jnp.sum(jnp.where(reached, lengths[:, None, :], 0), axis=-1))
    return (episode, frame_ids[None, :] - episode_start)

def sequence_layout():
    frame_visual = jnp.repeat(jnp.arange(FRAMES, dtype=jnp.int32), PATCHES)
    patch_ids = jnp.tile(jnp.arange(PATCHES, dtype=jnp.int32), FRAMES)
    frame_extra = jnp.repeat(jnp.arange(FRAMES, dtype=jnp.int32), COND)
    zeros_extra = jnp.zeros(FRAMES * COND, dtype=jnp.int32)
    frame_rows = jnp.concatenate([frame_visual, frame_extra])
    grid_rows = jnp.concatenate([patch_ids // GRID, zeros_extra])
    grid_cols = jnp.concatenate([patch_ids % GRID, zeros_extra])
    return (frame_rows, grid_rows, grid_cols)

def forward(rows, params, cosine_table, sine_table, allowed):
    ln1_gain, ln1_bias, w_qkv, b_qkv, w_proj, b_proj, ln2_gain, ln2_bias, w_in, b_in, w_out, b_out = params
    row_count = rows.shape[0]
    normed_one = low(layer_norm(rows, ln1_gain, ln1_bias))
    projected = jnp.dot(normed_one, w_qkv, precision=HIGHEST) + b_qkv
    queries = low(rotate(low_back(projected[:, :D]).reshape(row_count, HEADS, HEAD_DIM), cosine_table, sine_table))
    keys = low(rotate(low_back(projected[:, D:2 * D]).reshape(row_count, HEADS, HEAD_DIM), cosine_table, sine_table))
    values = low(low_back(projected[:, 2 * D:])).reshape(row_count, HEADS, HEAD_DIM)
    score_scale = HEAD_DIM ** (-0.5)

    def one_head(operands):
        query_head, key_head, value_head = operands
        scores = low_back(score_scale * jnp.dot(query_head, key_head.T, precision=HIGHEST))
        scores = jnp.where(allowed, scores, -1e+30)
        weights = low(jax.nn.softmax(scores, axis=-1))
        return jnp.dot(weights, value_head, precision=HIGHEST)
    blended = lax.map(jax.checkpoint(one_head), (queries.transpose(1, 0, 2), keys.transpose(1, 0, 2), values.transpose(1, 0, 2)))
    attended = low_back(low(blended.transpose(1, 0, 2).reshape(row_count, D)))
    residual = rows + low_back(jnp.dot(attended, w_proj, precision=HIGHEST) + b_proj)
    normed_two = low(layer_norm(residual, ln2_gain, ln2_bias))
    hidden = low(jax.nn.gelu(low_back(jnp.dot(normed_two, w_in, precision=HIGHEST) + b_in), approximate=False))
    return residual + low_back(jnp.dot(hidden, w_out, precision=HIGHEST) + b_out)

def reference(visual, conditioning, d_visual, d_conditioning, episode_frames, patch_mask, ln1_gain, ln1_bias, w_qkv, b_qkv, w_proj, b_proj, ln2_gain, ln2_bias, w_in, b_in, w_out, b_out):
    params = tuple((weight_arg.astype(jnp.float32) for weight_arg in (ln1_gain, ln1_bias, w_qkv, b_qkv, w_proj, b_proj, ln2_gain, ln2_bias, w_in, b_in, w_out, b_out)))
    frame_rows, grid_rows, grid_cols = sequence_layout()
    visual_count = FRAMES * PATCHES

    def one_sequence(totals, operands):
        visual_seq, extra_seq, visual_grad, extra_grad, lengths, pad_mask = operands
        episode, times = episode_of(lengths[None, :], frame_rows)
        cosine_table, sine_table = rotary_tables(times[0].astype(jnp.float32), grid_rows.astype(jnp.float32), grid_cols.astype(jnp.float32), HEAD_DIM // 2)
        valid = jnp.concatenate([pad_mask.reshape(-1), jnp.ones(FRAMES * COND, dtype=jnp.int32)]) == 1
        allowed = (episode[0][:, None] == episode[0][None, :]) & (frame_rows[None, :] <= frame_rows[:, None]) & valid[None, :]
        rows = jnp.concatenate([visual_seq.reshape(-1, D), extra_seq.reshape(-1, D)], axis=0).astype(jnp.float32)
        cotangent = jnp.concatenate([visual_grad.reshape(-1, D), extra_grad.reshape(-1, D)], axis=0).astype(jnp.float32)
        result, pullback = jax.vjp(lambda inputs, weights: forward(inputs, weights, cosine_table, sine_table, allowed), rows, params)
        grad_rows, grad_params = pullback(cotangent)
        totals = tuple((total + term for total, term in zip(totals, grad_params)))
        return (totals, (result.astype(jnp.bfloat16), grad_rows))
    start_totals = tuple((jnp.zeros_like(weight_arg) for weight_arg in params))
    sums, (results, grad_rows) = lax.scan(one_sequence, start_totals, (visual, conditioning, d_visual, d_conditioning, episode_frames, patch_mask))
    out_visual = results[:, :visual_count].reshape(visual.shape)
    out_conditioning = results[:, visual_count:].reshape(conditioning.shape)
    grad_visual = grad_rows[:, :visual_count].reshape(visual.shape)
    grad_conditioning = grad_rows[:, visual_count:].reshape(conditioning.shape)
    return (out_visual, out_conditioning, grad_visual, grad_conditioning, sums[0], sums[1], sums[2], sums[3][:2 * D], sums[3][2 * D:], sums[4], sums[5], sums[6], sums[7], sums[8], sums[9], sums[10], sums[11])
```

```python
import functools
import math

import jax
import jax.numpy as jnp
import numpy as np
from jax import lax
from jax.experimental import pallas as pl
from jax.experimental.pallas import tpu as pltpu
from jax.sharding import PartitionSpec as P

D = 1024
HEADS = 16
HEAD_DIM = 64
GRID = 16
COND = 2
FRAMES = 8
MOST = 5
MIDDLE = 7
STREAMS = 4
GROUP = 4
GW = GROUP * HEAD_DIM
PART = 64
PATCHES = 256
VIS = FRAMES * PART
CROWS = 16
ROWS = VIS + CROWS
WIDE = GROUP * 128
NEG = -1e30
EPS = 1e-06
F32 = jnp.float32
BF16 = jnp.bfloat16
VM = pltpu.VMEM
FULL = pl.BlockSpec(memory_space=pltpu.VMEM)
ANYM = pl.BlockSpec(memory_space=pltpu.HBM)
LIMIT = 60 * 1024 * 1024


def nn(a, b):
    return lax.dot_general(a, b, (((1,), (0,)), ((), ())), preferred_element_type=F32)


def nt(a, b):
    return lax.dot_general(a, b, (((1,), (1,)), ((), ())), preferred_element_type=F32)


def rope_constants():
    pair = np.arange(HEAD_DIM // 2)
    exponent = np.where(pair < 30, (pair % 10) / 10.0, 0.0).astype(np.float32)
    freq = np.exp(-math.log(10000.0) * exponent).astype(np.float32)
    patch = np.arange(PATCHES)
    slot_time = np.array([0, 1, 2, 3, 4, 0, 1, 0])
    is_time = (pair < 10)[None, :]
    place = np.where(
        (pair >= 20)[None, :], (patch % GRID)[:, None], (patch // GRID)[:, None]
    ) * ((pair >= 10) & (pair < 30))[None, :]
    angle_patch = (place * freq[None, :]).astype(np.float32)
    angle_time = (slot_time[:, None] * freq[None, :]).astype(np.float32)
    cos_patch = np.where(is_time, 0.0, np.cos(angle_patch))
    sin_patch = np.where(is_time, 0.0, np.sin(angle_patch))
    cos_time = np.where(is_time, np.cos(angle_time), 0.0)
    sin_time = np.where(is_time, np.sin(angle_time), 0.0)

    def spread(table, signed):
        two = np.repeat(table, 2, axis=1)
        if signed:
            two = two * np.where(np.arange(HEAD_DIM) % 2 == 0, -1.0, 1.0)[None, :]
        return np.tile(two, (1, GROUP)).astype(np.float32)

    return (
        spread(cos_patch, False),
        spread(sin_patch, True),
        spread(cos_time, False),
        spread(sin_time, True),
    )


def swap_pairs(v):
    lane = lax.broadcasted_iota(jnp.int32, v.shape, 1)
    width = v.shape[1]
    return jnp.where(lane % 2 == 0, pltpu.roll(v, width - 1, 1), pltpu.roll(v, 1, 1))


def turn(v, cosine, sine):
    return v * cosine + swap_pairs(v) * sine


def pad_heads(t, extra):
    pieces = []
    for h in range(GROUP):
        pieces += [t[:, h * HEAD_DIM : (h + 1) * HEAD_DIM], extra]
    return jnp.concatenate(pieces, axis=1)


def unpad_heads(t):
    return jnp.concatenate([t[:, h * 128 : h * 128 + HEAD_DIM] for h in range(GROUP)], axis=1)


def head(t, h):
    return t[:, h * 128 : (h + 1) * 128]


def first_slot(i):
    return jnp.where(i < MOST, 0, jnp.where(i < MIDDLE, MOST, MIDDLE))


def cond_tables(cs_col, ct, st):
    cosine = jnp.zeros((PART, GW), F32)
    sine = jnp.zeros((PART, GW), F32)
    for j in range(FRAMES):
        here = cs_col == j
        cosine = cosine + jnp.where(here, ct[j : j + 1, :], 0.0)
        sine = sine + jnp.where(here, st[j : j + 1, :], 0.0)
    lane = lax.broadcasted_iota(jnp.int32, (PART, GW), 1) % HEAD_DIM
    return jnp.where(lane < 20, cosine, 1.0), sine


def forward_kernel(
    perm, x_ref, wq_ref, wk_ref, wv_ref, bq_ref, bk_ref, bv_ref, g_ref, b_ref,
    cg_ref, sg_ref, ct_ref, st_ref, bias_ref, csc_ref, csr_ref,
    a_ref, q_ref, k_ref, v_ref, qc_ref, kc_ref, vc_ref, lse_ref, lsec_ref, o_ref,
    vt_ref,
):
    gain, shift = g_ref[...], b_ref[...]
    bq, bk, bv = bq_ref[...], bk_ref[...], bv_ref[...]
    cs_col, cs_row = csc_ref[...], csr_ref[...]
    bias_t = jnp.transpose(bias_ref[...])
    col_id = lax.broadcasted_iota(jnp.int32, (PATCHES, FRAMES), 1)

    def project(x, cosine, sine):
        x = x.astype(F32)
        centre = x - jnp.mean(x, axis=1, keepdims=True)
        spread = jnp.mean(centre * centre, axis=1, keepdims=True)
        a = (centre * lax.rsqrt(spread + EPS) * gain + shift).astype(BF16)
        q = turn(nn(a, wq_ref[...]) + bq, cosine, sine)
        k = turn(nn(a, wk_ref[...]) + bk, cosine, sine)
        v = nn(a, wv_ref[...]) + bv
        return a, (q.astype(BF16).astype(F32) * 0.125).astype(BF16), k.astype(BF16), v

    def lanes(rows):
        return lax.broadcasted_iota(jnp.int32, (rows, 64), 1)

    xc = x_ref[:, VIS:, :].reshape(PART, D)
    a, q, k, v = project(xc, *cond_tables(cs_col, ct_ref[...], st_ref[...]))
    a_ref[:, VIS:, :] = a.reshape(STREAMS, CROWS, D)
    one = jnp.where(lanes(PART) == 0, 1.0, 0.0).astype(BF16)
    zero = jnp.zeros((PART, 64), BF16)
    qc_ref[...] = pad_heads(q, one)
    kc_ref[...] = pad_heads(k, zero)
    vc_ref[...] = pad_heads(v.astype(BF16), zero)
    vct = jnp.transpose(v).astype(BF16)

    def slot(i, carry):
        f = perm[i]
        start = pl.multiple_of(f * PART, PART)
        x = x_ref[:, pl.ds(start, PART), :].reshape(PATCHES, D)
        cosine = cg_ref[...] + ct_ref[pl.ds(i, 1), :]
        sine = sg_ref[...] + st_ref[pl.ds(i, 1), :]
        a, q, k, v = project(x, cosine, sine)
        a_ref[:, pl.ds(start, PART), :] = a.reshape(STREAMS, PART, D)
        lane = lanes(PATCHES)
        bias = jnp.sum(jnp.where(col_id == f, bias_t, 0.0), axis=1, keepdims=True)
        q_ref[i] = pad_heads(q, jnp.where(lane == 0, 1.0, 0.0).astype(BF16))
        k_ref[i] = pad_heads(k, jnp.where(lane == 0, bias, 0.0).astype(BF16))
        v_ref[i] = pad_heads(v.astype(BF16), jnp.zeros((PATCHES, 64), BF16))
        vt_ref[i] = jnp.transpose(v).astype(BF16)
        lo = first_slot(i)
        near = (cs_col >= lo) & (cs_col <= i)
        tops, totals, blends = [], [], []
        for h in range(GROUP):
            s = jnp.where(near, nt(head(kc_ref, h), head(q_ref[i], h)), NEG)
            top = jnp.max(s, axis=0, keepdims=True)
            p = jnp.exp(s - top)
            tops.append(top)
            totals.append(jnp.sum(p, axis=0, keepdims=True))
            blends.append(nn(vct[h * HEAD_DIM : (h + 1) * HEAD_DIM], p.astype(BF16)))

        def step(j, state):
            tops, totals, blends = state
            new = ([], [], [])
            for h in range(GROUP):
                s = nt(k_ref[j, :, h * 128 : (h + 1) * 128], q_ref[i, :, h * 128 : (h + 1) * 128])
                top = jnp.maximum(tops[h], jnp.max(s, axis=0, keepdims=True))
                p = jnp.exp(s - top)
                keep = jnp.exp(tops[h] - top)
                new[0].append(top)
                new[1].append(totals[h] * keep + jnp.sum(p, axis=0, keepdims=True))
                vt = vt_ref[j, h * HEAD_DIM : (h + 1) * HEAD_DIM, :]
                new[2].append(blends[h] * keep + nn(vt, p.astype(BF16)))
            return new

        tops, totals, blends = lax.fori_loop(lo, i + 1, step, (tops, totals, blends))
        o = jnp.transpose(jnp.concatenate([blends[h] / totals[h] for h in range(GROUP)], axis=0))
        o_ref[:, pl.ds(start, PART), :] = o.astype(BF16).reshape(STREAMS, PART, GW)
        lse_ref[i] = jnp.concatenate([tops[h] + jnp.log(totals[h]) for h in range(GROUP)] * 2, axis=0)
        return carry

    lax.fori_loop(0, FRAMES, slot, 0)

    lo_col = first_slot(cs_col)
    near = (cs_row >= lo_col) & (cs_row <= cs_col)
    tops, totals, blends = [], [], []
    for h in range(GROUP):
        s = jnp.where(near, nt(head(qc_ref, h), head(kc_ref, h)), NEG)
        top = jnp.max(s, axis=1, keepdims=True)
        p = jnp.exp(s - top)
        tops.append(top)
        totals.append(jnp.sum(p, axis=1, keepdims=True))
        blends.append(nn(p.astype(BF16), head(vc_ref, h)))

    def cond_step(j, state):
        tops, totals, blends = state
        near = (lo_col <= j) & (cs_col >= j)
        new = ([], [], [])
        for h in range(GROUP):
            s = nt(head(qc_ref, h), k_ref[j, :, h * 128 : (h + 1) * 128])
            s = jnp.where(near, s, NEG)
            top = jnp.maximum(tops[h], jnp.max(s, axis=1, keepdims=True))
            p = jnp.exp(s - top)
            keep = jnp.exp(tops[h] - top)
            new[0].append(top)
            new[1].append(totals[h] * keep + jnp.sum(p, axis=1, keepdims=True))
            new[2].append(blends[h] * keep + nn(p.astype(BF16), v_ref[j, :, h * 128 : (h + 1) * 128]))
        return new

    tops, totals, blends = lax.fori_loop(0, FRAMES, cond_step, (tops, totals, blends))
    o = jnp.concatenate([(blends[h] / totals[h])[:, :HEAD_DIM] for h in range(GROUP)], axis=1)
    o_ref[:, VIS:, :] = o.astype(BF16).reshape(STREAMS, CROWS, GW)
    lane = lax.broadcasted_iota(jnp.int32, (PART, 128), 1)
    lsec = jnp.zeros((PART, 128), F32)
    for h in range(GROUP):
        lsec = lsec + jnp.where(lane == h, tops[h] + jnp.log(totals[h]), 0.0)
    lsec_ref[...] = lsec


def whole(shape):
    return pl.BlockSpec(shape, lambda i, s: (0,) * len(shape))


def attend_forward(scalars, x, w_qkv, b_qkv, gain, shift, tables, bias, cs_col, cs_row):
    def weight(part):
        return pl.BlockSpec((D, GW), lambda i, s: (0, s[8] + part * GROUP))

    def offset(part):
        return pl.BlockSpec((1, GW), lambda i, s: (0, s[8] + part * GROUP))

    shapes = (
        ((STREAMS, ROWS, D), BF16),
        ((FRAMES, PATCHES, WIDE), BF16),
        ((FRAMES, PATCHES, WIDE), BF16),
        ((FRAMES, PATCHES, WIDE), BF16),
        ((PART, WIDE), BF16),
        ((PART, WIDE), BF16),
        ((PART, WIDE), BF16),
        ((FRAMES, 8, PATCHES), F32),
        ((PART, 128), F32),
        ((STREAMS, ROWS, GW), BF16),
    )
    ops = (x, w_qkv, w_qkv, w_qkv, b_qkv, b_qkv, b_qkv, gain, shift) + tables + (bias, cs_col, cs_row)
    specs = [whole(x.shape), weight(0), weight(1), weight(2), offset(0), offset(1), offset(2)]
    specs += [whole(t.shape) for t in ops[7:]]
    return pl.pallas_call(
        forward_kernel,
        name="attend_forward",
        out_shape=tuple(jax.ShapeDtypeStruct(s, t) for s, t in shapes),
        grid_spec=pltpu.PrefetchScalarGridSpec(
            num_scalar_prefetch=1,
            grid=(1,),
            in_specs=specs,
            out_specs=tuple(whole(s) for s, _ in shapes),
            scratch_shapes=[VM((FRAMES, GW, PATCHES), BF16)],
        ),
        compiler_params=pltpu.CompilerParams(vmem_limit_bytes=LIMIT),
        cost_estimate=pl.CostEstimate(flops=8 * 10**9, bytes_accessed=2 * 10**7, transcendentals=6 * 10**6),
    )(scalars, *ops)


def backward_kernel(
    perm, q_ref, k_ref, v_ref, qc_ref, kc_ref, vc_ref, lse_ref, lsec_ref, o_ref, do_ref,
    cg_ref, sg_ref, ct_ref, st_ref, csc_ref, csr_ref,
    g_ref, dk_ref, dv_ref, dkc_ref, dvc_ref, kt_ref,
):
    cs_col, cs_row = csc_ref[...], csr_ref[...]
    dk_ref[...] = jnp.zeros_like(dk_ref)
    dv_ref[...] = jnp.zeros_like(dv_ref)
    dkc_ref[...] = jnp.zeros_like(dkc_ref)
    dvc_ref[...] = jnp.zeros_like(dvc_ref)
    kct = jnp.transpose(unpad_heads(kc_ref[...].astype(F32))).astype(BF16)

    def slot(i, carry):
        f = perm[i]
        start = pl.multiple_of(f * PART, PART)
        do = do_ref[:, pl.ds(start, PART), :].reshape(PATCHES, GW)
        o = o_ref[:, pl.ds(start, PART), :].reshape(PATCHES, GW)
        prod = jnp.transpose(do.astype(F32) * o.astype(F32))
        deltas = [
            jnp.sum(prod[h * HEAD_DIM : (h + 1) * HEAD_DIM], axis=0, keepdims=True)
            for h in range(GROUP)
        ]
        dop = pad_heads(do, jnp.zeros((PATCHES, 64), BF16))
        kt_ref[i] = jnp.transpose(unpad_heads(k_ref[i].astype(F32))).astype(BF16)
        lo = first_slot(i)
        near = (cs_col >= lo) & (cs_col <= i)
        dqs = []
        for h in range(GROUP):
            cols = slice(h * 128, (h + 1) * 128)
            q = q_ref[i, :, cols]
            s = jnp.where(near, nt(kc_ref[:, cols], q), NEG)
            p = jnp.exp(s - lse_ref[i, h : h + 1, :])
            dp = nt(vc_ref[:, cols], dop[:, cols])
            ds = (p * (dp - deltas[h])).astype(BF16)
            dvc_ref[:, cols] += nn(p.astype(BF16), dop[:, cols])
            dkc_ref[:, cols] += nn(ds, q)
            dqs.append(nn(kct[h * HEAD_DIM : (h + 1) * HEAD_DIM], ds))

        def step(j, dqs):
            new = []
            for h in range(GROUP):
                cols = slice(h * 128, (h + 1) * 128)
                q = q_ref[i, :, cols]
                p = jnp.exp(nt(k_ref[j, :, cols], q) - lse_ref[i, h : h + 1, :])
                dp = nt(v_ref[j, :, cols], dop[:, cols])
                ds = (p * (dp - deltas[h])).astype(BF16)
                dv_ref[j, :, cols] += nn(p.astype(BF16), dop[:, cols])
                dk_ref[j, :, cols] += nn(ds, q)
                new.append(dqs[h] + nn(kt_ref[j, h * HEAD_DIM : (h + 1) * HEAD_DIM, :], ds))
            return new

        dqs = lax.fori_loop(lo, i + 1, step, dqs)
        dq = jnp.transpose(jnp.concatenate(dqs, axis=0)) * 0.125
        cosine = cg_ref[...] + ct_ref[pl.ds(i, 1), :]
        sine = sg_ref[...] + st_ref[pl.ds(i, 1), :]
        dq = turn(dq, cosine, -sine).astype(BF16).reshape(STREAMS, PART, GW)
        g_ref[:, pl.ds(start, PART), 0:GW] = dq
        return carry

    lax.fori_loop(0, FRAMES, slot, 0)

    doc = do_ref[:, VIS:, :].reshape(PART, GW)
    oc = o_ref[:, VIS:, :].reshape(PART, GW)
    docp = pad_heads(doc, jnp.zeros((PART, 64), BF16))
    prod = doc.astype(F32) * oc.astype(F32)
    lo_col = first_slot(cs_col)
    near = (cs_row >= lo_col) & (cs_row <= cs_col)
    deltas = [
        jnp.sum(prod[:, h * HEAD_DIM : (h + 1) * HEAD_DIM], axis=1, keepdims=True)
        for h in range(GROUP)
    ]
    lses = [lsec_ref[:, h : h + 1] for h in range(GROUP)]
    dqs = []
    for h in range(GROUP):
        cols = slice(h * 128, (h + 1) * 128)
        s = jnp.where(near, nt(qc_ref[:, cols], kc_ref[:, cols]), NEG)
        p = jnp.exp(s - lses[h])
        ds = p * (nt(docp[:, cols], vc_ref[:, cols]) - deltas[h])
        dvc_ref[:, cols] += nn(jnp.transpose(p).astype(BF16), docp[:, cols])
        dkc_ref[:, cols] += nn(jnp.transpose(ds).astype(BF16), qc_ref[:, cols])
        dqs.append(nn(ds.astype(BF16), kc_ref[:, cols]))

    def cond_step(j, dqs):
        near = (lo_col <= j) & (cs_col >= j)
        new = []
        for h in range(GROUP):
            cols = slice(h * 128, (h + 1) * 128)
            s = jnp.where(near, nt(qc_ref[:, cols], k_ref[j, :, cols]), NEG)
            p = jnp.exp(s - lses[h])
            ds = p * (nt(docp[:, cols], v_ref[j, :, cols]) - deltas[h])
            dv_ref[j, :, cols] += nn(jnp.transpose(p).astype(BF16), docp[:, cols])
            dk_ref[j, :, cols] += nn(jnp.transpose(ds).astype(BF16), qc_ref[:, cols])
            new.append(dqs[h] + nn(ds.astype(BF16), k_ref[j, :, cols]))
        return new

    dqs = lax.fori_loop(0, FRAMES, cond_step, dqs)
    cosine, sine = cond_tables(cs_col, ct_ref[...], st_ref[...])
    valid = cs_col < FRAMES
    dq = jnp.concatenate([t[:, :HEAD_DIM] for t in dqs], axis=1) * 0.125
    for part, t in ((0, turn(dq, cosine, -sine)), (1, turn(unpad_heads(dkc_ref[...]), cosine, -sine)), (2, unpad_heads(dvc_ref[...]))):
        t = jnp.where(valid, t, 0.0).astype(BF16)
        g_ref[:, VIS:, part * GW : (part + 1) * GW] = t.reshape(STREAMS, CROWS, GW)

    def finish(i, carry):
        start = pl.multiple_of(perm[i] * PART, PART)
        cosine = cg_ref[...] + ct_ref[pl.ds(i, 1), :]
        sine = sg_ref[...] + st_ref[pl.ds(i, 1), :]
        dk = turn(unpad_heads(dk_ref[i]), cosine, -sine)
        g_ref[:, pl.ds(start, PART), GW : 2 * GW] = dk.astype(BF16).reshape(STREAMS, PART, GW)
        dv = unpad_heads(dv_ref[i])
        g_ref[:, pl.ds(start, PART), 2 * GW :] = dv.astype(BF16).reshape(STREAMS, PART, GW)
        return carry

    lax.fori_loop(0, FRAMES, finish, 0)


def attend_backward(scalars, saved, o, do, tables, cs_col, cs_row):
    ops = tuple(saved) + (o, do) + tables + (cs_col, cs_row)
    out = (STREAMS, ROWS, 3 * GW)
    return pl.pallas_call(
        backward_kernel,
        name="attend_backward",
        out_shape=jax.ShapeDtypeStruct(out, BF16),
        grid_spec=pltpu.PrefetchScalarGridSpec(
            num_scalar_prefetch=1,
            grid=(1,),
            in_specs=[whole(t.shape) for t in ops],
            out_specs=whole(out),
            scratch_shapes=[
                VM((FRAMES, PATCHES, WIDE), F32),
                VM((FRAMES, PATCHES, WIDE), F32),
                VM((PART, WIDE), F32),
                VM((PART, WIDE), F32),
                VM((FRAMES, GW, PATCHES), BF16),
            ],
        ),
        compiler_params=pltpu.CompilerParams(vmem_limit_bytes=LIMIT),
        cost_estimate=pl.CostEstimate(flops=10**10, bytes_accessed=2 * 10**7, transcendentals=6 * 10**6),
    )(scalars, *ops)


def where_am_i():
    d, z = lax.axis_index("dp"), lax.axis_index("stream")
    return d // 2, d % 2, z // 2, z % 2, z


def greet_column():
    p, c, q, r, z = where_am_i()
    barrier = pltpu.get_barrier_semaphore()
    for core in range(2):
        for chip in range(STREAMS):
            @pl.when((core != c) | (chip != z))
            def _():
                pl.semaphore_signal(
                    barrier, inc=1, device_id=(2 * p + core, chip),
                    device_id_type=pl.DeviceIdType.MESH,
                )
    pl.semaphore_wait(barrier, 2 * STREAMS - 1)


def remote(src, dst, send, recv, device):
    return pltpu.make_async_remote_copy(
        src_ref=src, dst_ref=dst, send_sem=send, recv_sem=recv, device_id=device,
        device_id_type=pl.DeviceIdType.MESH,
    )


def comm_call(kernel, name, ident, outs, scratch, *ops):
    return pl.pallas_call(
        kernel,
        name=name,
        out_shape=tuple(jax.ShapeDtypeStruct(s, t) for s, t in outs),
        in_specs=[ANYM] * len(ops),
        out_specs=tuple(ANYM for _ in outs),
        scratch_shapes=scratch,
        compiler_params=pltpu.CompilerParams(
            collective_id=ident, has_side_effects=True, vmem_limit_bytes=LIMIT
        ),
    )(*ops)


def dma(*shape):
    return pltpu.SemaphoreType.DMA(shape)


HALF = VIS // 2


def gather_kernel(x_ref, m_ref, xa_ref, ma_ref, send, recv, csend, crecv, fsend, frecv, lsem, msem):
    p, c, q, r, z = where_am_i()
    greet_column()
    tail = pl.ds(VIS, CROWS)
    for core in range(2):
        rows = pl.ds(core * HALF, HALF)
        for side in range(2):
            n = core * 2 + side
            mine = (core == c) & (2 * c + side == z)
            device = (2 * p + core, 2 * c + side)

            @pl.when(mine)
            def _():
                pltpu.make_async_copy(x_ref.at[rows], xa_ref.at[z, rows], lsem.at[0]).start()
                pltpu.make_async_copy(x_ref.at[tail], xa_ref.at[z, tail], lsem.at[1]).start()

            @pl.when(jnp.logical_not(mine))
            def _():
                remote(x_ref.at[rows], xa_ref.at[z, rows], send.at[n], recv.at[z], device).start()
                remote(x_ref.at[tail], xa_ref.at[z, tail], csend.at[n], crecv.at[z], device).start()

    other = (2 * p + 1 - c, z)

    @pl.when(q == c)
    def _():
        remote(m_ref, ma_ref, msem.at[0], msem.at[1], other).start()
        pltpu.make_async_copy(m_ref, ma_ref, msem.at[2]).start()

    rows = pl.ds(c * HALF, HALF)
    for s in range(STREAMS):
        mine = (q == c) & (s == z)

        @pl.when(mine)
        def _():
            pltpu.make_async_copy(x_ref.at[rows], xa_ref.at[s, rows], lsem.at[0]).wait()
            pltpu.make_async_copy(x_ref.at[tail], xa_ref.at[s, tail], lsem.at[1]).wait()

        @pl.when(jnp.logical_not(mine))
        def _():
            remote(x_ref.at[rows], xa_ref.at[s, rows], send.at[0], recv.at[s], other).wait_recv()
            remote(x_ref.at[tail], xa_ref.at[s, tail], csend.at[0], crecv.at[s], other).wait_recv()

        remote(xa_ref.at[s, rows], xa_ref.at[s, rows], fsend.at[s], frecv.at[s], other).start()
    rest = pl.ds((1 - c) * HALF, HALF)
    for s in range(STREAMS):
        copy = remote(xa_ref.at[s, rest], xa_ref.at[s, rest], fsend.at[s], frecv.at[s], other)
        copy.wait_send()
        copy.wait_recv()
    for core in range(2):
        for side in range(2):
            n = core * 2 + side

            @pl.when((core != c) | (2 * c + side != z))
            def _():
                remote(x_ref.at[rows], xa_ref.at[0, rows], send.at[n], recv.at[0], other).wait_send()
                remote(x_ref.at[tail], xa_ref.at[0, tail], csend.at[n], crecv.at[0], other).wait_send()

    @pl.when(q == c)
    def _():
        remote(m_ref, ma_ref, msem.at[0], msem.at[1], other).wait_send()
        pltpu.make_async_copy(m_ref, ma_ref, msem.at[2]).wait()

    @pl.when(q != c)
    def _():
        remote(m_ref, ma_ref, msem.at[0], msem.at[1], other).wait_recv()


def gather_rows(x, meta):
    return comm_call(
        gather_kernel, "gather_rows", 0,
        (((STREAMS, ROWS, D), BF16), (meta.shape, F32)),
        [dma(4), dma(4), dma(4), dma(4), dma(4), dma(4), dma(2), dma(3)],
        x, meta,
    )


def to_owner_kernel(o_ref, out_ref, send, recv, lsem):
    p, c, q, r, z = where_am_i()
    greet_column()
    group = 2 * r + c
    place = pl.ds(pl.multiple_of(group * GW, GW), GW)
    for s in range(STREAMS):
        mine = (q == c) & (s == z)

        @pl.when(mine)
        def _():
            pltpu.make_async_copy(o_ref.at[s], out_ref.at[:, place], lsem).start()

        @pl.when(jnp.logical_not(mine))
        def _():
            remote(o_ref.at[s], out_ref.at[:, place], send.at[s], recv.at[group], (2 * p + q, s)).start()
    for s in range(STREAMS):
        mine = (q == c) & (s == z)

        @pl.when(mine)
        def _():
            pltpu.make_async_copy(o_ref.at[s], out_ref.at[:, place], lsem).wait()

        @pl.when(jnp.logical_not(mine))
        def _():
            remote(o_ref.at[s], out_ref.at[:, place], send.at[s], recv.at[group], (2 * p + q, s)).wait_send()
    for side in range(2):
        for core in range(2):
            g = 2 * side + core

            @pl.when((core != c) | (2 * c + side != z))
            def _():
                cols = pl.ds(g * GW, GW)
                remote(o_ref.at[0], out_ref.at[:, cols], send.at[0], recv.at[g], (2 * p + q, 0)).wait_recv()


def to_owner(o):
    return comm_call(
        to_owner_kernel, "to_owner", 1, (((ROWS, D), BF16),), [dma(4), dma(4), pltpu.SemaphoreType.DMA], o
    )[0]


def to_heads_kernel(d_ref, out_ref, send, recv, lsem):
    p, c, q, r, z = where_am_i()
    greet_column()
    for side in range(2):
        for core in range(2):
            g = 2 * side + core
            cols = pl.ds(g * GW, GW)
            mine = (core == c) & (2 * c + side == z)

            @pl.when(mine)
            def _():
                pltpu.make_async_copy(d_ref.at[:, cols], out_ref.at[z], lsem).start()

            @pl.when(jnp.logical_not(mine))
            def _():
                remote(d_ref.at[:, cols], out_ref.at[z], send.at[g], recv.at[z], (2 * p + core, 2 * c + side)).start()
    for side in range(2):
        for core in range(2):
            g = 2 * side + core
            cols = pl.ds(g * GW, GW)
            mine = (core == c) & (2 * c + side == z)

            @pl.when(mine)
            def _():
                pltpu.make_async_copy(d_ref.at[:, cols], out_ref.at[z], lsem).wait()

            @pl.when(jnp.logical_not(mine))
            def _():
                remote(d_ref.at[:, cols], out_ref.at[z], send.at[g], recv.at[z], (2 * p + core, 2 * c + side)).wait_send()
    for s in range(STREAMS):
        @pl.when((q != c) | (s != z))
        def _():
            remote(d_ref.at[:, pl.ds(0, GW)], out_ref.at[s], send.at[0], recv.at[s], (2 * p + q, s)).wait_recv()


def to_heads(d):
    return comm_call(
        to_heads_kernel, "to_heads", 2, (((STREAMS, ROWS, GW), BF16),), [dma(4), dma(4), pltpu.SemaphoreType.DMA], d
    )[0]


def sum_rows_kernel(
    d_ref, out_ref, dsend, drecv, send, recv, csend, crecv, lsem, near, mine_buf, own, land, tail, total
):
    p, c, q, r, z = where_am_i()
    greet_column()
    other = (2 * p + 1 - c, z)
    rows = pl.ds(c * HALF, HALF)
    rest = pl.ds((1 - c) * HALF, HALF)
    last = pl.ds(VIS, CROWS)
    for s in range(STREAMS):
        remote(d_ref.at[s, rest], near.at[s], dsend.at[s], drecv.at[s], other).start()
        pltpu.make_async_copy(d_ref.at[s, rows], mine_buf.at[s], lsem.at[s]).start()
    group = 2 * r + c
    for s in range(STREAMS):
        mine = (q == c) & (s == z)

        @pl.when(mine)
        def _():
            pltpu.make_async_copy(d_ref.at[s, last], tail.at[group], lsem.at[4]).start()

        @pl.when(jnp.logical_not(mine))
        def _():
            remote(d_ref.at[s, last], tail.at[group], csend.at[s], crecv.at[group], (2 * p + q, s)).start()
    for s in range(STREAMS):
        mine = (q == c) & (s == z)
        pltpu.make_async_copy(d_ref.at[s, rows], mine_buf.at[s], lsem.at[s]).wait()
        remote(d_ref.at[s, rest], near.at[s], dsend.at[s], drecv.at[s], other).wait_recv()
        for t in range(HALF // 64):
            part = pl.ds(t * 64, 64)
            both = near[s, part].astype(F32) + mine_buf[s, part].astype(F32)
            own[s, part] = both.astype(BF16)

        @pl.when(mine)
        def _():
            pltpu.make_async_copy(own.at[s], land.at[r, rows], lsem.at[5]).start()

        @pl.when(jnp.logical_not(mine))
        def _():
            remote(own.at[s], land.at[r, rows], send.at[s], recv.at[r, c], (2 * p + q, s)).start()
    for s in range(STREAMS):
        mine = (q == c) & (s == z)
        remote(d_ref.at[s, rest], near.at[s], dsend.at[s], drecv.at[s], other).wait_send()

        @pl.when(mine)
        def _():
            pltpu.make_async_copy(d_ref.at[s, last], tail.at[group], lsem.at[4]).wait()
            pltpu.make_async_copy(own.at[s], land.at[r, rows], lsem.at[5]).wait()

        @pl.when(jnp.logical_not(mine))
        def _():
            remote(d_ref.at[s, last], tail.at[group], csend.at[s], crecv.at[group], (2 * p + q, s)).wait_send()
            remote(own.at[s], land.at[r, rows], send.at[s], recv.at[r, c], (2 * p + q, s)).wait_send()
    for side in range(2):
        for core in range(2):
            @pl.when((core != c) | (2 * c + side != z))
            def _():
                part = pl.ds(core * HALF, HALF)
                remote(own.at[0], land.at[side, part], send.at[0], recv.at[side, core], other).wait_recv()
                g = 2 * side + core
                remote(d_ref.at[0, last], tail.at[g], csend.at[0], crecv.at[g], other).wait_recv()
    for t in range(VIS // 64):
        part = pl.ds(t * 64, 64)
        total[part] = land[0, part].astype(F32) + land[1, part].astype(F32)
    ends = [tail[g].astype(F32) for g in range(4)]
    total[last] = (ends[0] + ends[1]) + (ends[2] + ends[3])
    done = pltpu.make_async_copy(total, out_ref, lsem.at[6])
    done.start()
    done.wait()


def sum_rows(d):
    return comm_call(
        sum_rows_kernel, "sum_rows", 3, (((ROWS, D), F32),),
        [
            dma(4), dma(4), dma(4), dma(2, 2), dma(4), dma(4), dma(7),
            VM((STREAMS, HALF, D), BF16), VM((STREAMS, HALF, D), BF16), VM((STREAMS, HALF, D), BF16),
            VM((2, VIS, D), BF16), VM((4, CROWS, D), BF16), VM((ROWS, D), F32),
        ],
        d,
    )[0]


def layer_norm(values, norm_gain, norm_shift):
    centre = values - jnp.mean(values, axis=-1, keepdims=True)
    spread = jnp.mean(centre * centre, axis=-1, keepdims=True)
    return centre * lax.rsqrt(spread + EPS) * norm_gain + norm_shift


def norm_parts(values):
    centre = values - jnp.mean(values, axis=-1, keepdims=True)
    scale = lax.rsqrt(jnp.mean(centre * centre, axis=-1, keepdims=True) + EPS)
    return centre * scale, scale


def norm_back(normed, scale, gain, grad):
    g = grad * gain
    return scale * (
        g - jnp.mean(g, axis=-1, keepdims=True) - normed * jnp.mean(g * normed, axis=-1, keepdims=True)
    )


def own_meta(lengths, mask):
    frames = jnp.arange(FRAMES, dtype=jnp.int32)
    ends = jnp.cumsum(lengths)
    reached = ends[None, :] <= frames[:, None]
    begin = jnp.sum(jnp.where(reached, lengths[None, :], 0), axis=1)
    length = jnp.sum(
        jnp.where((jnp.sum(reached, axis=1)[:, None] == jnp.arange(3)[None, :]), lengths[None, :], 0), axis=1
    )
    base = jnp.where(length == MOST, 0, jnp.where(length == MIDDLE - MOST, MOST, MIDDLE))
    slot = base + frames - begin
    perm = jnp.sum(jnp.where(slot[:, None] == frames[None, :], frames[:, None], 0), axis=0)
    stream = jnp.arange(STREAMS)[:, None]
    row = jnp.arange(CROWS)[None, :]
    part = FRAMES // STREAMS
    frame = jnp.where(row < part * COND, part * stream + row // COND, FRAMES)
    cslot = jnp.sum(jnp.where(frame[..., None] == frames, slot[None, None, :], 0), axis=-1)
    cslot = jnp.where(frame < FRAMES, cslot, 99).reshape(1, PART)
    bias = jnp.where(mask == 1, 0.0, NEG).astype(F32)
    line = jnp.concatenate([perm[None].astype(F32), cslot.astype(F32), jnp.zeros((1, PATCHES - PART - FRAMES), F32)], axis=1)
    return jnp.concatenate([bias, jnp.broadcast_to(line, (8, PATCHES))], axis=0)


def per_device(
    visual, conditioning, d_visual, d_conditioning, episode_frames, patch_mask,
    ln1_gain, ln1_bias, w_qkv, b_qkv, w_proj, b_proj, ln2_gain, ln2_bias, w_in, b_in, w_out, b_out,
):
    d, z = lax.axis_index("dp"), lax.axis_index("stream")
    group = 2 * (z % 2) + d % 2
    blank = jnp.zeros((CROWS - conditioning.shape[1] * COND, D), BF16)

    def chunk(rows, extra):
        return jnp.concatenate([rows.reshape(VIS, D), extra.reshape(-1, D), blank], axis=0)

    x = chunk(visual, conditioning)
    dy = chunk(d_visual, d_conditioning)
    gain_one, shift_one = ln1_gain.astype(F32), ln1_bias.astype(F32)
    gain_two, shift_two = ln2_gain.astype(F32), ln2_bias.astype(F32)
    x_all, meta = gather_rows(x, own_meta(episode_frames[0], patch_mask[0]))
    bias = meta[:FRAMES]
    perm = meta[FRAMES, :FRAMES].astype(jnp.int32)
    cslot = meta[FRAMES, FRAMES : FRAMES + PART].astype(jnp.int32)
    cs_col, cs_row = cslot.reshape(PART, 1), cslot.reshape(1, PART)
    scalars = jnp.concatenate([perm, group.reshape(1).astype(jnp.int32)])
    tables = tuple(jnp.asarray(t) for t in rope_constants())
    a, *saved, o = attend_forward(
        scalars, x_all, w_qkv, b_qkv.astype(F32).reshape(1, -1), gain_one.reshape(1, -1),
        shift_one.reshape(1, -1), tables, bias, cs_col, cs_row,
    )
    attended = to_owner(o)

    inputs = x.astype(F32)
    residual = inputs + jnp.dot(attended, w_proj, preferred_element_type=F32) + b_proj.astype(F32)
    normed_two, scale_two = norm_parts(residual)
    n = (normed_two * gain_two + shift_two).astype(BF16)
    u = jnp.dot(n, w_in, preferred_element_type=F32) + b_in.astype(F32)
    phi = 0.5 * (1.0 + lax.erf(u * (2.0**-0.5)))
    hidden = (u * phi).astype(BF16)
    slope = phi + u * (jnp.exp(-0.5 * u * u) * ((2.0 * math.pi) ** -0.5))
    output = residual + jnp.dot(hidden, w_out, preferred_element_type=F32) + b_out.astype(F32)
    out_visual = output[:VIS].astype(BF16).reshape(visual.shape)
    out_conditioning = output[VIS : VIS + conditioning.shape[1] * COND].astype(BF16).reshape(conditioning.shape)

    dy32 = dy.astype(F32)
    grad_b_out = jnp.sum(dy32, axis=0)
    grad_hidden = jnp.einsum("rd,hd->rh", dy, w_out, preferred_element_type=F32)
    grad_u = (grad_hidden * slope).astype(BF16)
    grad_b_in = jnp.sum(grad_u, axis=0, dtype=F32)
    grad_n = jnp.einsum("rh,dh->rd", grad_u, w_in, preferred_element_type=F32)
    grad_ln2_gain = jnp.sum(grad_n * normed_two, axis=0)
    grad_ln2_bias = jnp.sum(grad_n, axis=0)
    grad_h = dy32 + norm_back(normed_two, scale_two, gain_two, grad_n)
    grad_hb = grad_h.astype(BF16)
    grad_b_proj = jnp.sum(grad_hb, axis=0, dtype=F32)
    grad_o = jnp.einsum("re,de->rd", grad_hb, w_proj, preferred_element_type=F32).astype(BF16)
    grad_o_heads = to_heads(grad_o)
    grad_qkv = attend_backward(scalars, saved, o, grad_o_heads, tables, cs_col, cs_row)

    flat = grad_qkv.reshape(STREAMS * ROWS, 3 * GW)
    role_w = jnp.concatenate(
        [lax.dynamic_slice_in_dim(w_qkv, part * D + group * GW, GW, 1) for part in range(3)], axis=1
    )
    partial = jnp.einsum("re,de->rd", flat, role_w, preferred_element_type=F32).astype(BF16)
    grad_a = sum_rows(partial.reshape(STREAMS, ROWS, D))
    normed_one, scale_one = norm_parts(inputs)
    grad_ln1_gain = jnp.sum(grad_a * normed_one, axis=0)
    grad_ln1_bias = jnp.sum(grad_a, axis=0)
    grad_x = grad_h + norm_back(normed_one, scale_one, gain_one, grad_a)
    grad_visual = grad_x[:VIS].reshape(visual.shape)
    grad_conditioning = grad_x[VIS : VIS + conditioning.shape[1] * COND].reshape(conditioning.shape)

    role_grad = jnp.einsum("rd,re->de", a.reshape(STREAMS * ROWS, D), flat, preferred_element_type=F32)
    role_bias = jnp.sum(flat, axis=0, dtype=F32)
    grad_w_qkv = jnp.zeros((D, 3 * D), BF16)
    grad_b_qkv = jnp.zeros((3 * D,), F32)
    for part in range(3):
        cut = slice(part * GW, (part + 1) * GW)
        at = part * D + group * GW
        grad_w_qkv = lax.dynamic_update_slice_in_dim(grad_w_qkv, role_grad[:, cut].astype(BF16), at, 1)
        grad_b_qkv = lax.dynamic_update_slice_in_dim(grad_b_qkv, role_bias[cut], at, 0)
    grad_w_in = jnp.einsum("rd,rh->dh", n, grad_u, preferred_element_type=F32)
    grad_w_out = jnp.einsum("rh,rd->hd", hidden, dy, preferred_element_type=F32)
    grad_w_proj = jnp.einsum("rd,re->de", attended, grad_hb, preferred_element_type=F32)

    def reduce(g, kind):
        return lax.psum_scatter(g.astype(kind), ("dp", "stream"), scatter_dimension=0, tiled=True).astype(F32)

    return (
        out_visual, out_conditioning, grad_visual, grad_conditioning,
        reduce(grad_ln1_gain, F32), reduce(grad_ln1_bias, F32), reduce(grad_w_qkv, BF16),
        reduce(grad_b_qkv[: 2 * D], F32), reduce(grad_b_qkv[2 * D :], F32), reduce(grad_w_proj, BF16),
        reduce(grad_b_proj, F32), reduce(grad_ln2_gain, F32), reduce(grad_ln2_bias, F32), reduce(grad_w_in, BF16),
        reduce(grad_b_in, F32), reduce(grad_w_out, BF16), reduce(grad_b_out, F32),
    )


def solution(mesh):
    rows = P("dp", None, "stream", None)
    extra = P("dp", "stream", None, None)
    vector = P(("dp", "stream"))
    matrix = P(("dp", "stream"), None)
    in_specs = (rows, extra, rows, extra, P("dp", None), P("dp", None, None)) + (P(),) * 12
    out_specs = (
        rows, extra, rows, extra, vector, vector, matrix, vector, vector, matrix, vector, vector, vector, matrix,
        vector, matrix, vector,
    )
    return jax.shard_map(per_device, mesh=mesh, in_specs=in_specs, out_specs=out_specs, check_vma=False)
```

```python
import functools
import math

import jax
import jax.numpy as jnp
import numpy as np
from jax import lax
from jax.experimental import pallas as pl
from jax.experimental.pallas import tpu as pltpu
from jax.sharding import PartitionSpec as P

D = 1024
HEADS = 16
HEAD_DIM = 64
GRID = 16
COND = 2
FRAMES = 8
MOST = 5
MIDDLE = 7
STREAMS = 4
GROUP = 4
GW = GROUP * HEAD_DIM
PART = 64
PATCHES = 256
VIS = FRAMES * PART
CROWS = 16
ROWS = VIS + CROWS
WIDE = GROUP * 128
NEG = -1e30
EPS = 1e-06
F32 = jnp.float32
BF16 = jnp.bfloat16
VM = pltpu.VMEM
FULL = pl.BlockSpec(memory_space=pltpu.VMEM)
ANYM = pl.BlockSpec(memory_space=pltpu.HBM)
LIMIT = 60 * 1024 * 1024


def nn(a, b):
    return lax.dot_general(a, b, (((1,), (0,)), ((), ())), preferred_element_type=F32)


def nt(a, b):
    return lax.dot_general(a, b, (((1,), (1,)), ((), ())), preferred_element_type=F32)


def rope_constants():
    pair = np.arange(HEAD_DIM // 2)
    exponent = np.where(pair < 30, (pair % 10) / 10.0, 0.0).astype(np.float32)
    freq = np.exp(-math.log(10000.0) * exponent).astype(np.float32)
    patch = np.arange(PATCHES)
    slot_time = np.array([0, 1, 2, 3, 4, 0, 1, 0])
    is_time = (pair < 10)[None, :]
    place = np.where(
        (pair >= 20)[None, :], (patch % GRID)[:, None], (patch // GRID)[:, None]
    ) * ((pair >= 10) & (pair < 30))[None, :]
    angle_patch = (place * freq[None, :]).astype(np.float32)
    angle_time = (slot_time[:, None] * freq[None, :]).astype(np.float32)
    cos_patch = np.where(is_time, 0.0, np.cos(angle_patch))
    sin_patch = np.where(is_time, 0.0, np.sin(angle_patch))
    cos_time = np.where(is_time, np.cos(angle_time), 0.0)
    sin_time = np.where(is_time, np.sin(angle_time), 0.0)

    def spread(table, signed):
        two = np.repeat(table, 2, axis=1)
        if signed:
            two = two * np.where(np.arange(HEAD_DIM) % 2 == 0, -1.0, 1.0)[None, :]
        return np.tile(two, (1, GROUP)).astype(np.float32)

    return (
        spread(cos_patch, False),
        spread(sin_patch, True),
        spread(cos_time, False),
        spread(sin_time, True),
    )


def swap_pairs(v):
    lane = lax.broadcasted_iota(jnp.int32, v.shape, 1)
    width = v.shape[1]
    return jnp.where(lane % 2 == 0, pltpu.roll(v, width - 1, 1), pltpu.roll(v, 1, 1))


def turn(v, cosine, sine):
    return v * cosine + swap_pairs(v) * sine


def pad_heads(t, extra):
    pieces = []
    for h in range(GROUP):
        pieces += [t[:, h * HEAD_DIM : (h + 1) * HEAD_DIM], extra]
    return jnp.concatenate(pieces, axis=1)


def unpad_heads(t):
    return jnp.concatenate([t[:, h * 128 : h * 128 + HEAD_DIM] for h in range(GROUP)], axis=1)


def head(t, h):
    return t[:, h * 128 : (h + 1) * 128]


def first_slot(i):
    return jnp.where(i < MOST, 0, jnp.where(i < MIDDLE, MOST, MIDDLE))


def cond_tables(cs_col, ct, st):
    cosine = jnp.zeros((PART, GW), F32)
    sine = jnp.zeros((PART, GW), F32)
    for j in range(FRAMES):
        here = cs_col == j
        cosine = cosine + jnp.where(here, ct[j : j + 1, :], 0.0)
        sine = sine + jnp.where(here, st[j : j + 1, :], 0.0)
    lane = lax.broadcasted_iota(jnp.int32, (PART, GW), 1) % HEAD_DIM
    return jnp.where(lane < 20, cosine, 1.0), sine


def forward_kernel(
    perm, x_ref, wq_ref, wk_ref, wv_ref, bq_ref, bk_ref, bv_ref, g_ref, b_ref,
    cg_ref, sg_ref, ct_ref, st_ref, bias_ref, csc_ref, csr_ref,
    a_ref, q_ref, k_ref, v_ref, qc_ref, kc_ref, vc_ref, lse_ref, lsec_ref, o_ref,
    vt_ref,
):
    gain, shift = g_ref[...], b_ref[...]
    bq, bk, bv = bq_ref[...], bk_ref[...], bv_ref[...]
    cs_col, cs_row = csc_ref[...], csr_ref[...]
    bias_t = jnp.transpose(bias_ref[...])
    col_id = lax.broadcasted_iota(jnp.int32, (PATCHES, FRAMES), 1)

    def project(x, cosine, sine):
        x = x.astype(F32)
        centre = x - jnp.mean(x, axis=1, keepdims=True)
        spread = jnp.mean(centre * centre, axis=1, keepdims=True)
        a = (centre * lax.rsqrt(spread + EPS) * gain + shift).astype(BF16)
        q = turn(nn(a, wq_ref[...]) + bq, cosine, sine)
        k = turn(nn(a, wk_ref[...]) + bk, cosine, sine)
        v = nn(a, wv_ref[...]) + bv
        return a, (q.astype(BF16).astype(F32) * 0.125).astype(BF16), k.astype(BF16), v

    def lanes(rows):
        return lax.broadcasted_iota(jnp.int32, (rows, 64), 1)

    xc = x_ref[:, VIS:, :].reshape(PART, D)
    a, q, k, v = project(xc, *cond_tables(cs_col, ct_ref[...], st_ref[...]))
    a_ref[:, VIS:, :] = a.reshape(STREAMS, CROWS, D)
    one = jnp.where(lanes(PART) == 0, 1.0, 0.0).astype(BF16)
    zero = jnp.zeros((PART, 64), BF16)
    qc_ref[...] = pad_heads(q, one)
    kc_ref[...] = pad_heads(k, zero)
    vc_ref[...] = pad_heads(v.astype(BF16), zero)
    vct = jnp.transpose(v).astype(BF16)

    def slot(i, carry):
        f = perm[i]
        start = pl.multiple_of(f * PART, PART)
        x = x_ref[:, pl.ds(start, PART), :].reshape(PATCHES, D)
        cosine = cg_ref[...] + ct_ref[pl.ds(i, 1), :]
        sine = sg_ref[...] + st_ref[pl.ds(i, 1), :]
        a, q, k, v = project(x, cosine, sine)
        a_ref[:, pl.ds(start, PART), :] = a.reshape(STREAMS, PART, D)
        lane = lanes(PATCHES)
        bias = jnp.sum(jnp.where(col_id == f, bias_t, 0.0), axis=1, keepdims=True)
        q_ref[i] = pad_heads(q, jnp.where(lane == 0, 1.0, 0.0).astype(BF16))
        k_ref[i] = pad_heads(k, jnp.where(lane == 0, bias, 0.0).astype(BF16))
        v_ref[i] = pad_heads(v.astype(BF16), jnp.zeros((PATCHES, 64), BF16))
        vt_ref[i] = jnp.transpose(v).astype(BF16)
        lo = first_slot(i)
        near = (cs_col >= lo) & (cs_col <= i)
        tops, totals, blends = [], [], []
        for h in range(GROUP):
            s = jnp.where(near, nt(head(kc_ref, h), head(q_ref[i], h)), NEG)
            top = jnp.max(s, axis=0, keepdims=True)
            p = jnp.exp(s - top)
            tops.append(top)
            totals.append(jnp.sum(p, axis=0, keepdims=True))
            blends.append(nn(vct[h * HEAD_DIM : (h + 1) * HEAD_DIM], p.astype(BF16)))

        def step(j, state):
            tops, totals, blends = state
            new = ([], [], [])
            for h in range(GROUP):
                s = nt(k_ref[j, :, h * 128 : (h + 1) * 128], q_ref[i, :, h * 128 : (h + 1) * 128])
                top = jnp.maximum(tops[h], jnp.max(s, axis=0, keepdims=True))
                p = jnp.exp(s - top)
                keep = jnp.exp(tops[h] - top)
                new[0].append(top)
                new[1].append(totals[h] * keep + jnp.sum(p, axis=0, keepdims=True))
                vt = vt_ref[j, h * HEAD_DIM : (h + 1) * HEAD_DIM, :]
                new[2].append(blends[h] * keep + nn(vt, p.astype(BF16)))
            return new

        tops, totals, blends = lax.fori_loop(lo, i + 1, step, (tops, totals, blends))
        o = jnp.transpose(jnp.concatenate([blends[h] / totals[h] for h in range(GROUP)], axis=0))
        o_ref[:, pl.ds(start, PART), :] = o.astype(BF16).reshape(STREAMS, PART, GW)
        lse_ref[i] = jnp.concatenate([tops[h] + jnp.log(totals[h]) for h in range(GROUP)] * 2, axis=0)
        return carry

    lax.fori_loop(0, FRAMES, slot, 0)

    lo_col = first_slot(cs_col)
    near = (cs_row >= lo_col) & (cs_row <= cs_col)
    tops, totals, blends = [], [], []
    for h in range(GROUP):
        s = jnp.where(near, nt(head(qc_ref, h), head(kc_ref, h)), NEG)
        top = jnp.max(s, axis=1, keepdims=True)
        p = jnp.exp(s - top)
        tops.append(top)
        totals.append(jnp.sum(p, axis=1, keepdims=True))
        blends.append(nn(p.astype(BF16), head(vc_ref, h)))

    def cond_step(j, state):
        tops, totals, blends = state
        near = (lo_col <= j) & (cs_col >= j)
        new = ([], [], [])
        for h in range(GROUP):
            s = nt(head(qc_ref, h), k_ref[j, :, h * 128 : (h + 1) * 128])
            s = jnp.where(near, s, NEG)
            top = jnp.maximum(tops[h], jnp.max(s, axis=1, keepdims=True))
            p = jnp.exp(s - top)
            keep = jnp.exp(tops[h] - top)
            new[0].append(top)
            new[1].append(totals[h] * keep + jnp.sum(p, axis=1, keepdims=True))
            new[2].append(blends[h] * keep + nn(p.astype(BF16), v_ref[j, :, h * 128 : (h + 1) * 128]))
        return new

    tops, totals, blends = lax.fori_loop(0, FRAMES, cond_step, (tops, totals, blends))
    o = jnp.concatenate([(blends[h] / totals[h])[:, :HEAD_DIM] for h in range(GROUP)], axis=1)
    o_ref[:, VIS:, :] = o.astype(BF16).reshape(STREAMS, CROWS, GW)
    lane = lax.broadcasted_iota(jnp.int32, (PART, 128), 1)
    lsec = jnp.zeros((PART, 128), F32)
    for h in range(GROUP):
        lsec = lsec + jnp.where(lane == h, tops[h] + jnp.log(totals[h]), 0.0)
    lsec_ref[...] = lsec


def whole(shape):
    return pl.BlockSpec(shape, lambda i, s: (0,) * len(shape))


def attend_forward(scalars, x, w_qkv, b_qkv, gain, shift, tables, bias, cs_col, cs_row):
    def weight(part):
        return pl.BlockSpec((D, GW), lambda i, s: (0, s[8] + part * GROUP))

    def offset(part):
        return pl.BlockSpec((1, GW), lambda i, s: (0, s[8] + part * GROUP))

    shapes = (
        ((STREAMS, ROWS, D), BF16),
        ((FRAMES, PATCHES, WIDE), BF16),
        ((FRAMES, PATCHES, WIDE), BF16),
        ((FRAMES, PATCHES, WIDE), BF16),
        ((PART, WIDE), BF16),
        ((PART, WIDE), BF16),
        ((PART, WIDE), BF16),
        ((FRAMES, 8, PATCHES), F32),
        ((PART, 128), F32),
        ((STREAMS, ROWS, GW), BF16),
    )
    ops = (x, w_qkv, w_qkv, w_qkv, b_qkv, b_qkv, b_qkv, gain, shift) + tables + (bias, cs_col, cs_row)
    specs = [whole(x.shape), weight(0), weight(1), weight(2), offset(0), offset(1), offset(2)]
    specs += [whole(t.shape) for t in ops[7:]]
    return pl.pallas_call(
        forward_kernel,
        name="attend_forward",
        out_shape=tuple(jax.ShapeDtypeStruct(s, t) for s, t in shapes),
        grid_spec=pltpu.PrefetchScalarGridSpec(
            num_scalar_prefetch=1,
            grid=(1,),
            in_specs=specs,
            out_specs=tuple(whole(s) for s, _ in shapes),
            scratch_shapes=[VM((FRAMES, GW, PATCHES), BF16)],
        ),
        compiler_params=pltpu.CompilerParams(vmem_limit_bytes=LIMIT),
        cost_estimate=pl.CostEstimate(flops=8 * 10**9, bytes_accessed=2 * 10**7, transcendentals=6 * 10**6),
    )(scalars, *ops)


def backward_kernel(
    perm, q_ref, k_ref, v_ref, qc_ref, kc_ref, vc_ref, lse_ref, lsec_ref, o_ref, do_ref,
    cg_ref, sg_ref, ct_ref, st_ref, csc_ref, csr_ref,
    g_ref, dk_ref, dv_ref, dkc_ref, dvc_ref, kt_ref,
):
    cs_col, cs_row = csc_ref[...], csr_ref[...]
    dk_ref[...] = jnp.zeros_like(dk_ref)
    dv_ref[...] = jnp.zeros_like(dv_ref)
    dkc_ref[...] = jnp.zeros_like(dkc_ref)
    dvc_ref[...] = jnp.zeros_like(dvc_ref)
    kct = jnp.transpose(unpad_heads(kc_ref[...].astype(F32))).astype(BF16)

    def slot(i, carry):
        f = perm[i]
        start = pl.multiple_of(f * PART, PART)
        do = do_ref[:, pl.ds(start, PART), :].reshape(PATCHES, GW)
        o = o_ref[:, pl.ds(start, PART), :].reshape(PATCHES, GW)
        prod = jnp.transpose(do.astype(F32) * o.astype(F32))
        deltas = [
            jnp.sum(prod[h * HEAD_DIM : (h + 1) * HEAD_DIM], axis=0, keepdims=True)
            for h in range(GROUP)
        ]
        dop = pad_heads(do, jnp.zeros((PATCHES, 64), BF16))
        kt_ref[i] = jnp.transpose(unpad_heads(k_ref[i].astype(F32))).astype(BF16)
        lo = first_slot(i)
        near = (cs_col >= lo) & (cs_col <= i)
        dqs = []
        for h in range(GROUP):
            cols = slice(h * 128, (h + 1) * 128)
            q = q_ref[i, :, cols]
            s = jnp.where(near, nt(kc_ref[:, cols], q), NEG)
            p = jnp.exp(s - lse_ref[i, h : h + 1, :])
            dp = nt(vc_ref[:, cols], dop[:, cols])
            ds = (p * (dp - deltas[h])).astype(BF16)
            dvc_ref[:, cols] += nn(p.astype(BF16), dop[:, cols])
            dkc_ref[:, cols] += nn(ds, q)
            dqs.append(nn(kct[h * HEAD_DIM : (h + 1) * HEAD_DIM], ds))

        def step(j, dqs):
            new = []
            for h in range(GROUP):
                cols = slice(h * 128, (h + 1) * 128)
                q = q_ref[i, :, cols]
                p = jnp.exp(nt(k_ref[j, :, cols], q) - lse_ref[i, h : h + 1, :])
                dp = nt(v_ref[j, :, cols], dop[:, cols])
                ds = (p * (dp - deltas[h])).astype(BF16)
                dv_ref[j, :, cols] += nn(p.astype(BF16), dop[:, cols])
                dk_ref[j, :, cols] += nn(ds, q)
                new.append(dqs[h] + nn(kt_ref[j, h * HEAD_DIM : (h + 1) * HEAD_DIM, :], ds))
            return new

        dqs = lax.fori_loop(lo, i + 1, step, dqs)
        dq = jnp.transpose(jnp.concatenate(dqs, axis=0)) * 0.125
        cosine = cg_ref[...] + ct_ref[pl.ds(i, 1), :]
        sine = sg_ref[...] + st_ref[pl.ds(i, 1), :]
        dq = turn(dq, cosine, -sine).astype(BF16).reshape(STREAMS, PART, GW)
        g_ref[:, pl.ds(start, PART), 0:GW] = dq
        return carry

    lax.fori_loop(0, FRAMES, slot, 0)

    doc = do_ref[:, VIS:, :].reshape(PART, GW)
    oc = o_ref[:, VIS:, :].reshape(PART, GW)
    docp = pad_heads(doc, jnp.zeros((PART, 64), BF16))
    prod = doc.astype(F32) * oc.astype(F32)
    lo_col = first_slot(cs_col)
    near = (cs_row >= lo_col) & (cs_row <= cs_col)
    deltas = [
        jnp.sum(prod[:, h * HEAD_DIM : (h + 1) * HEAD_DIM], axis=1, keepdims=True)
        for h in range(GROUP)
    ]
    lses = [lsec_ref[:, h : h + 1] for h in range(GROUP)]
    dqs = []
    for h in range(GROUP):
        cols = slice(h * 128, (h + 1) * 128)
        s = jnp.where(near, nt(qc_ref[:, cols], kc_ref[:, cols]), NEG)
        p = jnp.exp(s - lses[h])
        ds = p * (nt(docp[:, cols], vc_ref[:, cols]) - deltas[h])
        dvc_ref[:, cols] += nn(jnp.transpose(p).astype(BF16), docp[:, cols])
        dkc_ref[:, cols] += nn(jnp.transpose(ds).astype(BF16), qc_ref[:, cols])
        dqs.append(nn(ds.astype(BF16), kc_ref[:, cols]))

    def cond_step(j, dqs):
        near = (lo_col <= j) & (cs_col >= j)
        new = []
        for h in range(GROUP):
            cols = slice(h * 128, (h + 1) * 128)
            s = jnp.where(near, nt(qc_ref[:, cols], k_ref[j, :, cols]), NEG)
            p = jnp.exp(s - lses[h])
            ds = p * (nt(docp[:, cols], v_ref[j, :, cols]) - deltas[h])
            dv_ref[j, :, cols] += nn(jnp.transpose(p).astype(BF16), docp[:, cols])
            dk_ref[j, :, cols] += nn(jnp.transpose(ds).astype(BF16), qc_ref[:, cols])
            new.append(dqs[h] + nn(ds.astype(BF16), k_ref[j, :, cols]))
        return new

    dqs = lax.fori_loop(0, FRAMES, cond_step, dqs)
    cosine, sine = cond_tables(cs_col, ct_ref[...], st_ref[...])
    valid = cs_col < FRAMES
    dq = jnp.concatenate([t[:, :HEAD_DIM] for t in dqs], axis=1) * 0.125
    for part, t in ((0, turn(dq, cosine, -sine)), (1, turn(unpad_heads(dkc_ref[...]), cosine, -sine)), (2, unpad_heads(dvc_ref[...]))):
        t = jnp.where(valid, t, 0.0).astype(BF16)
        g_ref[:, VIS:, part * GW : (part + 1) * GW] = t.reshape(STREAMS, CROWS, GW)

    def finish(i, carry):
        start = pl.multiple_of(perm[i] * PART, PART)
        cosine = cg_ref[...] + ct_ref[pl.ds(i, 1), :]
        sine = sg_ref[...] + st_ref[pl.ds(i, 1), :]
        dk = turn(unpad_heads(dk_ref[i]), cosine, -sine)
        g_ref[:, pl.ds(start, PART), GW : 2 * GW] = dk.astype(BF16).reshape(STREAMS, PART, GW)
        dv = unpad_heads(dv_ref[i])
        g_ref[:, pl.ds(start, PART), 2 * GW :] = dv.astype(BF16).reshape(STREAMS, PART, GW)
        return carry

    lax.fori_loop(0, FRAMES, finish, 0)


def attend_backward(scalars, saved, o, do, tables, cs_col, cs_row):
    ops = tuple(saved) + (o, do) + tables + (cs_col, cs_row)
    out = (STREAMS, ROWS, 3 * GW)
    return pl.pallas_call(
        backward_kernel,
        name="attend_backward",
        out_shape=jax.ShapeDtypeStruct(out, BF16),
        grid_spec=pltpu.PrefetchScalarGridSpec(
            num_scalar_prefetch=1,
            grid=(1,),
            in_specs=[whole(t.shape) for t in ops],
            out_specs=whole(out),
            scratch_shapes=[
                VM((FRAMES, PATCHES, WIDE), F32),
                VM((FRAMES, PATCHES, WIDE), F32),
                VM((PART, WIDE), F32),
                VM((PART, WIDE), F32),
                VM((FRAMES, GW, PATCHES), BF16),
            ],
        ),
        compiler_params=pltpu.CompilerParams(vmem_limit_bytes=LIMIT),
        cost_estimate=pl.CostEstimate(flops=10**10, bytes_accessed=2 * 10**7, transcendentals=6 * 10**6),
    )(scalars, *ops)


def where_am_i():
    d, z = lax.axis_index("dp"), lax.axis_index("stream")
    return d // 2, d % 2, z // 2, z % 2, z


def greet_column():
    p, c, q, r, z = where_am_i()
    barrier = pltpu.get_barrier_semaphore()
    for core in range(2):
        for chip in range(STREAMS):
            @pl.when((core != c) | (chip != z))
            def _():
                pl.semaphore_signal(
                    barrier, inc=1, device_id=(2 * p + core, chip),
                    device_id_type=pl.DeviceIdType.MESH,
                )
    pl.semaphore_wait(barrier, 2 * STREAMS - 1)


def remote(src, dst, send, recv, device):
    return pltpu.make_async_remote_copy(
        src_ref=src, dst_ref=dst, send_sem=send, recv_sem=recv, device_id=device,
        device_id_type=pl.DeviceIdType.MESH,
    )


def comm_call(kernel, name, ident, outs, scratch, *ops):
    return pl.pallas_call(
        kernel,
        name=name,
        out_shape=tuple(jax.ShapeDtypeStruct(s, t) for s, t in outs),
        in_specs=[ANYM] * len(ops),
        out_specs=tuple(ANYM for _ in outs),
        scratch_shapes=scratch,
        compiler_params=pltpu.CompilerParams(
            collective_id=ident, has_side_effects=True, vmem_limit_bytes=LIMIT
        ),
    )(*ops)


def dma(*shape):
    return pltpu.SemaphoreType.DMA(shape)


HALF = VIS // 2


def gather_kernel(x_ref, m_ref, xa_ref, ma_ref, send, recv, csend, crecv, fsend, frecv, lsem, msem):
    p, c, q, r, z = where_am_i()
    greet_column()
    tail = pl.ds(VIS, CROWS)
    for core in range(2):
        rows = pl.ds(core * HALF, HALF)
        for side in range(2):
            n = core * 2 + side
            mine = (core == c) & (2 * c + side == z)
            device = (2 * p + core, 2 * c + side)

            @pl.when(mine)
            def _():
                pltpu.make_async_copy(x_ref.at[rows], xa_ref.at[z, rows], lsem.at[0]).start()
                pltpu.make_async_copy(x_ref.at[tail], xa_ref.at[z, tail], lsem.at[1]).start()

            @pl.when(jnp.logical_not(mine))
            def _():
                remote(x_ref.at[rows], xa_ref.at[z, rows], send.at[n], recv.at[z], device).start()
                remote(x_ref.at[tail], xa_ref.at[z, tail], csend.at[n], crecv.at[z], device).start()

    other = (2 * p + 1 - c, z)

    @pl.when(q == c)
    def _():
        remote(m_ref, ma_ref, msem.at[0], msem.at[1], other).start()
        pltpu.make_async_copy(m_ref, ma_ref, msem.at[2]).start()

    rows = pl.ds(c * HALF, HALF)
    for s in range(STREAMS):
        mine = (q == c) & (s == z)

        @pl.when(mine)
        def _():
            pltpu.make_async_copy(x_ref.at[rows], xa_ref.at[s, rows], lsem.at[0]).wait()
            pltpu.make_async_copy(x_ref.at[tail], xa_ref.at[s, tail], lsem.at[1]).wait()

        @pl.when(jnp.logical_not(mine))
        def _():
            remote(x_ref.at[rows], xa_ref.at[s, rows], send.at[0], recv.at[s], other).wait_recv()
            remote(x_ref.at[tail], xa_ref.at[s, tail], csend.at[0], crecv.at[s], other).wait_recv()

        remote(xa_ref.at[s, rows], xa_ref.at[s, rows], fsend.at[s], frecv.at[s], other).start()
    rest = pl.ds((1 - c) * HALF, HALF)
    for s in range(STREAMS):
        copy = remote(xa_ref.at[s, rest], xa_ref.at[s, rest], fsend.at[s], frecv.at[s], other)
        copy.wait_send()
        copy.wait_recv()
    for core in range(2):
        for side in range(2):
            n = core * 2 + side

            @pl.when((core != c) | (2 * c + side != z))
            def _():
                remote(x_ref.at[rows], xa_ref.at[0, rows], send.at[n], recv.at[0], other).wait_send()
                remote(x_ref.at[tail], xa_ref.at[0, tail], csend.at[n], crecv.at[0], other).wait_send()

    @pl.when(q == c)
    def _():
        remote(m_ref, ma_ref, msem.at[0], msem.at[1], other).wait_send()
        pltpu.make_async_copy(m_ref, ma_ref, msem.at[2]).wait()

    @pl.when(q != c)
    def _():
        remote(m_ref, ma_ref, msem.at[0], msem.at[1], other).wait_recv()


def gather_rows(x, meta):
    return comm_call(
        gather_kernel, "gather_rows", 0,
        (((STREAMS, ROWS, D), BF16), (meta.shape, F32)),
        [dma(4), dma(4), dma(4), dma(4), dma(4), dma(4), dma(2), dma(3)],
        x, meta,
    )


def to_owner_kernel(o_ref, out_ref, send, recv, lsem):
    p, c, q, r, z = where_am_i()
    greet_column()
    group = 2 * r + c
    place = pl.ds(pl.multiple_of(group * GW, GW), GW)
    for s in range(STREAMS):
        mine = (q == c) & (s == z)

        @pl.when(mine)
        def _():
            pltpu.make_async_copy(o_ref.at[s], out_ref.at[:, place], lsem).start()

        @pl.when(jnp.logical_not(mine))
        def _():
            remote(o_ref.at[s], out_ref.at[:, place], send.at[s], recv.at[group], (2 * p + q, s)).start()
    for s in range(STREAMS):
        mine = (q == c) & (s == z)

        @pl.when(mine)
        def _():
            pltpu.make_async_copy(o_ref.at[s], out_ref.at[:, place], lsem).wait()

        @pl.when(jnp.logical_not(mine))
        def _():
            remote(o_ref.at[s], out_ref.at[:, place], send.at[s], recv.at[group], (2 * p + q, s)).wait_send()
    for side in range(2):
        for core in range(2):
            g = 2 * side + core

            @pl.when((core != c) | (2 * c + side != z))
            def _():
                cols = pl.ds(g * GW, GW)
                remote(o_ref.at[0], out_ref.at[:, cols], send.at[0], recv.at[g], (2 * p + q, 0)).wait_recv()


def to_owner(o):
    return comm_call(
        to_owner_kernel, "to_owner", 1, (((ROWS, D), BF16),), [dma(4), dma(4), pltpu.SemaphoreType.DMA], o
    )[0]


def to_heads_kernel(d_ref, out_ref, send, recv, lsem):
    p, c, q, r, z = where_am_i()
    greet_column()
    for side in range(2):
        for core in range(2):
            g = 2 * side + core
            cols = pl.ds(g * GW, GW)
            mine = (core == c) & (2 * c + side == z)

            @pl.when(mine)
            def _():
                pltpu.make_async_copy(d_ref.at[:, cols], out_ref.at[z], lsem).start()

            @pl.when(jnp.logical_not(mine))
            def _():
                remote(d_ref.at[:, cols], out_ref.at[z], send.at[g], recv.at[z], (2 * p + core, 2 * c + side)).start()
    for side in range(2):
        for core in range(2):
            g = 2 * side + core
            cols = pl.ds(g * GW, GW)
            mine = (core == c) & (2 * c + side == z)

            @pl.when(mine)
            def _():
                pltpu.make_async_copy(d_ref.at[:, cols], out_ref.at[z], lsem).wait()

            @pl.when(jnp.logical_not(mine))
            def _():
                remote(d_ref.at[:, cols], out_ref.at[z], send.at[g], recv.at[z], (2 * p + core, 2 * c + side)).wait_send()
    for s in range(STREAMS):
        @pl.when((q != c) | (s != z))
        def _():
            remote(d_ref.at[:, pl.ds(0, GW)], out_ref.at[s], send.at[0], recv.at[s], (2 * p + q, s)).wait_recv()


def to_heads(d):
    return comm_call(
        to_heads_kernel, "to_heads", 2, (((STREAMS, ROWS, GW), BF16),), [dma(4), dma(4), pltpu.SemaphoreType.DMA], d
    )[0]


def sum_rows_kernel(
    d_ref, out_ref, dsend, drecv, send, recv, csend, crecv, lsem, near, mine_buf, own, land, tail, total
):
    p, c, q, r, z = where_am_i()
    greet_column()
    other = (2 * p + 1 - c, z)
    rows = pl.ds(c * HALF, HALF)
    rest = pl.ds((1 - c) * HALF, HALF)
    last = pl.ds(VIS, CROWS)
    for s in range(STREAMS):
        remote(d_ref.at[s, rest], near.at[s], dsend.at[s], drecv.at[s], other).start()
        pltpu.make_async_copy(d_ref.at[s, rows], mine_buf.at[s], lsem.at[s]).start()
    group = 2 * r + c
    for s in range(STREAMS):
        mine = (q == c) & (s == z)

        @pl.when(mine)
        def _():
            pltpu.make_async_copy(d_ref.at[s, last], tail.at[group], lsem.at[4]).start()

        @pl.when(jnp.logical_not(mine))
        def _():
            remote(d_ref.at[s, last], tail.at[group], csend.at[s], crecv.at[group], (2 * p + q, s)).start()
    for s in range(STREAMS):
        mine = (q == c) & (s == z)
        pltpu.make_async_copy(d_ref.at[s, rows], mine_buf.at[s], lsem.at[s]).wait()
        remote(d_ref.at[s, rest], near.at[s], dsend.at[s], drecv.at[s], other).wait_recv()
        for t in range(HALF // 64):
            part = pl.ds(t * 64, 64)
            both = near[s, part].astype(F32) + mine_buf[s, part].astype(F32)
            own[s, part] = both.astype(BF16)

        @pl.when(mine)
        def _():
            pltpu.make_async_copy(own.at[s], land.at[r, rows], lsem.at[5]).start()

        @pl.when(jnp.logical_not(mine))
        def _():
            remote(own.at[s], land.at[r, rows], send.at[s], recv.at[r, c], (2 * p + q, s)).start()
    for s in range(STREAMS):
        mine = (q == c) & (s == z)
        remote(d_ref.at[s, rest], near.at[s], dsend.at[s], drecv.at[s], other).wait_send()

        @pl.when(mine)
        def _():
            pltpu.make_async_copy(d_ref.at[s, last], tail.at[group], lsem.at[4]).wait()
            pltpu.make_async_copy(own.at[s], land.at[r, rows], lsem.at[5]).wait()

        @pl.when(jnp.logical_not(mine))
        def _():
            remote(d_ref.at[s, last], tail.at[group], csend.at[s], crecv.at[group], (2 * p + q, s)).wait_send()
            remote(own.at[s], land.at[r, rows], send.at[s], recv.at[r, c], (2 * p + q, s)).wait_send()
    for side in range(2):
        for core in range(2):
            @pl.when((core != c) | (2 * c + side != z))
            def _():
                part = pl.ds(core * HALF, HALF)
                remote(own.at[0], land.at[side, part], send.at[0], recv.at[side, core], other).wait_recv()
                g = 2 * side + core
                remote(d_ref.at[0, last], tail.at[g], csend.at[0], crecv.at[g], other).wait_recv()
    for t in range(VIS // 64):
        part = pl.ds(t * 64, 64)
        total[part] = land[0, part].astype(F32) + land[1, part].astype(F32)
    ends = [tail[g].astype(F32) for g in range(4)]
    total[last] = (ends[0] + ends[1]) + (ends[2] + ends[3])
    done = pltpu.make_async_copy(total, out_ref, lsem.at[6])
    done.start()
    done.wait()


def sum_rows(d):
    return comm_call(
        sum_rows_kernel, "sum_rows", 3, (((ROWS, D), F32),),
        [
            dma(4), dma(4), dma(4), dma(2, 2), dma(4), dma(4), dma(7),
            VM((STREAMS, HALF, D), BF16), VM((STREAMS, HALF, D), BF16), VM((STREAMS, HALF, D), BF16),
            VM((2, VIS, D), BF16), VM((4, CROWS, D), BF16), VM((ROWS, D), F32),
        ],
        d,
    )[0]


CHUNKS = 9
CUT = D // 2
QCUT = 3 * GW // 2


def add_up(*terms):
    total = terms[0].astype(F32)
    for t in terms[1:]:
        total = total + t.astype(F32)
    return total


def reduce_kernel(
    nx, ny, rb,
    go_ref, gi_ref, gp_ref, gq_ref, v_ref,
    oo_ref, oi_ref, op_ref, oq_ref, ov_ref,
    mine, rd, r2a, r2b, s2a, s2b, r3a, r3b, s3, r4, s4, r5, fin,
    q1, rq1a, rq1b, sq1a, sq1b, rq2a, rq2b, sq2, rq3, sq3, vm, vd, vx, vy, vz1, vz2,
    lsem, ds, dr, as2, ar2, bs2, br2, as3, ar3, bs3, br3, s4s, s4r, s5s, s5r,
    qs1a, qr1a, qs1b, qr1b, qs2a, qr2a, qs2b, qr2b, qs3, qr3, qs4, qr4, vs, vr, vsx, vrx, vsy, vry, osem,
):
    d, z = lax.axis_index("dp"), lax.axis_index("stream")
    p, c, hi, lo = d // 2, d % 2, z // 2, z % 2
    x, y = p % nx, p // nx
    near = (d + 1 - 2 * c, z)
    z_one = (d, z + 1 - 2 * lo)
    z_two = (d, z + 2 - 4 * hi)
    slant = (d + 1 - 2 * c, z + 1 - 2 * lo)

    def along_x(n):
        return lax.rem(x + n, nx)

    def along_y(n):
        return lax.rem(y + n, ny)

    def x_device(n):
        return ((y * nx + along_x(n)) * 2 + c, z)

    def y_device(n):
        return ((along_y(n) * nx + x) * 2 + c, z)

    barrier = pltpu.get_barrier_semaphore()
    friends = [near, z_one, z_two, slant]
    friends += [x_device(n) for n in range(1, nx)] + [y_device(n) for n in range(1, ny)]
    for device in friends:
        pl.semaphore_signal(barrier, inc=1, device_id=device, device_id_type=pl.DeviceIdType.MESH)
    pl.semaphore_wait(barrier, len(friends))

    first, second = pl.ds(0, CUT), pl.ds(CUT, CUT)

    def source(k, core):
        if k < 4:
            return go_ref.at[:, :, core, :, k]
        if k < 8:
            return gi_ref.at[:, :, core, :, :, pl.ds((k - 4) * D, D)]
        return gp_ref.at[:, :, core]

    def core_copy(k):
        return remote(source(k, 1 - c), rd.at[k], ds.at[k], dr.at[k], near)

    def own_copy(k):
        return pltpu.make_async_copy(source(k, c), mine.at[k], lsem.at[k])

    def a2(k, n):
        return remote(mine.at[k, :, along_x(n), :, :, first], r2a.at[k, n - 1], as2.at[k, n - 1], ar2.at[k, n - 1], x_device(n))

    def b2(k, n):
        return remote(mine.at[k, along_y(n), :, :, :, second], r2b.at[k, n - 1], bs2.at[k, n - 1], br2.at[k, n - 1], y_device(n))

    def a3(k, n):
        return remote(s2a.at[k, along_y(n)], r3a.at[k, n - 1], as3.at[k, n - 1], ar3.at[k, n - 1], y_device(n))

    def b3(k, n):
        return remote(s2b.at[k, along_x(n)], r3b.at[k, n - 1], bs3.at[k, n - 1], br3.at[k, n - 1], x_device(n))

    def c4(k):
        return remote(s3.at[k, :, 1 - lo], r4.at[k], s4s.at[k], s4r.at[k], z_one)

    def c5(k):
        return remote(s4.at[k, 1 - hi], r5.at[k], s5s.at[k], s5r.at[k], z_two)

    qa, qb = pl.ds(0, QCUT), pl.ds(QCUT, QCUT)

    def q1a(n):
        return remote(q1.at[:, along_x(n), :, :, qa], rq1a.at[n - 1], qs1a.at[n - 1], qr1a.at[n - 1], x_device(n))

    def q1b(n):
        return remote(q1.at[along_y(n), :, :, :, qb], rq1b.at[n - 1], qs1b.at[n - 1], qr1b.at[n - 1], y_device(n))

    def q2a(n):
        return remote(sq1a.at[along_y(n)], rq2a.at[n - 1], qs2a.at[n - 1], qr2a.at[n - 1], y_device(n))

    def q2b(n):
        return remote(sq1b.at[along_x(n)], rq2b.at[n - 1], qs2b.at[n - 1], qr2b.at[n - 1], x_device(n))

    def q3():
        return remote(sq2.at[:, 1 - hi], rq3, qs3, qr3, z_two)

    group = 2 * lo + c
    mates = [(near, 1, 0), (z_one, 0, 1), (slant, 1, 1)]

    def q4(n, part):
        device, core, side = mates[n]
        to_core = c + core - 2 * c * core
        to_side = lo + side - 2 * lo * side
        place = pl.ds(pl.multiple_of(part * D + group * GW, GW), GW)
        return remote(
            sq3.at[to_core, to_side, :, pl.ds(part * GW, GW)], oq_ref.at[:, place],
            qs4.at[n, part], qr4.at[n, part], device,
        )

    def q4_own(part):
        place = pl.ds(pl.multiple_of(part * D + group * GW, GW), GW)
        return pltpu.make_async_copy(sq3.at[c, lo, :, pl.ds(part * GW, GW)], oq_ref.at[:, place], lsem.at[CHUNKS + 2 + part])

    def v_core():
        return remote(v_ref.at[:, :, 1 - c], vd, vs.at[0], vr.at[0], near)

    def v_x(n):
        return remote(vm.at[:, along_x(n)], vx.at[n - 1], vsx.at[n - 1], vrx.at[n - 1], x_device(n))

    def v_y(n):
        return remote(vm.at[along_y(n), x], vy.at[n - 1], vsy.at[n - 1], vry.at[n - 1], y_device(n))

    def v_z1():
        return remote(vm.at[y, x, :, 1 - lo], vz1, vs.at[1], vr.at[1], z_one)

    def v_z2():
        return remote(vm.at[y, x, 1 - hi, lo], vz2, vs.at[2], vr.at[2], z_two)

    q_own = pltpu.make_async_copy(gq_ref, q1, lsem.at[CHUNKS])
    v_own = pltpu.make_async_copy(v_ref.at[:, :, c], vm, lsem.at[CHUNKS + 1])
    v_own.start()
    v_core().start()
    q_own.start()
    for k in range(CHUNKS):
        core_copy(k).start()
        own_copy(k).start()
    q_own.wait()
    for n in range(1, nx):
        q1a(n).start()
    for n in range(1, ny):
        q1b(n).start()

    def at(k, value, body):
        pl.when(k == value)(body)

    def q_second():
        for n in range(1, nx):
            q1a(n).wait_recv()
        for n in range(1, ny):
            q1b(n).wait_recv()
        for b in range(ny):
            sq1a[b] = add_up(q1[b, x, :, :, 0:QCUT], *[rq1a[n, b] for n in range(nx - 1)]).astype(BF16)
        for n in range(1, ny):
            q2a(n).start()
        for b in range(nx):
            sq1b[b] = add_up(q1[y, b, :, :, QCUT:], *[rq1b[n, b] for n in range(ny - 1)]).astype(BF16)
        for n in range(1, nx):
            q2b(n).start()

    def q_third():
        for n in range(1, ny):
            q2a(n).wait_recv()
        for n in range(1, nx):
            q2b(n).wait_recv()
        left = add_up(sq1a[y], *[rq2a[n] for n in range(ny - 1)]).astype(BF16)
        right = add_up(sq1b[x], *[rq2b[n] for n in range(nx - 1)]).astype(BF16)
        sq2[:, :, :, :, 0:QCUT] = left.reshape(2, 2, 2, rb, QCUT)
        sq2[:, :, :, :, QCUT:] = right.reshape(2, 2, 2, rb, QCUT)
        q3().start()

    def q_fourth():
        q3().wait_recv()
        sq3[...] = add_up(sq2[:, hi], rq3[...])
        for part in range(3):
            for n in range(3):
                q4(n, part).start()
            q4_own(part).start()

    def v_first():
        v_own.wait()
        v_core().wait_recv()
        vm[...] = vm[...] + vd[...]
        for n in range(1, nx):
            v_x(n).start()

    def v_second():
        for n in range(1, nx):
            v_x(n).wait_recv()
        for b in range(ny):
            vm[b, x] = add_up(vm[b, x], *[vx[n, b] for n in range(nx - 1)])
        for n in range(1, ny):
            v_y(n).start()

    def v_third():
        for n in range(1, ny):
            v_y(n).wait_recv()
        vm[y, x] = add_up(vm[y, x], *[vy[n] for n in range(ny - 1)])
        v_z1().start()

    def v_fourth():
        v_z1().wait_recv()
        vm[y, x, :, lo] = vm[y, x, :, lo] + vz1[...]
        v_z2().start()

    def turn_loop(k, carry):
        @pl.when(k < CHUNKS)
        def _():
            own_copy_k = pltpu.make_async_copy(gp_ref.at[:, :, c], mine.at[k], lsem.at[k])
            own_copy_k.wait()
            remote(gp_ref.at[:, :, 1 - c], rd.at[k], ds.at[k], dr.at[k], near).wait_recv()
            for b in range(ny):
                for e in range(nx):
                    mine[k, b, e] = add_up(mine[k, b, e], rd[k, b, e]).astype(BF16)
            for n in range(1, nx):
                a2(k, n).start()
            for n in range(1, ny):
                b2(k, n).start()

        at(k, 0, v_first)
        at(k, 1, v_second)
        at(k, 2, v_third)
        at(k, 3, v_fourth)
        at(k, 1, q_second)
        at(k, 3, q_third)
        at(k, 5, q_fourth)

        @pl.when((k >= 1) & (k < CHUNKS + 1))
        def _():
            j = k - 1
            for n in range(1, nx):
                a2(j, n).wait_recv()
            for b in range(ny):
                s2a[j, b] = add_up(mine[j, b, x, :, :, 0:CUT], *[r2a[j, n, b] for n in range(nx - 1)]).astype(BF16)
            for n in range(1, ny):
                a3(j, n).start()
            for n in range(1, ny):
                b2(j, n).wait_recv()
            for b in range(nx):
                s2b[j, b] = add_up(mine[j, y, b, :, :, CUT:], *[r2b[j, n, b] for n in range(ny - 1)]).astype(BF16)
            for n in range(1, nx):
                b3(j, n).start()

        @pl.when((k >= 2) & (k < CHUNKS + 2))
        def _():
            j = k - 2
            for n in range(1, ny):
                a3(j, n).wait_recv()
            for n in range(1, nx):
                b3(j, n).wait_recv()
            left = add_up(s2a[j, y], *[r3a[j, n] for n in range(ny - 1)]).astype(BF16)
            right = add_up(s2b[j, x], *[r3b[j, n] for n in range(nx - 1)]).astype(BF16)
            s3[j, :, :, :, 0:CUT] = left.reshape(2, 2, rb, CUT)
            s3[j, :, :, :, CUT:] = right.reshape(2, 2, rb, CUT)
            c4(j).start()

        @pl.when((k >= 3) & (k < CHUNKS + 3))
        def _():
            j = k - 3
            c4(j).wait_recv()
            s4[j] = add_up(s3[j, :, lo], r4[j]).astype(BF16)
            c5(j).start()

        @pl.when(k >= 4)
        def _():
            j = k - 4
            c5(j).wait_recv()
            fin[j] = add_up(s4[j, hi], r5[j])

        return carry

    lax.fori_loop(0, CHUNKS + 4, turn_loop, 0)
    v_z2().wait_recv()
    vm[y, x, hi, lo] = vm[y, x, hi, lo] + vz2[...]
    outs = [pltpu.make_async_copy(fin.at[k], oo_ref.at[k], osem.at[k]) for k in range(4)]
    outs += [
        pltpu.make_async_copy(fin.at[4 + k], oi_ref.at[:, pl.ds(k * D, D)], osem.at[4 + k]) for k in range(4)
    ]
    outs += [pltpu.make_async_copy(fin.at[8], op_ref, osem.at[8])]
    outs += [pltpu.make_async_copy(vm.at[y, x, hi, lo], ov_ref, osem.at[9])]
    for copy in outs:
        copy.start()

    def drain(k, carry):
        remote(gp_ref.at[:, :, 1 - c], rd.at[k], ds.at[k], dr.at[k], near).wait_send()
        for n in range(1, nx):
            a2(k, n).wait_send()
            b3(k, n).wait_send()
        for n in range(1, ny):
            b2(k, n).wait_send()
            a3(k, n).wait_send()
        c4(k).wait_send()
        c5(k).wait_send()
        return carry

    lax.fori_loop(0, CHUNKS, drain, 0)
    for n in range(1, nx):
        q1a(n).wait_send()
        q2b(n).wait_send()
        v_x(n).wait_send()
    for n in range(1, ny):
        q1b(n).wait_send()
        q2a(n).wait_send()
        v_y(n).wait_send()
    q3().wait_send()
    v_core().wait_send()
    v_z1().wait_send()
    v_z2().wait_send()
    for part in range(3):
        q4_own(part).wait()
        for n in range(3):
            q4(n, part).wait_send()
            q4(n, part).wait_recv()
    for copy in outs:
        copy.wait()


def reduce_grads(g_out, g_in, g_proj, g_qkv, vectors):
    cores = lax.axis_size("dp") // 2
    nx = 1 << ((cores.bit_length() - 1) // 2)
    ny = cores // nx
    rb = D // (cores * 2 * STREAMS)

    def v(*shape):
        return VM(shape, BF16)

    def vf(*shape):
        return VM(shape, F32)

    n = CHUNKS
    scratch = [
        v(n, ny, nx, STREAMS, rb, D), v(n, ny, nx, STREAMS, rb, D),
        v(n, nx - 1, ny, STREAMS, rb, CUT), v(n, ny - 1, nx, STREAMS, rb, CUT),
        v(n, ny, STREAMS, rb, CUT), v(n, nx, STREAMS, rb, CUT),
        v(n, ny - 1, STREAMS, rb, CUT), v(n, nx - 1, STREAMS, rb, CUT),
        v(n, 2, 2, rb, D), v(n, 2, rb, D), v(n, 2, rb, D), v(n, rb, D), vf(n, rb, D),
        v(ny, nx, 8, rb, 3 * GW), v(nx - 1, ny, 8, rb, QCUT), v(ny - 1, nx, 8, rb, QCUT),
        v(ny, 8, rb, QCUT), v(nx, 8, rb, QCUT), v(ny - 1, 8, rb, QCUT), v(nx - 1, 8, rb, QCUT),
        v(2, 2, 2, rb, 3 * GW), v(2, 2, rb, 3 * GW), vf(2, 2, rb, 3 * GW),
        vf(ny, nx, 2, 2, 8, 128), vf(ny, nx, 2, 2, 8, 128), vf(nx - 1, ny, 2, 2, 8, 128),
        vf(ny - 1, 2, 2, 8, 128), vf(2, 8, 128), vf(8, 128),
        dma(n + 5), dma(n), dma(n),
        dma(n, nx - 1), dma(n, nx - 1), dma(n, ny - 1), dma(n, ny - 1),
        dma(n, ny - 1), dma(n, ny - 1), dma(n, nx - 1), dma(n, nx - 1),
        dma(n), dma(n), dma(n), dma(n),
        dma(nx - 1), dma(nx - 1), dma(ny - 1), dma(ny - 1), dma(ny - 1), dma(ny - 1), dma(nx - 1), dma(nx - 1),
        pltpu.SemaphoreType.DMA, pltpu.SemaphoreType.DMA, dma(3, 3), dma(3, 3),
        dma(3), dma(3), dma(nx - 1), dma(nx - 1), dma(ny - 1), dma(ny - 1), dma(10),
    ]
    outs = (((4, rb, D), F32), ((rb, 4 * D), F32), ((rb, D), F32), ((rb, 3 * D), F32), ((8, 128), F32))
    return comm_call(
        functools.partial(reduce_kernel, nx, ny, rb), "reduce_grads", 4, outs, scratch,
        g_out.reshape(ny, nx, 2, STREAMS, 4, rb, D), g_in.reshape(ny, nx, 2, STREAMS, rb, 4 * D),
        g_proj.reshape(ny, nx, 2, STREAMS, rb, D), g_qkv.reshape(ny, nx, 8, rb, 3 * GW),
        vectors.reshape(ny, nx, 2, 2, 2, 8, 128),
    )


def layer_norm(values, norm_gain, norm_shift):
    centre = values - jnp.mean(values, axis=-1, keepdims=True)
    spread = jnp.mean(centre * centre, axis=-1, keepdims=True)
    return centre * lax.rsqrt(spread + EPS) * norm_gain + norm_shift


def norm_parts(values):
    centre = values - jnp.mean(values, axis=-1, keepdims=True)
    scale = lax.rsqrt(jnp.mean(centre * centre, axis=-1, keepdims=True) + EPS)
    return centre * scale, scale


def norm_back(normed, scale, gain, grad):
    g = grad * gain
    return scale * (
        g - jnp.mean(g, axis=-1, keepdims=True) - normed * jnp.mean(g * normed, axis=-1, keepdims=True)
    )


def own_meta(lengths, mask):
    frames = jnp.arange(FRAMES, dtype=jnp.int32)
    ends = jnp.cumsum(lengths)
    reached = ends[None, :] <= frames[:, None]
    begin = jnp.sum(jnp.where(reached, lengths[None, :], 0), axis=1)
    length = jnp.sum(
        jnp.where((jnp.sum(reached, axis=1)[:, None] == jnp.arange(3)[None, :]), lengths[None, :], 0), axis=1
    )
    base = jnp.where(length == MOST, 0, jnp.where(length == MIDDLE - MOST, MOST, MIDDLE))
    slot = base + frames - begin
    perm = jnp.sum(jnp.where(slot[:, None] == frames[None, :], frames[:, None], 0), axis=0)
    stream = jnp.arange(STREAMS)[:, None]
    row = jnp.arange(CROWS)[None, :]
    part = FRAMES // STREAMS
    frame = jnp.where(row < part * COND, part * stream + row // COND, FRAMES)
    cslot = jnp.sum(jnp.where(frame[..., None] == frames, slot[None, None, :], 0), axis=-1)
    cslot = jnp.where(frame < FRAMES, cslot, 99).reshape(1, PART)
    bias = jnp.where(mask == 1, 0.0, NEG).astype(F32)
    line = jnp.concatenate([perm[None].astype(F32), cslot.astype(F32), jnp.zeros((1, PATCHES - PART - FRAMES), F32)], axis=1)
    return jnp.concatenate([bias, jnp.broadcast_to(line, (8, PATCHES))], axis=0)


def per_device(
    visual, conditioning, d_visual, d_conditioning, episode_frames, patch_mask,
    ln1_gain, ln1_bias, w_qkv, b_qkv, w_proj, b_proj, ln2_gain, ln2_bias, w_in, b_in, w_out, b_out,
):
    d, z = lax.axis_index("dp"), lax.axis_index("stream")
    group = 2 * (z % 2) + d % 2
    blank = jnp.zeros((CROWS - conditioning.shape[1] * COND, D), BF16)

    def chunk(rows, extra):
        return jnp.concatenate([rows.reshape(VIS, D), extra.reshape(-1, D), blank], axis=0)

    x = chunk(visual, conditioning)
    dy = chunk(d_visual, d_conditioning)
    gain_one, shift_one = ln1_gain.astype(F32), ln1_bias.astype(F32)
    gain_two, shift_two = ln2_gain.astype(F32), ln2_bias.astype(F32)
    x_all, meta = gather_rows(x, own_meta(episode_frames[0], patch_mask[0]))
    bias = meta[:FRAMES]
    perm = meta[FRAMES, :FRAMES].astype(jnp.int32)
    cslot = meta[FRAMES, FRAMES : FRAMES + PART].astype(jnp.int32)
    cs_col, cs_row = cslot.reshape(PART, 1), cslot.reshape(1, PART)
    scalars = jnp.concatenate([perm, group.reshape(1).astype(jnp.int32)])
    tables = tuple(jnp.asarray(t) for t in rope_constants())
    a, *saved, o = attend_forward(
        scalars, x_all, w_qkv, b_qkv.astype(F32).reshape(1, -1), gain_one.reshape(1, -1),
        shift_one.reshape(1, -1), tables, bias, cs_col, cs_row,
    )
    attended = to_owner(o)

    inputs = x.astype(F32)
    residual = inputs + jnp.dot(attended, w_proj, preferred_element_type=F32) + b_proj.astype(F32)
    normed_two, scale_two = norm_parts(residual)
    n = (normed_two * gain_two + shift_two).astype(BF16)
    u = jnp.dot(n, w_in, preferred_element_type=F32) + b_in.astype(F32)
    phi = 0.5 * (1.0 + lax.erf(u * (2.0**-0.5)))
    hidden = (u * phi).astype(BF16)
    slope = phi + u * (jnp.exp(-0.5 * u * u) * ((2.0 * math.pi) ** -0.5))
    output = residual + jnp.dot(hidden, w_out, preferred_element_type=F32) + b_out.astype(F32)
    out_visual = output[:VIS].astype(BF16).reshape(visual.shape)
    out_conditioning = output[VIS : VIS + conditioning.shape[1] * COND].astype(BF16).reshape(conditioning.shape)

    dy32 = dy.astype(F32)
    grad_b_out = jnp.sum(dy32, axis=0)
    grad_hidden = jnp.einsum("rd,hd->rh", dy, w_out, preferred_element_type=F32)
    grad_u = (grad_hidden * slope).astype(BF16)
    grad_b_in = jnp.sum(grad_u, axis=0, dtype=F32)
    grad_n = jnp.einsum("rh,dh->rd", grad_u, w_in, preferred_element_type=F32)
    grad_ln2_gain = jnp.sum(grad_n * normed_two, axis=0)
    grad_ln2_bias = jnp.sum(grad_n, axis=0)
    grad_h = dy32 + norm_back(normed_two, scale_two, gain_two, grad_n)
    grad_hb = grad_h.astype(BF16)
    grad_b_proj = jnp.sum(grad_hb, axis=0, dtype=F32)
    grad_o = jnp.einsum("re,de->rd", grad_hb, w_proj, preferred_element_type=F32).astype(BF16)
    grad_o_heads = to_heads(grad_o)
    grad_qkv = attend_backward(scalars, saved, o, grad_o_heads, tables, cs_col, cs_row)

    flat = grad_qkv.reshape(STREAMS * ROWS, 3 * GW)
    role_w = jnp.concatenate(
        [lax.dynamic_slice_in_dim(w_qkv, part * D + group * GW, GW, 1) for part in range(3)], axis=1
    )
    partial = jnp.einsum("re,de->rd", flat, role_w, preferred_element_type=F32).astype(BF16)
    grad_a = sum_rows(partial.reshape(STREAMS, ROWS, D))
    normed_one, scale_one = norm_parts(inputs)
    grad_ln1_gain = jnp.sum(grad_a * normed_one, axis=0)
    grad_ln1_bias = jnp.sum(grad_a, axis=0)
    grad_x = grad_h + norm_back(normed_one, scale_one, gain_one, grad_a)
    grad_visual = grad_x[:VIS].reshape(visual.shape)
    grad_conditioning = grad_x[VIS : VIS + conditioning.shape[1] * COND].reshape(conditioning.shape)

    role_grad = jnp.einsum("rd,re->de", a.reshape(STREAMS * ROWS, D), flat, preferred_element_type=F32)
    role_bias = jnp.sum(flat, axis=0, dtype=F32)
    grad_b_qkv = jnp.zeros((3, HEADS // GROUP, GW), F32)
    grad_b_qkv = lax.dynamic_update_slice_in_dim(grad_b_qkv, role_bias.reshape(3, 1, GW), group, 1).reshape(3 * D)
    grad_w_in = jnp.einsum("rd,rh->dh", n, grad_u, preferred_element_type=F32).astype(BF16)
    grad_w_out = jnp.einsum("rh,rd->hd", hidden, dy, preferred_element_type=F32).astype(BF16)
    grad_w_proj = jnp.einsum("rd,re->de", attended, grad_hb, preferred_element_type=F32).astype(BF16)
    owners = lax.axis_size("dp") * STREAMS
    pieces = [
        grad_ln1_gain, grad_ln1_bias, grad_b_qkv[: 2 * D], grad_b_qkv[2 * D :], grad_b_proj,
        grad_ln2_gain, grad_ln2_bias, grad_b_in, grad_b_out,
    ]
    sizes = [t.shape[0] // owners for t in pieces]
    packed = jnp.concatenate([t.reshape(owners, -1) for t in pieces], axis=1)
    packed = jnp.pad(packed, ((0, 0), (0, 1024 - sum(sizes))))
    red_out, red_in, red_proj, red_qkv, red_small = reduce_grads(
        grad_w_out, grad_w_in, grad_w_proj, role_grad.astype(BF16), packed
    )
    small = []
    start = 0
    for size in sizes:
        small.append(lax.slice_in_dim(red_small.reshape(-1), start, start + size, axis=0))
        start += size
    return (
        out_visual, out_conditioning, grad_visual, grad_conditioning,
        small[0], small[1], red_qkv, small[2], small[3], red_proj, small[4], small[5], small[6], red_in,
        small[7], red_out.reshape(-1, D), small[8],
    )


def solution(mesh):
    rows = P("dp", None, "stream", None)
    extra = P("dp", "stream", None, None)
    vector = P(("dp", "stream"))
    matrix = P(("dp", "stream"), None)
    in_specs = (rows, extra, rows, extra, P("dp", None), P("dp", None, None)) + (P(),) * 12
    out_specs = (
        rows, extra, rows, extra, vector, vector, matrix, vector, vector, matrix, vector, vector, vector, matrix,
        vector, matrix, vector,
    )
    return jax.shard_map(per_device, mesh=mesh, in_specs=in_specs, out_specs=out_specs, check_vma=False)
```

```python
import functools
import math

import jax
import jax.numpy as jnp
import numpy as np
from jax import lax
from jax.experimental import pallas as pl
from jax.experimental.pallas import tpu as pltpu
from jax.sharding import PartitionSpec as P

D = 1024
HEADS = 16
HEAD_DIM = 64
GRID = 16
COND = 2
FRAMES = 8
MOST = 5
MIDDLE = 7
STREAMS = 4
GROUP = 4
GW = GROUP * HEAD_DIM
PART = 64
PATCHES = 256
VIS = FRAMES * PART
CROWS = 16
ROWS = VIS + CROWS
WIDE = GROUP * 128
NEG = -1e30
EPS = 1e-06
F32 = jnp.float32
BF16 = jnp.bfloat16
VM = pltpu.VMEM
FULL = pl.BlockSpec(memory_space=pltpu.VMEM)
ANYM = pl.BlockSpec(memory_space=pltpu.HBM)
LIMIT = 60 * 1024 * 1024


def nn(a, b):
    return lax.dot_general(a, b, (((1,), (0,)), ((), ())), preferred_element_type=F32)


def nt(a, b):
    return lax.dot_general(a, b, (((1,), (1,)), ((), ())), preferred_element_type=F32)


def rope_constants():
    pair = np.arange(HEAD_DIM // 2)
    exponent = np.where(pair < 30, (pair % 10) / 10.0, 0.0).astype(np.float32)
    freq = np.exp(-math.log(10000.0) * exponent).astype(np.float32)
    patch = np.arange(PATCHES)
    slot_time = np.array([0, 1, 2, 3, 4, 0, 1, 0])
    is_time = (pair < 10)[None, :]
    place = np.where(
        (pair >= 20)[None, :], (patch % GRID)[:, None], (patch // GRID)[:, None]
    ) * ((pair >= 10) & (pair < 30))[None, :]
    angle_patch = (place * freq[None, :]).astype(np.float32)
    angle_time = (slot_time[:, None] * freq[None, :]).astype(np.float32)
    cos_patch = np.where(is_time, 0.0, np.cos(angle_patch))
    sin_patch = np.where(is_time, 0.0, np.sin(angle_patch))
    cos_time = np.where(is_time, np.cos(angle_time), 0.0)
    sin_time = np.where(is_time, np.sin(angle_time), 0.0)

    def spread(table, signed):
        two = np.repeat(table, 2, axis=1)
        if signed:
            two = two * np.where(np.arange(HEAD_DIM) % 2 == 0, -1.0, 1.0)[None, :]
        return np.tile(two, (1, GROUP)).astype(np.float32)

    return (
        spread(cos_patch, False),
        spread(sin_patch, True),
        spread(cos_time, False),
        spread(sin_time, True),
    )


def swap_pairs(v):
    lane = lax.broadcasted_iota(jnp.int32, v.shape, 1)
    width = v.shape[1]
    return jnp.where(lane % 2 == 0, pltpu.roll(v, width - 1, 1), pltpu.roll(v, 1, 1))


def turn(v, cosine, sine):
    return v * cosine + swap_pairs(v) * sine


def pad_heads(t, extra):
    pieces = []
    for h in range(GROUP):
        pieces += [t[:, h * HEAD_DIM : (h + 1) * HEAD_DIM], extra]
    return jnp.concatenate(pieces, axis=1)


def pad_right(t):
    extra = jnp.zeros((t.shape[0], HEAD_DIM), t.dtype)
    pieces = []
    for h in range(GROUP):
        pieces += [extra, t[:, h * HEAD_DIM : (h + 1) * HEAD_DIM]]
    return jnp.concatenate(pieces, axis=1)


def unpad_heads(t):
    return jnp.concatenate([t[:, h * 128 : h * 128 + HEAD_DIM] for h in range(GROUP)], axis=1)


def head(t, h):
    return t[:, h * 128 : (h + 1) * 128]


def first_slot(i):
    return jnp.where(i < MOST, 0, jnp.where(i < MIDDLE, MOST, MIDDLE))


def cond_tables(cs_col, ct, st):
    cosine = jnp.zeros((PART, GW), F32)
    sine = jnp.zeros((PART, GW), F32)
    for j in range(FRAMES):
        here = cs_col == j
        cosine = cosine + jnp.where(here, ct[j : j + 1, :], 0.0)
        sine = sine + jnp.where(here, st[j : j + 1, :], 0.0)
    lane = lax.broadcasted_iota(jnp.int32, (PART, GW), 1) % HEAD_DIM
    return jnp.where(lane < 20, cosine, 1.0), sine


def read_meta(meta_ref):
    bias_t = jnp.transpose(meta_ref[0:FRAMES])
    cs_row = meta_ref[FRAMES : FRAMES + 1, 0:PART].astype(jnp.int32)
    cs_col = jnp.transpose(meta_ref[FRAMES:, :])[0:PART, 0:1].astype(jnp.int32)
    return cs_col, cs_row, bias_t


def place_kernel(perm, xv_ref, xc_ref, dv_ref, dc_ref, x_ref, dy_ref, sem):
    copies = []
    for n, (rows, out) in enumerate(((xv_ref, x_ref), (dv_ref, dy_ref))):
        for i in range(FRAMES):
            copies.append(pltpu.make_async_copy(rows.at[perm[i]], out.at[pl.ds(i * PART, PART)], sem.at[n, i]))
    for copy in copies:
        copy.start()
    for extra, out in ((xc_ref, x_ref), (dc_ref, dy_ref)):
        out[VIS:, :] = jnp.zeros((CROWS, D), BF16)
        out[VIS : VIS + extra.shape[0], :] = extra[...]
    for copy in copies:
        copy.wait()


def place_rows(perm, visual, extra, d_visual, d_extra):
    return pl.pallas_call(
        place_kernel,
        name="place_rows",
        out_shape=(jax.ShapeDtypeStruct((ROWS, D), BF16),) * 2,
        in_specs=[pl.BlockSpec(memory_space=pltpu.SMEM), ANYM, FULL, ANYM, FULL],
        out_specs=(FULL, FULL),
        scratch_shapes=[pltpu.SemaphoreType.DMA((2, FRAMES))],
    )(perm, visual.reshape(FRAMES, PART, D), extra.reshape(-1, D), d_visual.reshape(FRAMES, PART, D), d_extra.reshape(-1, D))


def restore_kernel(slot, y_ref, g_ref, yo_ref, go_ref, sem):
    copies = []
    for f in range(FRAMES):
        rows = pl.ds(pl.multiple_of(slot[f] * PART, PART), PART)
        copies.append(pltpu.make_async_copy(y_ref.at[rows], yo_ref.at[f], sem.at[0, f]))
        copies.append(pltpu.make_async_copy(g_ref.at[rows], go_ref.at[f], sem.at[1, f]))
    for copy in copies:
        copy.start()
    for copy in copies:
        copy.wait()


def restore_rows(slot, y, g):
    shape = (FRAMES, PART, D)
    return pl.pallas_call(
        restore_kernel,
        name="restore_rows",
        out_shape=(jax.ShapeDtypeStruct(shape, BF16), jax.ShapeDtypeStruct(shape, F32)),
        in_specs=[pl.BlockSpec(memory_space=pltpu.SMEM), ANYM, ANYM],
        out_specs=(FULL, FULL),
        scratch_shapes=[pltpu.SemaphoreType.DMA((2, FRAMES))],
    )(slot, y, g)


def where_am_i():
    d, z = lax.axis_index("dp"), lax.axis_index("stream")
    return d // 2, d % 2, z // 2, z % 2, z


def greet_column():
    p, c, q, r, z = where_am_i()
    barrier = pltpu.get_barrier_semaphore()
    for core in range(2):
        for chip in range(STREAMS):
            @pl.when((core != c) | (chip != z))
            def _():
                pl.semaphore_signal(
                    barrier, inc=1, device_id=(2 * p + core, chip),
                    device_id_type=pl.DeviceIdType.MESH,
                )
    pl.semaphore_wait(barrier, 2 * STREAMS - 1)


def remote(src, dst, send, recv, device):
    return pltpu.make_async_remote_copy(
        src_ref=src, dst_ref=dst, send_sem=send, recv_sem=recv, device_id=device,
        device_id_type=pl.DeviceIdType.MESH,
    )


def comm_call(kernel, name, ident, outs, scratch, far, close=(), near_outs=()):
    return pl.pallas_call(
        kernel,
        name=name,
        out_shape=tuple(jax.ShapeDtypeStruct(s, t) for s, t in tuple(outs) + tuple(near_outs)),
        in_specs=[ANYM] * len(far) + [FULL] * len(close),
        out_specs=tuple(ANYM for _ in outs) + tuple(FULL for _ in near_outs),
        scratch_shapes=scratch,
        compiler_params=pltpu.CompilerParams(
            collective_id=ident, has_side_effects=True, vmem_limit_bytes=LIMIT
        ),
    )(*far, *close)


def dma(*shape):
    return pltpu.SemaphoreType.DMA(shape)


HALF = VIS // 2


PIECE = HALF // 2


def forward_kernel(
    x_hbm, w_hbm, m_hbm, par_ref, cg_ref, sg_ref, ct_ref, st_ref,
    att_ref, xa_out, a_out, q_out, k_out, v_out, o_out,
    meta_ref, qc_ref, kc_ref, vc_ref, lse_ref, lsec_ref,
    xa, a_ref, q_ref, k_ref, v_ref, o_ref, vt_ref, w, bias_ref,
    isem, whole_s, whole_r, far_s, far_r, pass_s, near_s, near_r, tail_s, tail_r, msem, out_s, out_r, out_l, keep,
):
    p, c, q, r, z = where_am_i()
    group = 2 * r + c
    in_pair = q == c
    away = q != c
    inner = z == 1 + q
    z_one, z_two, z_three = z + 1 - 2 * r, z + 2 - 4 * q, STREAMS - 1 - z
    other = (2 * p + 1 - c, z)
    across = (2 * p + c, z_one)
    loads = []
    for part in range(3):
        cols = pl.ds(pl.multiple_of(part * D + group * GW, GW), GW)
        loads.append(pltpu.make_async_copy(w_hbm.at[:, cols], w.at[part], isem.at[part]))
    for copy in loads:
        copy.start()
    own_rows = pltpu.make_async_copy(x_hbm, xa.at[z], isem.at[3])

    @pl.when(in_pair)
    def _():
        own_rows.start()

    greet_column()
    tail = pl.ds(VIS, CROWS)

    def piece(half, g):
        return pl.ds(pl.multiple_of(half * HALF + g * PIECE, PIECE), PIECE)

    def whole_copy():
        return remote(x_hbm, xa.at[z], whole_s, whole_r, other)

    def far_copy(half, g):
        rows = piece(half, g)
        return remote(x_hbm.at[rows], xa.at[z, rows], far_s.at[half, g], far_r.at[z, g], (2 * p + half, 1 + c))

    def own_pass(g):
        rows = piece(c, g)
        return remote(x_hbm.at[rows], xa.at[z, rows], pass_s.at[z, g], far_r.at[z, g], across)

    def far_pass(s, g):
        rows = piece(c, g)
        return remote(xa.at[s, rows], xa.at[s, rows], pass_s.at[s, g], far_r.at[s, g], across)

    def near_copy(s, g, half):
        rows = piece(half, g)
        return remote(xa.at[s, rows], xa.at[s, rows], near_s.at[s, g], near_r.at[s, g], other)

    def tail_copy(half, side):
        n = half * 2 + side
        return remote(x_hbm.at[tail], xa.at[z, tail], tail_s.at[n], tail_r.at[z], (2 * p + half, 2 * c + side))

    def tail_needed(half, side):
        return jnp.logical_not((2 * c + side == z))

    def meta_copy():
        return remote(m_hbm, meta_ref, msem.at[0], msem.at[1], other)

    def meta_own():
        return pltpu.make_async_copy(m_hbm, meta_ref, msem.at[2])

    @pl.when(in_pair)
    def _():
        meta_own().start()
        meta_copy().start()
        whole_copy().start()
        own_pass(0).start()
        own_pass(1).start()

    for half in range(2):
        @pl.when(away)
        def _():
            far_copy(half, 0).start()

        for side in range(2):
            @pl.when(tail_needed(half, side))
            def _():
                tail_copy(half, side).start()

    def arrive(s, g, relay):
        far_pass(s, g).wait_recv()
        near_copy(s, g, c).start()
        if relay:
            @pl.when(inner)
            def _():
                far_pass(s, g).start()

    gain, shift = par_ref[0:1], par_ref[1:2]
    cut = pl.ds(pl.multiple_of(group * GW, GW), GW)
    lane64 = lax.broadcasted_iota(jnp.int32, (PATCHES, 64), 1)
    one = jnp.where(lane64 == 0, 1.0, 0.0).astype(BF16)

    def project(x, cosine, sine):
        x = x.astype(F32)
        centre = x - jnp.mean(x, axis=1, keepdims=True)
        spread = jnp.mean(centre * centre, axis=1, keepdims=True)
        a = (centre * lax.rsqrt(spread + EPS) * gain + shift).astype(BF16)
        q = turn(nn(a, w[0]) + par_ref[2:3, cut], cosine, sine)
        k = turn(nn(a, w[1]) + par_ref[3:4, cut], cosine, sine)
        v = (nn(a, w[2]) + par_ref[4:5, cut]).astype(BF16)
        return a, (q.astype(BF16).astype(F32) * 0.125).astype(BF16), k.astype(BF16), v

    def unit(t, carry):
        @pl.when(t == 0)
        def _():
            for copy in loads:
                copy.wait()

            @pl.when(in_pair)
            def _():
                own_rows.wait()
                meta_own().wait()

            @pl.when(away)
            def _():
                whole_copy().wait_recv()
                far_pass(z, 0).start()
                far_pass(z, 1).start()
                meta_copy().wait_recv()

            bias_ref[...] = jnp.transpose(meta_ref[0:FRAMES])

        @pl.when(t == 2)
        def _():
            arrive(z_one, 0, False)
            arrive(z_one, 1, False)

            @pl.when(away)
            def _():
                for half in range(2):
                    far_copy(half, 0).wait_send()
                    far_copy(half, 1).start()

            arrive(z_two, 0, True)
            arrive(z_three, 0, True)
            near_copy(z_one, 0, 1 - c).wait_recv()
            near_copy(z_one, 1, 1 - c).wait_recv()

        @pl.when(t == 4)
        def _():
            near_copy(z_two, 0, 1 - c).wait_recv()
            near_copy(z_three, 0, 1 - c).wait_recv()

        @pl.when(t == 6)
        def _():
            arrive(z_two, 1, True)
            arrive(z_three, 1, True)
            near_copy(z_two, 1, 1 - c).wait_recv()
            near_copy(z_three, 1, 1 - c).wait_recv()

        g = jnp.where(t < 4, t % 2, (t - 4) // 2)
        s = jnp.where(t < 2, z, jnp.where(t < 4, z_one, jnp.where(t % 2 == 0, z_two, z_three)))
        x = jnp.concatenate([xa[s, piece(0, g)], xa[s, piece(1, g)]], axis=0)
        place = pl.ds(pl.multiple_of(s * PART, PART), PART)
        cosine, sine, bias = [], [], []
        ids = lax.broadcasted_iota(jnp.int32, (PART, FRAMES), 1)
        for n in range(4):
            i = 2 * g + n % 2 + 4 * (n // 2)
            cosine.append(cg_ref[place] + ct_ref[pl.ds(i, 1), :])
            sine.append(sg_ref[place] + st_ref[pl.ds(i, 1), :])
            bias.append(jnp.sum(jnp.where(ids == i, bias_ref[place], 0.0), axis=1, keepdims=True))
        a, qs, ks, vs = project(x, jnp.concatenate(cosine, axis=0), jnp.concatenate(sine, axis=0))
        a_ref[s, piece(0, g)] = a[:PIECE]
        a_ref[s, piece(1, g)] = a[PIECE:]
        bias = jnp.concatenate(bias, axis=0)
        qs = pad_heads(qs, one)
        ks = pad_heads(ks, jnp.where(lane64 == 0, bias, 0.0).astype(BF16))
        vs = pad_right(vs)
        for n in range(4):
            i = 2 * g + n % 2 + 4 * (n // 2)
            rows = slice(n * PART, (n + 1) * PART)
            q_ref[i, place] = qs[rows]
            k_ref[i, place] = ks[rows]
            v_ref[i, place] = vs[rows]
        return carry

    lax.fori_loop(0, 8, unit, 0)

    for s in range(STREAMS):
        @pl.when(s != z)
        def _():
            remote(x_hbm.at[tail], xa.at[s, tail], tail_s.at[0], tail_r.at[s], other).wait_recv()
    cs_col, cs_row, _ = read_meta(meta_ref)
    a, qs, ks, vs = project(xa[:, VIS:, :].reshape(PART, D), *cond_tables(cs_col, ct_ref[...], st_ref[...]))
    a_ref[:, VIS:, :] = a.reshape(STREAMS, CROWS, D)
    qc_ref[...] = pad_heads(qs, one[:PART])
    kc_ref[...] = pad_heads(ks, jnp.zeros((PART, 64), BF16))
    vc_ref[...] = pad_right(vs)
    vct = jnp.transpose(vs.astype(F32)).astype(BF16)
    saves = [(xa, xa_out), (a_ref, a_out), (q_ref, q_out), (k_ref, k_out), (v_ref, v_out)]
    saves = [pltpu.make_async_copy(src, dst, keep.at[n]) for n, (src, dst) in enumerate(saves)]
    for copy in saves:
        copy.start()

    def out_rows(i):
        return pl.ds(pl.multiple_of(i * PART, PART), PART)

    def out_copy(s, n, rows):
        place = pl.ds(pl.multiple_of(group * GW, GW), GW)
        return remote(o_ref.at[s, rows], att_ref.at[rows, place], out_s.at[s, n], out_r.at[group, n], (2 * p + q, s))

    def out_own(s, n, rows):
        place = pl.ds(pl.multiple_of(group * GW, GW), GW)
        return pltpu.make_async_copy(o_ref.at[s, rows], att_ref.at[rows, place], out_l.at[n])

    def send_out(n, rows):
        for s in range(STREAMS):
            mine = in_pair & (s == z)

            @pl.when(mine)
            def _():
                out_own(s, n, rows).start()

            @pl.when(jnp.logical_not(mine))
            def _():
                out_copy(s, n, rows).start()

    def slot(i, carry):
        vt_ref[i] = jnp.transpose(unpad_right(v_ref[i].astype(F32))).astype(BF16)
        low = first_slot(i)
        near = (cs_col >= low) & (cs_col <= i)
        tops, totals, blends = [], [], []
        for h in range(GROUP):
            s = jnp.where(near, nt(head(kc_ref, h), q_ref[i, :, h * 128 : (h + 1) * 128]), NEG)
            top = jnp.max(s, axis=0, keepdims=True)
            pt = jnp.exp(s - top)
            tops.append(top)
            totals.append(jnp.sum(pt, axis=0, keepdims=True))
            blends.append(nn(vct[h * HEAD_DIM : (h + 1) * HEAD_DIM], pt.astype(BF16)))

        def step(j, state):
            tops, totals, blends = state
            new = ([], [], [])
            for h in range(GROUP):
                s = nt(k_ref[j, :, h * 128 : (h + 1) * 128], q_ref[i, :, h * 128 : (h + 1) * 128])
                top = jnp.maximum(tops[h], jnp.max(s, axis=0, keepdims=True))
                pt = jnp.exp(s - top)
                stay = jnp.exp(tops[h] - top)
                new[0].append(top)
                new[1].append(totals[h] * stay + jnp.sum(pt, axis=0, keepdims=True))
                vt = vt_ref[j, h * HEAD_DIM : (h + 1) * HEAD_DIM, :]
                new[2].append(blends[h] * stay + nn(vt, pt.astype(BF16)))
            return new

        tops, totals, blends = lax.fori_loop(low, i + 1, step, (tops, totals, blends))
        o = jnp.transpose(jnp.concatenate([blends[h] / totals[h] for h in range(GROUP)], axis=0))
        o_ref[:, out_rows(i), :] = o.astype(BF16).reshape(STREAMS, PART, GW)
        lse_ref[i] = jnp.concatenate([tops[h] + jnp.log(totals[h]) for h in range(GROUP)] * 2, axis=0)
        send_out(i, out_rows(i))
        return carry

    lo_col = first_slot(cs_col)

    def cond_queries():
        near = (cs_row >= lo_col) & (cs_row <= cs_col)
        tops, totals, blends = [], [], []
        for h in range(GROUP):
            s = jnp.where(near, nt(head(qc_ref, h), head(kc_ref, h)), NEG)
            top = jnp.max(s, axis=1, keepdims=True)
            pt = jnp.exp(s - top)
            tops.append(top)
            totals.append(jnp.sum(pt, axis=1, keepdims=True))
            blends.append(nn(pt.astype(BF16), head(vc_ref, h)))

        def cond_step(j, state):
            tops, totals, blends = state
            near = (lo_col <= j) & (cs_col >= j)
            new = ([], [], [])
            for h in range(GROUP):
                s = nt(head(qc_ref, h), k_ref[j, :, h * 128 : (h + 1) * 128])
                s = jnp.where(near, s, NEG)
                top = jnp.maximum(tops[h], jnp.max(s, axis=1, keepdims=True))
                pt = jnp.exp(s - top)
                stay = jnp.exp(tops[h] - top)
                new[0].append(top)
                new[1].append(totals[h] * stay + jnp.sum(pt, axis=1, keepdims=True))
                new[2].append(blends[h] * stay + nn(pt.astype(BF16), v_ref[j, :, h * 128 : (h + 1) * 128]))
            return new

        tops, totals, blends = lax.fori_loop(0, FRAMES, cond_step, (tops, totals, blends))
        o = jnp.concatenate([(blends[h] / totals[h])[:, HEAD_DIM:] for h in range(GROUP)], axis=1)
        o_ref[:, VIS:, :] = o.astype(BF16).reshape(STREAMS, CROWS, GW)
        lane = lax.broadcasted_iota(jnp.int32, (PART, 128), 1)
        lsec = jnp.zeros((PART, 128), F32)
        for h in range(GROUP):
            lsec = lsec + jnp.where(lane == h, tops[h] + jnp.log(totals[h]), 0.0)
        lsec_ref[...] = lsec
        send_out(FRAMES, tail)

    cond_queries()
    lax.fori_loop(0, FRAMES, slot, 0)
    last = pltpu.make_async_copy(o_ref, o_out, keep.at[5])
    last.start()

    def settle(n, rows):
        for s in range(STREAMS):
            mine = in_pair & (s == z)

            @pl.when(mine)
            def _():
                out_own(s, n, rows).wait()

            @pl.when(jnp.logical_not(mine))
            def _():
                out_copy(s, n, rows).wait_send()
        for g in range(4):
            @pl.when((g % 2 != c) | (2 * c + g // 2 != z))
            def _():
                place = pl.ds(g * GW, GW)
                remote(o_ref.at[0, rows], att_ref.at[rows, place], out_s.at[0, n], out_r.at[g, n], other).wait_recv()

    def settle_slot(i, carry):
        settle(i, out_rows(i))
        return carry

    lax.fori_loop(0, FRAMES, settle_slot, 0)
    settle(FRAMES, tail)

    @pl.when(in_pair)
    def _():
        meta_copy().wait_send()
        whole_copy().wait_send()
        own_pass(0).wait_send()
        own_pass(1).wait_send()

    @pl.when(away)
    def _():
        far_pass(z, 0).wait_send()
        far_pass(z, 1).wait_send()
        far_copy(0, 1).wait_send()
        far_copy(1, 1).wait_send()

    for half in range(2):
        for side in range(2):
            @pl.when(tail_needed(half, side))
            def _():
                tail_copy(half, side).wait_send()
    for g in range(2):
        for s in (z_one, z_two, z_three):
            near_copy(s, g, c).wait_send()
        for s in (z_two, z_three):
            @pl.when(inner)
            def _():
                far_pass(s, g).wait_send()
    for copy in saves:
        copy.wait()
    last.wait()


def attend_forward(x, w_qkv, meta, params, tables):
    def v16(*shape):
        return VM(shape, BF16)

    wide = (FRAMES, PATCHES, WIDE)
    rows = (STREAMS, ROWS, D)
    outs = (
        ((ROWS, D), BF16), (rows, BF16), (rows, BF16), (wide, BF16), (wide, BF16), (wide, BF16),
        ((STREAMS, ROWS, GW), BF16),
    )
    near_outs = (
        (meta.shape, F32), ((PART, WIDE), BF16), ((PART, WIDE), BF16), ((PART, WIDE), BF16),
        ((FRAMES, 8, PATCHES), F32), ((PART, 128), F32),
    )
    scratch = [
        v16(*rows), v16(*rows), v16(*wide), v16(*wide), v16(*wide), v16(STREAMS, ROWS, GW), v16(FRAMES, GW, PATCHES),
        v16(3, D, GW), VM((PATCHES, FRAMES), F32),
        dma(4), pltpu.SemaphoreType.DMA, pltpu.SemaphoreType.DMA, dma(2, 2), dma(4, 2), dma(4, 2), dma(4, 2), dma(4, 2),
        dma(4), dma(4), dma(3), dma(4, 9), dma(4, 9), dma(9), dma(6),
    ]
    return comm_call(
        forward_kernel, "attend_forward", 0, outs, scratch, (x, w_qkv, meta), (params,) + tables, near_outs
    )
CHUNKS = 9
CUT = D // 2
QCUT = 3 * GW // 2


def add_up(*terms):
    total = terms[0].astype(F32)
    for t in terms[1:]:
        total = total + t.astype(F32)
    return total


def grid_shape():
    cores = lax.axis_size("dp") // 2
    nx = 1 << ((cores.bit_length() - 1) // 2)
    return nx, cores // nx, D // (cores * 2 * STREAMS)


class Place:
    def __init__(self, nx, ny):
        d, z = lax.axis_index("dp"), lax.axis_index("stream")
        self.nx, self.ny, self.d, self.z = nx, ny, d, z
        self.p, self.c, self.hi, self.lo = d // 2, d % 2, z // 2, z % 2
        self.x, self.y = self.p % nx, self.p // nx
        self.near = (d + 1 - 2 * self.c, z)
        self.z_one = (d, z + 1 - 2 * self.lo)
        self.z_two = (d, z + 2 - 4 * self.hi)
        self.slant = (d + 1 - 2 * self.c, z + 1 - 2 * self.lo)

    def along_x(self, n):
        return lax.rem(self.x + n, self.nx)

    def along_y(self, n):
        return lax.rem(self.y + n, self.ny)

    def x_device(self, n):
        return ((self.y * self.nx + self.along_x(n)) * 2 + self.c, self.z)

    def y_device(self, n):
        return ((self.along_y(n) * self.nx + self.x) * 2 + self.c, self.z)

    def greet(self):
        barrier = pltpu.get_barrier_semaphore()
        p, c, z, nx, ny = self.p, self.c, self.z, self.nx, self.ny
        for core in range(2):
            for chip in range(STREAMS):
                @pl.when((core != c) | (chip != z))
                def _():
                    pl.semaphore_signal(
                        barrier, inc=1, device_id=(2 * p + core, chip), device_id_type=pl.DeviceIdType.MESH
                    )
        others = [self.x_device(n) for n in range(1, nx)] + [self.y_device(n) for n in range(1, ny)]
        for device in others:
            pl.semaphore_signal(barrier, inc=1, device_id=device, device_id_type=pl.DeviceIdType.MESH)
        pl.semaphore_wait(barrier, 2 * STREAMS - 1 + len(others))


class Reducer:
    def __init__(self, at, rb, count, sources, refs):
        self.at, self.rb, self.count, self.sources = at, rb, count, sources
        (self.mine, self.rd, self.r2a, self.r2b, self.r3a, self.r3b, self.s3, self.r4, self.s4, self.r5, self.fin,
         self.lsem, self.ds, self.dr, self.as2, self.ar2, self.bs2, self.br2, self.as3, self.ar3, self.bs3, self.br3,
         self.s4s, self.s4r, self.s5s, self.s5r) = refs

    @staticmethod
    def scratch(n, nx, ny, rb):
        def v(*shape):
            return VM(shape, BF16)

        return [
            v(n, ny, nx, STREAMS, rb, D), v(n, ny, nx, STREAMS, rb, D),
            v(n, nx - 1, ny, STREAMS, rb, CUT), v(n, ny - 1, nx, STREAMS, rb, CUT),
            v(n, ny - 1, STREAMS, rb, CUT), v(n, nx - 1, STREAMS, rb, CUT),
            v(n, 2, 2, rb, D), v(n, 2, rb, D), v(n, 2, rb, D), v(n, rb, D), VM((n, rb, D), F32),
            dma(n), dma(n), dma(n),
            dma(n, nx - 1), dma(n, nx - 1), dma(n, ny - 1), dma(n, ny - 1),
            dma(n, ny - 1), dma(n, ny - 1), dma(n, nx - 1), dma(n, nx - 1),
            dma(n), dma(n), dma(n), dma(n),
        ]

    def issue(self, k):
        c = self.at.c
        begin = 0
        for size, get in self.sources:
            start = begin
            begin += size

            @pl.when((k >= start) & (k < start + size))
            def _():
                t = k - start
                remote(get(t, 1 - c), self.rd.at[k], self.ds.at[k], self.dr.at[k], self.at.near).start()
                pltpu.make_async_copy(get(t, c), self.mine.at[k], self.lsem.at[k]).start()

    def core(self, k):
        return remote(self.rd.at[k], self.rd.at[k], self.ds.at[k], self.dr.at[k], self.at.near)

    def a2(self, k, n):
        at = self.at
        src = self.mine.at[k, :, at.along_x(n), :, :, pl.ds(0, CUT)]
        return remote(src, self.r2a.at[k, n - 1], self.as2.at[k, n - 1], self.ar2.at[k, n - 1], at.x_device(n))

    def b2(self, k, n):
        at = self.at
        src = self.mine.at[k, at.along_y(n), :, :, :, pl.ds(CUT, CUT)]
        return remote(src, self.r2b.at[k, n - 1], self.bs2.at[k, n - 1], self.br2.at[k, n - 1], at.y_device(n))

    def a3(self, k, n):
        at = self.at
        src = self.r2a.at[k, 0, at.along_y(n)]
        return remote(src, self.r3a.at[k, n - 1], self.as3.at[k, n - 1], self.ar3.at[k, n - 1], at.y_device(n))

    def b3(self, k, n):
        at = self.at
        src = self.r2b.at[k, 0, at.along_x(n)]
        return remote(src, self.r3b.at[k, n - 1], self.bs3.at[k, n - 1], self.br3.at[k, n - 1], at.x_device(n))

    def c4(self, k):
        return remote(self.s3.at[k, :, 1 - self.at.lo], self.r4.at[k], self.s4s.at[k], self.s4r.at[k], self.at.z_one)

    def c5(self, k):
        return remote(self.s4.at[k, 1 - self.at.hi], self.r5.at[k], self.s5s.at[k], self.s5r.at[k], self.at.z_two)

    def tick(self, t, carry=0):
        at, rb, count = self.at, self.rb, self.count
        nx, ny, x, y = at.nx, at.ny, at.x, at.y

        @pl.when(t < count)
        def _():
            k = t
            pltpu.make_async_copy(self.rd.at[k], self.mine.at[k], self.lsem.at[k]).wait()
            self.core(k).wait_recv()
            self.issue(k + 2)
            for b in range(ny):
                for e in range(nx):
                    self.mine[k, b, e] = add_up(self.mine[k, b, e], self.rd[k, b, e]).astype(BF16)
            for n in range(1, nx):
                self.a2(k, n).start()
            for n in range(1, ny):
                self.b2(k, n).start()

        @pl.when((t >= 2) & (t < count + 2))
        def _():
            k = t - 2
            for n in range(1, nx):
                self.a2(k, n).wait_recv()
            for b in range(ny):
                self.r2a[k, 0, b] = add_up(
                    self.mine[k, b, x, :, :, 0:CUT], *[self.r2a[k, n, b] for n in range(nx - 1)]
                ).astype(BF16)
            for n in range(1, ny):
                self.a3(k, n).start()
            for n in range(1, ny):
                self.b2(k, n).wait_recv()
            for b in range(nx):
                self.r2b[k, 0, b] = add_up(
                    self.mine[k, y, b, :, :, CUT:], *[self.r2b[k, n, b] for n in range(ny - 1)]
                ).astype(BF16)
            for n in range(1, nx):
                self.b3(k, n).start()

        @pl.when((t >= 4) & (t < count + 4))
        def _():
            k = t - 4
            for n in range(1, ny):
                self.a3(k, n).wait_recv()
            for n in range(1, nx):
                self.b3(k, n).wait_recv()
            left = add_up(self.r2a[k, 0, y], *[self.r3a[k, n] for n in range(ny - 1)]).astype(BF16)
            right = add_up(self.r2b[k, 0, x], *[self.r3b[k, n] for n in range(nx - 1)]).astype(BF16)
            self.s3[k, :, :, :, 0:CUT] = left.reshape(2, 2, rb, CUT)
            self.s3[k, :, :, :, CUT:] = right.reshape(2, 2, rb, CUT)
            self.c4(k).start()

        @pl.when((t >= 5) & (t < count + 5))
        def _():
            k = t - 5
            self.c4(k).wait_recv()
            self.s4[k] = add_up(self.s3[k, :, at.lo], self.r4[k]).astype(BF16)
            self.c5(k).start()

        @pl.when((t >= 6) & (t < count + 6))
        def _():
            k = t - 6
            self.c5(k).wait_recv()
            self.fin[k] = add_up(self.s4[k, at.hi], self.r5[k])

        return carry

    def start(self):
        self.issue(0)
        self.issue(1)

    def drain(self):
        def one(k, carry):
            self.core(k).wait_send()
            for n in range(1, self.at.nx):
                self.a2(k, n).wait_send()
                self.b3(k, n).wait_send()
            for n in range(1, self.at.ny):
                self.b2(k, n).wait_send()
                self.a3(k, n).wait_send()
            self.c4(k).wait_send()
            self.c5(k).wait_send()
            return carry

        lax.fori_loop(0, self.count, one, 0)


def backward_kernel(
    nx, ny, rb,
    go_ref, gi_ref, gp_ref, d_ref, q_hbm, k_hbm, v_hbm, o_hbm,
    qc_ref, kc_ref, vc_ref, lse_ref, lsec_ref, cg_ref, sg_ref, ct_ref, st_ref, meta_ref,
    oo_ref, oi_ref, op_ref, g_out,
    q_ref, k_ref, v_ref, o_ref, do_ref, g_ref, acc, accc, kt_ref, right,
    osem, isem, *refs,
):
    at = Place(nx, ny)
    p, c, q, r, z = at.p, at.c, at.hi, at.lo, at.z
    at.greet()
    reducer = Reducer(
        at, rb, CHUNKS,
        (
            (4, lambda t, core: go_ref.at[:, :, core, :, t]),
            (4, lambda t, core: gi_ref.at[:, :, core, :, :, pl.ds(pl.multiple_of(t * D, D), D)]),
            (1, lambda t, core: gp_ref.at[:, :, core]),
        ),
        refs,
    )

    reducer.start()
    loads = [(q_hbm, q_ref), (k_hbm, k_ref), (v_hbm, v_ref), (o_hbm, o_ref), (d_ref, do_ref)]
    loads = [pltpu.make_async_copy(src, dst, isem.at[n]) for n, (src, dst) in enumerate(loads)]
    for copy in loads:
        copy.start()

    lax.fori_loop(0, 2, reducer.tick, 0)
    cs_col, cs_row, _ = read_meta(meta_ref)
    acc[...] = jnp.zeros_like(acc)
    accc[...] = jnp.zeros_like(accc)
    kct = jnp.transpose(unpad_heads(kc_ref[...].astype(F32))).astype(BF16)
    for copy in loads:
        copy.wait()
    def slot(i):
        start = pl.multiple_of(i * PART, PART)
        do = do_ref[:, pl.ds(start, PART), :].reshape(PATCHES, GW)
        o = o_ref[:, pl.ds(start, PART), :].reshape(PATCHES, GW)
        prod = jnp.transpose(do.astype(F32) * o.astype(F32))
        deltas = [
            jnp.sum(prod[h * HEAD_DIM : (h + 1) * HEAD_DIM], axis=0, keepdims=True) for h in range(GROUP)
        ]
        right[0:PATCHES] = pad_right(do)
        lane = lax.broadcasted_iota(jnp.int32, (PATCHES, WIDE), 1) % 128
        right[PATCHES:] = jnp.where(lane < HEAD_DIM, q_ref[i].astype(F32), 0.0).astype(BF16)
        kt_ref[i] = jnp.transpose(unpad_heads(k_ref[i].astype(F32))).astype(BF16)
        low = first_slot(i)
        near = (cs_col >= low) & (cs_col <= i)
        dqs = []
        for h in range(GROUP):
            cols = slice(h * 128, (h + 1) * 128)
            s = jnp.where(near, nt(kc_ref[:, cols], q_ref[i, :, cols]), NEG)
            pt = jnp.exp(s - lse_ref[i, h : h + 1, :])
            dst = (pt * (nt(vc_ref[:, cols], right[0:PATCHES, cols]) - deltas[h])).astype(BF16)
            accc[:, cols] += nn(jnp.concatenate([pt.astype(BF16), dst], axis=1), right[:, cols])
            dqs.append(nn(kct[h * HEAD_DIM : (h + 1) * HEAD_DIM], dst))

        def step(j, dqs):
            new = []
            for h in range(GROUP):
                cols = slice(h * 128, (h + 1) * 128)
                pt = jnp.exp(nt(k_ref[j, :, cols], q_ref[i, :, cols]) - lse_ref[i, h : h + 1, :])
                dst = (pt * (nt(v_ref[j, :, cols], right[0:PATCHES, cols]) - deltas[h])).astype(BF16)
                acc[j, :, cols] += nn(jnp.concatenate([pt.astype(BF16), dst], axis=1), right[:, cols])
                new.append(dqs[h] + nn(kt_ref[j, h * HEAD_DIM : (h + 1) * HEAD_DIM, :], dst))
            return new

        dqs = lax.fori_loop(low, i + 1, step, dqs)
        dq = jnp.transpose(jnp.concatenate(dqs, axis=0)) * 0.125
        cosine = cg_ref[...] + ct_ref[pl.ds(i, 1), :]
        sine = sg_ref[...] + st_ref[pl.ds(i, 1), :]
        dq = turn(dq, cosine, -sine).astype(BF16).reshape(STREAMS, PART, GW)
        g_ref[:, pl.ds(start, PART), 0:GW] = dq

    def sweep(i, carry):
        slot(i)
        reducer.tick(i + 2)
        return carry

    lax.fori_loop(0, FRAMES, sweep, 0)

    doc = do_ref[:, VIS:, :].reshape(PART, GW)
    oc = o_ref[:, VIS:, :].reshape(PART, GW)
    docp = pad_right(doc)
    lane = lax.broadcasted_iota(jnp.int32, (PART, WIDE), 1) % 128
    qcl = jnp.where(lane < HEAD_DIM, qc_ref[...].astype(F32), 0.0).astype(BF16)
    prod = doc.astype(F32) * oc.astype(F32)
    lo_col = first_slot(cs_col)
    near = (cs_row >= lo_col) & (cs_row <= cs_col)
    deltas = [
        jnp.sum(prod[:, h * HEAD_DIM : (h + 1) * HEAD_DIM], axis=1, keepdims=True) for h in range(GROUP)
    ]
    lses = [lsec_ref[:, h : h + 1] for h in range(GROUP)]
    dqs = []
    for h in range(GROUP):
        cols = slice(h * 128, (h + 1) * 128)
        s = jnp.where(near, nt(qc_ref[:, cols], kc_ref[:, cols]), NEG)
        pt = jnp.exp(s - lses[h])
        dst = pt * (nt(docp[:, cols], vc_ref[:, cols]) - deltas[h])
        accc[:, cols] += nn(jnp.transpose(pt).astype(BF16), docp[:, cols]) + nn(
            jnp.transpose(dst).astype(BF16), qcl[:, cols]
        )
        dqs.append(nn(dst.astype(BF16), kc_ref[:, cols]))

    def cond_step(j, dqs):
        near = (lo_col <= j) & (cs_col >= j)
        new = []
        for h in range(GROUP):
            cols = slice(h * 128, (h + 1) * 128)
            s = jnp.where(near, nt(qc_ref[:, cols], k_ref[j, :, cols]), NEG)
            pt = jnp.exp(s - lses[h])
            dst = pt * (nt(docp[:, cols], v_ref[j, :, cols]) - deltas[h])
            acc[j, :, cols] += nn(jnp.transpose(pt).astype(BF16), docp[:, cols]) + nn(
                jnp.transpose(dst).astype(BF16), qcl[:, cols]
            )
            new.append(dqs[h] + nn(dst.astype(BF16), k_ref[j, :, cols]))
        return new

    dqs = lax.fori_loop(0, FRAMES, cond_step, dqs)
    cosine, sine = cond_tables(cs_col, ct_ref[...], st_ref[...])
    valid = cs_col < FRAMES
    dq = jnp.concatenate([t[:, :HEAD_DIM] for t in dqs], axis=1) * 0.125
    both = accc[...]
    parts = (turn(dq, cosine, -sine), turn(unpad_heads(both), cosine, -sine), unpad_right(both))
    for part, t in enumerate(parts):
        t = jnp.where(valid, t, 0.0).astype(BF16)
        g_ref[:, VIS:, part * GW : (part + 1) * GW] = t.reshape(STREAMS, CROWS, GW)

    def finish(i, carry):
        start = pl.multiple_of(i * PART, PART)
        cosine = cg_ref[...] + ct_ref[pl.ds(i, 1), :]
        sine = sg_ref[...] + st_ref[pl.ds(i, 1), :]
        both = acc[i]
        dk = turn(unpad_heads(both), cosine, -sine)
        g_ref[:, pl.ds(start, PART), GW : 2 * GW] = dk.astype(BF16).reshape(STREAMS, PART, GW)
        g_ref[:, pl.ds(start, PART), 2 * GW :] = unpad_right(both).astype(BF16).reshape(STREAMS, PART, GW)
        return carry

    lax.fori_loop(0, FRAMES, finish, 0)
    save = pltpu.make_async_copy(g_ref, g_out, isem.at[5])
    save.start()
    lax.fori_loop(10, CHUNKS + 6, reducer.tick, 0)
    fin = reducer.fin
    outs = [pltpu.make_async_copy(fin.at[k], oo_ref.at[k], osem.at[k]) for k in range(4)]
    outs += [
        pltpu.make_async_copy(fin.at[k], oi_ref.at[:, pl.ds((k - 4) * D, D)], osem.at[k]) for k in range(4, 8)
    ]
    outs += [pltpu.make_async_copy(fin.at[8], op_ref, osem.at[8])]
    for copy in outs:
        copy.start()

    reducer.drain()
    save.wait()
    for copy in outs:
        copy.wait()


def unpad_right(t):
    return jnp.concatenate([t[:, h * 128 + HEAD_DIM : (h + 1) * 128] for h in range(GROUP)], axis=1)


def attend_backward(g_out, g_in, g_proj, grad_o, saved, o, tables, meta):
    nx, ny, rb = grid_shape()
    q, k, v, *rest = saved

    def v16(*shape):
        return VM(shape, BF16)

    scratch = [
        v16(*q.shape), v16(*k.shape), v16(*v.shape), v16(*o.shape), v16(*o.shape), v16(STREAMS, ROWS, 3 * GW),
        VM((FRAMES, PATCHES, WIDE), F32), VM((PART, WIDE), F32), v16(FRAMES, GW, PATCHES), v16(2 * PATCHES, WIDE),
        dma(CHUNKS), dma(6),
    ] + Reducer.scratch(CHUNKS, nx, ny, rb)
    outs = (((4, rb, D), F32), ((rb, 4 * D), F32), ((rb, D), F32), ((STREAMS, ROWS, 3 * GW), BF16))
    ops = (
        g_out.reshape(ny, nx, 2, STREAMS, 4, rb, D), g_in.reshape(ny, nx, 2, STREAMS, rb, 4 * D),
        g_proj.reshape(ny, nx, 2, STREAMS, rb, D), grad_o, q, k, v, o,
    )
    return comm_call(
        functools.partial(backward_kernel, nx, ny, rb), "attend_backward", 3, outs, scratch, ops,
        tuple(rest) + tables + (meta,),
    )


def finish_kernel(
    nx, ny, rb,
    f_hbm, xa_hbm, gq_ref, w_hbm, x_hbm, h_hbm, v_ref, gain_ref,
    gx_ref, oq_ref, ov_ref,
    f, xa, w, x_own, h_own, big, near_in, near_out, own, land, tail, tail_out, total,
    q1, rq1a, rq1b, sq1a, sq1b, rq2a, rq2b, sq2, rq3, sq3, vm, vd, vx, vy, vz1, vz2, hold,
    isem, dsend, drecv, send, recv, csend, crecv, lsem,
    qs1a, qr1a, qs1b, qr1b, qs2a, qr2a, qs2b, qr2b, qs3, qr3, qs4, qr4, vs, vr, vsx, vrx, vsy, vry, relay, rsend, rrecv, cols_sum,
):
    at = Place(nx, ny)
    p, c, q, r, z, x, y, hi, lo = at.p, at.c, at.hi, at.lo, at.z, at.x, at.y, at.hi, at.lo
    group = 2 * r + c
    in_pair, inner = q == c, z == 1 + q
    loads = []
    for part in range(3):
        cols = pl.ds(pl.multiple_of(part * D + group * GW, GW), GW)
        loads.append(pltpu.make_async_copy(w_hbm.at[:, cols], w.at[:, pl.ds(part * GW, GW)], isem.at[part]))
    loads.append(pltpu.make_async_copy(f_hbm, f, isem.at[3]))
    loads.append(pltpu.make_async_copy(xa_hbm, xa, isem.at[4]))
    late = [
        pltpu.make_async_copy(gq_ref, q1, isem.at[5]),
        pltpu.make_async_copy(x_hbm, x_own, isem.at[6]),
        pltpu.make_async_copy(h_hbm, h_own, isem.at[7]),
    ]
    for copy in loads + late:
        copy.start()
    at.greet()
    rows = pl.ds(pl.multiple_of(c * HALF, HALF), HALF)
    rest = pl.ds(pl.multiple_of((1 - c) * HALF, HALF), HALF)
    last = pl.ds(VIS, CROWS)
    qa, qb = pl.ds(0, QCUT), pl.ds(QCUT, QCUT)

    def q1a(n):
        return remote(q1.at[:, at.along_x(n), :, :, qa], rq1a.at[n - 1], qs1a.at[n - 1], qr1a.at[n - 1], at.x_device(n))

    def q1b(n):
        return remote(q1.at[at.along_y(n), :, :, :, qb], rq1b.at[n - 1], qs1b.at[n - 1], qr1b.at[n - 1], at.y_device(n))

    def q2a(n):
        return remote(sq1a.at[at.along_y(n)], rq2a.at[n - 1], qs2a.at[n - 1], qr2a.at[n - 1], at.y_device(n))

    def q2b(n):
        return remote(sq1b.at[at.along_x(n)], rq2b.at[n - 1], qs2b.at[n - 1], qr2b.at[n - 1], at.x_device(n))

    def q3():
        return remote(sq2.at[:, 1 - hi], rq3, qs3, qr3, at.z_two)

    mates = [(at.near, 1, 0), (at.z_one, 0, 1), (at.slant, 1, 1)]

    def q4(n, part):
        device, core, side = mates[n]
        to_core = c + core - 2 * c * core
        to_side = lo + side - 2 * lo * side
        place = pl.ds(pl.multiple_of(part * D + group * GW, GW), GW)
        return remote(
            sq3.at[to_core, to_side, :, pl.ds(part * GW, GW)], oq_ref.at[:, place],
            qs4.at[n, part], qr4.at[n, part], device,
        )

    def q4_own(part):
        place = pl.ds(pl.multiple_of(part * D + group * GW, GW), GW)
        return pltpu.make_async_copy(sq3.at[c, lo, :, pl.ds(part * GW, GW)], oq_ref.at[:, place], lsem.at[2 + part])

    def v_core():
        return remote(vm.at[0], vd, vs.at[0], vr.at[0], at.near)

    def v_x(n):
        return remote(vm.at[1], vx.at[n - 1], vsx.at[n - 1], vrx.at[n - 1], at.x_device(n))

    def v_y(n):
        return remote(vm.at[2], vy.at[n - 1], vsy.at[n - 1], vry.at[n - 1], at.y_device(n))

    def v_z1():
        return remote(vm.at[3], vz1, vs.at[1], vr.at[1], at.z_one)

    def v_z2():
        return remote(vm.at[4], vz2, vs.at[2], vr.at[2], at.z_two)

    def near_copy(s):
        return remote(near_out.at[s], near_in.at[s], dsend.at[s], drecv.at[s], at.near)

    def row_copy(s):
        mark = jnp.where(s // 2 == q, r, 0)
        return remote(own.at[s], land.at[mark, rows], send.at[s], recv.at[mark, c], (2 * p + q, s))

    def row_own(s):
        return pltpu.make_async_copy(own.at[s], land.at[r, rows], lsem.at[0])

    def relay_copy(n, s):
        return remote(own.at[s], relay.at[n], rsend.at[n], rrecv.at[n], at.z_one)

    def tail_copy(s):
        return remote(tail_out.at[s], tail.at[group], csend.at[s], crecv.at[group], (2 * p + q, s))

    def tail_own(s):
        return pltpu.make_async_copy(tail_out.at[s], tail.at[group], lsem.at[1])

    def mine(s):
        return (q == c) & (s == z)

    def go(s, far, near):
        @pl.when(mine(s))
        def _():
            near(s)

        @pl.when(jnp.logical_not(mine(s)))
        def _():
            far(s)

    late[0].wait()
    for n in range(1, nx):
        q1a(n).start()
    for n in range(1, ny):
        q1b(n).start()
    for copy in loads:
        copy.wait()
    hold[...] = jnp.zeros_like(hold)
    cols_sum[...] = jnp.zeros_like(cols_sum)

    far = (STREAMS - 1 - z, z + 2 - 4 * hi, z + 1 - 2 * lo, z)

    @pl.when(jnp.logical_not(in_pair))
    def _():
        land[1] = jnp.zeros_like(land[1])

    def combine(s):
        near_copy(s).wait_recv()
        for t in range(HALF // 64):
            part = pl.ds(t * 64, 64)
            own[s, part] = add_up(near_in[s, part], own[s, part]).astype(BF16)

    def pass_on(n):
        s = far[n]
        combine(s)
        if n >= 2:
            go(s, lambda s: row_copy(s).start(), lambda s: row_own(s).start())
        else:
            @pl.when(jnp.logical_not(inner))
            def _():
                relay_copy(n, s).start()

    def pass_far(n):
        s = far[1 - n]

        @pl.when(inner)
        def _():
            relay_copy(n, s).wait_recv()
            for t in range(HALF // 64):
                part = pl.ds(t * 64, 64)
                own[s, part] = add_up(relay[n, part], own[s, part]).astype(BF16)
            row_copy(s).start()

    def partial_rows(t, carry):
        s = jnp.where(t == 0, far[0], jnp.where(t == 1, far[1], jnp.where(t == 2, far[2], far[3])))
        big[...] = nt(f[s], w[...])
        near_out[s] = big[rest].astype(BF16)
        near_copy(s).start()
        own[s] = big[rows].astype(BF16)
        tail_out[s] = big[last].astype(BF16)
        go(s, lambda s: tail_copy(s).start(), lambda s: tail_own(s).start())
        for e in range(ROWS // 48):
            part = pl.ds(e * 48, 48)
            values = xa[s, part].astype(F32)
            centre = values - jnp.mean(values, axis=1, keepdims=True)
            scale = lax.rsqrt(jnp.mean(centre * centre, axis=1, keepdims=True) + EPS)
            g = big[part]
            gh = g * (centre * scale)
            flat = f[s, part].astype(F32)
            for m in range(6):
                cols_sum[...] += flat[m * 8 : m * 8 + 8]
                hold[0] += gh[m * 8 : m * 8 + 8]
                hold[1] += g[m * 8 : m * 8 + 8]

        for n in range(STREAMS - 1):
            @pl.when(t == n + 1)
            def _():
                pass_on(n)

        return carry

    lax.fori_loop(0, STREAMS, partial_rows, 0)
    pass_on(STREAMS - 1)
    vm[0] = v_ref[...]
    vm[0, 0:1] = jnp.sum(hold[0], axis=0, keepdims=True)
    vm[0, 1:2] = jnp.sum(hold[1], axis=0, keepdims=True)
    for part in range(3):
        place = pl.ds(pl.multiple_of(group * GW, GW), GW)
        vm[0, 2 + part : 3 + part, place] = jnp.sum(cols_sum[:, part * GW : (part + 1) * GW], axis=0, keepdims=True)
    v_core().start()

    for n in range(1, nx):
        q1a(n).wait_recv()
    for n in range(1, ny):
        q1b(n).wait_recv()
    for b in range(ny):
        sq1a[b] = add_up(q1[b, x, :, :, 0:QCUT], *[rq1a[n, b] for n in range(nx - 1)]).astype(BF16)
    for n in range(1, ny):
        q2a(n).start()
    for b in range(nx):
        sq1b[b] = add_up(q1[y, b, :, :, QCUT:], *[rq1b[n, b] for n in range(ny - 1)]).astype(BF16)
    for n in range(1, nx):
        q2b(n).start()
    v_core().wait_recv()
    vm[1] = vm[0] + vd[...]
    for n in range(1, nx):
        v_x(n).start()
    pass_far(0)
    for n in range(1, ny):
        q2a(n).wait_recv()
    for n in range(1, nx):
        q2b(n).wait_recv()
    left = add_up(sq1a[y], *[rq2a[n] for n in range(ny - 1)]).astype(BF16)
    right = add_up(sq1b[x], *[rq2b[n] for n in range(nx - 1)]).astype(BF16)
    sq2[:, :, :, :, 0:QCUT] = left.reshape(2, 2, 2, rb, QCUT)
    sq2[:, :, :, :, QCUT:] = right.reshape(2, 2, 2, rb, QCUT)
    q3().start()
    for n in range(1, nx):
        v_x(n).wait_recv()
    vm[2] = add_up(vm[1], *[vx[n] for n in range(nx - 1)])
    for n in range(1, ny):
        v_y(n).start()
    for n in range(1, ny):
        v_y(n).wait_recv()
    vm[3] = add_up(vm[2], *[vy[n] for n in range(ny - 1)])
    v_z1().start()
    pass_far(1)
    q3().wait_recv()
    sq3[...] = add_up(sq2[:, hi], rq3[...])
    for part in range(3):
        for n in range(3):
            q4(n, part).start()
        q4_own(part).start()
    v_z1().wait_recv()
    vm[4] = vm[3] + vz1[...]
    v_z2().start()

    late[1].wait()
    late[2].wait()
    for side in range(2):
        for core in range(2):
            part = pl.ds(core * HALF, HALF)
            g = 2 * side + core
            self_made = (core == c) & (2 * c + side == z)

            @pl.when(jnp.logical_not(self_made))
            def _():
                remote(tail_out.at[0], tail.at[g], csend.at[0], crecv.at[g], at.near).wait_recv()

            @pl.when(jnp.logical_not(self_made) & (in_pair | (side == 0)))
            def _():
                remote(own.at[0], land.at[side, part], send.at[0], recv.at[side, core], at.near).wait_recv()

            @pl.when(self_made)
            def _():
                row_own(0).wait()
                tail_own(0).wait()

    gain = gain_ref[0:1]

    def back(dst, grad):
        values = x_own[dst].astype(F32)
        centre = values - jnp.mean(values, axis=1, keepdims=True)
        scale = lax.rsqrt(jnp.mean(centre * centre, axis=1, keepdims=True) + EPS)
        normed = centre * scale
        g = grad * gain
        total[dst] = h_own[dst] + scale * (
            g - jnp.mean(g, axis=1, keepdims=True) - normed * jnp.mean(g * normed, axis=1, keepdims=True)
        )

    def back_rows(t, carry):
        part = pl.ds(pl.multiple_of(t * 64, 64), 64)
        back(part, add_up(land[0, part], land[1, part]))
        return carry

    lax.fori_loop(0, VIS // 64, back_rows, 0)
    back(last, add_up(tail[0], tail[1], tail[2], tail[3]))
    done = pltpu.make_async_copy(total, gx_ref, lsem.at[5])
    done.start()
    v_z2().wait_recv()
    vm[5] = vm[4] + vz2[...]
    v_done = pltpu.make_async_copy(vm.at[5], ov_ref, lsem.at[6])
    v_done.start()
    for n in range(1, nx):
        q1a(n).wait_send()
        q2b(n).wait_send()
        v_x(n).wait_send()
    for n in range(1, ny):
        q1b(n).wait_send()
        q2a(n).wait_send()
        v_y(n).wait_send()
    q3().wait_send()
    v_core().wait_send()
    v_z1().wait_send()
    v_z2().wait_send()
    for n in range(STREAMS):
        s = far[n]
        near_copy(s).wait_send()
        if n < 2:
            @pl.when(inner)
            def _():
                row_copy(s).wait_send()

            @pl.when(jnp.logical_not(inner))
            def _():
                relay_copy(n, s).wait_send()

            tail_copy(s).wait_send()
        else:
            @pl.when(jnp.logical_not(mine(s)))
            def _():
                row_copy(s).wait_send()
                tail_copy(s).wait_send()
    for part in range(3):
        q4_own(part).wait()
        for n in range(3):
            q4(n, part).wait_send()
            q4(n, part).wait_recv()
    done.wait()
    v_done.wait()


def finish_rows(flat, x_all, g_qkv, w_qkv, x, h, vectors, gain):
    nx, ny, rb = grid_shape()

    def v(*shape):
        return VM(shape, BF16)

    def vf(*shape):
        return VM(shape, F32)

    scratch = [
        v(STREAMS, ROWS, 3 * GW), v(STREAMS, ROWS, D), v(D, 3 * GW), v(ROWS, D), vf(ROWS, D), vf(ROWS, D),
        v(STREAMS, HALF, D), v(STREAMS, HALF, D), v(STREAMS, HALF, D), v(2, VIS, D), v(4, CROWS, D), v(4, CROWS, D),
        vf(ROWS, D),
        v(ny, nx, 8, rb, 3 * GW), v(nx - 1, ny, 8, rb, QCUT), v(ny - 1, nx, 8, rb, QCUT),
        v(ny, 8, rb, QCUT), v(nx, 8, rb, QCUT), v(ny - 1, 8, rb, QCUT), v(nx - 1, 8, rb, QCUT),
        v(2, 2, 2, rb, 3 * GW), v(2, 2, rb, 3 * GW), vf(2, 2, rb, 3 * GW),
        vf(6, 16, D), vf(16, D), vf(nx - 1, 16, D), vf(ny - 1, 16, D), vf(16, D), vf(16, D), vf(2, 8, D),
        dma(8), dma(4), dma(4), dma(4), dma(2, 2), dma(4), dma(4), dma(7),
        dma(nx - 1), dma(nx - 1), dma(ny - 1), dma(ny - 1), dma(ny - 1), dma(ny - 1), dma(nx - 1), dma(nx - 1),
        pltpu.SemaphoreType.DMA, pltpu.SemaphoreType.DMA, dma(3, 3), dma(3, 3),
        dma(3), dma(3), dma(nx - 1), dma(nx - 1), dma(ny - 1), dma(ny - 1),
        v(2, HALF, D), dma(2), dma(2), vf(8, 3 * GW),
    ]
    outs = (((ROWS, D), F32), ((rb, 3 * D), F32), ((16, D), F32))
    ops = (flat, x_all, g_qkv.reshape(ny, nx, 8, rb, 3 * GW), w_qkv, x, h)
    return comm_call(
        functools.partial(finish_kernel, nx, ny, rb), "finish_rows", 4, outs, scratch, ops, (vectors, gain)
    )


TILE = 48
TILES = ROWS // TILE


def tn(a, b):
    return lax.dot_general(a, b, (((0,), (0,)), ((), ())), preferred_element_type=F32)


def mlp_kernel(
    win_hbm, wout_hbm, att_ref, x_ref, dy_ref, wp_ref, par_ref,
    do_out, gi_out, go_out, gp_out, y_ref, gh_ref, vec_ref,
    wi, wo, n_ref, h_ref, buf, dbuf, hid, du, yacc, dn, dhb, do_ref, stage, sums,
    isem, ssem, hs, hr, hl,
):
    p, c, q, r, z = where_am_i()

    def fetch(t, slot):
        cols = pl.ds(pl.multiple_of(t * D, D), D)
        return (
            pltpu.make_async_copy(win_hbm.at[:, cols], wi.at[slot], isem.at[0, slot]),
            pltpu.make_async_copy(wout_hbm.at[cols, :], wo.at[slot], isem.at[1, slot]),
        )

    for copy in fetch(0, 0):
        copy.start()
    greet_column()
    sums[...] = jnp.zeros_like(sums)
    for j in range(2):
        cols = slice(j * CUT, (j + 1) * CUT)
        buf[:, cols] = nn(att_ref[...], wp_ref[:, cols])

    def tile(t):
        return pl.ds(pl.multiple_of(t * TILE, 16), TILE)

    def fold(row, values):
        total = values[0:8]
        for m in range(1, TILE // 8):
            total = total + values[m * 8 : m * 8 + 8]
        sums[row] += total

    def enter(t, carry):
        rows = tile(t)
        h = x_ref[rows].astype(F32) + buf[rows] + par_ref[9:10]
        h_ref[rows] = h
        centre = h - jnp.mean(h, axis=1, keepdims=True)
        scale = lax.rsqrt(jnp.mean(centre * centre, axis=1, keepdims=True) + EPS)
        n_ref[rows] = (centre * scale * par_ref[10:11] + par_ref[11:12]).astype(BF16)
        return carry

    lax.fori_loop(0, TILES, enter, 0)

    def block(t, carry):
        slot = t % 2
        for copy in fetch(t, slot):
            copy.wait()

        @pl.when(t < 3)
        def _():
            for copy in fetch(t + 1, 1 - slot):
                copy.start()

        for j in range(2):
            cols = slice(j * CUT, (j + 1) * CUT)
            buf[:, cols] = nn(n_ref[...], wi[slot, :, cols])
            dbuf[:, cols] = nt(dy_ref[...], wo[slot, cols, :])
        place = pl.ds(pl.multiple_of(t * D, D), D)

        def act(e, carry):
            rows = tile(e)
            for j in range(4):
                cols = slice(j * 256, (j + 1) * 256)
                u = buf[rows, cols] + par_ref[pl.ds(5 + t, 1), cols]
                phi = 0.5 * (1.0 + lax.erf(u * (2.0**-0.5)))
                hid[rows, pl.ds(pl.multiple_of(t * D + j * 256, 256), 256)] = (u * phi).astype(BF16)
                slope = phi + u * (jnp.exp(-0.5 * u * u) * ((2.0 * math.pi) ** -0.5))
                g = (dbuf[rows, cols] * slope).astype(BF16)
                du[rows, pl.ds(pl.multiple_of(t * D + j * 256, 256), 256)] = g
                g = g.astype(F32)
                total = g[0:8]
                for m in range(1, TILE // 8):
                    total = total + g[m * 8 : m * 8 + 8]
                sums[t, :, cols] += total
            return carry

        lax.fori_loop(0, TILES, act, 0)
        for j in range(2):
            cols = slice(j * CUT, (j + 1) * CUT)
            more = nn(hid[:, place], wo[slot, :, cols])
            back = nt(du[:, place], wi[slot, cols, :])

            @pl.when(t == 0)
            def _():
                yacc[:, cols] = more
                dn[:, cols] = back

            @pl.when(t > 0)
            def _():
                yacc[:, cols] += more
                dn[:, cols] += back

        return carry

    lax.fori_loop(0, 4, block, 0)

    def leave(t, carry):
        rows = tile(t)
        h = h_ref[rows]
        y_ref[rows] = (h + yacc[rows] + par_ref[12:13]).astype(BF16)
        centre = h - jnp.mean(h, axis=1, keepdims=True)
        scale = lax.rsqrt(jnp.mean(centre * centre, axis=1, keepdims=True) + EPS)
        normed = centre * scale
        grad = dn[rows]
        dy = dy_ref[rows].astype(F32)
        fold(5, grad * normed)
        fold(6, grad)
        fold(7, dy)
        g = grad * par_ref[10:11]
        gh = dy + scale * (
            g - jnp.mean(g, axis=1, keepdims=True) - normed * jnp.mean(g * normed, axis=1, keepdims=True)
        )
        gh_ref[rows] = gh
        low = gh.astype(BF16)
        dhb[rows] = low
        fold(4, low.astype(F32))
        return carry

    lax.fori_loop(0, TILES, leave, 0)
    for j in range(2):
        rows = slice(j * CUT, (j + 1) * CUT)
        do_ref[:, rows] = nt(dhb[...], wp_ref[rows, :]).astype(BF16)

    def heads_copy(g):
        device = (2 * p + g % 2, 2 * c + g // 2)
        return remote(do_ref.at[:, pl.ds(g * GW, GW)], do_out.at[z], hs.at[g], hr.at[z], device)

    def heads_own(g):
        return pltpu.make_async_copy(do_ref.at[:, pl.ds(g * GW, GW)], do_out.at[z], hl)

    for g in range(4):
        self_made = (g % 2 == c) & (2 * c + g // 2 == z)

        @pl.when(self_made)
        def _():
            heads_own(g).start()

        @pl.when(jnp.logical_not(self_made))
        def _():
            heads_copy(g).start()

    vec_ref[...] = jnp.zeros_like(vec_ref)
    for n in range(8):
        vec_ref[5 + n : 6 + n] = jnp.sum(sums[n], axis=0, keepdims=True)

    def in_save(t):
        return pltpu.make_async_copy(stage.at[0], gi_out.at[:, pl.ds(pl.multiple_of(t * D, D), D)], ssem.at[0])

    def out_save(t):
        return pltpu.make_async_copy(stage.at[1], go_out.at[pl.ds(pl.multiple_of(t * D, D), D), :], ssem.at[1])

    def weights(t, carry):
        @pl.when(t > 0)
        def _():
            in_save(t - 1).wait()

        for m in range(2):
            half = pl.ds(m * CUT, CUT)
            place = pl.ds(pl.multiple_of(t * D, D), D)
            stage[0, half, :] = tn(n_ref[:, half], du[:, place]).astype(BF16)
        in_save(t).start()

        @pl.when(t > 0)
        def _():
            out_save(t - 1).wait()

        for m in range(2):
            half = pl.ds(m * CUT, CUT)
            place = pl.ds(pl.multiple_of(t * D + m * CUT, CUT), CUT)
            stage[1, half, :] = tn(hid[:, place], dy_ref[...]).astype(BF16)
        out_save(t).start()
        return carry

    lax.fori_loop(0, 4, weights, 0)
    in_save(3).wait()
    for m in range(2):
        half = pl.ds(m * CUT, CUT)
        stage[0, half, :] = tn(att_ref[:, half], dhb[...]).astype(BF16)
    proj_save = pltpu.make_async_copy(stage.at[0], gp_out, ssem.at[0])
    proj_save.start()
    for g in range(4):
        self_made = (g % 2 == c) & (2 * c + g // 2 == z)

        @pl.when(self_made)
        def _():
            heads_own(g).wait()

        @pl.when(jnp.logical_not(self_made))
        def _():
            heads_copy(g).wait_send()
    for s in range(STREAMS):
        @pl.when((q != c) | (s != z))
        def _():
            remote(do_ref.at[:, pl.ds(0, GW)], do_out.at[s], hs.at[0], hr.at[s], (2 * p + 1 - c, z)).wait_recv()
    out_save(3).wait()
    proj_save.wait()


def mlp(w_in, w_out, attended, x, dy, w_proj, params):
    def v16(*shape):
        return VM(shape, BF16)

    def vf(*shape):
        return VM(shape, F32)

    scratch = [
        v16(2, D, D), v16(2, D, D), v16(ROWS, D), vf(ROWS, D), vf(ROWS, D), vf(ROWS, D),
        v16(ROWS, 4 * D), v16(ROWS, 4 * D), vf(ROWS, D), vf(ROWS, D), v16(ROWS, D), v16(ROWS, D),
        v16(2, D, D), vf(8, 8, D),
        dma(2, 2), dma(2), dma(4), dma(4), pltpu.SemaphoreType.DMA,
    ]
    outs = (((STREAMS, ROWS, GW), BF16), ((D, 4 * D), BF16), ((4 * D, D), BF16), ((D, D), BF16))
    near_outs = (((ROWS, D), BF16), ((ROWS, D), F32), ((16, D), F32))
    return comm_call(
        mlp_kernel, "mlp", 1, outs, scratch, (w_in, w_out), (attended, x, dy, w_proj, params), near_outs
    )


def own_meta(lengths, mask):
    frames = jnp.arange(FRAMES, dtype=jnp.int32)
    ends = jnp.cumsum(lengths)
    reached = ends[None, :] <= frames[:, None]
    begin = jnp.sum(jnp.where(reached, lengths[None, :], 0), axis=1)
    episode = jnp.sum(reached, axis=1)[:, None] == jnp.arange(lengths.shape[0])[None, :]
    length = jnp.sum(jnp.where(episode, lengths[None, :], 0), axis=1)
    base = jnp.where(length == MOST, 0, jnp.where(length == MIDDLE - MOST, MOST, MIDDLE))
    slot = base + frames - begin
    perm = jnp.sum(jnp.where(slot[:, None] == frames[None, :], frames[:, None], 0), axis=0)
    stream = jnp.arange(STREAMS)[:, None]
    row = jnp.arange(CROWS)[None, :]
    part = FRAMES // STREAMS
    frame = jnp.where(row < part * COND, part * stream + row // COND, FRAMES)
    cslot = jnp.sum(jnp.where(frame[..., None] == frames, slot[None, None, :], 0), axis=-1)
    cslot = jnp.where(frame < FRAMES, cslot, 99).reshape(1, PART)
    hidden = jnp.where(mask == 1, 0.0, NEG).astype(F32)
    bias = jnp.sum(jnp.where((perm[:, None] == frames[None, :])[:, :, None], hidden[None], 0.0), axis=1)
    line = jnp.pad(cslot.astype(F32), ((0, 7), (0, PATCHES - PART)))
    return perm.astype(jnp.int32), slot.astype(jnp.int32), jnp.concatenate([bias, line], axis=0)


def per_device(
    visual, conditioning, d_visual, d_conditioning, episode_frames, patch_mask,
    ln1_gain, ln1_bias, w_qkv, b_qkv, w_proj, b_proj, ln2_gain, ln2_bias, w_in, b_in, w_out, b_out,
):
    d, z = lax.axis_index("dp"), lax.axis_index("stream")
    extra = conditioning.shape[1] * COND
    perm, slot, own = own_meta(episode_frames[0], patch_mask[0])
    x, dy = place_rows(perm, visual, conditioning, d_visual, d_conditioning)
    params = jnp.concatenate(
        [ln1_gain, ln1_bias, b_qkv, b_in, b_proj, ln2_gain, ln2_bias, b_out, jnp.zeros((3 * D,), BF16)]
    ).astype(F32).reshape(16, D)
    tables = tuple(jnp.asarray(t) for t in rope_constants())
    attended, x_all, a, q, k, v, o, meta, *rest = attend_forward(x, w_qkv, own, params, tables)
    grad_heads, grad_w_in, grad_w_out, grad_w_proj, output, grad_h, vectors = mlp(
        w_in, w_out, attended, x, dy, w_proj, params
    )
    red_out, red_in, red_proj, grad_qkv = attend_backward(
        grad_w_out, grad_w_in, grad_w_proj, grad_heads, (q, k, v, *rest), o, tables, meta
    )
    role_grad = jnp.einsum(
        "rd,re->de", a.reshape(STREAMS * ROWS, D), grad_qkv.reshape(STREAMS * ROWS, 3 * GW), preferred_element_type=F32
    )
    grad_x, red_qkv, sums = finish_rows(
        grad_qkv, x_all, role_grad.astype(BF16), w_qkv, x, grad_h, vectors, params
    )
    out_visual, grad_visual = restore_rows(slot, output, grad_x)
    owner = d * STREAMS + z
    owners = lax.axis_size("dp") * STREAMS

    def share(start, rows):
        size = rows * D // owners
        return lax.dynamic_slice_in_dim(sums[start : start + rows].reshape(-1), owner * size, size, 0)

    return (
        out_visual.reshape(visual.shape), output[VIS : VIS + extra].reshape(conditioning.shape),
        grad_visual.reshape(visual.shape), grad_x[VIS : VIS + extra].reshape(conditioning.shape),
        share(0, 1), share(1, 1), red_qkv, share(2, 2), share(4, 1), red_proj, share(9, 1), share(10, 1), share(11, 1),
        red_in, share(5, 4), red_out.reshape(-1, D), share(12, 1),
    )


def solution(mesh):
    rows = P("dp", None, "stream", None)
    extra = P("dp", "stream", None, None)
    vector = P(("dp", "stream"))
    matrix = P(("dp", "stream"), None)
    in_specs = (rows, extra, rows, extra, P("dp", None), P("dp", None, None)) + (P(),) * 12
    out_specs = (
        rows, extra, rows, extra, vector, vector, matrix, vector, vector, matrix, vector, vector, vector, matrix,
        vector, matrix, vector,
    )
    return jax.shard_map(per_device, mesh=mesh, in_specs=in_specs, out_specs=out_specs, check_vma=False)
```

```python
import functools
import math

import jax
import jax.numpy as jnp
import numpy as np
from jax import lax
from jax.experimental import pallas as pl
from jax.experimental.pallas import tpu as pltpu
from jax.sharding import PartitionSpec as P

D = 1024
HEADS = 16
HEAD_DIM = 64
GRID = 16
COND = 2
FRAMES = 8
MOST = 5
MIDDLE = 7
STREAMS = 4
GROUP = 4
GW = GROUP * HEAD_DIM
PART = 64
PATCHES = 256
VIS = FRAMES * PART
CROWS = 16
ROWS = VIS + CROWS
WIDE = GROUP * 128
NEG = -1e30
EPS = 1e-06
F32 = jnp.float32
BF16 = jnp.bfloat16
VM = pltpu.VMEM
FULL = pl.BlockSpec(memory_space=pltpu.VMEM)
ANYM = pl.BlockSpec(memory_space=pltpu.HBM)
LIMIT = 60 * 1024 * 1024


def nn(a, b):
    return lax.dot_general(a, b, (((1,), (0,)), ((), ())), preferred_element_type=F32)


def nt(a, b):
    return lax.dot_general(a, b, (((1,), (1,)), ((), ())), preferred_element_type=F32)


def rope_constants():
    pair = np.arange(HEAD_DIM // 2)
    exponent = np.where(pair < 30, (pair % 10) / 10.0, 0.0).astype(np.float32)
    freq = np.exp(-math.log(10000.0) * exponent).astype(np.float32)
    patch = np.arange(PATCHES)
    slot_time = np.array([0, 1, 2, 3, 4, 0, 1, 0])
    is_time = (pair < 10)[None, :]
    place = np.where(
        (pair >= 20)[None, :], (patch % GRID)[:, None], (patch // GRID)[:, None]
    ) * ((pair >= 10) & (pair < 30))[None, :]
    angle_patch = (place * freq[None, :]).astype(np.float32)
    angle_time = (slot_time[:, None] * freq[None, :]).astype(np.float32)
    cos_patch = np.where(is_time, 0.0, np.cos(angle_patch))
    sin_patch = np.where(is_time, 0.0, np.sin(angle_patch))
    cos_time = np.where(is_time, np.cos(angle_time), 0.0)
    sin_time = np.where(is_time, np.sin(angle_time), 0.0)

    def spread(table, signed):
        two = np.repeat(table, 2, axis=1)
        if signed:
            two = two * np.where(np.arange(HEAD_DIM) % 2 == 0, -1.0, 1.0)[None, :]
        return np.tile(two, (1, GROUP)).astype(np.float32)

    return (
        spread(cos_patch, False),
        spread(sin_patch, True),
        spread(cos_time, False),
        spread(sin_time, True),
    )


def swap_pairs(v):
    lane = lax.broadcasted_iota(jnp.int32, v.shape, 1)
    width = v.shape[1]
    return jnp.where(lane % 2 == 0, pltpu.roll(v, width - 1, 1), pltpu.roll(v, 1, 1))


def turn(v, cosine, sine):
    return v * cosine + swap_pairs(v) * sine


def pad_heads(t, extra):
    pieces = []
    for h in range(GROUP):
        pieces += [t[:, h * HEAD_DIM : (h + 1) * HEAD_DIM], extra]
    return jnp.concatenate(pieces, axis=1)


def pad_right(t):
    extra = jnp.zeros((t.shape[0], HEAD_DIM), t.dtype)
    pieces = []
    for h in range(GROUP):
        pieces += [extra, t[:, h * HEAD_DIM : (h + 1) * HEAD_DIM]]
    return jnp.concatenate(pieces, axis=1)


def unpad_heads(t):
    return jnp.concatenate([t[:, h * 128 : h * 128 + HEAD_DIM] for h in range(GROUP)], axis=1)


def head(t, h):
    return t[:, h * 128 : (h + 1) * 128]


def first_slot(i):
    return jnp.where(i < MOST, 0, jnp.where(i < MIDDLE, MOST, MIDDLE))


def cond_tables(cs_col, ct, st):
    cosine = jnp.zeros((PART, GW), F32)
    sine = jnp.zeros((PART, GW), F32)
    for j in range(FRAMES):
        here = cs_col == j
        cosine = cosine + jnp.where(here, ct[j : j + 1, :], 0.0)
        sine = sine + jnp.where(here, st[j : j + 1, :], 0.0)
    lane = lax.broadcasted_iota(jnp.int32, (PART, GW), 1) % HEAD_DIM
    return jnp.where(lane < 20, cosine, 1.0), sine


def read_meta(meta_ref):
    bias_t = jnp.transpose(meta_ref[0:FRAMES])
    cs_row = meta_ref[FRAMES : FRAMES + 1, 0:PART].astype(jnp.int32)
    cs_col = jnp.transpose(meta_ref[FRAMES:, :])[0:PART, 0:1].astype(jnp.int32)
    return cs_col, cs_row, bias_t


def place_kernel(perm, xv_ref, xc_ref, dv_ref, dc_ref, x_ref, dy_ref, sem):
    copies = []
    for n, (rows, out) in enumerate(((xv_ref, x_ref), (dv_ref, dy_ref))):
        for i in range(FRAMES):
            copies.append(pltpu.make_async_copy(rows.at[perm[i]], out.at[pl.ds(i * PART, PART)], sem.at[n, i]))
    for copy in copies:
        copy.start()
    for extra, out in ((xc_ref, x_ref), (dc_ref, dy_ref)):
        out[VIS:, :] = jnp.zeros((CROWS, D), BF16)
        out[VIS : VIS + extra.shape[0], :] = extra[...]
    for copy in copies:
        copy.wait()


def place_rows(perm, visual, extra, d_visual, d_extra):
    return pl.pallas_call(
        place_kernel,
        name="place_rows",
        out_shape=(jax.ShapeDtypeStruct((ROWS, D), BF16),) * 2,
        in_specs=[pl.BlockSpec(memory_space=pltpu.SMEM), ANYM, FULL, ANYM, FULL],
        out_specs=(FULL, FULL),
        scratch_shapes=[pltpu.SemaphoreType.DMA((2, FRAMES))],
    )(perm, visual.reshape(FRAMES, PART, D), extra.reshape(-1, D), d_visual.reshape(FRAMES, PART, D), d_extra.reshape(-1, D))


def restore_kernel(slot, y_ref, g_ref, yo_ref, go_ref, sem):
    copies = []
    for f in range(FRAMES):
        rows = pl.ds(pl.multiple_of(slot[f] * PART, PART), PART)
        copies.append(pltpu.make_async_copy(y_ref.at[rows], yo_ref.at[f], sem.at[0, f]))
        copies.append(pltpu.make_async_copy(g_ref.at[rows], go_ref.at[f], sem.at[1, f]))
    for copy in copies:
        copy.start()
    for copy in copies:
        copy.wait()


def restore_rows(slot, y, g):
    shape = (FRAMES, PART, D)
    return pl.pallas_call(
        restore_kernel,
        name="restore_rows",
        out_shape=(jax.ShapeDtypeStruct(shape, BF16), jax.ShapeDtypeStruct(shape, F32)),
        in_specs=[pl.BlockSpec(memory_space=pltpu.SMEM), ANYM, ANYM],
        out_specs=(FULL, FULL),
        scratch_shapes=[pltpu.SemaphoreType.DMA((2, FRAMES))],
    )(slot, y, g)


def where_am_i():
    d, z = lax.axis_index("dp"), lax.axis_index("stream")
    return d // 2, d % 2, z // 2, z % 2, z


def greet_column():
    p, c, q, r, z = where_am_i()
    barrier = pltpu.get_barrier_semaphore()
    for core in range(2):
        for chip in range(STREAMS):
            @pl.when((core != c) | (chip != z))
            def _():
                pl.semaphore_signal(
                    barrier, inc=1, device_id=(2 * p + core, chip),
                    device_id_type=pl.DeviceIdType.MESH,
                )
    pl.semaphore_wait(barrier, 2 * STREAMS - 1)


def remote(src, dst, send, recv, device):
    return pltpu.make_async_remote_copy(
        src_ref=src, dst_ref=dst, send_sem=send, recv_sem=recv, device_id=device,
        device_id_type=pl.DeviceIdType.MESH,
    )


def comm_call(kernel, name, ident, outs, scratch, far, close=(), near_outs=()):
    return pl.pallas_call(
        kernel,
        name=name,
        out_shape=tuple(jax.ShapeDtypeStruct(s, t) for s, t in tuple(outs) + tuple(near_outs)),
        in_specs=[ANYM] * len(far) + [FULL] * len(close),
        out_specs=tuple(ANYM for _ in outs) + tuple(FULL for _ in near_outs),
        scratch_shapes=scratch,
        compiler_params=pltpu.CompilerParams(
            collective_id=ident, has_side_effects=True, vmem_limit_bytes=LIMIT
        ),
    )(*far, *close)


def dma(*shape):
    return pltpu.SemaphoreType.DMA(shape)


HALF = VIS // 2


PIECE = HALF // 2


def forward_kernel(
    x_hbm, w_hbm, m_hbm, par_ref, cg_ref, sg_ref, ct_ref, st_ref,
    att_ref, xa_out, a_out, q_out, k_out, v_out, o_out,
    meta_ref, qc_ref, kc_ref, vc_ref, lse_ref, lsec_ref,
    xa, a_ref, q_ref, k_ref, v_ref, o_ref, vt_ref, w, bias_ref,
    isem, whole_s, whole_r, far_s, far_r, pass_s, near_s, near_r, tail_s, tail_r, msem, out_s, out_r, out_l, keep,
):
    p, c, q, r, z = where_am_i()
    group = 2 * r + c
    in_pair = q == c
    away = q != c
    inner = z == 1 + q
    z_one, z_two, z_three = z + 1 - 2 * r, z + 2 - 4 * q, STREAMS - 1 - z
    other = (2 * p + 1 - c, z)
    across = (2 * p + c, z_one)
    loads = []
    for part in range(3):
        cols = pl.ds(pl.multiple_of(part * D + group * GW, GW), GW)
        loads.append(pltpu.make_async_copy(w_hbm.at[:, cols], w.at[part], isem.at[part]))
    for copy in loads:
        copy.start()
    own_rows = pltpu.make_async_copy(x_hbm, xa.at[z], isem.at[3])

    @pl.when(in_pair)
    def _():
        own_rows.start()

    greet_column()
    tail = pl.ds(VIS, CROWS)

    def piece(half, g):
        return pl.ds(pl.multiple_of(half * HALF + g * PIECE, PIECE), PIECE)

    def whole_copy():
        return remote(x_hbm, xa.at[z], whole_s, whole_r, other)

    def far_copy(half, g):
        rows = piece(half, g)
        return remote(x_hbm.at[rows], xa.at[z, rows], far_s.at[half, g], far_r.at[z, g], (2 * p + half, 1 + c))

    def own_pass(g):
        rows = piece(c, g)
        return remote(x_hbm.at[rows], xa.at[z, rows], pass_s.at[z, g], far_r.at[z, g], across)

    def far_pass(s, g):
        rows = piece(c, g)
        return remote(xa.at[s, rows], xa.at[s, rows], pass_s.at[s, g], far_r.at[s, g], across)

    def near_copy(s, g, half):
        rows = piece(half, g)
        return remote(xa.at[s, rows], xa.at[s, rows], near_s.at[s, g], near_r.at[s, g], other)

    def tail_copy(half, side):
        n = half * 2 + side
        return remote(x_hbm.at[tail], xa.at[z, tail], tail_s.at[n], tail_r.at[z], (2 * p + half, 2 * c + side))

    def tail_needed(half, side):
        return jnp.logical_not((2 * c + side == z))

    def meta_copy():
        return remote(m_hbm, meta_ref, msem.at[0], msem.at[1], other)

    def meta_own():
        return pltpu.make_async_copy(m_hbm, meta_ref, msem.at[2])

    @pl.when(in_pair)
    def _():
        meta_own().start()
        meta_copy().start()
        whole_copy().start()
        own_pass(0).start()
        own_pass(1).start()

    for half in range(2):
        @pl.when(away)
        def _():
            far_copy(half, 0).start()

        for side in range(2):
            @pl.when(tail_needed(half, side))
            def _():
                tail_copy(half, side).start()

    def arrive(s, g, relay):
        far_pass(s, g).wait_recv()
        near_copy(s, g, c).start()
        if relay:
            @pl.when(inner)
            def _():
                far_pass(s, g).start()

    gain, shift = par_ref[0:1], par_ref[1:2]
    cut = pl.ds(pl.multiple_of(group * GW, GW), GW)
    lane64 = lax.broadcasted_iota(jnp.int32, (PATCHES, 64), 1)
    one = jnp.where(lane64 == 0, 1.0, 0.0).astype(BF16)

    def project(x, cosine, sine):
        x = x.astype(F32)
        centre = x - jnp.mean(x, axis=1, keepdims=True)
        spread = jnp.mean(centre * centre, axis=1, keepdims=True)
        a = (centre * lax.rsqrt(spread + EPS) * gain + shift).astype(BF16)
        q = turn(nn(a, w[0]) + par_ref[2:3, cut], cosine, sine)
        k = turn(nn(a, w[1]) + par_ref[3:4, cut], cosine, sine)
        v = (nn(a, w[2]) + par_ref[4:5, cut]).astype(BF16)
        return a, (q.astype(BF16).astype(F32) * 0.125).astype(BF16), k.astype(BF16), v

    def unit(t, carry):
        @pl.when(t == 0)
        def _():
            for copy in loads:
                copy.wait()

            @pl.when(in_pair)
            def _():
                own_rows.wait()
                meta_own().wait()

            @pl.when(away)
            def _():
                whole_copy().wait_recv()
                far_pass(z, 0).start()
                far_pass(z, 1).start()
                meta_copy().wait_recv()

            bias_ref[...] = jnp.transpose(meta_ref[0:FRAMES])

        @pl.when(t == 2)
        def _():
            arrive(z_one, 0, False)
            arrive(z_one, 1, False)

            @pl.when(away)
            def _():
                for half in range(2):
                    far_copy(half, 0).wait_send()
                    far_copy(half, 1).start()

            arrive(z_two, 0, True)
            arrive(z_three, 0, True)
            near_copy(z_one, 0, 1 - c).wait_recv()
            near_copy(z_one, 1, 1 - c).wait_recv()

        @pl.when(t == 4)
        def _():
            near_copy(z_two, 0, 1 - c).wait_recv()
            near_copy(z_three, 0, 1 - c).wait_recv()

        @pl.when(t == 6)
        def _():
            arrive(z_two, 1, True)
            arrive(z_three, 1, True)
            near_copy(z_two, 1, 1 - c).wait_recv()
            near_copy(z_three, 1, 1 - c).wait_recv()

        g = jnp.where(t < 4, t % 2, (t - 4) // 2)
        s = jnp.where(t < 2, z, jnp.where(t < 4, z_one, jnp.where(t % 2 == 0, z_two, z_three)))
        x = jnp.concatenate([xa[s, piece(0, g)], xa[s, piece(1, g)]], axis=0)
        place = pl.ds(pl.multiple_of(s * PART, PART), PART)
        cosine, sine, bias = [], [], []
        ids = lax.broadcasted_iota(jnp.int32, (PART, FRAMES), 1)
        for n in range(4):
            i = 2 * g + n % 2 + 4 * (n // 2)
            cosine.append(cg_ref[place] + ct_ref[pl.ds(i, 1), :])
            sine.append(sg_ref[place] + st_ref[pl.ds(i, 1), :])
            bias.append(jnp.sum(jnp.where(ids == i, bias_ref[place], 0.0), axis=1, keepdims=True))
        a, qs, ks, vs = project(x, jnp.concatenate(cosine, axis=0), jnp.concatenate(sine, axis=0))
        a_ref[s, piece(0, g)] = a[:PIECE]
        a_ref[s, piece(1, g)] = a[PIECE:]
        bias = jnp.concatenate(bias, axis=0)
        qs = pad_heads(qs, one)
        ks = pad_heads(ks, jnp.where(lane64 == 0, bias, 0.0).astype(BF16))
        vs = pad_right(vs)
        for n in range(4):
            i = 2 * g + n % 2 + 4 * (n // 2)
            rows = slice(n * PART, (n + 1) * PART)
            q_ref[i, place] = qs[rows]
            k_ref[i, place] = ks[rows]
            v_ref[i, place] = vs[rows]
        return carry

    lax.fori_loop(0, 8, unit, 0)

    for s in range(STREAMS):
        @pl.when(s != z)
        def _():
            remote(x_hbm.at[tail], xa.at[s, tail], tail_s.at[0], tail_r.at[s], other).wait_recv()
    cs_col, cs_row, _ = read_meta(meta_ref)
    a, qs, ks, vs = project(xa[:, VIS:, :].reshape(PART, D), *cond_tables(cs_col, ct_ref[...], st_ref[...]))
    a_ref[:, VIS:, :] = a.reshape(STREAMS, CROWS, D)
    qc_ref[...] = pad_heads(qs, one[:PART])
    kc_ref[...] = pad_heads(ks, jnp.zeros((PART, 64), BF16))
    vc_ref[...] = pad_right(vs)
    vct = jnp.transpose(vs.astype(F32)).astype(BF16)
    saves = [(xa, xa_out), (a_ref, a_out), (q_ref, q_out), (k_ref, k_out), (v_ref, v_out)]
    saves = [pltpu.make_async_copy(src, dst, keep.at[n]) for n, (src, dst) in enumerate(saves)]
    for copy in saves:
        copy.start()

    def out_rows(i):
        return pl.ds(pl.multiple_of(i * PART, PART), PART)

    def out_copy(s, n, rows):
        place = pl.ds(pl.multiple_of(group * GW, GW), GW)
        return remote(o_ref.at[s, rows], att_ref.at[rows, place], out_s.at[s, n], out_r.at[group, n], (2 * p + q, s))

    def out_own(s, n, rows):
        place = pl.ds(pl.multiple_of(group * GW, GW), GW)
        return pltpu.make_async_copy(o_ref.at[s, rows], att_ref.at[rows, place], out_l.at[n])

    def send_out(n, rows):
        for s in range(STREAMS):
            mine = in_pair & (s == z)

            @pl.when(mine)
            def _():
                out_own(s, n, rows).start()

            @pl.when(jnp.logical_not(mine))
            def _():
                out_copy(s, n, rows).start()

    def slot(i, carry):
        vt_ref[i] = jnp.transpose(unpad_right(v_ref[i].astype(F32))).astype(BF16)
        low = first_slot(i)
        near = (cs_col >= low) & (cs_col <= i)
        tops, totals, blends = [], [], []
        for h in range(GROUP):
            s = jnp.where(near, nt(head(kc_ref, h), q_ref[i, :, h * 128 : (h + 1) * 128]), NEG)
            top = jnp.max(s, axis=0, keepdims=True)
            pt = jnp.exp(s - top)
            tops.append(top)
            totals.append(jnp.sum(pt, axis=0, keepdims=True))
            blends.append(nn(vct[h * HEAD_DIM : (h + 1) * HEAD_DIM], pt.astype(BF16)))

        def step(j, state):
            tops, totals, blends = state
            cols = [slice(h * 128, (h + 1) * 128) for h in range(GROUP)]
            scores = [nt(k_ref[j, :, w], q_ref[i, :, w]) for w in cols]
            peaks = [jnp.maximum(tops[h], jnp.max(scores[h], axis=0, keepdims=True)) for h in range(GROUP)]
            pts = [jnp.exp(scores[h] - peaks[h]) for h in range(GROUP)]
            stay = [jnp.exp(tops[h] - peaks[h]) for h in range(GROUP)]
            sums = [totals[h] * stay[h] + jnp.sum(pts[h], axis=0, keepdims=True) for h in range(GROUP)]
            lows = [pt.astype(BF16) for pt in pts]
            more = [nn(vt_ref[j, h * HEAD_DIM : (h + 1) * HEAD_DIM, :], lows[h]) for h in range(GROUP)]
            return peaks, sums, [blends[h] * stay[h] + more[h] for h in range(GROUP)]

        tops, totals, blends = lax.fori_loop(low, i + 1, step, (tops, totals, blends))
        o = jnp.transpose(jnp.concatenate([blends[h] / totals[h] for h in range(GROUP)], axis=0))
        o_ref[:, out_rows(i), :] = o.astype(BF16).reshape(STREAMS, PART, GW)
        lse_ref[i] = jnp.concatenate([tops[h] + jnp.log(totals[h]) for h in range(GROUP)] * 2, axis=0)
        send_out(i, out_rows(i))
        return carry

    lo_col = first_slot(cs_col)

    def cond_queries():
        near = (cs_row >= lo_col) & (cs_row <= cs_col)
        tops, totals, blends = [], [], []
        for h in range(GROUP):
            s = jnp.where(near, nt(head(qc_ref, h), head(kc_ref, h)), NEG)
            top = jnp.max(s, axis=1, keepdims=True)
            pt = jnp.exp(s - top)
            tops.append(top)
            totals.append(jnp.sum(pt, axis=1, keepdims=True))
            blends.append(nn(pt.astype(BF16), head(vc_ref, h)))

        def cond_step(j, state):
            tops, totals, blends = state
            near = (lo_col <= j) & (cs_col >= j)
            new = ([], [], [])
            for h in range(GROUP):
                s = nt(head(qc_ref, h), k_ref[j, :, h * 128 : (h + 1) * 128])
                s = jnp.where(near, s, NEG)
                top = jnp.maximum(tops[h], jnp.max(s, axis=1, keepdims=True))
                pt = jnp.exp(s - top)
                stay = jnp.exp(tops[h] - top)
                new[0].append(top)
                new[1].append(totals[h] * stay + jnp.sum(pt, axis=1, keepdims=True))
                new[2].append(blends[h] * stay + nn(pt.astype(BF16), v_ref[j, :, h * 128 : (h + 1) * 128]))
            return new

        tops, totals, blends = lax.fori_loop(0, FRAMES, cond_step, (tops, totals, blends))
        o = jnp.concatenate([(blends[h] / totals[h])[:, HEAD_DIM:] for h in range(GROUP)], axis=1)
        o_ref[:, VIS:, :] = o.astype(BF16).reshape(STREAMS, CROWS, GW)
        lane = lax.broadcasted_iota(jnp.int32, (PART, 128), 1)
        lsec = jnp.zeros((PART, 128), F32)
        for h in range(GROUP):
            lsec = lsec + jnp.where(lane == h, tops[h] + jnp.log(totals[h]), 0.0)
        lsec_ref[...] = lsec
        send_out(FRAMES, tail)

    cond_queries()
    lax.fori_loop(0, FRAMES, slot, 0)
    last = pltpu.make_async_copy(o_ref, o_out, keep.at[5])
    last.start()

    def settle(n, rows):
        for s in range(STREAMS):
            mine = in_pair & (s == z)

            @pl.when(mine)
            def _():
                out_own(s, n, rows).wait()

            @pl.when(jnp.logical_not(mine))
            def _():
                out_copy(s, n, rows).wait_send()
        for g in range(4):
            @pl.when((g % 2 != c) | (2 * c + g // 2 != z))
            def _():
                place = pl.ds(g * GW, GW)
                remote(o_ref.at[0, rows], att_ref.at[rows, place], out_s.at[0, n], out_r.at[g, n], other).wait_recv()

    def settle_slot(i, carry):
        settle(i, out_rows(i))
        return carry

    lax.fori_loop(0, FRAMES, settle_slot, 0)
    settle(FRAMES, tail)

    @pl.when(in_pair)
    def _():
        meta_copy().wait_send()
        whole_copy().wait_send()
        own_pass(0).wait_send()
        own_pass(1).wait_send()

    @pl.when(away)
    def _():
        far_pass(z, 0).wait_send()
        far_pass(z, 1).wait_send()
        far_copy(0, 1).wait_send()
        far_copy(1, 1).wait_send()

    for half in range(2):
        for side in range(2):
            @pl.when(tail_needed(half, side))
            def _():
                tail_copy(half, side).wait_send()
    for g in range(2):
        for s in (z_one, z_two, z_three):
            near_copy(s, g, c).wait_send()
        for s in (z_two, z_three):
            @pl.when(inner)
            def _():
                far_pass(s, g).wait_send()
    for copy in saves:
        copy.wait()
    last.wait()


def attend_forward(x, w_qkv, meta, params, tables):
    def v16(*shape):
        return VM(shape, BF16)

    wide = (FRAMES, PATCHES, WIDE)
    rows = (STREAMS, ROWS, D)
    outs = (
        ((ROWS, D), BF16), (rows, BF16), (rows, BF16), (wide, BF16), (wide, BF16), (wide, BF16),
        ((STREAMS, ROWS, GW), BF16),
    )
    near_outs = (
        (meta.shape, F32), ((PART, WIDE), BF16), ((PART, WIDE), BF16), ((PART, WIDE), BF16),
        ((FRAMES, 8, PATCHES), F32), ((PART, 128), F32),
    )
    scratch = [
        v16(*rows), v16(*rows), v16(*wide), v16(*wide), v16(*wide), v16(STREAMS, ROWS, GW), v16(FRAMES, GW, PATCHES),
        v16(3, D, GW), VM((PATCHES, FRAMES), F32),
        dma(4), pltpu.SemaphoreType.DMA, pltpu.SemaphoreType.DMA, dma(2, 2), dma(4, 2), dma(4, 2), dma(4, 2), dma(4, 2),
        dma(4), dma(4), dma(3), dma(4, 9), dma(4, 9), dma(9), dma(6),
    ]
    return comm_call(
        forward_kernel, "attend_forward", 0, outs, scratch, (x, w_qkv, meta), (params,) + tables, near_outs
    )
CHUNKS = 9
EARLY = 3
LATE = 4
LAST = CHUNKS - EARLY - LATE
CUT = D // 2
QCUT = 3 * GW // 2


def add_up(*terms):
    total = terms[0].astype(F32)
    for t in terms[1:]:
        total = total + t.astype(F32)
    return total


def grid_shape():
    cores = lax.axis_size("dp") // 2
    nx = 1 << ((cores.bit_length() - 1) // 2)
    return nx, cores // nx, D // (cores * 2 * STREAMS)


class Place:
    def __init__(self, nx, ny):
        d, z = lax.axis_index("dp"), lax.axis_index("stream")
        self.nx, self.ny, self.d, self.z = nx, ny, d, z
        self.p, self.c, self.hi, self.lo = d // 2, d % 2, z // 2, z % 2
        self.x, self.y = self.p % nx, self.p // nx
        self.near = (d + 1 - 2 * self.c, z)
        self.z_one = (d, z + 1 - 2 * self.lo)
        self.z_two = (d, z + 2 - 4 * self.hi)
        self.slant = (d + 1 - 2 * self.c, z + 1 - 2 * self.lo)

    def along_x(self, n):
        return lax.rem(self.x + n, self.nx)

    def along_y(self, n):
        return lax.rem(self.y + n, self.ny)

    def x_device(self, n):
        return ((self.y * self.nx + self.along_x(n)) * 2 + self.c, self.z)

    def y_device(self, n):
        return ((self.along_y(n) * self.nx + self.x) * 2 + self.c, self.z)

    def greet(self):
        barrier = pltpu.get_barrier_semaphore()
        p, c, z, nx, ny = self.p, self.c, self.z, self.nx, self.ny
        for core in range(2):
            for chip in range(STREAMS):
                @pl.when((core != c) | (chip != z))
                def _():
                    pl.semaphore_signal(
                        barrier, inc=1, device_id=(2 * p + core, chip), device_id_type=pl.DeviceIdType.MESH
                    )
        others = [self.x_device(n) for n in range(1, nx)] + [self.y_device(n) for n in range(1, ny)]
        for device in others:
            pl.semaphore_signal(barrier, inc=1, device_id=device, device_id_type=pl.DeviceIdType.MESH)
        pl.semaphore_wait(barrier, 2 * STREAMS - 1 + len(others))


class Reducer:
    def __init__(self, at, rb, count, sources, refs, ahead=True):
        self.at, self.rb, self.count, self.sources, self.ahead = at, rb, count, sources, ahead
        (self.mine, self.rd, self.r2a, self.r2b, self.r3a, self.r3b, self.s3, self.r4, self.s4, self.r5, self.fin,
         self.lsem, self.ds, self.dr, self.as2, self.ar2, self.bs2, self.br2, self.as3, self.ar3, self.bs3, self.br3,
         self.s4s, self.s4r, self.s5s, self.s5r) = refs

    @staticmethod
    def scratch(n, nx, ny, rb):
        def v(*shape):
            return VM(shape, BF16)

        return [
            v(n, ny, nx, STREAMS, rb, D), v(n, ny, nx, STREAMS, rb, D),
            v(n, nx - 1, ny, STREAMS, rb, CUT), v(n, ny - 1, nx, STREAMS, rb, CUT),
            v(n, ny - 1, STREAMS, rb, CUT), v(n, nx - 1, STREAMS, rb, CUT),
            v(n, 2, 2, rb, D), v(n, 2, rb, D), v(n, 2, rb, D), v(n, rb, D), VM((n, rb, D), F32),
            dma(n), dma(n), dma(n),
            dma(n, nx - 1), dma(n, nx - 1), dma(n, ny - 1), dma(n, ny - 1),
            dma(n, ny - 1), dma(n, ny - 1), dma(n, nx - 1), dma(n, nx - 1),
            dma(n), dma(n), dma(n), dma(n),
        ]

    def issue(self, k):
        c = self.at.c
        begin = 0
        for size, get in self.sources:
            start = begin
            begin += size

            @pl.when((k >= start) & (k < start + size))
            def _():
                t = k - start
                remote(get(t, 1 - c), self.rd.at[k], self.ds.at[k], self.dr.at[k], self.at.near).start()
                pltpu.make_async_copy(get(t, c), self.mine.at[k], self.lsem.at[k]).start()

    def core(self, k):
        return remote(self.rd.at[k], self.rd.at[k], self.ds.at[k], self.dr.at[k], self.at.near)

    def a2(self, k, n):
        at = self.at
        src = self.mine.at[k, :, at.along_x(n), :, :, pl.ds(0, CUT)]
        return remote(src, self.r2a.at[k, n - 1], self.as2.at[k, n - 1], self.ar2.at[k, n - 1], at.x_device(n))

    def b2(self, k, n):
        at = self.at
        src = self.mine.at[k, at.along_y(n), :, :, :, pl.ds(CUT, CUT)]
        return remote(src, self.r2b.at[k, n - 1], self.bs2.at[k, n - 1], self.br2.at[k, n - 1], at.y_device(n))

    def a3(self, k, n):
        at = self.at
        src = self.r2a.at[k, 0, at.along_y(n)]
        return remote(src, self.r3a.at[k, n - 1], self.as3.at[k, n - 1], self.ar3.at[k, n - 1], at.y_device(n))

    def b3(self, k, n):
        at = self.at
        src = self.r2b.at[k, 0, at.along_x(n)]
        return remote(src, self.r3b.at[k, n - 1], self.bs3.at[k, n - 1], self.br3.at[k, n - 1], at.x_device(n))

    def c4(self, k):
        return remote(self.s3.at[k, :, 1 - self.at.lo], self.r4.at[k], self.s4s.at[k], self.s4r.at[k], self.at.z_one)

    def c5(self, k):
        return remote(self.s4.at[k, 1 - self.at.hi], self.r5.at[k], self.s5s.at[k], self.s5r.at[k], self.at.z_two)

    def tick(self, t, carry=0):
        self.run(t, t - 2, t - 4, t - 5, t - 6)
        return carry

    def run(self, *turns):
        at, rb, count = self.at, self.rb, self.count
        nx, ny, x, y = at.nx, at.ny, at.x, at.y

        def on(turn, body):
            k = turns[turn]
            if k is not None:
                pl.when((k >= 0) & (k < count))(lambda: body(k))

        def first(k):
            pltpu.make_async_copy(self.rd.at[k], self.mine.at[k], self.lsem.at[k]).wait()
            self.core(k).wait_recv()
            if self.ahead:
                self.issue(k + 2)
            for b in range(ny):
                for e in range(nx):
                    self.mine[k, b, e] = add_up(self.mine[k, b, e], self.rd[k, b, e]).astype(BF16)
            for n in range(1, nx):
                self.a2(k, n).start()
            for n in range(1, ny):
                self.b2(k, n).start()

        def second(k):
            for n in range(1, nx):
                self.a2(k, n).wait_recv()
            for b in range(ny):
                self.r2a[k, 0, b] = add_up(
                    self.mine[k, b, x, :, :, 0:CUT], *[self.r2a[k, n, b] for n in range(nx - 1)]
                ).astype(BF16)
            for n in range(1, ny):
                self.a3(k, n).start()
            for n in range(1, ny):
                self.b2(k, n).wait_recv()
            for b in range(nx):
                self.r2b[k, 0, b] = add_up(
                    self.mine[k, y, b, :, :, CUT:], *[self.r2b[k, n, b] for n in range(ny - 1)]
                ).astype(BF16)
            for n in range(1, nx):
                self.b3(k, n).start()

        def third(k):
            for n in range(1, ny):
                self.a3(k, n).wait_recv()
            for n in range(1, nx):
                self.b3(k, n).wait_recv()
            left = add_up(self.r2a[k, 0, y], *[self.r3a[k, n] for n in range(ny - 1)]).astype(BF16)
            right = add_up(self.r2b[k, 0, x], *[self.r3b[k, n] for n in range(nx - 1)]).astype(BF16)
            self.s3[k, :, :, :, 0:CUT] = left.reshape(2, 2, rb, CUT)
            self.s3[k, :, :, :, CUT:] = right.reshape(2, 2, rb, CUT)
            self.c4(k).start()

        def fourth(k):
            self.c4(k).wait_recv()
            self.s4[k] = add_up(self.s3[k, :, at.lo], self.r4[k]).astype(BF16)
            self.c5(k).start()

        def fifth(k):
            self.c5(k).wait_recv()
            self.fin[k] = add_up(self.s4[k, at.hi], self.r5[k])

        for turn, body in enumerate((first, second, third, fourth, fifth)):
            on(turn, body)

    def start(self):
        self.issue(0)
        self.issue(1)

    def drain(self):
        def one(k, carry):
            self.core(k).wait_send()
            for n in range(1, self.at.nx):
                self.a2(k, n).wait_send()
                self.b3(k, n).wait_send()
            for n in range(1, self.at.ny):
                self.b2(k, n).wait_send()
                self.a3(k, n).wait_send()
            self.c4(k).wait_send()
            self.c5(k).wait_send()
            return carry

        lax.fori_loop(0, self.count, one, 0)


def backward_kernel(
    nx, ny, rb,
    go_ref, d_ref, q_hbm, k_hbm, v_hbm, o_hbm,
    qc_ref, kc_ref, vc_ref, lse_ref, lsec_ref, cg_ref, sg_ref, ct_ref, st_ref, meta_ref,
    oo_ref, g_out,
    q_ref, k_ref, v_ref, o_ref, do_ref, g_ref, acc, accc, kt_ref, right, dqc,
    osem, isem, *refs,
):
    at = Place(nx, ny)
    p, c, q, r, z = at.p, at.c, at.hi, at.lo, at.z
    at.greet()
    reducer = Reducer(
        at, rb, LATE,
        (
            (LATE, lambda t, core: go_ref.at[:, :, core, :, t]),
        ),
        refs,
    )

    reducer.start()
    loads = [(q_hbm, q_ref), (k_hbm, k_ref), (v_hbm, v_ref), (o_hbm, o_ref), (d_ref, do_ref)]
    loads = [pltpu.make_async_copy(src, dst, isem.at[n]) for n, (src, dst) in enumerate(loads)]
    for copy in loads:
        copy.start()

    reducer.tick(0)
    cs_col, cs_row, _ = read_meta(meta_ref)
    acc[...] = jnp.zeros_like(acc)
    accc[...] = jnp.zeros_like(accc)
    kct = jnp.transpose(unpad_heads(kc_ref[...].astype(F32))).astype(BF16)
    for copy in loads:
        copy.wait()
    doc = do_ref[:, VIS:, :].reshape(PART, GW)
    oc = o_ref[:, VIS:, :].reshape(PART, GW)
    docp = pad_right(doc)
    lane = lax.broadcasted_iota(jnp.int32, (PART, WIDE), 1) % 128
    qcl = jnp.where(lane < HEAD_DIM, qc_ref[...].astype(F32), 0.0).astype(BF16)
    prod = doc.astype(F32) * oc.astype(F32)
    lo_col = first_slot(cs_col)
    near = (cs_row >= lo_col) & (cs_row <= cs_col)
    deltas = [
        jnp.sum(prod[:, h * HEAD_DIM : (h + 1) * HEAD_DIM], axis=1, keepdims=True) for h in range(GROUP)
    ]
    lses = [lsec_ref[:, h : h + 1] for h in range(GROUP)]
    dqs = []
    for h in range(GROUP):
        cols = slice(h * 128, (h + 1) * 128)
        s = jnp.where(near, nt(qc_ref[:, cols], kc_ref[:, cols]), NEG)
        pt = jnp.exp(s - lses[h])
        dst = pt * (nt(docp[:, cols], vc_ref[:, cols]) - deltas[h])
        accc[:, cols] += nn(jnp.transpose(pt).astype(BF16), docp[:, cols]) + nn(
            jnp.transpose(dst).astype(BF16), qcl[:, cols]
        )
        dqs.append(nn(dst.astype(BF16), kc_ref[:, cols]))

    def cond_step(j, dqs):
        near = (lo_col <= j) & (cs_col >= j)
        new = []
        for h in range(GROUP):
            cols = slice(h * 128, (h + 1) * 128)
            s = jnp.where(near, nt(qc_ref[:, cols], k_ref[j, :, cols]), NEG)
            pt = jnp.exp(s - lses[h])
            dst = pt * (nt(docp[:, cols], v_ref[j, :, cols]) - deltas[h])
            acc[j, :, cols] += nn(jnp.transpose(pt).astype(BF16), docp[:, cols]) + nn(
                jnp.transpose(dst).astype(BF16), qcl[:, cols]
            )
            new.append(dqs[h] + nn(dst.astype(BF16), k_ref[j, :, cols]))
        return new

    dqs = lax.fori_loop(0, FRAMES, cond_step, dqs)
    dqc[...] = jnp.concatenate([t[:, :HEAD_DIM] for t in dqs], axis=1) * 0.125
    reducer.tick(1)

    def slot(i):
        start = pl.multiple_of(i * PART, PART)
        do = do_ref[:, pl.ds(start, PART), :].reshape(PATCHES, GW)
        o = o_ref[:, pl.ds(start, PART), :].reshape(PATCHES, GW)
        prod = jnp.transpose(do.astype(F32) * o.astype(F32))
        deltas = [
            jnp.sum(prod[h * HEAD_DIM : (h + 1) * HEAD_DIM], axis=0, keepdims=True) for h in range(GROUP)
        ]
        right[0:PATCHES] = pad_right(do)
        lane = lax.broadcasted_iota(jnp.int32, (PATCHES, WIDE), 1) % 128
        right[PATCHES:] = jnp.where(lane < HEAD_DIM, q_ref[i].astype(F32), 0.0).astype(BF16)
        kt_ref[i] = jnp.transpose(unpad_heads(k_ref[i].astype(F32))).astype(BF16)
        low = first_slot(i)
        near = (cs_col >= low) & (cs_col <= i)
        dqs = []
        for h in range(GROUP):
            cols = slice(h * 128, (h + 1) * 128)
            s = jnp.where(near, nt(kc_ref[:, cols], q_ref[i, :, cols]), NEG)
            pt = jnp.exp(s - lse_ref[i, h : h + 1, :])
            dst = (pt * (nt(vc_ref[:, cols], right[0:PATCHES, cols]) - deltas[h])).astype(BF16)
            accc[:, cols] += nn(jnp.concatenate([pt.astype(BF16), dst], axis=1), right[:, cols])
            dqs.append(nn(kct[h * HEAD_DIM : (h + 1) * HEAD_DIM], dst))

        def step(j, dqs):
            cols = [slice(h * 128, (h + 1) * 128) for h in range(GROUP)]
            scores = [nt(k_ref[j, :, w], q_ref[i, :, w]) for w in cols]
            grads = [nt(v_ref[j, :, w], right[0:PATCHES, w]) for w in cols]
            pts = [jnp.exp(scores[h] - lse_ref[i, h : h + 1, :]) for h in range(GROUP)]
            dsts = [(pts[h] * (grads[h] - deltas[h])).astype(BF16) for h in range(GROUP)]
            both = [jnp.concatenate([pts[h].astype(BF16), dsts[h]], axis=1) for h in range(GROUP)]
            for h in range(GROUP):
                acc[j, :, cols[h]] += nn(both[h], right[:, cols[h]])
            return [dqs[h] + nn(kt_ref[j, h * HEAD_DIM : (h + 1) * HEAD_DIM, :], dsts[h]) for h in range(GROUP)]

        dqs = lax.fori_loop(low, i + 1, step, dqs)
        dq = jnp.transpose(jnp.concatenate(dqs, axis=0)) * 0.125
        cosine = cg_ref[...] + ct_ref[pl.ds(i, 1), :]
        sine = sg_ref[...] + st_ref[pl.ds(i, 1), :]
        dq = turn(dq, cosine, -sine).astype(BF16).reshape(STREAMS, PART, GW)
        g_ref[:, pl.ds(start, PART), 0:GW] = dq

    def sweep(i, carry):
        slot(i)
        reducer.tick(i + 2)
        return carry

    lax.fori_loop(0, FRAMES, sweep, 0)

    cosine, sine = cond_tables(cs_col, ct_ref[...], st_ref[...])
    valid = cs_col < FRAMES
    dq = dqc[...]
    both = accc[...]
    parts = (turn(dq, cosine, -sine), turn(unpad_heads(both), cosine, -sine), unpad_right(both))
    for part, t in enumerate(parts):
        t = jnp.where(valid, t, 0.0).astype(BF16)
        g_ref[:, VIS:, part * GW : (part + 1) * GW] = t.reshape(STREAMS, CROWS, GW)

    def finish(i, carry):
        start = pl.multiple_of(i * PART, PART)
        cosine = cg_ref[...] + ct_ref[pl.ds(i, 1), :]
        sine = sg_ref[...] + st_ref[pl.ds(i, 1), :]
        both = acc[i]
        dk = turn(unpad_heads(both), cosine, -sine)
        g_ref[:, pl.ds(start, PART), GW : 2 * GW] = dk.astype(BF16).reshape(STREAMS, PART, GW)
        g_ref[:, pl.ds(start, PART), 2 * GW :] = unpad_right(both).astype(BF16).reshape(STREAMS, PART, GW)
        return carry

    lax.fori_loop(0, FRAMES, finish, 0)
    save = pltpu.make_async_copy(g_ref, g_out, isem.at[5])
    save.start()
    fin = reducer.fin
    outs = [pltpu.make_async_copy(fin.at[k], oo_ref.at[k], osem.at[k]) for k in range(4)]
    for copy in outs:
        copy.start()

    reducer.drain()
    save.wait()
    for copy in outs:
        copy.wait()


def unpad_right(t):
    return jnp.concatenate([t[:, h * 128 + HEAD_DIM : (h + 1) * 128] for h in range(GROUP)], axis=1)


def attend_backward(g_out, grad_o, saved, o, tables, meta):
    nx, ny, rb = grid_shape()
    q, k, v, *rest = saved

    def v16(*shape):
        return VM(shape, BF16)

    scratch = [
        v16(*q.shape), v16(*k.shape), v16(*v.shape), v16(*o.shape), v16(*o.shape), v16(STREAMS, ROWS, 3 * GW),
        VM((FRAMES, PATCHES, WIDE), F32), VM((PART, WIDE), F32), v16(FRAMES, GW, PATCHES), v16(2 * PATCHES, WIDE),
        VM((PART, GW), F32),
        dma(LATE), dma(6),
    ] + Reducer.scratch(LATE, nx, ny, rb)
    outs = (((4, rb, D), F32), ((STREAMS, ROWS, 3 * GW), BF16))
    ops = (g_out.reshape(ny, nx, 2, STREAMS, 4, rb, D), grad_o, q, k, v, o)
    return comm_call(
        functools.partial(backward_kernel, nx, ny, rb), "attend_backward", 3, outs, scratch, ops,
        tuple(rest) + tables + (meta,),
    )


def finish_kernel(
    nx, ny, rb,
    f_hbm, xa_hbm, gq_ref, w_hbm, x_hbm, h_hbm, gi_ref, gp_ref, v_ref, gain_ref,
    gx_ref, oq_ref, ov_ref, oi_ref, op_ref,
    f, xa, w, x_own, h_own, big, near_in, near_out, own, land, tail, tail_out, total,
    q1, rq1a, rq1b, sq1a, sq1b, rq2a, rq2b, sq2, rq3, sq3, vm, vd, vx, vy, vz1, vz2, hold,
    isem, dsend, drecv, send, recv, csend, crecv, lsem,
    qs1a, qr1a, qs1b, qr1b, qs2a, qr2a, qs2b, qr2b, qs3, qr3, qs4, qr4, vs, vr, vsx, vrx, vsy, vry, relay, rsend, rrecv, cols_sum, osem,
    *refs,
):
    at = Place(nx, ny)
    p, c, q, r, z, x, y, hi, lo = at.p, at.c, at.hi, at.lo, at.z, at.x, at.y, at.hi, at.lo
    group = 2 * r + c
    in_pair, inner = q == c, z == 1 + q
    reducer = Reducer(
        at, rb, LAST,
        ((LAST - 1, lambda t, core: gi_ref.at[:, :, core]), (1, lambda t, core: gp_ref.at[:, :, core])),
        refs, ahead=False,
    )
    loads = []
    for part in range(3):
        cols = pl.ds(pl.multiple_of(part * D + group * GW, GW), GW)
        loads.append(pltpu.make_async_copy(w_hbm.at[:, cols], w.at[:, pl.ds(part * GW, GW)], isem.at[part]))
    loads.append(pltpu.make_async_copy(f_hbm, f, isem.at[3]))
    loads.append(pltpu.make_async_copy(xa_hbm, xa, isem.at[4]))
    late = [
        pltpu.make_async_copy(gq_ref, q1, isem.at[5]),
        pltpu.make_async_copy(x_hbm, x_own, isem.at[6]),
        pltpu.make_async_copy(h_hbm, h_own, isem.at[7]),
    ]
    for copy in loads + late:
        copy.start()
    at.greet()
    rows = pl.ds(pl.multiple_of(c * HALF, HALF), HALF)
    rest = pl.ds(pl.multiple_of((1 - c) * HALF, HALF), HALF)
    last = pl.ds(VIS, CROWS)
    qa, qb = pl.ds(0, QCUT), pl.ds(QCUT, QCUT)

    def q1a(n):
        return remote(q1.at[:, at.along_x(n), :, :, qa], rq1a.at[n - 1], qs1a.at[n - 1], qr1a.at[n - 1], at.x_device(n))

    def q1b(n):
        return remote(q1.at[at.along_y(n), :, :, :, qb], rq1b.at[n - 1], qs1b.at[n - 1], qr1b.at[n - 1], at.y_device(n))

    def q2a(n):
        return remote(sq1a.at[at.along_y(n)], rq2a.at[n - 1], qs2a.at[n - 1], qr2a.at[n - 1], at.y_device(n))

    def q2b(n):
        return remote(sq1b.at[at.along_x(n)], rq2b.at[n - 1], qs2b.at[n - 1], qr2b.at[n - 1], at.x_device(n))

    def q3():
        return remote(sq2.at[:, 1 - hi], rq3, qs3, qr3, at.z_two)

    mates = [(at.near, 1, 0), (at.z_one, 0, 1), (at.slant, 1, 1)]

    def q4(n, part):
        device, core, side = mates[n]
        to_core = c + core - 2 * c * core
        to_side = lo + side - 2 * lo * side
        place = pl.ds(pl.multiple_of(part * D + group * GW, GW), GW)
        return remote(
            sq3.at[to_core, to_side, :, pl.ds(part * GW, GW)], oq_ref.at[:, place],
            qs4.at[n, part], qr4.at[n, part], device,
        )

    def q4_own(part):
        place = pl.ds(pl.multiple_of(part * D + group * GW, GW), GW)
        return pltpu.make_async_copy(sq3.at[c, lo, :, pl.ds(part * GW, GW)], oq_ref.at[:, place], lsem.at[2 + part])

    def v_core():
        return remote(vm.at[0], vd, vs.at[0], vr.at[0], at.near)

    def v_x(n):
        return remote(vm.at[1], vx.at[n - 1], vsx.at[n - 1], vrx.at[n - 1], at.x_device(n))

    def v_y(n):
        return remote(vm.at[2], vy.at[n - 1], vsy.at[n - 1], vry.at[n - 1], at.y_device(n))

    def v_z1():
        return remote(vm.at[3], vz1, vs.at[1], vr.at[1], at.z_one)

    def v_z2():
        return remote(vm.at[4], vz2, vs.at[2], vr.at[2], at.z_two)

    def near_copy(s):
        return remote(near_out.at[s], near_in.at[s], dsend.at[s], drecv.at[s], at.near)

    def row_copy(s):
        mark = jnp.where(s // 2 == q, r, 0)
        return remote(own.at[s], land.at[mark, rows], send.at[s], recv.at[mark, c], (2 * p + q, s))

    def row_own(s):
        return pltpu.make_async_copy(own.at[s], land.at[r, rows], lsem.at[0])

    def relay_copy(n, s):
        return remote(own.at[s], relay.at[n], rsend.at[n], rrecv.at[n], at.z_one)

    def tail_copy(s):
        return remote(tail_out.at[s], tail.at[group], csend.at[s], crecv.at[group], (2 * p + q, s))

    def tail_own(s):
        return pltpu.make_async_copy(tail_out.at[s], tail.at[group], lsem.at[1])

    def mine(s):
        return (q == c) & (s == z)

    def go(s, far, near):
        @pl.when(mine(s))
        def _():
            near(s)

        @pl.when(jnp.logical_not(mine(s)))
        def _():
            far(s)

    for k in range(LAST):
        reducer.issue(jnp.int32(k))
    late[0].wait()
    for n in range(1, nx):
        q1a(n).start()
    for n in range(1, ny):
        q1b(n).start()
    for copy in loads:
        copy.wait()
    hold[...] = jnp.zeros_like(hold)
    cols_sum[...] = jnp.zeros_like(cols_sum)

    far = (STREAMS - 1 - z, z + 2 - 4 * hi, z + 1 - 2 * lo, z)

    @pl.when(jnp.logical_not(in_pair))
    def _():
        land[1] = jnp.zeros_like(land[1])

    def combine(s):
        near_copy(s).wait_recv()
        for t in range(HALF // 64):
            part = pl.ds(t * 64, 64)
            own[s, part] = add_up(near_in[s, part], own[s, part]).astype(BF16)

    def pass_on(n):
        s = far[n]
        combine(s)
        if n >= 2:
            go(s, lambda s: row_copy(s).start(), lambda s: row_own(s).start())
        else:
            @pl.when(jnp.logical_not(inner))
            def _():
                relay_copy(n, s).start()

    def pass_far(n):
        s = far[1 - n]

        @pl.when(inner)
        def _():
            relay_copy(n, s).wait_recv()
            for t in range(HALF // 64):
                part = pl.ds(t * 64, 64)
                own[s, part] = add_up(relay[n, part], own[s, part]).astype(BF16)
            row_copy(s).start()

    def partial_rows(t, carry):
        s = jnp.where(t == 0, far[0], jnp.where(t == 1, far[1], jnp.where(t == 2, far[2], far[3])))
        big[...] = nt(f[s], w[...])
        near_out[s] = big[rest].astype(BF16)
        near_copy(s).start()
        own[s] = big[rows].astype(BF16)
        tail_out[s] = big[last].astype(BF16)
        go(s, lambda s: tail_copy(s).start(), lambda s: tail_own(s).start())
        for e in range(ROWS // 48):
            part = pl.ds(e * 48, 48)
            values = xa[s, part].astype(F32)
            centre = values - jnp.mean(values, axis=1, keepdims=True)
            scale = lax.rsqrt(jnp.mean(centre * centre, axis=1, keepdims=True) + EPS)
            g = big[part]
            gh = g * (centre * scale)
            flat = f[s, part].astype(F32)
            for m in range(6):
                cols_sum[...] += flat[m * 8 : m * 8 + 8]
                hold[0] += gh[m * 8 : m * 8 + 8]
                hold[1] += g[m * 8 : m * 8 + 8]

        for n in range(STREAMS - 1):
            @pl.when(t == n + 1)
            def _():
                pass_on(n)

        return carry

    lax.fori_loop(0, STREAMS, partial_rows, 0)
    pass_on(STREAMS - 1)

    def move(turn):
        def one(k, carry):
            reducer.run(*[k if n == turn else None for n in range(5)])
            return carry

        lax.fori_loop(0, LAST, one, 0)

    move(0)
    vm[0] = v_ref[...]
    vm[0, 0:1] = jnp.sum(hold[0], axis=0, keepdims=True)
    vm[0, 1:2] = jnp.sum(hold[1], axis=0, keepdims=True)
    for part in range(3):
        place = pl.ds(pl.multiple_of(group * GW, GW), GW)
        vm[0, 2 + part : 3 + part, place] = jnp.sum(cols_sum[:, part * GW : (part + 1) * GW], axis=0, keepdims=True)
    v_core().start()

    for n in range(1, nx):
        q1a(n).wait_recv()
    for n in range(1, ny):
        q1b(n).wait_recv()
    for b in range(ny):
        sq1a[b] = add_up(q1[b, x, :, :, 0:QCUT], *[rq1a[n, b] for n in range(nx - 1)]).astype(BF16)
    for n in range(1, ny):
        q2a(n).start()
    for b in range(nx):
        sq1b[b] = add_up(q1[y, b, :, :, QCUT:], *[rq1b[n, b] for n in range(ny - 1)]).astype(BF16)
    for n in range(1, nx):
        q2b(n).start()
    v_core().wait_recv()
    vm[1] = vm[0] + vd[...]
    for n in range(1, nx):
        v_x(n).start()
    pass_far(0)
    move(1)
    for n in range(1, ny):
        q2a(n).wait_recv()
    for n in range(1, nx):
        q2b(n).wait_recv()
    left = add_up(sq1a[y], *[rq2a[n] for n in range(ny - 1)]).astype(BF16)
    right = add_up(sq1b[x], *[rq2b[n] for n in range(nx - 1)]).astype(BF16)
    sq2[:, :, :, :, 0:QCUT] = left.reshape(2, 2, 2, rb, QCUT)
    sq2[:, :, :, :, QCUT:] = right.reshape(2, 2, 2, rb, QCUT)
    q3().start()
    for n in range(1, nx):
        v_x(n).wait_recv()
    vm[2] = add_up(vm[1], *[vx[n] for n in range(nx - 1)])
    for n in range(1, ny):
        v_y(n).start()
    for n in range(1, ny):
        v_y(n).wait_recv()
    vm[3] = add_up(vm[2], *[vy[n] for n in range(ny - 1)])
    v_z1().start()
    pass_far(1)
    move(2)
    q3().wait_recv()
    sq3[...] = add_up(sq2[:, hi], rq3[...])
    for part in range(3):
        for n in range(3):
            q4(n, part).start()
        q4_own(part).start()
    v_z1().wait_recv()
    vm[4] = vm[3] + vz1[...]
    v_z2().start()
    move(3)

    late[1].wait()
    late[2].wait()
    for side in range(2):
        for core in range(2):
            part = pl.ds(core * HALF, HALF)
            g = 2 * side + core
            self_made = (core == c) & (2 * c + side == z)

            @pl.when(jnp.logical_not(self_made))
            def _():
                remote(tail_out.at[0], tail.at[g], csend.at[0], crecv.at[g], at.near).wait_recv()

            @pl.when(jnp.logical_not(self_made) & (in_pair | (side == 0)))
            def _():
                remote(own.at[0], land.at[side, part], send.at[0], recv.at[side, core], at.near).wait_recv()

            @pl.when(self_made)
            def _():
                row_own(0).wait()
                tail_own(0).wait()

    gain = gain_ref[0:1]

    def back(dst, grad):
        values = x_own[dst].astype(F32)
        centre = values - jnp.mean(values, axis=1, keepdims=True)
        scale = lax.rsqrt(jnp.mean(centre * centre, axis=1, keepdims=True) + EPS)
        normed = centre * scale
        g = grad * gain
        total[dst] = h_own[dst] + scale * (
            g - jnp.mean(g, axis=1, keepdims=True) - normed * jnp.mean(g * normed, axis=1, keepdims=True)
        )

    def back_rows(t, carry):
        part = pl.ds(pl.multiple_of(t * 64, 64), 64)
        back(part, add_up(land[0, part], land[1, part]))
        return carry

    lax.fori_loop(0, VIS // 64, back_rows, 0)
    back(last, add_up(tail[0], tail[1], tail[2], tail[3]))
    done = pltpu.make_async_copy(total, gx_ref, lsem.at[5])
    done.start()
    move(4)
    outs = [
        pltpu.make_async_copy(reducer.fin.at[k], oi_ref.at[:, pl.ds(k * D, D)], osem.at[k]) for k in range(LAST - 1)
    ]
    outs += [pltpu.make_async_copy(reducer.fin.at[LAST - 1], op_ref, osem.at[LAST - 1])]
    for copy in outs:
        copy.start()
    v_z2().wait_recv()
    vm[5] = vm[4] + vz2[...]
    v_done = pltpu.make_async_copy(vm.at[5], ov_ref, lsem.at[6])
    v_done.start()
    for n in range(1, nx):
        q1a(n).wait_send()
        q2b(n).wait_send()
        v_x(n).wait_send()
    for n in range(1, ny):
        q1b(n).wait_send()
        q2a(n).wait_send()
        v_y(n).wait_send()
    q3().wait_send()
    v_core().wait_send()
    v_z1().wait_send()
    v_z2().wait_send()
    for n in range(STREAMS):
        s = far[n]
        near_copy(s).wait_send()
        if n < 2:
            @pl.when(inner)
            def _():
                row_copy(s).wait_send()

            @pl.when(jnp.logical_not(inner))
            def _():
                relay_copy(n, s).wait_send()

            tail_copy(s).wait_send()
        else:
            @pl.when(jnp.logical_not(mine(s)))
            def _():
                row_copy(s).wait_send()
                tail_copy(s).wait_send()
    for part in range(3):
        q4_own(part).wait()
        for n in range(3):
            q4(n, part).wait_send()
            q4(n, part).wait_recv()
    reducer.drain()
    for copy in outs:
        copy.wait()
    done.wait()
    v_done.wait()


def finish_rows(flat, x_all, g_qkv, w_qkv, x, h, g_in, g_proj, vectors, gain):
    nx, ny, rb = grid_shape()

    def v(*shape):
        return VM(shape, BF16)

    def vf(*shape):
        return VM(shape, F32)

    scratch = [
        v(STREAMS, ROWS, 3 * GW), v(STREAMS, ROWS, D), v(D, 3 * GW), v(ROWS, D), vf(ROWS, D), vf(ROWS, D),
        v(STREAMS, HALF, D), v(STREAMS, HALF, D), v(STREAMS, HALF, D), v(2, VIS, D), v(4, CROWS, D), v(4, CROWS, D),
        vf(ROWS, D),
        v(ny, nx, 8, rb, 3 * GW), v(nx - 1, ny, 8, rb, QCUT), v(ny - 1, nx, 8, rb, QCUT),
        v(ny, 8, rb, QCUT), v(nx, 8, rb, QCUT), v(ny - 1, 8, rb, QCUT), v(nx - 1, 8, rb, QCUT),
        v(2, 2, 2, rb, 3 * GW), v(2, 2, rb, 3 * GW), vf(2, 2, rb, 3 * GW),
        vf(6, 16, D), vf(16, D), vf(nx - 1, 16, D), vf(ny - 1, 16, D), vf(16, D), vf(16, D), vf(2, 8, D),
        dma(8), dma(4), dma(4), dma(4), dma(2, 2), dma(4), dma(4), dma(7),
        dma(nx - 1), dma(nx - 1), dma(ny - 1), dma(ny - 1), dma(ny - 1), dma(ny - 1), dma(nx - 1), dma(nx - 1),
        pltpu.SemaphoreType.DMA, pltpu.SemaphoreType.DMA, dma(3, 3), dma(3, 3),
        dma(3), dma(3), dma(nx - 1), dma(nx - 1), dma(ny - 1), dma(ny - 1),
        v(2, HALF, D), dma(2), dma(2), vf(8, 3 * GW), dma(LAST),
    ] + Reducer.scratch(LAST, nx, ny, rb)
    outs = (
        ((ROWS, D), F32), ((rb, 3 * D), F32), ((16, D), F32), ((rb, (LAST - 1) * D), F32), ((rb, D), F32),
    )
    ops = (
        flat, x_all, g_qkv.reshape(ny, nx, 8, rb, 3 * GW), w_qkv, x, h,
        g_in.reshape(ny, nx, 2, STREAMS, rb, (LAST - 1) * D), g_proj.reshape(ny, nx, 2, STREAMS, rb, D),
    )
    return comm_call(
        functools.partial(finish_kernel, nx, ny, rb), "finish_rows", 4, outs, scratch, ops, (vectors, gain)
    )


TILE = 48
TILES = ROWS // TILE


def tn(a, b):
    return lax.dot_general(a, b, (((0,), (0,)), ((), ())), preferred_element_type=F32)


def mlp_kernel(
    nx, ny, rb,
    win_hbm, wout_hbm, att_ref, x_ref, dy_ref, wp_ref, par_ref,
    do_out, gi_out, go_out, gp_out, oi_ref, y_ref, gh_ref, vec_ref,
    wi, wo, n_ref, h_ref, buf, dbuf, hid, du, yacc, dn, dhb, do_ref, stage, sums,
    gi, isem, ssem, hs, hr, hl, osem, *refs,
):
    at = Place(nx, ny)
    p, c, q, r, z = at.p, at.c, at.hi, at.lo, at.z
    reducer = Reducer(at, rb, EARLY, ((EARLY, lambda t, core: gi.at[t, :, :, core]),), refs, ahead=False)

    def fetch(t, slot):
        cols = pl.ds(pl.multiple_of(t * D, D), D)
        return (
            pltpu.make_async_copy(win_hbm.at[:, cols], wi.at[slot], isem.at[0, slot]),
            pltpu.make_async_copy(wout_hbm.at[cols, :], wo.at[slot], isem.at[1, slot]),
        )

    for copy in fetch(0, 0):
        copy.start()
    at.greet()
    sums[...] = jnp.zeros_like(sums)
    for j in range(2):
        cols = slice(j * CUT, (j + 1) * CUT)
        buf[:, cols] = nn(att_ref[...], wp_ref[:, cols])

    def tile(t):
        return pl.ds(pl.multiple_of(t * TILE, 16), TILE)

    def fold(row, values):
        total = values[0:8]
        for m in range(1, TILE // 8):
            total = total + values[m * 8 : m * 8 + 8]
        sums[row] += total

    def enter(t, carry):
        rows = tile(t)
        h = x_ref[rows].astype(F32) + buf[rows] + par_ref[9:10]
        h_ref[rows] = h
        centre = h - jnp.mean(h, axis=1, keepdims=True)
        scale = lax.rsqrt(jnp.mean(centre * centre, axis=1, keepdims=True) + EPS)
        n_ref[rows] = (centre * scale * par_ref[10:11] + par_ref[11:12]).astype(BF16)
        return carry

    lax.fori_loop(0, TILES, enter, 0)

    def block(t, carry):
        slot = t % 2
        for copy in fetch(t, slot):
            copy.wait()

        @pl.when(t < 3)
        def _():
            for copy in fetch(t + 1, 1 - slot):
                copy.start()

        reducer.run(t - 1, None, t - 2, None, t - 3)
        for j in range(2):
            cols = slice(j * CUT, (j + 1) * CUT)
            buf[:, cols] = nn(n_ref[...], wi[slot, :, cols])
            dbuf[:, cols] = nt(dy_ref[...], wo[slot, cols, :])
        place = pl.ds(pl.multiple_of(t * D, D), D)

        def act(e, carry):
            rows = tile(e)
            for j in range(4):
                cols = slice(j * 256, (j + 1) * 256)
                u = buf[rows, cols] + par_ref[pl.ds(5 + t, 1), cols]
                phi = 0.5 * (1.0 + lax.erf(u * (2.0**-0.5)))
                hid[rows, pl.ds(pl.multiple_of(t * D + j * 256, 256), 256)] = (u * phi).astype(BF16)
                slope = phi + u * (jnp.exp(-0.5 * u * u) * ((2.0 * math.pi) ** -0.5))
                g = (dbuf[rows, cols] * slope).astype(BF16)
                du[rows, cols] = g
                g = g.astype(F32)
                total = g[0:8]
                for m in range(1, TILE // 8):
                    total = total + g[m * 8 : m * 8 + 8]
                sums[t, :, cols] += total
            return carry

        lax.fori_loop(0, TILES, act, 0)

        @pl.when(t < EARLY)
        def _():
            for b in range(ny):
                block_rows = tn(n_ref[:, b * (D // ny) : (b + 1) * (D // ny)], du[...])
                gi[t, b] = block_rows.astype(BF16).reshape(nx, 2, STREAMS, rb, D)
            reducer.issue(t)

        reducer.run(None, t - 1, None, t - 2, None)
        for j in range(2):
            cols = slice(j * CUT, (j + 1) * CUT)
            more = nn(hid[:, place], wo[slot, :, cols])
            back = nt(du[...], wi[slot, cols, :])

            @pl.when(t == 0)
            def _():
                yacc[:, cols] = more
                dn[:, cols] = back

            @pl.when(t > 0)
            def _():
                yacc[:, cols] += more
                dn[:, cols] += back

        return carry

    lax.fori_loop(0, 4, block, 0)
    reducer.run(None, None, EARLY - 1, None, EARLY - 2)

    def leave(t, carry):
        rows = tile(t)
        h = h_ref[rows]
        y_ref[rows] = (h + yacc[rows] + par_ref[12:13]).astype(BF16)
        centre = h - jnp.mean(h, axis=1, keepdims=True)
        scale = lax.rsqrt(jnp.mean(centre * centre, axis=1, keepdims=True) + EPS)
        normed = centre * scale
        grad = dn[rows]
        dy = dy_ref[rows].astype(F32)
        fold(5, grad * normed)
        fold(6, grad)
        fold(7, dy)
        g = grad * par_ref[10:11]
        gh = dy + scale * (
            g - jnp.mean(g, axis=1, keepdims=True) - normed * jnp.mean(g * normed, axis=1, keepdims=True)
        )
        gh_ref[rows] = gh
        low = gh.astype(BF16)
        dhb[rows] = low
        fold(4, low.astype(F32))
        return carry

    lax.fori_loop(0, TILES, leave, 0)
    reducer.run(None, None, None, EARLY - 1, None)
    for j in range(2):
        rows = slice(j * CUT, (j + 1) * CUT)
        do_ref[:, rows] = nt(dhb[...], wp_ref[rows, :]).astype(BF16)

    def heads_copy(g):
        device = (2 * p + g % 2, 2 * c + g // 2)
        return remote(do_ref.at[:, pl.ds(g * GW, GW)], do_out.at[z], hs.at[g], hr.at[z], device)

    def heads_own(g):
        return pltpu.make_async_copy(do_ref.at[:, pl.ds(g * GW, GW)], do_out.at[z], hl)

    for g in range(4):
        self_made = (g % 2 == c) & (2 * c + g // 2 == z)

        @pl.when(self_made)
        def _():
            heads_own(g).start()

        @pl.when(jnp.logical_not(self_made))
        def _():
            heads_copy(g).start()

    vec_ref[...] = jnp.zeros_like(vec_ref)
    for n in range(8):
        vec_ref[5 + n : 6 + n] = jnp.sum(sums[n], axis=0, keepdims=True)

    def out_save(t, slot):
        return pltpu.make_async_copy(stage.at[slot], go_out.at[pl.ds(pl.multiple_of(t * D, D), D), :], ssem.at[slot])

    def weights(t, carry):
        slot = t % 2

        @pl.when(t > 1)
        def _():
            out_save(t - 2, slot).wait()

        for m in range(2):
            half = pl.ds(m * CUT, CUT)
            place = pl.ds(pl.multiple_of(t * D + m * CUT, CUT), CUT)
            stage[slot, half, :] = tn(hid[:, place], dy_ref[...]).astype(BF16)
        out_save(t, slot).start()
        return carry

    lax.fori_loop(0, 4, weights, 0)
    saves = []
    for slot, (lhs, rhs, out) in enumerate(((att_ref, dhb, gp_out), (n_ref, du, gi_out))):
        out_save(2 + slot, slot).wait()
        for m in range(2):
            half = pl.ds(m * CUT, CUT)
            stage[slot, half, :] = tn(lhs[:, half], rhs[...]).astype(BF16)
        saves.append(pltpu.make_async_copy(stage.at[slot], out, ssem.at[slot]))
        saves[-1].start()
    reducer.run(None, None, None, None, EARLY - 1)
    fin_saves = [
        pltpu.make_async_copy(reducer.fin.at[k], oi_ref.at[:, pl.ds(k * D, D)], osem.at[k]) for k in range(EARLY)
    ]
    for copy in fin_saves:
        copy.start()
    reducer.drain()
    for g in range(4):
        self_made = (g % 2 == c) & (2 * c + g // 2 == z)

        @pl.when(self_made)
        def _():
            heads_own(g).wait()

        @pl.when(jnp.logical_not(self_made))
        def _():
            heads_copy(g).wait_send()
    for s in range(STREAMS):
        @pl.when((q != c) | (s != z))
        def _():
            remote(do_ref.at[:, pl.ds(0, GW)], do_out.at[s], hs.at[0], hr.at[s], (2 * p + 1 - c, z)).wait_recv()
    for copy in saves + fin_saves:
        copy.wait()


def mlp(w_in, w_out, attended, x, dy, w_proj, params):
    nx, ny, rb = grid_shape()

    def v16(*shape):
        return VM(shape, BF16)

    def vf(*shape):
        return VM(shape, F32)

    scratch = [
        v16(2, D, D), v16(2, D, D), v16(ROWS, D), vf(ROWS, D), vf(ROWS, D), vf(ROWS, D),
        v16(ROWS, 4 * D), v16(ROWS, D), vf(ROWS, D), vf(ROWS, D), v16(ROWS, D), v16(ROWS, D),
        v16(2, D, D), vf(8, 8, D), v16(EARLY, ny, nx, 2, STREAMS, rb, D),
        dma(2, 2), dma(2), dma(4), dma(4), pltpu.SemaphoreType.DMA, dma(EARLY),
    ] + Reducer.scratch(EARLY, nx, ny, rb)
    outs = (
        ((STREAMS, ROWS, GW), BF16), ((D, (4 - EARLY) * D), BF16), ((4 * D, D), BF16), ((D, D), BF16),
        ((rb, EARLY * D), F32),
    )
    near_outs = (((ROWS, D), BF16), ((ROWS, D), F32), ((16, D), F32))
    return comm_call(
        functools.partial(mlp_kernel, nx, ny, rb), "mlp", 1, outs, scratch, (w_in, w_out), (attended, x, dy, w_proj, params), near_outs
    )


def own_meta(lengths, mask):
    frames = jnp.arange(FRAMES, dtype=jnp.int32)
    ends = jnp.cumsum(lengths)
    reached = ends[None, :] <= frames[:, None]
    begin = jnp.sum(jnp.where(reached, lengths[None, :], 0), axis=1)
    episode = jnp.sum(reached, axis=1)[:, None] == jnp.arange(lengths.shape[0])[None, :]
    length = jnp.sum(jnp.where(episode, lengths[None, :], 0), axis=1)
    base = jnp.where(length == MOST, 0, jnp.where(length == MIDDLE - MOST, MOST, MIDDLE))
    slot = base + frames - begin
    perm = jnp.sum(jnp.where(slot[:, None] == frames[None, :], frames[:, None], 0), axis=0)
    stream = jnp.arange(STREAMS)[:, None]
    row = jnp.arange(CROWS)[None, :]
    part = FRAMES // STREAMS
    frame = jnp.where(row < part * COND, part * stream + row // COND, FRAMES)
    cslot = jnp.sum(jnp.where(frame[..., None] == frames, slot[None, None, :], 0), axis=-1)
    cslot = jnp.where(frame < FRAMES, cslot, 99).reshape(1, PART)
    hidden = jnp.where(mask == 1, 0.0, NEG).astype(F32)
    bias = jnp.sum(jnp.where((perm[:, None] == frames[None, :])[:, :, None], hidden[None], 0.0), axis=1)
    line = jnp.pad(cslot.astype(F32), ((0, 7), (0, PATCHES - PART)))
    return perm.astype(jnp.int32), slot.astype(jnp.int32), jnp.concatenate([bias, line], axis=0)


def per_device(
    visual, conditioning, d_visual, d_conditioning, episode_frames, patch_mask,
    ln1_gain, ln1_bias, w_qkv, b_qkv, w_proj, b_proj, ln2_gain, ln2_bias, w_in, b_in, w_out, b_out,
):
    d, z = lax.axis_index("dp"), lax.axis_index("stream")
    extra = conditioning.shape[1] * COND
    perm, slot, own = own_meta(episode_frames[0], patch_mask[0])
    x, dy = place_rows(perm, visual, conditioning, d_visual, d_conditioning)
    params = jnp.concatenate(
        [ln1_gain, ln1_bias, b_qkv, b_in, b_proj, ln2_gain, ln2_bias, b_out, jnp.zeros((3 * D,), BF16)]
    ).astype(F32).reshape(16, D)
    tables = tuple(jnp.asarray(t) for t in rope_constants())
    attended, x_all, a, q, k, v, o, meta, *rest = attend_forward(x, w_qkv, own, params, tables)
    grad_heads, grad_w_in, grad_w_out, grad_w_proj, red_in, output, grad_h, vectors = mlp(
        w_in, w_out, attended, x, dy, w_proj, params
    )
    red_out, grad_qkv = attend_backward(grad_w_out, grad_heads, (q, k, v, *rest), o, tables, meta)
    role_grad = jnp.einsum(
        "rd,re->de", a.reshape(STREAMS * ROWS, D), grad_qkv.reshape(STREAMS * ROWS, 3 * GW), preferred_element_type=F32
    )
    grad_x, red_qkv, sums, red_in_last, red_proj = finish_rows(
        grad_qkv, x_all, role_grad.astype(BF16), w_qkv, x, grad_h, grad_w_in, grad_w_proj, vectors, params
    )
    red_in = jnp.concatenate([red_in, red_in_last], axis=1)
    out_visual, grad_visual = restore_rows(slot, output, grad_x)
    owner = d * STREAMS + z
    owners = lax.axis_size("dp") * STREAMS

    def share(start, rows):
        size = rows * D // owners
        return lax.dynamic_slice_in_dim(sums[start : start + rows].reshape(-1), owner * size, size, 0)

    return (
        out_visual.reshape(visual.shape), output[VIS : VIS + extra].reshape(conditioning.shape),
        grad_visual.reshape(visual.shape), grad_x[VIS : VIS + extra].reshape(conditioning.shape),
        share(0, 1), share(1, 1), red_qkv, share(2, 2), share(4, 1), red_proj, share(9, 1), share(10, 1), share(11, 1),
        red_in, share(5, 4), red_out.reshape(-1, D), share(12, 1),
    )


def solution(mesh):
    rows = P("dp", None, "stream", None)
    extra = P("dp", "stream", None, None)
    vector = P(("dp", "stream"))
    matrix = P(("dp", "stream"), None)
    in_specs = (rows, extra, rows, extra, P("dp", None), P("dp", None, None)) + (P(),) * 12
    out_specs = (
        rows, extra, rows, extra, vector, vector, matrix, vector, vector, matrix, vector, vector, vector, matrix,
        vector, matrix, vector,
    )
    return jax.shard_map(per_device, mesh=mesh, in_specs=in_specs, out_specs=out_specs, check_vma=False)
```

```python
import functools
import math

import jax
import jax.numpy as jnp
import numpy as np
from jax import lax
from jax.experimental import pallas as pl
from jax.experimental.pallas import tpu as pltpu
from jax.sharding import PartitionSpec as P

D = 1024
HEADS = 16
HEAD_DIM = 64
GRID = 16
COND = 2
FRAMES = 8
MOST = 5
MIDDLE = 7
STREAMS = 4
GROUP = 4
GW = GROUP * HEAD_DIM
PART = 64
PATCHES = 256
VIS = FRAMES * PART
CROWS = 16
ROWS = VIS + CROWS
WIDE = GROUP * 128
NEG = -1e30
EPS = 1e-06
F32 = jnp.float32
BF16 = jnp.bfloat16
VM = pltpu.VMEM
FULL = pl.BlockSpec(memory_space=pltpu.VMEM)
ANYM = pl.BlockSpec(memory_space=pltpu.HBM)
LIMIT = 60 * 1024 * 1024


def nn(a, b):
    return lax.dot_general(a, b, (((1,), (0,)), ((), ())), preferred_element_type=F32)


def nt(a, b):
    return lax.dot_general(a, b, (((1,), (1,)), ((), ())), preferred_element_type=F32)


def rope_constants():
    pair = np.arange(HEAD_DIM // 2)
    exponent = np.where(pair < 30, (pair % 10) / 10.0, 0.0).astype(np.float32)
    freq = np.exp(-math.log(10000.0) * exponent).astype(np.float32)
    patch = np.arange(PATCHES)
    slot_time = np.array([0, 1, 2, 3, 4, 0, 1, 0])
    is_time = (pair < 10)[None, :]
    place = np.where(
        (pair >= 20)[None, :], (patch % GRID)[:, None], (patch // GRID)[:, None]
    ) * ((pair >= 10) & (pair < 30))[None, :]
    angle_patch = (place * freq[None, :]).astype(np.float32)
    angle_time = (slot_time[:, None] * freq[None, :]).astype(np.float32)
    cos_patch = np.where(is_time, 0.0, np.cos(angle_patch))
    sin_patch = np.where(is_time, 0.0, np.sin(angle_patch))
    cos_time = np.where(is_time, np.cos(angle_time), 0.0)
    sin_time = np.where(is_time, np.sin(angle_time), 0.0)

    def spread(table, signed):
        two = np.repeat(table, 2, axis=1)
        if signed:
            two = two * np.where(np.arange(HEAD_DIM) % 2 == 0, -1.0, 1.0)[None, :]
        return np.tile(two, (1, GROUP)).astype(np.float32)

    return (
        spread(cos_patch, False),
        spread(sin_patch, True),
        spread(cos_time, False),
        spread(sin_time, True),
    )


def swap_pairs(v):
    lane = lax.broadcasted_iota(jnp.int32, v.shape, 1)
    width = v.shape[1]
    return jnp.where(lane % 2 == 0, pltpu.roll(v, width - 1, 1), pltpu.roll(v, 1, 1))


def turn(v, cosine, sine):
    return v * cosine + swap_pairs(v) * sine


def pad_heads(t, extra):
    pieces = []
    for h in range(GROUP):
        pieces += [t[:, h * HEAD_DIM : (h + 1) * HEAD_DIM], extra]
    return jnp.concatenate(pieces, axis=1)


def pad_right(t):
    extra = jnp.zeros((t.shape[0], HEAD_DIM), t.dtype)
    pieces = []
    for h in range(GROUP):
        pieces += [extra, t[:, h * HEAD_DIM : (h + 1) * HEAD_DIM]]
    return jnp.concatenate(pieces, axis=1)


def unpad_heads(t):
    return jnp.concatenate([t[:, h * 128 : h * 128 + HEAD_DIM] for h in range(GROUP)], axis=1)


def head(t, h):
    return t[:, h * 128 : (h + 1) * 128]


def first_slot(i):
    return jnp.where(i < MOST, 0, jnp.where(i < MIDDLE, MOST, MIDDLE))


def cond_tables(cs_col, ct, st):
    cosine = jnp.zeros((PART, GW), F32)
    sine = jnp.zeros((PART, GW), F32)
    for j in range(FRAMES):
        here = cs_col == j
        cosine = cosine + jnp.where(here, ct[j : j + 1, :], 0.0)
        sine = sine + jnp.where(here, st[j : j + 1, :], 0.0)
    lane = lax.broadcasted_iota(jnp.int32, (PART, GW), 1) % HEAD_DIM
    return jnp.where(lane < 20, cosine, 1.0), sine


def read_meta(meta_ref):
    bias_t = jnp.transpose(meta_ref[0:FRAMES])
    cs_row = meta_ref[FRAMES : FRAMES + 1, 0:PART].astype(jnp.int32)
    cs_col = jnp.transpose(meta_ref[FRAMES:, :])[0:PART, 0:1].astype(jnp.int32)
    return cs_col, cs_row, bias_t


def place_kernel(perm, xv_ref, xc_ref, dv_ref, dc_ref, x_ref, dy_ref, sem):
    copies = []
    for n, (rows, out) in enumerate(((xv_ref, x_ref), (dv_ref, dy_ref))):
        for i in range(FRAMES):
            copies.append(pltpu.make_async_copy(rows.at[perm[i]], out.at[pl.ds(i * PART, PART)], sem.at[n, i]))
    for copy in copies:
        copy.start()
    for extra, out in ((xc_ref, x_ref), (dc_ref, dy_ref)):
        out[VIS:, :] = jnp.zeros((CROWS, D), BF16)
        for n in range(extra.shape[0]):
            out[VIS + n * COND : VIS + (n + 1) * COND, :] = extra[n]
    for copy in copies:
        copy.wait()


def place_rows(perm, visual, extra, d_visual, d_extra):
    return pl.pallas_call(
        place_kernel,
        name="place_rows",
        out_shape=(jax.ShapeDtypeStruct((ROWS, D), BF16),) * 2,
        in_specs=[pl.BlockSpec(memory_space=pltpu.SMEM), ANYM, FULL, ANYM, FULL],
        out_specs=(FULL, FULL),
        scratch_shapes=[pltpu.SemaphoreType.DMA((2, FRAMES))],
    )(perm, visual.reshape(FRAMES, PART, D), extra[0], d_visual.reshape(FRAMES, PART, D), d_extra[0])


def restore_kernel(slot, y_ref, g_ref, yo_ref, go_ref, yc_ref, gc_ref, yt, gt, sem):
    copies = []
    for f in range(FRAMES):
        rows = pl.ds(pl.multiple_of(slot[f] * PART, PART), PART)
        copies.append(pltpu.make_async_copy(y_ref.at[rows], yo_ref.at[f], sem.at[0, f]))
        copies.append(pltpu.make_async_copy(g_ref.at[rows], go_ref.at[f], sem.at[1, f]))
    last = pl.ds(VIS, CROWS)
    tails = [
        pltpu.make_async_copy(y_ref.at[last], yt, sem.at[0, FRAMES]),
        pltpu.make_async_copy(g_ref.at[last], gt, sem.at[1, FRAMES]),
    ]
    for copy in copies + tails:
        copy.start()
    for copy in tails:
        copy.wait()
    for n in range(yc_ref.shape[0]):
        yc_ref[n] = yt[n * COND : (n + 1) * COND]
        gc_ref[n] = gt[n * COND : (n + 1) * COND]
    for copy in copies:
        copy.wait()


def restore_rows(slot, y, g, parts):
    shape = (FRAMES, PART, D)
    small = (parts, COND, D)
    return pl.pallas_call(
        restore_kernel,
        name="restore_rows",
        out_shape=(
            jax.ShapeDtypeStruct(shape, BF16), jax.ShapeDtypeStruct(shape, F32),
            jax.ShapeDtypeStruct(small, BF16), jax.ShapeDtypeStruct(small, F32),
        ),
        in_specs=[pl.BlockSpec(memory_space=pltpu.SMEM), ANYM, ANYM],
        out_specs=(FULL,) * 4,
        scratch_shapes=[VM((CROWS, D), BF16), VM((CROWS, D), F32), pltpu.SemaphoreType.DMA((2, FRAMES + 1))],
    )(slot, y, g)


def where_am_i():
    d, z = lax.axis_index("dp"), lax.axis_index("stream")
    return d // 2, d % 2, z // 2, z % 2, z


def greet_column():
    p, c, q, r, z = where_am_i()
    barrier = pltpu.get_barrier_semaphore()
    for core in range(2):
        for chip in range(STREAMS):
            @pl.when((core != c) | (chip != z))
            def _():
                pl.semaphore_signal(
                    barrier, inc=1, device_id=(2 * p + core, chip),
                    device_id_type=pl.DeviceIdType.MESH,
                )
    pl.semaphore_wait(barrier, 2 * STREAMS - 1)


def remote(src, dst, send, recv, device):
    return pltpu.make_async_remote_copy(
        src_ref=src, dst_ref=dst, send_sem=send, recv_sem=recv, device_id=device,
        device_id_type=pl.DeviceIdType.MESH,
    )


def comm_call(kernel, name, ident, outs, scratch, far, close=(), near_outs=()):
    return pl.pallas_call(
        kernel,
        name=name,
        out_shape=tuple(jax.ShapeDtypeStruct(s, t) for s, t in tuple(outs) + tuple(near_outs)),
        in_specs=[ANYM] * len(far) + [FULL] * len(close),
        out_specs=tuple(ANYM for _ in outs) + tuple(FULL for _ in near_outs),
        scratch_shapes=scratch,
        compiler_params=pltpu.CompilerParams(
            collective_id=ident, has_side_effects=True, vmem_limit_bytes=LIMIT
        ),
    )(*far, *close)


def dma(*shape):
    return pltpu.SemaphoreType.DMA(shape)


HALF = VIS // 2


PIECE = HALF // 2


def forward_kernel(
    x_hbm, w_hbm, m_hbm, par_ref, cg_ref, sg_ref, ct_ref, st_ref,
    att_ref, xa_out, a_out, q_out, k_out, v_out, o_out,
    meta_ref, qc_ref, kc_ref, vc_ref, lse_ref, lsec_ref,
    xa, a_ref, q_ref, k_ref, v_ref, o_ref, vt_ref, w, bias_ref,
    isem, whole_s, whole_r, far_s, far_r, pass_s, near_s, near_r, tail_s, tail_r, msem, out_s, out_r, out_l, keep,
):
    p, c, q, r, z = where_am_i()
    group = 2 * r + c
    in_pair = q == c
    away = q != c
    inner = z == 1 + q
    z_one, z_two, z_three = z + 1 - 2 * r, z + 2 - 4 * q, STREAMS - 1 - z
    other = (2 * p + 1 - c, z)
    across = (2 * p + c, z_one)
    loads = []
    for part in range(3):
        cols = pl.ds(pl.multiple_of(part * D + group * GW, GW), GW)
        loads.append(pltpu.make_async_copy(w_hbm.at[:, cols], w.at[part], isem.at[part]))
    for copy in loads:
        copy.start()
    own_rows = pltpu.make_async_copy(x_hbm, xa.at[z], isem.at[3])

    @pl.when(in_pair)
    def _():
        own_rows.start()

    greet_column()
    tail = pl.ds(VIS, CROWS)

    def piece(half, g):
        return pl.ds(pl.multiple_of(half * HALF + g * PIECE, PIECE), PIECE)

    def whole_copy():
        return remote(x_hbm, xa.at[z], whole_s, whole_r, other)

    def far_copy(half, g):
        rows = piece(half, g)
        return remote(x_hbm.at[rows], xa.at[z, rows], far_s.at[half, g], far_r.at[z, g], (2 * p + half, 1 + c))

    def own_pass(g):
        rows = piece(c, g)
        return remote(x_hbm.at[rows], xa.at[z, rows], pass_s.at[z, g], far_r.at[z, g], across)

    def far_pass(s, g):
        rows = piece(c, g)
        return remote(xa.at[s, rows], xa.at[s, rows], pass_s.at[s, g], far_r.at[s, g], across)

    def near_copy(s, g, half):
        rows = piece(half, g)
        return remote(xa.at[s, rows], xa.at[s, rows], near_s.at[s, g], near_r.at[s, g], other)

    def tail_copy(half, side):
        n = half * 2 + side
        return remote(x_hbm.at[tail], xa.at[z, tail], tail_s.at[n], tail_r.at[z], (2 * p + half, 2 * c + side))

    def tail_needed(half, side):
        return jnp.logical_not((2 * c + side == z))

    def meta_copy():
        return remote(m_hbm, meta_ref, msem.at[0], msem.at[1], other)

    def meta_own():
        return pltpu.make_async_copy(m_hbm, meta_ref, msem.at[2])

    @pl.when(in_pair)
    def _():
        meta_own().start()
        meta_copy().start()
        whole_copy().start()
        own_pass(0).start()
        own_pass(1).start()

    for half in range(2):
        @pl.when(away)
        def _():
            far_copy(half, 0).start()

        for side in range(2):
            @pl.when(tail_needed(half, side))
            def _():
                tail_copy(half, side).start()

    def arrive(s, g, relay):
        far_pass(s, g).wait_recv()
        near_copy(s, g, c).start()
        if relay:
            @pl.when(inner)
            def _():
                far_pass(s, g).start()

    gain, shift = par_ref[0:1], par_ref[1:2]
    cut = pl.ds(pl.multiple_of(group * GW, GW), GW)
    lane64 = lax.broadcasted_iota(jnp.int32, (PATCHES, 64), 1)
    one = jnp.where(lane64 == 0, 1.0, 0.0).astype(BF16)

    def project(x, cosine, sine):
        x = x.astype(F32)
        centre = x - jnp.mean(x, axis=1, keepdims=True)
        spread = jnp.mean(centre * centre, axis=1, keepdims=True)
        a = (centre * lax.rsqrt(spread + EPS) * gain + shift).astype(BF16)
        q = turn(nn(a, w[0]) + par_ref[2:3, cut], cosine, sine)
        k = turn(nn(a, w[1]) + par_ref[3:4, cut], cosine, sine)
        v = (nn(a, w[2]) + par_ref[4:5, cut]).astype(BF16)
        return a, (q.astype(BF16).astype(F32) * 0.125).astype(BF16), k.astype(BF16), v

    def unit(t, carry):
        @pl.when(t == 0)
        def _():
            for copy in loads:
                copy.wait()

            @pl.when(in_pair)
            def _():
                own_rows.wait()
                meta_own().wait()

            @pl.when(away)
            def _():
                whole_copy().wait_recv()
                far_pass(z, 0).start()
                far_pass(z, 1).start()
                meta_copy().wait_recv()

            bias_ref[...] = jnp.transpose(meta_ref[0:FRAMES])

        @pl.when(t == 2)
        def _():
            arrive(z_one, 0, False)
            arrive(z_one, 1, False)

            @pl.when(away)
            def _():
                for half in range(2):
                    far_copy(half, 0).wait_send()
                    far_copy(half, 1).start()

            arrive(z_two, 0, True)
            arrive(z_three, 0, True)
            near_copy(z_one, 0, 1 - c).wait_recv()
            near_copy(z_one, 1, 1 - c).wait_recv()

        @pl.when(t == 4)
        def _():
            near_copy(z_two, 0, 1 - c).wait_recv()
            near_copy(z_three, 0, 1 - c).wait_recv()

        @pl.when(t == 6)
        def _():
            arrive(z_two, 1, True)
            arrive(z_three, 1, True)
            near_copy(z_two, 1, 1 - c).wait_recv()
            near_copy(z_three, 1, 1 - c).wait_recv()

        g = jnp.where(t < 4, t % 2, (t - 4) // 2)
        s = jnp.where(t < 2, z, jnp.where(t < 4, z_one, jnp.where(t % 2 == 0, z_two, z_three)))
        x = jnp.concatenate([xa[s, piece(0, g)], xa[s, piece(1, g)]], axis=0)
        place = pl.ds(pl.multiple_of(s * PART, PART), PART)
        cosine, sine, bias = [], [], []
        ids = lax.broadcasted_iota(jnp.int32, (PART, FRAMES), 1)
        for n in range(4):
            i = 2 * g + n % 2 + 4 * (n // 2)
            cosine.append(cg_ref[place] + ct_ref[pl.ds(i, 1), :])
            sine.append(sg_ref[place] + st_ref[pl.ds(i, 1), :])
            bias.append(jnp.sum(jnp.where(ids == i, bias_ref[place], 0.0), axis=1, keepdims=True))
        a, qs, ks, vs = project(x, jnp.concatenate(cosine, axis=0), jnp.concatenate(sine, axis=0))
        a_ref[s, piece(0, g)] = a[:PIECE]
        a_ref[s, piece(1, g)] = a[PIECE:]
        bias = jnp.concatenate(bias, axis=0)
        qs = pad_heads(qs, one)
        ks = pad_heads(ks, jnp.where(lane64 == 0, bias, 0.0).astype(BF16))
        vs = pad_right(vs)
        for n in range(4):
            i = 2 * g + n % 2 + 4 * (n // 2)
            rows = slice(n * PART, (n + 1) * PART)
            q_ref[i, place] = qs[rows]
            k_ref[i, place] = ks[rows]
            v_ref[i, place] = vs[rows]
        return carry

    lax.fori_loop(0, 8, unit, 0)

    for s in range(STREAMS):
        @pl.when(s != z)
        def _():
            remote(x_hbm.at[tail], xa.at[s, tail], tail_s.at[0], tail_r.at[s], other).wait_recv()
    cs_col, cs_row, _ = read_meta(meta_ref)
    a, qs, ks, vs = project(xa[:, VIS:, :].reshape(PART, D), *cond_tables(cs_col, ct_ref[...], st_ref[...]))
    a_ref[:, VIS:, :] = a.reshape(STREAMS, CROWS, D)
    qc_ref[...] = pad_heads(qs, one[:PART])
    kc_ref[...] = pad_heads(ks, jnp.zeros((PART, 64), BF16))
    vc_ref[...] = pad_right(vs)
    vct = jnp.transpose(vs.astype(F32)).astype(BF16)
    saves = [(xa, xa_out), (a_ref, a_out), (q_ref, q_out), (k_ref, k_out), (v_ref, v_out)]
    saves = [pltpu.make_async_copy(src, dst, keep.at[n]) for n, (src, dst) in enumerate(saves)]
    for copy in saves:
        copy.start()

    def out_rows(i):
        return pl.ds(pl.multiple_of(i * PART, PART), PART)

    def out_copy(s, n, rows):
        place = pl.ds(pl.multiple_of(group * GW, GW), GW)
        return remote(o_ref.at[s, rows], att_ref.at[rows, place], out_s.at[s, n], out_r.at[group, n], (2 * p + q, s))

    def out_own(s, n, rows):
        place = pl.ds(pl.multiple_of(group * GW, GW), GW)
        return pltpu.make_async_copy(o_ref.at[s, rows], att_ref.at[rows, place], out_l.at[n])

    def send_out(n, rows):
        for s in range(STREAMS):
            mine = in_pair & (s == z)

            @pl.when(mine)
            def _():
                out_own(s, n, rows).start()

            @pl.when(jnp.logical_not(mine))
            def _():
                out_copy(s, n, rows).start()

    def slot(i, carry):
        vt_ref[i] = jnp.transpose(unpad_right(v_ref[i].astype(F32))).astype(BF16)
        low = first_slot(i)
        near = (cs_col >= low) & (cs_col <= i)
        tops, totals, blends = [], [], []
        for h in range(GROUP):
            s = jnp.where(near, nt(head(kc_ref, h), q_ref[i, :, h * 128 : (h + 1) * 128]), NEG)
            top = jnp.max(s, axis=0, keepdims=True)
            pt = jnp.exp(s - top)
            tops.append(top)
            totals.append(jnp.sum(pt, axis=0, keepdims=True))
            blends.append(nn(vct[h * HEAD_DIM : (h + 1) * HEAD_DIM], pt.astype(BF16)))

        def step(j, state):
            tops, totals, blends = state
            cols = [slice(h * 128, (h + 1) * 128) for h in range(GROUP)]
            scores = [nt(k_ref[j, :, w], q_ref[i, :, w]) for w in cols]
            peaks = [jnp.maximum(tops[h], jnp.max(scores[h], axis=0, keepdims=True)) for h in range(GROUP)]
            pts = [jnp.exp(scores[h] - peaks[h]) for h in range(GROUP)]
            stay = [jnp.exp(tops[h] - peaks[h]) for h in range(GROUP)]
            sums = [totals[h] * stay[h] + jnp.sum(pts[h], axis=0, keepdims=True) for h in range(GROUP)]
            lows = [pt.astype(BF16) for pt in pts]
            more = [nn(vt_ref[j, h * HEAD_DIM : (h + 1) * HEAD_DIM, :], lows[h]) for h in range(GROUP)]
            return peaks, sums, [blends[h] * stay[h] + more[h] for h in range(GROUP)]

        tops, totals, blends = lax.fori_loop(low, i + 1, step, (tops, totals, blends))
        o = jnp.transpose(jnp.concatenate([blends[h] / totals[h] for h in range(GROUP)], axis=0))
        o_ref[:, out_rows(i), :] = o.astype(BF16).reshape(STREAMS, PART, GW)
        lse_ref[i] = jnp.concatenate([tops[h] + jnp.log(totals[h]) for h in range(GROUP)] * 2, axis=0)
        send_out(i, out_rows(i))
        return carry

    lo_col = first_slot(cs_col)

    def cond_queries():
        near = (cs_row >= lo_col) & (cs_row <= cs_col)
        tops, totals, blends = [], [], []
        for h in range(GROUP):
            s = jnp.where(near, nt(head(qc_ref, h), head(kc_ref, h)), NEG)
            top = jnp.max(s, axis=1, keepdims=True)
            pt = jnp.exp(s - top)
            tops.append(top)
            totals.append(jnp.sum(pt, axis=1, keepdims=True))
            blends.append(nn(pt.astype(BF16), head(vc_ref, h)))

        def cond_step(j, state):
            tops, totals, blends = state
            near = (lo_col <= j) & (cs_col >= j)
            new = ([], [], [])
            for h in range(GROUP):
                s = nt(head(qc_ref, h), k_ref[j, :, h * 128 : (h + 1) * 128])
                s = jnp.where(near, s, NEG)
                top = jnp.maximum(tops[h], jnp.max(s, axis=1, keepdims=True))
                pt = jnp.exp(s - top)
                stay = jnp.exp(tops[h] - top)
                new[0].append(top)
                new[1].append(totals[h] * stay + jnp.sum(pt, axis=1, keepdims=True))
                new[2].append(blends[h] * stay + nn(pt.astype(BF16), v_ref[j, :, h * 128 : (h + 1) * 128]))
            return new

        tops, totals, blends = lax.fori_loop(0, FRAMES, cond_step, (tops, totals, blends))
        o = jnp.concatenate([(blends[h] / totals[h])[:, HEAD_DIM:] for h in range(GROUP)], axis=1)
        o_ref[:, VIS:, :] = o.astype(BF16).reshape(STREAMS, CROWS, GW)
        lane = lax.broadcasted_iota(jnp.int32, (PART, 128), 1)
        lsec = jnp.zeros((PART, 128), F32)
        for h in range(GROUP):
            lsec = lsec + jnp.where(lane == h, tops[h] + jnp.log(totals[h]), 0.0)
        lsec_ref[...] = lsec
        send_out(FRAMES, tail)

    cond_queries()
    lax.fori_loop(0, FRAMES, slot, 0)
    last = pltpu.make_async_copy(o_ref, o_out, keep.at[5])
    last.start()

    def settle(n, rows):
        for s in range(STREAMS):
            mine = in_pair & (s == z)

            @pl.when(mine)
            def _():
                out_own(s, n, rows).wait()

            @pl.when(jnp.logical_not(mine))
            def _():
                out_copy(s, n, rows).wait_send()
        for g in range(4):
            @pl.when((g % 2 != c) | (2 * c + g // 2 != z))
            def _():
                place = pl.ds(g * GW, GW)
                remote(o_ref.at[0, rows], att_ref.at[rows, place], out_s.at[0, n], out_r.at[g, n], other).wait_recv()

    def settle_slot(i, carry):
        settle(i, out_rows(i))
        return carry

    lax.fori_loop(0, FRAMES, settle_slot, 0)
    settle(FRAMES, tail)

    @pl.when(in_pair)
    def _():
        meta_copy().wait_send()
        whole_copy().wait_send()
        own_pass(0).wait_send()
        own_pass(1).wait_send()

    @pl.when(away)
    def _():
        far_pass(z, 0).wait_send()
        far_pass(z, 1).wait_send()
        far_copy(0, 1).wait_send()
        far_copy(1, 1).wait_send()

    for half in range(2):
        for side in range(2):
            @pl.when(tail_needed(half, side))
            def _():
                tail_copy(half, side).wait_send()
    for g in range(2):
        for s in (z_one, z_two, z_three):
            near_copy(s, g, c).wait_send()
        for s in (z_two, z_three):
            @pl.when(inner)
            def _():
                far_pass(s, g).wait_send()
    for copy in saves:
        copy.wait()
    last.wait()


def attend_forward(x, w_qkv, meta, params, tables):
    def v16(*shape):
        return VM(shape, BF16)

    wide = (FRAMES, PATCHES, WIDE)
    rows = (STREAMS, ROWS, D)
    outs = (
        ((ROWS, D), BF16), (rows, BF16), (rows, BF16), (wide, BF16), (wide, BF16), (wide, BF16),
        ((STREAMS, ROWS, GW), BF16),
    )
    near_outs = (
        (meta.shape, F32), ((PART, WIDE), BF16), ((PART, WIDE), BF16), ((PART, WIDE), BF16),
        ((FRAMES, 8, PATCHES), F32), ((PART, 128), F32),
    )
    scratch = [
        v16(*rows), v16(*rows), v16(*wide), v16(*wide), v16(*wide), v16(STREAMS, ROWS, GW), v16(FRAMES, GW, PATCHES),
        v16(3, D, GW), VM((PATCHES, FRAMES), F32),
        dma(4), pltpu.SemaphoreType.DMA, pltpu.SemaphoreType.DMA, dma(2, 2), dma(4, 2), dma(4, 2), dma(4, 2), dma(4, 2),
        dma(4), dma(4), dma(3), dma(4, 9), dma(4, 9), dma(9), dma(6),
    ]
    return comm_call(
        forward_kernel, "attend_forward", 0, outs, scratch, (x, w_qkv, meta), (params,) + tables, near_outs
    )
CHUNKS = 9
EARLY = 3
LATE = 4
LAST = CHUNKS - EARLY - LATE
CUT = D // 2
QCUT = 3 * GW // 2


def add_up(*terms):
    total = terms[0].astype(F32)
    for t in terms[1:]:
        total = total + t.astype(F32)
    return total


def grid_shape():
    cores = lax.axis_size("dp") // 2
    nx = 1 << ((cores.bit_length() - 1) // 2)
    return nx, cores // nx, D // (cores * 2 * STREAMS)


class Place:
    def __init__(self, nx, ny):
        d, z = lax.axis_index("dp"), lax.axis_index("stream")
        self.nx, self.ny, self.d, self.z = nx, ny, d, z
        self.p, self.c, self.hi, self.lo = d // 2, d % 2, z // 2, z % 2
        self.x, self.y = self.p % nx, self.p // nx
        self.near = (d + 1 - 2 * self.c, z)
        self.z_one = (d, z + 1 - 2 * self.lo)
        self.z_two = (d, z + 2 - 4 * self.hi)
        self.slant = (d + 1 - 2 * self.c, z + 1 - 2 * self.lo)

    def along_x(self, n):
        return lax.rem(self.x + n, self.nx)

    def along_y(self, n):
        return lax.rem(self.y + n, self.ny)

    def x_device(self, n):
        return ((self.y * self.nx + self.along_x(n)) * 2 + self.c, self.z)

    def y_device(self, n):
        return ((self.along_y(n) * self.nx + self.x) * 2 + self.c, self.z)

    def greet(self):
        barrier = pltpu.get_barrier_semaphore()
        p, c, z, nx, ny = self.p, self.c, self.z, self.nx, self.ny
        for core in range(2):
            for chip in range(STREAMS):
                @pl.when((core != c) | (chip != z))
                def _():
                    pl.semaphore_signal(
                        barrier, inc=1, device_id=(2 * p + core, chip), device_id_type=pl.DeviceIdType.MESH
                    )
        others = [self.x_device(n) for n in range(1, nx)] + [self.y_device(n) for n in range(1, ny)]
        for device in others:
            pl.semaphore_signal(barrier, inc=1, device_id=device, device_id_type=pl.DeviceIdType.MESH)
        pl.semaphore_wait(barrier, 2 * STREAMS - 1 + len(others))


class Reducer:
    def __init__(self, at, rb, count, sources, refs, ahead=True):
        self.at, self.rb, self.count, self.sources, self.ahead = at, rb, count, sources, ahead
        (self.mine, self.rd, self.r2a, self.r2b, self.r3a, self.r3b, self.s3, self.r4, self.s4, self.r5, self.fin,
         self.lsem, self.ds, self.dr, self.as2, self.ar2, self.bs2, self.br2, self.as3, self.ar3, self.bs3, self.br3,
         self.s4s, self.s4r, self.s5s, self.s5r) = refs

    @staticmethod
    def scratch(n, nx, ny, rb):
        def v(*shape):
            return VM(shape, BF16)

        return [
            v(n, ny, nx, STREAMS, rb, D), v(n, ny, nx, STREAMS, rb, D),
            v(n, nx - 1, ny, STREAMS, rb, CUT), v(n, ny - 1, nx, STREAMS, rb, CUT),
            v(n, ny - 1, STREAMS, rb, CUT), v(n, nx - 1, STREAMS, rb, CUT),
            v(n, 2, 2, rb, D), v(n, 2, rb, D), v(n, 2, rb, D), v(n, rb, D), VM((n, rb, D), F32),
            dma(n), dma(n), dma(n),
            dma(n, nx - 1), dma(n, nx - 1), dma(n, ny - 1), dma(n, ny - 1),
            dma(n, ny - 1), dma(n, ny - 1), dma(n, nx - 1), dma(n, nx - 1),
            dma(n), dma(n), dma(n), dma(n),
        ]

    def issue(self, k):
        c = self.at.c
        begin = 0
        for size, get in self.sources:
            start = begin
            begin += size

            @pl.when((k >= start) & (k < start + size))
            def _():
                t = k - start
                remote(get(t, 1 - c), self.rd.at[k], self.ds.at[k], self.dr.at[k], self.at.near).start()
                pltpu.make_async_copy(get(t, c), self.mine.at[k], self.lsem.at[k]).start()

    def core(self, k):
        return remote(self.rd.at[k], self.rd.at[k], self.ds.at[k], self.dr.at[k], self.at.near)

    def a2(self, k, n):
        at = self.at
        src = self.mine.at[k, :, at.along_x(n), :, :, pl.ds(0, CUT)]
        return remote(src, self.r2a.at[k, n - 1], self.as2.at[k, n - 1], self.ar2.at[k, n - 1], at.x_device(n))

    def b2(self, k, n):
        at = self.at
        src = self.mine.at[k, at.along_y(n), :, :, :, pl.ds(CUT, CUT)]
        return remote(src, self.r2b.at[k, n - 1], self.bs2.at[k, n - 1], self.br2.at[k, n - 1], at.y_device(n))

    def a3(self, k, n):
        at = self.at
        src = self.r2a.at[k, 0, at.along_y(n)]
        return remote(src, self.r3a.at[k, n - 1], self.as3.at[k, n - 1], self.ar3.at[k, n - 1], at.y_device(n))

    def b3(self, k, n):
        at = self.at
        src = self.r2b.at[k, 0, at.along_x(n)]
        return remote(src, self.r3b.at[k, n - 1], self.bs3.at[k, n - 1], self.br3.at[k, n - 1], at.x_device(n))

    def c4(self, k):
        return remote(self.s3.at[k, :, 1 - self.at.lo], self.r4.at[k], self.s4s.at[k], self.s4r.at[k], self.at.z_one)

    def c5(self, k):
        return remote(self.s4.at[k, 1 - self.at.hi], self.r5.at[k], self.s5s.at[k], self.s5r.at[k], self.at.z_two)

    def tick(self, t, carry=0):
        self.run(t, t - 2, t - 4, t - 5, t - 6)
        return carry

    def run(self, *turns):
        at, rb, count = self.at, self.rb, self.count
        nx, ny, x, y = at.nx, at.ny, at.x, at.y

        def on(turn, body):
            k = turns[turn]
            if k is not None:
                pl.when((k >= 0) & (k < count))(lambda: body(k))

        def first(k):
            pltpu.make_async_copy(self.rd.at[k], self.mine.at[k], self.lsem.at[k]).wait()
            self.core(k).wait_recv()
            if self.ahead:
                self.issue(k + 2)
            for b in range(ny):
                for e in range(nx):
                    self.mine[k, b, e] = add_up(self.mine[k, b, e], self.rd[k, b, e]).astype(BF16)
            for n in range(1, nx):
                self.a2(k, n).start()
            for n in range(1, ny):
                self.b2(k, n).start()

        def second(k):
            for n in range(1, nx):
                self.a2(k, n).wait_recv()
            for b in range(ny):
                self.r2a[k, 0, b] = add_up(
                    self.mine[k, b, x, :, :, 0:CUT], *[self.r2a[k, n, b] for n in range(nx - 1)]
                ).astype(BF16)
            for n in range(1, ny):
                self.a3(k, n).start()
            for n in range(1, ny):
                self.b2(k, n).wait_recv()
            for b in range(nx):
                self.r2b[k, 0, b] = add_up(
                    self.mine[k, y, b, :, :, CUT:], *[self.r2b[k, n, b] for n in range(ny - 1)]
                ).astype(BF16)
            for n in range(1, nx):
                self.b3(k, n).start()

        def third(k):
            for n in range(1, ny):
                self.a3(k, n).wait_recv()
            for n in range(1, nx):
                self.b3(k, n).wait_recv()
            left = add_up(self.r2a[k, 0, y], *[self.r3a[k, n] for n in range(ny - 1)]).astype(BF16)
            right = add_up(self.r2b[k, 0, x], *[self.r3b[k, n] for n in range(nx - 1)]).astype(BF16)
            self.s3[k, :, :, :, 0:CUT] = left.reshape(2, 2, rb, CUT)
            self.s3[k, :, :, :, CUT:] = right.reshape(2, 2, rb, CUT)
            self.c4(k).start()

        def fourth(k):
            self.c4(k).wait_recv()
            self.s4[k] = add_up(self.s3[k, :, at.lo], self.r4[k]).astype(BF16)
            self.c5(k).start()

        def fifth(k):
            self.c5(k).wait_recv()
            self.fin[k] = add_up(self.s4[k, at.hi], self.r5[k])

        for turn, body in enumerate((first, second, third, fourth, fifth)):
            on(turn, body)

    def start(self):
        self.issue(0)
        self.issue(1)

    def drain(self):
        def one(k, carry):
            self.core(k).wait_send()
            for n in range(1, self.at.nx):
                self.a2(k, n).wait_send()
                self.b3(k, n).wait_send()
            for n in range(1, self.at.ny):
                self.b2(k, n).wait_send()
                self.a3(k, n).wait_send()
            self.c4(k).wait_send()
            self.c5(k).wait_send()
            return carry

        lax.fori_loop(0, self.count, one, 0)


def backward_kernel(
    nx, ny, rb,
    go_ref, d_ref, q_hbm, k_hbm, v_hbm, o_hbm,
    qc_ref, kc_ref, vc_ref, lse_ref, lsec_ref, cg_ref, sg_ref, ct_ref, st_ref, meta_ref,
    oo_ref, g_out,
    q_ref, k_ref, v_ref, o_ref, do_ref, g_ref, acc, accc, kt_ref, right, dqc,
    osem, isem, *refs,
):
    at = Place(nx, ny)
    p, c, q, r, z = at.p, at.c, at.hi, at.lo, at.z
    at.greet()
    reducer = Reducer(
        at, rb, LATE,
        (
            (LATE, lambda t, core: go_ref.at[:, :, core, :, t]),
        ),
        refs,
    )

    reducer.start()
    loads = [(q_hbm, q_ref), (k_hbm, k_ref), (v_hbm, v_ref), (o_hbm, o_ref), (d_ref, do_ref)]
    loads = [pltpu.make_async_copy(src, dst, isem.at[n]) for n, (src, dst) in enumerate(loads)]
    for copy in loads:
        copy.start()

    reducer.tick(0)
    cs_col, cs_row, _ = read_meta(meta_ref)
    acc[...] = jnp.zeros_like(acc)
    accc[...] = jnp.zeros_like(accc)
    kct = jnp.transpose(unpad_heads(kc_ref[...].astype(F32))).astype(BF16)
    for copy in loads:
        copy.wait()
    doc = do_ref[:, VIS:, :].reshape(PART, GW)
    oc = o_ref[:, VIS:, :].reshape(PART, GW)
    docp = pad_right(doc)
    lane = lax.broadcasted_iota(jnp.int32, (PART, WIDE), 1) % 128
    qcl = jnp.where(lane < HEAD_DIM, qc_ref[...].astype(F32), 0.0).astype(BF16)
    prod = doc.astype(F32) * oc.astype(F32)
    lo_col = first_slot(cs_col)
    near = (cs_row >= lo_col) & (cs_row <= cs_col)
    deltas = [
        jnp.sum(prod[:, h * HEAD_DIM : (h + 1) * HEAD_DIM], axis=1, keepdims=True) for h in range(GROUP)
    ]
    lses = [lsec_ref[:, h : h + 1] for h in range(GROUP)]
    dqs = []
    for h in range(GROUP):
        cols = slice(h * 128, (h + 1) * 128)
        s = jnp.where(near, nt(qc_ref[:, cols], kc_ref[:, cols]), NEG)
        pt = jnp.exp(s - lses[h])
        dst = pt * (nt(docp[:, cols], vc_ref[:, cols]) - deltas[h])
        accc[:, cols] += nn(jnp.transpose(pt).astype(BF16), docp[:, cols]) + nn(
            jnp.transpose(dst).astype(BF16), qcl[:, cols]
        )
        dqs.append(nn(dst.astype(BF16), kc_ref[:, cols]))

    def cond_step(j, dqs):
        near = (lo_col <= j) & (cs_col >= j)
        new = []
        for h in range(GROUP):
            cols = slice(h * 128, (h + 1) * 128)
            s = jnp.where(near, nt(qc_ref[:, cols], k_ref[j, :, cols]), NEG)
            pt = jnp.exp(s - lses[h])
            dst = pt * (nt(docp[:, cols], v_ref[j, :, cols]) - deltas[h])
            acc[j, :, cols] += nn(jnp.transpose(pt).astype(BF16), docp[:, cols]) + nn(
                jnp.transpose(dst).astype(BF16), qcl[:, cols]
            )
            new.append(dqs[h] + nn(dst.astype(BF16), k_ref[j, :, cols]))
        return new

    dqs = lax.fori_loop(0, FRAMES, cond_step, dqs)
    dqc[...] = jnp.concatenate([t[:, :HEAD_DIM] for t in dqs], axis=1) * 0.125
    reducer.tick(1)

    def slot(i):
        start = pl.multiple_of(i * PART, PART)
        do = do_ref[:, pl.ds(start, PART), :].reshape(PATCHES, GW)
        o = o_ref[:, pl.ds(start, PART), :].reshape(PATCHES, GW)
        prod = jnp.transpose(do.astype(F32) * o.astype(F32))
        deltas = [
            jnp.sum(prod[h * HEAD_DIM : (h + 1) * HEAD_DIM], axis=0, keepdims=True) for h in range(GROUP)
        ]
        right[0:PATCHES] = pad_right(do)
        lane = lax.broadcasted_iota(jnp.int32, (PATCHES, WIDE), 1) % 128
        right[PATCHES:] = jnp.where(lane < HEAD_DIM, q_ref[i].astype(F32), 0.0).astype(BF16)
        kt_ref[i] = jnp.transpose(unpad_heads(k_ref[i].astype(F32))).astype(BF16)
        low = first_slot(i)
        near = (cs_col >= low) & (cs_col <= i)
        dqs = []
        for h in range(GROUP):
            cols = slice(h * 128, (h + 1) * 128)
            s = jnp.where(near, nt(kc_ref[:, cols], q_ref[i, :, cols]), NEG)
            pt = jnp.exp(s - lse_ref[i, h : h + 1, :])
            dst = (pt * (nt(vc_ref[:, cols], right[0:PATCHES, cols]) - deltas[h])).astype(BF16)
            accc[:, cols] += nn(jnp.concatenate([pt.astype(BF16), dst], axis=1), right[:, cols])
            dqs.append(nn(kct[h * HEAD_DIM : (h + 1) * HEAD_DIM], dst))

        def step(j, dqs):
            cols = [slice(h * 128, (h + 1) * 128) for h in range(GROUP)]
            scores = [nt(k_ref[j, :, w], q_ref[i, :, w]) for w in cols]
            grads = [nt(v_ref[j, :, w], right[0:PATCHES, w]) for w in cols]
            pts = [jnp.exp(scores[h] - lse_ref[i, h : h + 1, :]) for h in range(GROUP)]
            dsts = [(pts[h] * (grads[h] - deltas[h])).astype(BF16) for h in range(GROUP)]
            both = [jnp.concatenate([pts[h].astype(BF16), dsts[h]], axis=1) for h in range(GROUP)]
            for h in range(GROUP):
                acc[j, :, cols[h]] += nn(both[h], right[:, cols[h]])
            return [dqs[h] + nn(kt_ref[j, h * HEAD_DIM : (h + 1) * HEAD_DIM, :], dsts[h]) for h in range(GROUP)]

        dqs = lax.fori_loop(low, i + 1, step, dqs)
        dq = jnp.transpose(jnp.concatenate(dqs, axis=0)) * 0.125
        cosine = cg_ref[...] + ct_ref[pl.ds(i, 1), :]
        sine = sg_ref[...] + st_ref[pl.ds(i, 1), :]
        dq = turn(dq, cosine, -sine).astype(BF16).reshape(STREAMS, PART, GW)
        g_ref[:, pl.ds(start, PART), 0:GW] = dq

    def sweep(i, carry):
        slot(i)
        reducer.tick(i + 2)
        return carry

    lax.fori_loop(0, FRAMES, sweep, 0)

    cosine, sine = cond_tables(cs_col, ct_ref[...], st_ref[...])
    valid = cs_col < FRAMES
    dq = dqc[...]
    both = accc[...]
    parts = (turn(dq, cosine, -sine), turn(unpad_heads(both), cosine, -sine), unpad_right(both))
    for part, t in enumerate(parts):
        t = jnp.where(valid, t, 0.0).astype(BF16)
        g_ref[:, VIS:, part * GW : (part + 1) * GW] = t.reshape(STREAMS, CROWS, GW)

    def finish(i, carry):
        start = pl.multiple_of(i * PART, PART)
        cosine = cg_ref[...] + ct_ref[pl.ds(i, 1), :]
        sine = sg_ref[...] + st_ref[pl.ds(i, 1), :]
        both = acc[i]
        dk = turn(unpad_heads(both), cosine, -sine)
        g_ref[:, pl.ds(start, PART), GW : 2 * GW] = dk.astype(BF16).reshape(STREAMS, PART, GW)
        g_ref[:, pl.ds(start, PART), 2 * GW :] = unpad_right(both).astype(BF16).reshape(STREAMS, PART, GW)
        return carry

    lax.fori_loop(0, FRAMES, finish, 0)
    save = pltpu.make_async_copy(g_ref, g_out, isem.at[5])
    save.start()
    fin = reducer.fin
    outs = [pltpu.make_async_copy(fin.at[k], oo_ref.at[k], osem.at[k]) for k in range(4)]
    for copy in outs:
        copy.start()

    reducer.drain()
    save.wait()
    for copy in outs:
        copy.wait()


def unpad_right(t):
    return jnp.concatenate([t[:, h * 128 + HEAD_DIM : (h + 1) * 128] for h in range(GROUP)], axis=1)


def attend_backward(g_out, grad_o, saved, o, tables, meta):
    nx, ny, rb = grid_shape()
    q, k, v, *rest = saved

    def v16(*shape):
        return VM(shape, BF16)

    scratch = [
        v16(*q.shape), v16(*k.shape), v16(*v.shape), v16(*o.shape), v16(*o.shape), v16(STREAMS, ROWS, 3 * GW),
        VM((FRAMES, PATCHES, WIDE), F32), VM((PART, WIDE), F32), v16(FRAMES, GW, PATCHES), v16(2 * PATCHES, WIDE),
        VM((PART, GW), F32),
        dma(LATE), dma(6),
    ] + Reducer.scratch(LATE, nx, ny, rb)
    outs = (((4, rb, D), F32), ((STREAMS, ROWS, 3 * GW), BF16))
    ops = (g_out.reshape(ny, nx, 2, STREAMS, 4, rb, D), grad_o, q, k, v, o)
    return comm_call(
        functools.partial(backward_kernel, nx, ny, rb), "attend_backward", 3, outs, scratch, ops,
        tuple(rest) + tables + (meta,),
    )


def finish_kernel(
    nx, ny, rb,
    f_hbm, xa_hbm, gq_ref, w_hbm, x_hbm, h_hbm, gi_ref, gp_ref, v_ref, gain_ref,
    gx_ref, oq_ref, ov_ref, oi_ref, op_ref,
    f, xa, w, x_own, h_own, big, near_in, near_out, own, land, tail, tail_out, total,
    q1, rq1a, rq1b, sq1a, sq1b, rq2a, rq2b, sq2, rq3, sq3, vm, vd, vx, vy, vz1, vz2, hold,
    isem, dsend, drecv, send, recv, csend, crecv, lsem,
    qs1a, qr1a, qs1b, qr1b, qs2a, qr2a, qs2b, qr2b, qs3, qr3, qs4, qr4, vs, vr, vsx, vrx, vsy, vry, relay, rsend, rrecv, cols_sum, osem,
    *refs,
):
    at = Place(nx, ny)
    p, c, q, r, z, x, y, hi, lo = at.p, at.c, at.hi, at.lo, at.z, at.x, at.y, at.hi, at.lo
    group = 2 * r + c
    in_pair, inner = q == c, z == 1 + q
    reducer = Reducer(
        at, rb, LAST,
        ((LAST - 1, lambda t, core: gi_ref.at[:, :, core]), (1, lambda t, core: gp_ref.at[:, :, core])),
        refs, ahead=False,
    )
    loads = []
    for part in range(3):
        cols = pl.ds(pl.multiple_of(part * D + group * GW, GW), GW)
        loads.append(pltpu.make_async_copy(w_hbm.at[:, cols], w.at[:, pl.ds(part * GW, GW)], isem.at[part]))
    loads.append(pltpu.make_async_copy(f_hbm, f, isem.at[3]))
    loads.append(pltpu.make_async_copy(xa_hbm, xa, isem.at[4]))
    late = [
        pltpu.make_async_copy(gq_ref, q1, isem.at[5]),
        pltpu.make_async_copy(x_hbm, x_own, isem.at[6]),
        pltpu.make_async_copy(h_hbm, h_own, isem.at[7]),
    ]
    for copy in loads + late:
        copy.start()
    at.greet()
    rows = pl.ds(pl.multiple_of(c * HALF, HALF), HALF)
    rest = pl.ds(pl.multiple_of((1 - c) * HALF, HALF), HALF)
    last = pl.ds(VIS, CROWS)
    qa, qb = pl.ds(0, QCUT), pl.ds(QCUT, QCUT)

    def q1a(n):
        return remote(q1.at[:, at.along_x(n), :, :, qa], rq1a.at[n - 1], qs1a.at[n - 1], qr1a.at[n - 1], at.x_device(n))

    def q1b(n):
        return remote(q1.at[at.along_y(n), :, :, :, qb], rq1b.at[n - 1], qs1b.at[n - 1], qr1b.at[n - 1], at.y_device(n))

    def q2a(n):
        return remote(sq1a.at[at.along_y(n)], rq2a.at[n - 1], qs2a.at[n - 1], qr2a.at[n - 1], at.y_device(n))

    def q2b(n):
        return remote(sq1b.at[at.along_x(n)], rq2b.at[n - 1], qs2b.at[n - 1], qr2b.at[n - 1], at.x_device(n))

    def q3():
        return remote(sq2.at[:, 1 - hi], rq3, qs3, qr3, at.z_two)

    mates = [(at.near, 1, 0), (at.z_one, 0, 1), (at.slant, 1, 1)]

    def q4(n, part):
        device, core, side = mates[n]
        to_core = c + core - 2 * c * core
        to_side = lo + side - 2 * lo * side
        place = pl.ds(pl.multiple_of(part * D + group * GW, GW), GW)
        return remote(
            sq3.at[to_core, to_side, :, pl.ds(part * GW, GW)], oq_ref.at[:, place],
            qs4.at[n, part], qr4.at[n, part], device,
        )

    def q4_own(part):
        place = pl.ds(pl.multiple_of(part * D + group * GW, GW), GW)
        return pltpu.make_async_copy(sq3.at[c, lo, :, pl.ds(part * GW, GW)], oq_ref.at[:, place], lsem.at[2 + part])

    def v_core():
        return remote(vm.at[0], vd, vs.at[0], vr.at[0], at.near)

    def v_x(n):
        return remote(vm.at[1], vx.at[n - 1], vsx.at[n - 1], vrx.at[n - 1], at.x_device(n))

    def v_y(n):
        return remote(vm.at[2], vy.at[n - 1], vsy.at[n - 1], vry.at[n - 1], at.y_device(n))

    def v_z1():
        return remote(vm.at[3], vz1, vs.at[1], vr.at[1], at.z_one)

    def v_z2():
        return remote(vm.at[4], vz2, vs.at[2], vr.at[2], at.z_two)

    def near_copy(s):
        return remote(near_out.at[s], near_in.at[s], dsend.at[s], drecv.at[s], at.near)

    def row_copy(s):
        mark = jnp.where(s // 2 == q, r, 0)
        return remote(own.at[s], land.at[mark, rows], send.at[s], recv.at[mark, c], (2 * p + q, s))

    def row_own(s):
        return pltpu.make_async_copy(own.at[s], land.at[r, rows], lsem.at[0])

    def relay_copy(n, s):
        return remote(own.at[s], relay.at[n], rsend.at[n], rrecv.at[n], at.z_one)

    def tail_copy(s):
        return remote(tail_out.at[s], tail.at[group], csend.at[s], crecv.at[group], (2 * p + q, s))

    def tail_own(s):
        return pltpu.make_async_copy(tail_out.at[s], tail.at[group], lsem.at[1])

    def mine(s):
        return (q == c) & (s == z)

    def go(s, far, near):
        @pl.when(mine(s))
        def _():
            near(s)

        @pl.when(jnp.logical_not(mine(s)))
        def _():
            far(s)

    for k in range(LAST):
        reducer.issue(jnp.int32(k))
    late[0].wait()
    for n in range(1, nx):
        q1a(n).start()
    for n in range(1, ny):
        q1b(n).start()
    for copy in loads:
        copy.wait()
    hold[...] = jnp.zeros_like(hold)
    cols_sum[...] = jnp.zeros_like(cols_sum)

    far = (STREAMS - 1 - z, z + 2 - 4 * hi, z + 1 - 2 * lo, z)

    @pl.when(jnp.logical_not(in_pair))
    def _():
        land[1] = jnp.zeros_like(land[1])

    def combine(s):
        near_copy(s).wait_recv()
        for t in range(HALF // 64):
            part = pl.ds(t * 64, 64)
            own[s, part] = add_up(near_in[s, part], own[s, part]).astype(BF16)

    def pass_on(n):
        s = far[n]
        combine(s)
        if n >= 2:
            go(s, lambda s: row_copy(s).start(), lambda s: row_own(s).start())
        else:
            @pl.when(jnp.logical_not(inner))
            def _():
                relay_copy(n, s).start()

    def pass_far(n):
        s = far[1 - n]

        @pl.when(inner)
        def _():
            relay_copy(n, s).wait_recv()
            for t in range(HALF // 64):
                part = pl.ds(t * 64, 64)
                own[s, part] = add_up(relay[n, part], own[s, part]).astype(BF16)
            row_copy(s).start()

    def partial_rows(t, carry):
        s = jnp.where(t == 0, far[0], jnp.where(t == 1, far[1], jnp.where(t == 2, far[2], far[3])))
        big[...] = nt(f[s], w[...])
        near_out[s] = big[rest].astype(BF16)
        near_copy(s).start()
        own[s] = big[rows].astype(BF16)
        tail_out[s] = big[last].astype(BF16)
        go(s, lambda s: tail_copy(s).start(), lambda s: tail_own(s).start())
        for e in range(ROWS // 48):
            part = pl.ds(e * 48, 48)
            values = xa[s, part].astype(F32)
            centre = values - jnp.mean(values, axis=1, keepdims=True)
            scale = lax.rsqrt(jnp.mean(centre * centre, axis=1, keepdims=True) + EPS)
            g = big[part]
            gh = g * (centre * scale)
            flat = f[s, part].astype(F32)
            for m in range(6):
                cols_sum[...] += flat[m * 8 : m * 8 + 8]
                hold[0] += gh[m * 8 : m * 8 + 8]
                hold[1] += g[m * 8 : m * 8 + 8]

        for n in range(STREAMS - 1):
            @pl.when(t == n + 1)
            def _():
                pass_on(n)

        return carry

    lax.fori_loop(0, STREAMS, partial_rows, 0)
    pass_on(STREAMS - 1)

    def move(turn):
        def one(k, carry):
            reducer.run(*[k if n == turn else None for n in range(5)])
            return carry

        lax.fori_loop(0, LAST, one, 0)

    move(0)
    vm[0] = v_ref[...]
    vm[0, 0:1] = jnp.sum(hold[0], axis=0, keepdims=True)
    vm[0, 1:2] = jnp.sum(hold[1], axis=0, keepdims=True)
    for part in range(3):
        place = pl.ds(pl.multiple_of(group * GW, GW), GW)
        vm[0, 2 + part : 3 + part, place] = jnp.sum(cols_sum[:, part * GW : (part + 1) * GW], axis=0, keepdims=True)
    v_core().start()

    for n in range(1, nx):
        q1a(n).wait_recv()
    for n in range(1, ny):
        q1b(n).wait_recv()
    for b in range(ny):
        sq1a[b] = add_up(q1[b, x, :, :, 0:QCUT], *[rq1a[n, b] for n in range(nx - 1)]).astype(BF16)
    for n in range(1, ny):
        q2a(n).start()
    for b in range(nx):
        sq1b[b] = add_up(q1[y, b, :, :, QCUT:], *[rq1b[n, b] for n in range(ny - 1)]).astype(BF16)
    for n in range(1, nx):
        q2b(n).start()
    v_core().wait_recv()
    vm[1] = vm[0] + vd[...]
    for n in range(1, nx):
        v_x(n).start()
    pass_far(0)
    move(1)
    for n in range(1, ny):
        q2a(n).wait_recv()
    for n in range(1, nx):
        q2b(n).wait_recv()
    left = add_up(sq1a[y], *[rq2a[n] for n in range(ny - 1)]).astype(BF16)
    right = add_up(sq1b[x], *[rq2b[n] for n in range(nx - 1)]).astype(BF16)
    sq2[:, :, :, :, 0:QCUT] = left.reshape(2, 2, 2, rb, QCUT)
    sq2[:, :, :, :, QCUT:] = right.reshape(2, 2, 2, rb, QCUT)
    q3().start()
    for n in range(1, nx):
        v_x(n).wait_recv()
    vm[2] = add_up(vm[1], *[vx[n] for n in range(nx - 1)])
    for n in range(1, ny):
        v_y(n).start()
    for n in range(1, ny):
        v_y(n).wait_recv()
    vm[3] = add_up(vm[2], *[vy[n] for n in range(ny - 1)])
    v_z1().start()
    pass_far(1)
    move(2)
    q3().wait_recv()
    sq3[...] = add_up(sq2[:, hi], rq3[...])
    for part in range(3):
        for n in range(3):
            q4(n, part).start()
        q4_own(part).start()
    v_z1().wait_recv()
    vm[4] = vm[3] + vz1[...]
    v_z2().start()
    move(3)

    late[1].wait()
    late[2].wait()
    for side in range(2):
        for core in range(2):
            part = pl.ds(core * HALF, HALF)
            g = 2 * side + core
            self_made = (core == c) & (2 * c + side == z)

            @pl.when(jnp.logical_not(self_made))
            def _():
                remote(tail_out.at[0], tail.at[g], csend.at[0], crecv.at[g], at.near).wait_recv()

            @pl.when(jnp.logical_not(self_made) & (in_pair | (side == 0)))
            def _():
                remote(own.at[0], land.at[side, part], send.at[0], recv.at[side, core], at.near).wait_recv()

            @pl.when(self_made)
            def _():
                row_own(0).wait()
                tail_own(0).wait()

    gain = gain_ref[0:1]

    def back(dst, grad):
        values = x_own[dst].astype(F32)
        centre = values - jnp.mean(values, axis=1, keepdims=True)
        scale = lax.rsqrt(jnp.mean(centre * centre, axis=1, keepdims=True) + EPS)
        normed = centre * scale
        g = grad * gain
        total[dst] = h_own[dst] + scale * (
            g - jnp.mean(g, axis=1, keepdims=True) - normed * jnp.mean(g * normed, axis=1, keepdims=True)
        )

    def back_rows(t, carry):
        part = pl.ds(pl.multiple_of(t * 64, 64), 64)
        back(part, add_up(land[0, part], land[1, part]))
        return carry

    lax.fori_loop(0, VIS // 64, back_rows, 0)
    back(last, add_up(tail[0], tail[1], tail[2], tail[3]))
    done = pltpu.make_async_copy(total, gx_ref, lsem.at[5])
    done.start()
    move(4)
    outs = [
        pltpu.make_async_copy(reducer.fin.at[k], oi_ref.at[:, pl.ds(k * D, D)], osem.at[k]) for k in range(LAST - 1)
    ]
    outs += [pltpu.make_async_copy(reducer.fin.at[LAST - 1], op_ref, osem.at[LAST - 1])]
    for copy in outs:
        copy.start()
    v_z2().wait_recv()
    vm[5] = vm[4] + vz2[...]
    v_done = pltpu.make_async_copy(vm.at[5], ov_ref, lsem.at[6])
    v_done.start()
    for n in range(1, nx):
        q1a(n).wait_send()
        q2b(n).wait_send()
        v_x(n).wait_send()
    for n in range(1, ny):
        q1b(n).wait_send()
        q2a(n).wait_send()
        v_y(n).wait_send()
    q3().wait_send()
    v_core().wait_send()
    v_z1().wait_send()
    v_z2().wait_send()
    for n in range(STREAMS):
        s = far[n]
        near_copy(s).wait_send()
        if n < 2:
            @pl.when(inner)
            def _():
                row_copy(s).wait_send()

            @pl.when(jnp.logical_not(inner))
            def _():
                relay_copy(n, s).wait_send()

            tail_copy(s).wait_send()
        else:
            @pl.when(jnp.logical_not(mine(s)))
            def _():
                row_copy(s).wait_send()
                tail_copy(s).wait_send()
    for part in range(3):
        q4_own(part).wait()
        for n in range(3):
            q4(n, part).wait_send()
            q4(n, part).wait_recv()
    reducer.drain()
    for copy in outs:
        copy.wait()
    done.wait()
    v_done.wait()


def finish_rows(flat, x_all, g_qkv, w_qkv, x, h, g_in, g_proj, vectors, gain):
    nx, ny, rb = grid_shape()

    def v(*shape):
        return VM(shape, BF16)

    def vf(*shape):
        return VM(shape, F32)

    scratch = [
        v(STREAMS, ROWS, 3 * GW), v(STREAMS, ROWS, D), v(D, 3 * GW), v(ROWS, D), vf(ROWS, D), vf(ROWS, D),
        v(STREAMS, HALF, D), v(STREAMS, HALF, D), v(STREAMS, HALF, D), v(2, VIS, D), v(4, CROWS, D), v(4, CROWS, D),
        vf(ROWS, D),
        v(ny, nx, 8, rb, 3 * GW), v(nx - 1, ny, 8, rb, QCUT), v(ny - 1, nx, 8, rb, QCUT),
        v(ny, 8, rb, QCUT), v(nx, 8, rb, QCUT), v(ny - 1, 8, rb, QCUT), v(nx - 1, 8, rb, QCUT),
        v(2, 2, 2, rb, 3 * GW), v(2, 2, rb, 3 * GW), vf(2, 2, rb, 3 * GW),
        vf(6, 16, D), vf(16, D), vf(nx - 1, 16, D), vf(ny - 1, 16, D), vf(16, D), vf(16, D), vf(2, 8, D),
        dma(8), dma(4), dma(4), dma(4), dma(2, 2), dma(4), dma(4), dma(7),
        dma(nx - 1), dma(nx - 1), dma(ny - 1), dma(ny - 1), dma(ny - 1), dma(ny - 1), dma(nx - 1), dma(nx - 1),
        pltpu.SemaphoreType.DMA, pltpu.SemaphoreType.DMA, dma(3, 3), dma(3, 3),
        dma(3), dma(3), dma(nx - 1), dma(nx - 1), dma(ny - 1), dma(ny - 1),
        v(2, HALF, D), dma(2), dma(2), vf(8, 3 * GW), dma(LAST),
    ] + Reducer.scratch(LAST, nx, ny, rb)
    outs = (
        ((ROWS, D), F32), ((rb, 3 * D), F32), ((16, D), F32), ((rb, (LAST - 1) * D), F32), ((rb, D), F32),
    )
    ops = (
        flat, x_all, g_qkv.reshape(ny, nx, 8, rb, 3 * GW), w_qkv, x, h,
        g_in.reshape(ny, nx, 2, STREAMS, rb, (LAST - 1) * D), g_proj.reshape(ny, nx, 2, STREAMS, rb, D),
    )
    return comm_call(
        functools.partial(finish_kernel, nx, ny, rb), "finish_rows", 4, outs, scratch, ops, (vectors, gain)
    )


TILE = 48
TILES = ROWS // TILE


def tn(a, b):
    return lax.dot_general(a, b, (((0,), (0,)), ((), ())), preferred_element_type=F32)


def mlp_kernel(
    nx, ny, rb,
    win_hbm, wout_hbm, att_ref, x_ref, dy_ref, wp_ref, par_ref,
    do_out, gi_out, go_out, gp_out, oi_ref, y_ref, gh_ref, vec_ref,
    wi, wo, n_ref, h_ref, buf, dbuf, hid, du, yacc, dn, dhb, do_ref, stage, sums,
    gi, isem, ssem, hs, hr, hl, osem, *refs,
):
    at = Place(nx, ny)
    p, c, q, r, z = at.p, at.c, at.hi, at.lo, at.z
    reducer = Reducer(at, rb, EARLY, ((EARLY, lambda t, core: gi.at[t, :, :, core]),), refs, ahead=False)

    def fetch(t, slot):
        cols = pl.ds(pl.multiple_of(t * D, D), D)
        return (
            pltpu.make_async_copy(win_hbm.at[:, cols], wi.at[slot], isem.at[0, slot]),
            pltpu.make_async_copy(wout_hbm.at[cols, :], wo.at[slot], isem.at[1, slot]),
        )

    for copy in fetch(0, 0):
        copy.start()
    at.greet()
    sums[...] = jnp.zeros_like(sums)
    for j in range(2):
        cols = slice(j * CUT, (j + 1) * CUT)
        buf[:, cols] = nn(att_ref[...], wp_ref[:, cols])

    def tile(t):
        return pl.ds(pl.multiple_of(t * TILE, 16), TILE)

    def fold(row, values):
        total = values[0:8]
        for m in range(1, TILE // 8):
            total = total + values[m * 8 : m * 8 + 8]
        sums[row] += total

    def enter(t, carry):
        rows = tile(t)
        h = x_ref[rows].astype(F32) + buf[rows] + par_ref[9:10]
        h_ref[rows] = h
        centre = h - jnp.mean(h, axis=1, keepdims=True)
        scale = lax.rsqrt(jnp.mean(centre * centre, axis=1, keepdims=True) + EPS)
        n_ref[rows] = (centre * scale * par_ref[10:11] + par_ref[11:12]).astype(BF16)
        return carry

    lax.fori_loop(0, TILES, enter, 0)

    def block(t, carry):
        slot = t % 2
        for copy in fetch(t, slot):
            copy.wait()

        @pl.when(t < 3)
        def _():
            for copy in fetch(t + 1, 1 - slot):
                copy.start()

        reducer.run(t - 1, None, t - 2, None, t - 3)
        for j in range(2):
            cols = slice(j * CUT, (j + 1) * CUT)
            buf[:, cols] = nn(n_ref[...], wi[slot, :, cols])
            dbuf[:, cols] = nt(dy_ref[...], wo[slot, cols, :])
        place = pl.ds(pl.multiple_of(t * D, D), D)

        def act(e, carry):
            rows = tile(e)
            for j in range(4):
                cols = slice(j * 256, (j + 1) * 256)
                u = buf[rows, cols] + par_ref[pl.ds(5 + t, 1), cols]
                phi = 0.5 * (1.0 + lax.erf(u * (2.0**-0.5)))
                hid[rows, pl.ds(pl.multiple_of(t * D + j * 256, 256), 256)] = (u * phi).astype(BF16)
                slope = phi + u * (jnp.exp(-0.5 * u * u) * ((2.0 * math.pi) ** -0.5))
                g = (dbuf[rows, cols] * slope).astype(BF16)
                du[rows, cols] = g
                g = g.astype(F32)
                total = g[0:8]
                for m in range(1, TILE // 8):
                    total = total + g[m * 8 : m * 8 + 8]
                sums[t, :, cols] += total
            return carry

        lax.fori_loop(0, TILES, act, 0)

        @pl.when(t < EARLY)
        def _():
            for b in range(ny):
                block_rows = tn(n_ref[:, b * (D // ny) : (b + 1) * (D // ny)], du[...])
                gi[t, b] = block_rows.astype(BF16).reshape(nx, 2, STREAMS, rb, D)
            reducer.issue(t)

        reducer.run(None, t - 1, None, t - 2, None)
        for j in range(2):
            cols = slice(j * CUT, (j + 1) * CUT)
            more = nn(hid[:, place], wo[slot, :, cols])
            back = nt(du[...], wi[slot, cols, :])

            @pl.when(t == 0)
            def _():
                yacc[:, cols] = more
                dn[:, cols] = back

            @pl.when(t > 0)
            def _():
                yacc[:, cols] += more
                dn[:, cols] += back

        return carry

    lax.fori_loop(0, 4, block, 0)
    reducer.run(None, None, EARLY - 1, None, EARLY - 2)

    def leave(t, carry):
        rows = tile(t)
        h = h_ref[rows]
        y_ref[rows] = (h + yacc[rows] + par_ref[12:13]).astype(BF16)
        centre = h - jnp.mean(h, axis=1, keepdims=True)
        scale = lax.rsqrt(jnp.mean(centre * centre, axis=1, keepdims=True) + EPS)
        normed = centre * scale
        grad = dn[rows]
        dy = dy_ref[rows].astype(F32)
        fold(5, grad * normed)
        fold(6, grad)
        fold(7, dy)
        g = grad * par_ref[10:11]
        gh = dy + scale * (
            g - jnp.mean(g, axis=1, keepdims=True) - normed * jnp.mean(g * normed, axis=1, keepdims=True)
        )
        gh_ref[rows] = gh
        low = gh.astype(BF16)
        dhb[rows] = low
        fold(4, low.astype(F32))
        return carry

    lax.fori_loop(0, TILES, leave, 0)
    reducer.run(None, None, None, EARLY - 1, None)
    for j in range(2):
        rows = slice(j * CUT, (j + 1) * CUT)
        do_ref[:, rows] = nt(dhb[...], wp_ref[rows, :]).astype(BF16)

    def heads_copy(g):
        device = (2 * p + g % 2, 2 * c + g // 2)
        return remote(do_ref.at[:, pl.ds(g * GW, GW)], do_out.at[z], hs.at[g], hr.at[z], device)

    def heads_own(g):
        return pltpu.make_async_copy(do_ref.at[:, pl.ds(g * GW, GW)], do_out.at[z], hl)

    for g in range(4):
        self_made = (g % 2 == c) & (2 * c + g // 2 == z)

        @pl.when(self_made)
        def _():
            heads_own(g).start()

        @pl.when(jnp.logical_not(self_made))
        def _():
            heads_copy(g).start()

    vec_ref[...] = jnp.zeros_like(vec_ref)
    for n in range(8):
        vec_ref[5 + n : 6 + n] = jnp.sum(sums[n], axis=0, keepdims=True)

    def out_save(t, slot):
        return pltpu.make_async_copy(stage.at[slot], go_out.at[pl.ds(pl.multiple_of(t * D, D), D), :], ssem.at[slot])

    def weights(t, carry):
        slot = t % 2

        @pl.when(t > 1)
        def _():
            out_save(t - 2, slot).wait()

        for m in range(2):
            half = pl.ds(m * CUT, CUT)
            place = pl.ds(pl.multiple_of(t * D + m * CUT, CUT), CUT)
            stage[slot, half, :] = tn(hid[:, place], dy_ref[...]).astype(BF16)
        out_save(t, slot).start()
        return carry

    lax.fori_loop(0, 4, weights, 0)
    saves = []
    for slot, (lhs, rhs, out) in enumerate(((att_ref, dhb, gp_out), (n_ref, du, gi_out))):
        out_save(2 + slot, slot).wait()
        for m in range(2):
            half = pl.ds(m * CUT, CUT)
            stage[slot, half, :] = tn(lhs[:, half], rhs[...]).astype(BF16)
        saves.append(pltpu.make_async_copy(stage.at[slot], out, ssem.at[slot]))
        saves[-1].start()
    reducer.run(None, None, None, None, EARLY - 1)
    fin_saves = [
        pltpu.make_async_copy(reducer.fin.at[k], oi_ref.at[:, pl.ds(k * D, D)], osem.at[k]) for k in range(EARLY)
    ]
    for copy in fin_saves:
        copy.start()
    reducer.drain()
    for g in range(4):
        self_made = (g % 2 == c) & (2 * c + g // 2 == z)

        @pl.when(self_made)
        def _():
            heads_own(g).wait()

        @pl.when(jnp.logical_not(self_made))
        def _():
            heads_copy(g).wait_send()
    for s in range(STREAMS):
        @pl.when((q != c) | (s != z))
        def _():
            remote(do_ref.at[:, pl.ds(0, GW)], do_out.at[s], hs.at[0], hr.at[s], (2 * p + 1 - c, z)).wait_recv()
    for copy in saves + fin_saves:
        copy.wait()


def mlp(w_in, w_out, attended, x, dy, w_proj, params):
    nx, ny, rb = grid_shape()

    def v16(*shape):
        return VM(shape, BF16)

    def vf(*shape):
        return VM(shape, F32)

    scratch = [
        v16(2, D, D), v16(2, D, D), v16(ROWS, D), vf(ROWS, D), vf(ROWS, D), vf(ROWS, D),
        v16(ROWS, 4 * D), v16(ROWS, D), vf(ROWS, D), vf(ROWS, D), v16(ROWS, D), v16(ROWS, D),
        v16(2, D, D), vf(8, 8, D), v16(EARLY, ny, nx, 2, STREAMS, rb, D),
        dma(2, 2), dma(2), dma(4), dma(4), pltpu.SemaphoreType.DMA, dma(EARLY),
    ] + Reducer.scratch(EARLY, nx, ny, rb)
    outs = (
        ((STREAMS, ROWS, GW), BF16), ((D, (4 - EARLY) * D), BF16), ((4 * D, D), BF16), ((D, D), BF16),
        ((rb, EARLY * D), F32),
    )
    near_outs = (((ROWS, D), BF16), ((ROWS, D), F32), ((16, D), F32))
    return comm_call(
        functools.partial(mlp_kernel, nx, ny, rb), "mlp", 1, outs, scratch, (w_in, w_out), (attended, x, dy, w_proj, params), near_outs
    )


def own_meta(lengths, mask):
    frames = jnp.arange(FRAMES, dtype=jnp.int32)
    order = jnp.arange(lengths.shape[0])
    ends = jnp.sum(jnp.where(order[:, None] <= order[None, :], lengths[:, None], 0), axis=0)
    reached = ends[None, :] <= frames[:, None]
    begin = jnp.sum(jnp.where(reached, lengths[None, :], 0), axis=1)
    episode = jnp.sum(reached, axis=1)[:, None] == jnp.arange(lengths.shape[0])[None, :]
    length = jnp.sum(jnp.where(episode, lengths[None, :], 0), axis=1)
    base = jnp.where(length == MOST, 0, jnp.where(length == MIDDLE - MOST, MOST, MIDDLE))
    slot = base + frames - begin
    perm = jnp.sum(jnp.where(slot[:, None] == frames[None, :], frames[:, None], 0), axis=0)
    stream = jnp.arange(STREAMS)[:, None]
    row = jnp.arange(CROWS)[None, :]
    part = FRAMES // STREAMS
    frame = jnp.where(row < part * COND, part * stream + row // COND, FRAMES)
    cslot = jnp.sum(jnp.where(frame[..., None] == frames, slot[None, None, :], 0), axis=-1)
    cslot = jnp.where(frame < FRAMES, cslot, 99).reshape(1, PART)
    hidden = jnp.where(mask == 1, 0.0, NEG).astype(F32)
    bias = jnp.sum(jnp.where((perm[:, None] == frames[None, :])[:, :, None], hidden[None], 0.0), axis=1)
    line = jnp.pad(cslot.astype(F32), ((0, 7), (0, PATCHES - PART)))
    return perm.astype(jnp.int32), slot.astype(jnp.int32), jnp.concatenate([bias, line], axis=0)


def per_device(
    visual, conditioning, d_visual, d_conditioning, episode_frames, patch_mask,
    ln1_gain, ln1_bias, w_qkv, b_qkv, w_proj, b_proj, ln2_gain, ln2_bias, w_in, b_in, w_out, b_out,
):
    d, z = lax.axis_index("dp"), lax.axis_index("stream")
    perm, slot, own = own_meta(episode_frames[0], patch_mask[0])
    x, dy = place_rows(perm, visual, conditioning, d_visual, d_conditioning)
    params = jnp.concatenate(
        [ln1_gain, ln1_bias, b_qkv, b_in, b_proj, ln2_gain, ln2_bias, b_out, jnp.zeros((3 * D,), BF16)]
    ).astype(F32).reshape(16, D)
    tables = tuple(jnp.asarray(t) for t in rope_constants())
    attended, x_all, a, q, k, v, o, meta, *rest = attend_forward(x, w_qkv, own, params, tables)
    grad_heads, grad_w_in, grad_w_out, grad_w_proj, red_in, output, grad_h, vectors = mlp(
        w_in, w_out, attended, x, dy, w_proj, params
    )
    red_out, grad_qkv = attend_backward(grad_w_out, grad_heads, (q, k, v, *rest), o, tables, meta)
    role_grad = jnp.einsum(
        "rd,re->de", a.reshape(STREAMS * ROWS, D), grad_qkv.reshape(STREAMS * ROWS, 3 * GW), preferred_element_type=F32
    )
    grad_x, red_qkv, sums, red_in_last, red_proj = finish_rows(
        grad_qkv, x_all, role_grad.astype(BF16), w_qkv, x, grad_h, grad_w_in, grad_w_proj, vectors, params
    )
    red_in = jnp.concatenate([red_in, red_in_last], axis=1)
    out_visual, grad_visual, out_extra, grad_extra = restore_rows(slot, output, grad_x, conditioning.shape[1])
    owner = d * STREAMS + z
    owners = lax.axis_size("dp") * STREAMS

    def share(start, rows):
        size = rows * D // owners
        return lax.dynamic_slice_in_dim(sums[start : start + rows].reshape(-1), owner * size, size, 0)

    return (
        out_visual.reshape(visual.shape), out_extra.reshape(conditioning.shape),
        grad_visual.reshape(visual.shape), grad_extra.reshape(conditioning.shape),
        share(0, 1), share(1, 1), red_qkv, share(2, 2), share(4, 1), red_proj, share(9, 1), share(10, 1), share(11, 1),
        red_in, share(5, 4), red_out.reshape(-1, D), share(12, 1),
    )


def solution(mesh):
    rows = P("dp", None, "stream", None)
    extra = P("dp", "stream", None, None)
    vector = P(("dp", "stream"))
    matrix = P(("dp", "stream"), None)
    in_specs = (rows, extra, rows, extra, P("dp", None), P("dp", None, None)) + (P(),) * 12
    out_specs = (
        rows, extra, rows, extra, vector, vector, matrix, vector, vector, matrix, vector, vector, vector, matrix,
        vector, matrix, vector,
    )
    return jax.shard_map(per_device, mesh=mesh, in_specs=in_specs, out_specs=out_specs, check_vma=False)
```

```python
import functools
import math

import jax
import jax.numpy as jnp
import numpy as np
from jax import lax
from jax.experimental import pallas as pl
from jax.experimental.pallas import tpu as pltpu
from jax.sharding import PartitionSpec as P

D = 1024
HEADS = 16
HEAD_DIM = 64
GRID = 16
COND = 2
FRAMES = 8
MOST = 5
MIDDLE = 7
STREAMS = 4
GROUP = 4
GW = GROUP * HEAD_DIM
PART = 64
PATCHES = 256
VIS = FRAMES * PART
CROWS = 16
ROWS = VIS + CROWS
WIDE = GROUP * 128
NEG = -1e30
EPS = 1e-06
F32 = jnp.float32
BF16 = jnp.bfloat16
VM = pltpu.VMEM
FULL = pl.BlockSpec(memory_space=pltpu.VMEM)
ANYM = pl.BlockSpec(memory_space=pltpu.HBM)
LIMIT = 60 * 1024 * 1024


def nn(a, b):
    return lax.dot_general(a, b, (((1,), (0,)), ((), ())), preferred_element_type=F32)


def nt(a, b):
    return lax.dot_general(a, b, (((1,), (1,)), ((), ())), preferred_element_type=F32)


def rope_constants():
    pair = np.arange(HEAD_DIM // 2)
    exponent = np.where(pair < 30, (pair % 10) / 10.0, 0.0).astype(np.float32)
    freq = np.exp(-math.log(10000.0) * exponent).astype(np.float32)
    patch = np.arange(PATCHES)
    slot_time = np.array([0, 1, 2, 3, 4, 0, 1, 0])
    is_time = (pair < 10)[None, :]
    place = np.where(
        (pair >= 20)[None, :], (patch % GRID)[:, None], (patch // GRID)[:, None]
    ) * ((pair >= 10) & (pair < 30))[None, :]
    angle_patch = (place * freq[None, :]).astype(np.float32)
    angle_time = (slot_time[:, None] * freq[None, :]).astype(np.float32)
    cos_patch = np.where(is_time, 0.0, np.cos(angle_patch))
    sin_patch = np.where(is_time, 0.0, np.sin(angle_patch))
    cos_time = np.where(is_time, np.cos(angle_time), 0.0)
    sin_time = np.where(is_time, np.sin(angle_time), 0.0)

    def spread(table, signed):
        two = np.repeat(table, 2, axis=1)
        if signed:
            two = two * np.where(np.arange(HEAD_DIM) % 2 == 0, -1.0, 1.0)[None, :]
        return np.tile(two, (1, GROUP)).astype(np.float32)

    return (
        spread(cos_patch, False),
        spread(sin_patch, True),
        spread(cos_time, False),
        spread(sin_time, True),
    )


def swap_pairs(v):
    lane = lax.broadcasted_iota(jnp.int32, v.shape, 1)
    width = v.shape[1]
    return jnp.where(lane % 2 == 0, pltpu.roll(v, width - 1, 1), pltpu.roll(v, 1, 1))


def turn(v, cosine, sine):
    return v * cosine + swap_pairs(v) * sine


def pad_heads(t, extra):
    pieces = []
    for h in range(GROUP):
        pieces += [t[:, h * HEAD_DIM : (h + 1) * HEAD_DIM], extra]
    return jnp.concatenate(pieces, axis=1)


def pad_right(t):
    extra = jnp.zeros((t.shape[0], HEAD_DIM), t.dtype)
    pieces = []
    for h in range(GROUP):
        pieces += [extra, t[:, h * HEAD_DIM : (h + 1) * HEAD_DIM]]
    return jnp.concatenate(pieces, axis=1)


def unpad_heads(t):
    return jnp.concatenate([t[:, h * 128 : h * 128 + HEAD_DIM] for h in range(GROUP)], axis=1)


def head(t, h):
    return t[:, h * 128 : (h + 1) * 128]


def first_slot(i):
    return jnp.where(i < MOST, 0, jnp.where(i < MIDDLE, MOST, MIDDLE))


def cond_tables(cs_col, ct, st):
    cosine = jnp.zeros((PART, GW), F32)
    sine = jnp.zeros((PART, GW), F32)
    for j in range(FRAMES):
        here = cs_col == j
        cosine = cosine + jnp.where(here, ct[j : j + 1, :], 0.0)
        sine = sine + jnp.where(here, st[j : j + 1, :], 0.0)
    lane = lax.broadcasted_iota(jnp.int32, (PART, GW), 1) % HEAD_DIM
    return jnp.where(lane < 20, cosine, 1.0), sine


def read_meta(meta_ref):
    bias_t = jnp.transpose(meta_ref[0:FRAMES])
    cs_row = meta_ref[FRAMES : FRAMES + 1, 0:PART].astype(jnp.int32)
    cs_col = jnp.transpose(meta_ref[FRAMES:, :])[0:PART, 0:1].astype(jnp.int32)
    return cs_col, cs_row, bias_t


def place_kernel(perm, xv_ref, xc_ref, dv_ref, dc_ref, x_ref, dy_ref, sem):
    copies = []
    for n, (rows, out) in enumerate(((xv_ref, x_ref), (dv_ref, dy_ref))):
        for i in range(FRAMES):
            copies.append(pltpu.make_async_copy(rows.at[perm[i]], out.at[pl.ds(i * PART, PART)], sem.at[n, i]))
    for copy in copies:
        copy.start()
    for extra, out in ((xc_ref, x_ref), (dc_ref, dy_ref)):
        out[VIS:, :] = jnp.zeros((CROWS, D), BF16)
        for n in range(extra.shape[0]):
            out[VIS + n * COND : VIS + (n + 1) * COND, :] = extra[n]
    for copy in copies:
        copy.wait()


def place_rows(perm, visual, extra, d_visual, d_extra):
    return pl.pallas_call(
        place_kernel,
        name="place_rows",
        out_shape=(jax.ShapeDtypeStruct((ROWS, D), BF16),) * 2,
        in_specs=[pl.BlockSpec(memory_space=pltpu.SMEM), ANYM, FULL, ANYM, FULL],
        out_specs=(FULL, FULL),
        scratch_shapes=[pltpu.SemaphoreType.DMA((2, FRAMES))],
    )(perm, visual.reshape(FRAMES, PART, D), extra[0], d_visual.reshape(FRAMES, PART, D), d_extra[0])


def restore_kernel(slot, y_ref, g_ref, yo_ref, go_ref, yc_ref, gc_ref, yt, gt, sem):
    copies = []
    for f in range(FRAMES):
        rows = pl.ds(pl.multiple_of(slot[f] * PART, PART), PART)
        copies.append(pltpu.make_async_copy(y_ref.at[rows], yo_ref.at[f], sem.at[0, f]))
        copies.append(pltpu.make_async_copy(g_ref.at[rows], go_ref.at[f], sem.at[1, f]))
    last = pl.ds(VIS, CROWS)
    tails = [
        pltpu.make_async_copy(y_ref.at[last], yt, sem.at[0, FRAMES]),
        pltpu.make_async_copy(g_ref.at[last], gt, sem.at[1, FRAMES]),
    ]
    for copy in copies + tails:
        copy.start()
    for copy in tails:
        copy.wait()
    for n in range(yc_ref.shape[0]):
        yc_ref[n] = yt[n * COND : (n + 1) * COND]
        gc_ref[n] = gt[n * COND : (n + 1) * COND]
    for copy in copies:
        copy.wait()


def restore_rows(slot, y, g, parts):
    shape = (FRAMES, PART, D)
    small = (parts, COND, D)
    return pl.pallas_call(
        restore_kernel,
        name="restore_rows",
        out_shape=(
            jax.ShapeDtypeStruct(shape, BF16), jax.ShapeDtypeStruct(shape, F32),
            jax.ShapeDtypeStruct(small, BF16), jax.ShapeDtypeStruct(small, F32),
        ),
        in_specs=[pl.BlockSpec(memory_space=pltpu.SMEM), ANYM, ANYM],
        out_specs=(FULL,) * 4,
        scratch_shapes=[VM((CROWS, D), BF16), VM((CROWS, D), F32), pltpu.SemaphoreType.DMA((2, FRAMES + 1))],
    )(slot, y, g)


def where_am_i():
    d, z = lax.axis_index("dp"), lax.axis_index("stream")
    return d // 2, d % 2, z // 2, z % 2, z


def greet_column():
    p, c, q, r, z = where_am_i()
    barrier = pltpu.get_barrier_semaphore()
    for core in range(2):
        for chip in range(STREAMS):
            @pl.when((core != c) | (chip != z))
            def _():
                pl.semaphore_signal(
                    barrier, inc=1, device_id=(2 * p + core, chip),
                    device_id_type=pl.DeviceIdType.MESH,
                )
    pl.semaphore_wait(barrier, 2 * STREAMS - 1)


def remote(src, dst, send, recv, device):
    return pltpu.make_async_remote_copy(
        src_ref=src, dst_ref=dst, send_sem=send, recv_sem=recv, device_id=device,
        device_id_type=pl.DeviceIdType.MESH,
    )


def comm_call(kernel, name, ident, outs, scratch, far, close=(), near_outs=()):
    return pl.pallas_call(
        kernel,
        name=name,
        out_shape=tuple(jax.ShapeDtypeStruct(s, t) for s, t in tuple(outs) + tuple(near_outs)),
        in_specs=[ANYM] * len(far) + [FULL] * len(close),
        out_specs=tuple(ANYM for _ in outs) + tuple(FULL for _ in near_outs),
        scratch_shapes=scratch,
        compiler_params=pltpu.CompilerParams(
            collective_id=ident, has_side_effects=True, vmem_limit_bytes=LIMIT
        ),
    )(*far, *close)


def dma(*shape):
    return pltpu.SemaphoreType.DMA(shape)


HALF = VIS // 2


PIECE = HALF // 2


def forward_kernel(
    x_hbm, w_hbm, m_hbm, par_ref, cg_ref, sg_ref, ct_ref, st_ref,
    att_ref, xa_out, a_out, q_out, k_out, v_out, o_out,
    meta_ref, qc_ref, kc_ref, vc_ref, lse_ref, lsec_ref,
    xa, a_ref, q_ref, k_ref, v_ref, o_ref, vt_ref, w, bias_ref,
    isem, whole_s, whole_r, far_s, far_r, pass_s, near_s, near_r, tail_s, tail_r, msem, out_s, out_r, out_l, keep,
):
    p, c, q, r, z = where_am_i()
    group = 2 * r + c
    in_pair = q == c
    away = q != c
    inner = z == 1 + q
    z_one, z_two, z_three = z + 1 - 2 * r, z + 2 - 4 * q, STREAMS - 1 - z
    other = (2 * p + 1 - c, z)
    across = (2 * p + c, z_one)
    loads = []
    for part in range(3):
        cols = pl.ds(pl.multiple_of(part * D + group * GW, GW), GW)
        loads.append(pltpu.make_async_copy(w_hbm.at[:, cols], w.at[part], isem.at[part]))
    for copy in loads:
        copy.start()
    own_rows = pltpu.make_async_copy(x_hbm, xa.at[z], isem.at[3])

    @pl.when(in_pair)
    def _():
        own_rows.start()

    greet_column()
    tail = pl.ds(VIS, CROWS)

    def piece(half, g):
        return pl.ds(pl.multiple_of(half * HALF + g * PIECE, PIECE), PIECE)

    def whole_copy():
        return remote(x_hbm, xa.at[z], whole_s, whole_r, other)

    def far_copy(half, g):
        rows = piece(half, g)
        return remote(x_hbm.at[rows], xa.at[z, rows], far_s.at[half, g], far_r.at[z, g], (2 * p + half, 1 + c))

    def own_pass(g):
        rows = piece(c, g)
        return remote(x_hbm.at[rows], xa.at[z, rows], pass_s.at[z, g], far_r.at[z, g], across)

    def far_pass(s, g):
        rows = piece(c, g)
        return remote(xa.at[s, rows], xa.at[s, rows], pass_s.at[s, g], far_r.at[s, g], across)

    def near_copy(s, g, half):
        rows = piece(half, g)
        return remote(xa.at[s, rows], xa.at[s, rows], near_s.at[s, g], near_r.at[s, g], other)

    def tail_copy(half, side):
        n = half * 2 + side
        return remote(x_hbm.at[tail], xa.at[z, tail], tail_s.at[n], tail_r.at[z], (2 * p + half, 2 * c + side))

    def tail_needed(half, side):
        return jnp.logical_not((2 * c + side == z))

    def meta_copy():
        return remote(m_hbm, meta_ref, msem.at[0], msem.at[1], other)

    def meta_own():
        return pltpu.make_async_copy(m_hbm, meta_ref, msem.at[2])

    @pl.when(in_pair)
    def _():
        meta_own().start()
        meta_copy().start()
        whole_copy().start()
        own_pass(0).start()
        own_pass(1).start()

    for half in range(2):
        @pl.when(away)
        def _():
            far_copy(half, 0).start()

        for side in range(2):
            @pl.when(tail_needed(half, side))
            def _():
                tail_copy(half, side).start()

    def arrive(s, g, relay):
        far_pass(s, g).wait_recv()
        near_copy(s, g, c).start()
        if relay:
            @pl.when(inner)
            def _():
                far_pass(s, g).start()

    gain, shift = par_ref[0:1], par_ref[1:2]
    cut = pl.ds(pl.multiple_of(group * GW, GW), GW)
    lane64 = lax.broadcasted_iota(jnp.int32, (PATCHES, 64), 1)
    one = jnp.where(lane64 == 0, 1.0, 0.0).astype(BF16)

    def project(x, cosine, sine):
        x = x.astype(F32)
        centre = x - jnp.mean(x, axis=1, keepdims=True)
        spread = jnp.mean(centre * centre, axis=1, keepdims=True)
        a = (centre * lax.rsqrt(spread + EPS) * gain + shift).astype(BF16)
        q = turn(nn(a, w[0]) + par_ref[2:3, cut], cosine, sine)
        k = turn(nn(a, w[1]) + par_ref[3:4, cut], cosine, sine)
        v = (nn(a, w[2]) + par_ref[4:5, cut]).astype(BF16)
        return a, (q.astype(BF16).astype(F32) * 0.125).astype(BF16), k.astype(BF16), v

    def unit(t, carry):
        @pl.when(t == 0)
        def _():
            for copy in loads:
                copy.wait()

            @pl.when(in_pair)
            def _():
                own_rows.wait()
                meta_own().wait()

            @pl.when(away)
            def _():
                whole_copy().wait_recv()
                far_pass(z, 0).start()
                far_pass(z, 1).start()
                meta_copy().wait_recv()

            bias_ref[...] = jnp.transpose(meta_ref[0:FRAMES])

        @pl.when(t == 2)
        def _():
            arrive(z_one, 0, False)
            arrive(z_one, 1, False)

            @pl.when(away)
            def _():
                for half in range(2):
                    far_copy(half, 0).wait_send()
                    far_copy(half, 1).start()

            arrive(z_two, 0, True)
            arrive(z_three, 0, True)
            near_copy(z_one, 0, 1 - c).wait_recv()
            near_copy(z_one, 1, 1 - c).wait_recv()

        @pl.when(t == 4)
        def _():
            near_copy(z_two, 0, 1 - c).wait_recv()
            near_copy(z_three, 0, 1 - c).wait_recv()

        @pl.when(t == 6)
        def _():
            arrive(z_two, 1, True)
            arrive(z_three, 1, True)
            near_copy(z_two, 1, 1 - c).wait_recv()
            near_copy(z_three, 1, 1 - c).wait_recv()

        g = jnp.where(t < 4, t % 2, (t - 4) // 2)
        s = jnp.where(t < 2, z, jnp.where(t < 4, z_one, jnp.where(t % 2 == 0, z_two, z_three)))
        x = jnp.concatenate([xa[s, piece(0, g)], xa[s, piece(1, g)]], axis=0)
        place = pl.ds(pl.multiple_of(s * PART, PART), PART)
        cosine, sine, bias = [], [], []
        ids = lax.broadcasted_iota(jnp.int32, (PART, FRAMES), 1)
        for n in range(4):
            i = 2 * g + n % 2 + 4 * (n // 2)
            cosine.append(cg_ref[place] + ct_ref[pl.ds(i, 1), :])
            sine.append(sg_ref[place] + st_ref[pl.ds(i, 1), :])
            bias.append(jnp.sum(jnp.where(ids == i, bias_ref[place], 0.0), axis=1, keepdims=True))
        a, qs, ks, vs = project(x, jnp.concatenate(cosine, axis=0), jnp.concatenate(sine, axis=0))
        a_ref[s, piece(0, g)] = a[:PIECE]
        a_ref[s, piece(1, g)] = a[PIECE:]
        bias = jnp.concatenate(bias, axis=0)
        qs = pad_heads(qs, one)
        ks = pad_heads(ks, jnp.where(lane64 == 0, bias, 0.0).astype(BF16))
        vs = pad_right(vs)
        for n in range(4):
            i = 2 * g + n % 2 + 4 * (n // 2)
            rows = slice(n * PART, (n + 1) * PART)
            q_ref[i, place] = qs[rows]
            k_ref[i, place] = ks[rows]
            v_ref[i, place] = vs[rows]
        return carry

    lax.fori_loop(0, 8, unit, 0)

    for s in range(STREAMS):
        @pl.when(s != z)
        def _():
            remote(x_hbm.at[tail], xa.at[s, tail], tail_s.at[0], tail_r.at[s], other).wait_recv()
    cs_col, cs_row, _ = read_meta(meta_ref)
    a, qs, ks, vs = project(xa[:, VIS:, :].reshape(PART, D), *cond_tables(cs_col, ct_ref[...], st_ref[...]))
    a_ref[:, VIS:, :] = a.reshape(STREAMS, CROWS, D)
    qc_ref[...] = pad_heads(qs, one[:PART])
    kc_ref[...] = pad_heads(ks, jnp.zeros((PART, 64), BF16))
    vc_ref[...] = pad_right(vs)
    vct = jnp.transpose(vs.astype(F32)).astype(BF16)
    saves = [(xa, xa_out), (a_ref, a_out), (q_ref, q_out), (k_ref, k_out), (v_ref, v_out)]
    saves = [pltpu.make_async_copy(src, dst, keep.at[n]) for n, (src, dst) in enumerate(saves)]
    for copy in saves:
        copy.start()

    def out_rows(i):
        return pl.ds(pl.multiple_of(i * PART, PART), PART)

    def out_copy(s, n, rows):
        place = pl.ds(pl.multiple_of(group * GW, GW), GW)
        return remote(o_ref.at[s, rows], att_ref.at[rows, place], out_s.at[s, n], out_r.at[group, n], (2 * p + q, s))

    def out_own(s, n, rows):
        place = pl.ds(pl.multiple_of(group * GW, GW), GW)
        return pltpu.make_async_copy(o_ref.at[s, rows], att_ref.at[rows, place], out_l.at[n])

    def send_out(n, rows):
        for s in range(STREAMS):
            mine = in_pair & (s == z)

            @pl.when(mine)
            def _():
                out_own(s, n, rows).start()

            @pl.when(jnp.logical_not(mine))
            def _():
                out_copy(s, n, rows).start()

    def slot(i, carry):
        vt_ref[i] = jnp.transpose(unpad_right(v_ref[i].astype(F32))).astype(BF16)
        low = first_slot(i)
        near = (cs_col >= low) & (cs_col <= i)
        tops, totals, blends = [], [], []
        for h in range(GROUP):
            s = jnp.where(near, nt(head(kc_ref, h), q_ref[i, :, h * 128 : (h + 1) * 128]), NEG)
            top = jnp.max(s, axis=0, keepdims=True)
            pt = jnp.exp(s - top)
            tops.append(top)
            totals.append(jnp.sum(pt, axis=0, keepdims=True))
            blends.append(nn(vct[h * HEAD_DIM : (h + 1) * HEAD_DIM], pt.astype(BF16)))

        def step(j, state):
            tops, totals, blends = state
            cols = [slice(h * 128, (h + 1) * 128) for h in range(GROUP)]
            scores = [nt(k_ref[j, :, w], q_ref[i, :, w]) for w in cols]
            peaks = [jnp.maximum(tops[h], jnp.max(scores[h], axis=0, keepdims=True)) for h in range(GROUP)]
            pts = [jnp.exp(scores[h] - peaks[h]) for h in range(GROUP)]
            stay = [jnp.exp(tops[h] - peaks[h]) for h in range(GROUP)]
            sums = [totals[h] * stay[h] + jnp.sum(pts[h], axis=0, keepdims=True) for h in range(GROUP)]
            lows = [pt.astype(BF16) for pt in pts]
            more = [nn(vt_ref[j, h * HEAD_DIM : (h + 1) * HEAD_DIM, :], lows[h]) for h in range(GROUP)]
            return peaks, sums, [blends[h] * stay[h] + more[h] for h in range(GROUP)]

        tops, totals, blends = lax.fori_loop(low, i + 1, step, (tops, totals, blends))
        o = jnp.transpose(jnp.concatenate([blends[h] / totals[h] for h in range(GROUP)], axis=0))
        o_ref[:, out_rows(i), :] = o.astype(BF16).reshape(STREAMS, PART, GW)
        lse_ref[i] = jnp.concatenate([tops[h] + jnp.log(totals[h]) for h in range(GROUP)] * 2, axis=0)
        send_out(i, out_rows(i))
        return carry

    lo_col = first_slot(cs_col)

    def cond_queries():
        near = (cs_row >= lo_col) & (cs_row <= cs_col)
        tops, totals, blends = [], [], []
        for h in range(GROUP):
            s = jnp.where(near, nt(head(qc_ref, h), head(kc_ref, h)), NEG)
            top = jnp.max(s, axis=1, keepdims=True)
            pt = jnp.exp(s - top)
            tops.append(top)
            totals.append(jnp.sum(pt, axis=1, keepdims=True))
            blends.append(nn(pt.astype(BF16), head(vc_ref, h)))

        def cond_step(j, state):
            tops, totals, blends = state
            near = (lo_col <= j) & (cs_col >= j)
            new = ([], [], [])
            for h in range(GROUP):
                s = nt(head(qc_ref, h), k_ref[j, :, h * 128 : (h + 1) * 128])
                s = jnp.where(near, s, NEG)
                top = jnp.maximum(tops[h], jnp.max(s, axis=1, keepdims=True))
                pt = jnp.exp(s - top)
                stay = jnp.exp(tops[h] - top)
                new[0].append(top)
                new[1].append(totals[h] * stay + jnp.sum(pt, axis=1, keepdims=True))
                new[2].append(blends[h] * stay + nn(pt.astype(BF16), v_ref[j, :, h * 128 : (h + 1) * 128]))
            return new

        tops, totals, blends = lax.fori_loop(0, FRAMES, cond_step, (tops, totals, blends))
        o = jnp.concatenate([(blends[h] / totals[h])[:, HEAD_DIM:] for h in range(GROUP)], axis=1)
        o_ref[:, VIS:, :] = o.astype(BF16).reshape(STREAMS, CROWS, GW)
        lane = lax.broadcasted_iota(jnp.int32, (PART, 128), 1)
        lsec = jnp.zeros((PART, 128), F32)
        for h in range(GROUP):
            lsec = lsec + jnp.where(lane == h, tops[h] + jnp.log(totals[h]), 0.0)
        lsec_ref[...] = lsec
        send_out(FRAMES, tail)

    cond_queries()
    lax.fori_loop(0, FRAMES, slot, 0)
    last = pltpu.make_async_copy(o_ref, o_out, keep.at[5])
    last.start()

    def settle(n, rows):
        for s in range(STREAMS):
            mine = in_pair & (s == z)

            @pl.when(mine)
            def _():
                out_own(s, n, rows).wait()

            @pl.when(jnp.logical_not(mine))
            def _():
                out_copy(s, n, rows).wait_send()
        for g in range(4):
            @pl.when((g % 2 != c) | (2 * c + g // 2 != z))
            def _():
                place = pl.ds(g * GW, GW)
                remote(o_ref.at[0, rows], att_ref.at[rows, place], out_s.at[0, n], out_r.at[g, n], other).wait_recv()

    def settle_slot(i, carry):
        settle(i, out_rows(i))
        return carry

    lax.fori_loop(0, FRAMES, settle_slot, 0)
    settle(FRAMES, tail)

    @pl.when(in_pair)
    def _():
        meta_copy().wait_send()
        whole_copy().wait_send()
        own_pass(0).wait_send()
        own_pass(1).wait_send()

    @pl.when(away)
    def _():
        far_pass(z, 0).wait_send()
        far_pass(z, 1).wait_send()
        far_copy(0, 1).wait_send()
        far_copy(1, 1).wait_send()

    for half in range(2):
        for side in range(2):
            @pl.when(tail_needed(half, side))
            def _():
                tail_copy(half, side).wait_send()
    for g in range(2):
        for s in (z_one, z_two, z_three):
            near_copy(s, g, c).wait_send()
        for s in (z_two, z_three):
            @pl.when(inner)
            def _():
                far_pass(s, g).wait_send()
    for copy in saves:
        copy.wait()
    last.wait()


def attend_forward(x, w_qkv, meta, params, tables):
    def v16(*shape):
        return VM(shape, BF16)

    wide = (FRAMES, PATCHES, WIDE)
    rows = (STREAMS, ROWS, D)
    outs = (
        ((ROWS, D), BF16), (rows, BF16), (rows, BF16), (wide, BF16), (wide, BF16), (wide, BF16),
        ((STREAMS, ROWS, GW), BF16),
    )
    near_outs = (
        (meta.shape, F32), ((PART, WIDE), BF16), ((PART, WIDE), BF16), ((PART, WIDE), BF16),
        ((FRAMES, 8, PATCHES), F32), ((PART, 128), F32),
    )
    scratch = [
        v16(*rows), v16(*rows), v16(*wide), v16(*wide), v16(*wide), v16(STREAMS, ROWS, GW), v16(FRAMES, GW, PATCHES),
        v16(3, D, GW), VM((PATCHES, FRAMES), F32),
        dma(4), pltpu.SemaphoreType.DMA, pltpu.SemaphoreType.DMA, dma(2, 2), dma(4, 2), dma(4, 2), dma(4, 2), dma(4, 2),
        dma(4), dma(4), dma(3), dma(4, 9), dma(4, 9), dma(9), dma(6),
    ]
    return comm_call(
        forward_kernel, "attend_forward", 0, outs, scratch, (x, w_qkv, meta), (params,) + tables, near_outs
    )
CHUNKS = 9
EARLY = 3
LATE = 4
LAST = CHUNKS - EARLY - LATE
CUT = D // 2
QCUT = 3 * GW // 2


def add_up(*terms):
    total = terms[0].astype(F32)
    for t in terms[1:]:
        total = total + t.astype(F32)
    return total


def grid_shape():
    cores = lax.axis_size("dp") // 2
    nx = 1 << ((cores.bit_length() - 1) // 2)
    return nx, cores // nx, D // (cores * 2 * STREAMS)


class Place:
    def __init__(self, nx, ny):
        d, z = lax.axis_index("dp"), lax.axis_index("stream")
        self.nx, self.ny, self.d, self.z = nx, ny, d, z
        self.p, self.c, self.hi, self.lo = d // 2, d % 2, z // 2, z % 2
        self.x, self.y = self.p % nx, self.p // nx
        self.near = (d + 1 - 2 * self.c, z)
        self.z_one = (d, z + 1 - 2 * self.lo)
        self.z_two = (d, z + 2 - 4 * self.hi)
        self.slant = (d + 1 - 2 * self.c, z + 1 - 2 * self.lo)

    def along_x(self, n):
        return lax.rem(self.x + n, self.nx)

    def along_y(self, n):
        return lax.rem(self.y + n, self.ny)

    def x_device(self, n):
        return ((self.y * self.nx + self.along_x(n)) * 2 + self.c, self.z)

    def y_device(self, n):
        return ((self.along_y(n) * self.nx + self.x) * 2 + self.c, self.z)

    def greet(self):
        barrier = pltpu.get_barrier_semaphore()
        p, c, z, nx, ny = self.p, self.c, self.z, self.nx, self.ny
        for core in range(2):
            for chip in range(STREAMS):
                @pl.when((core != c) | (chip != z))
                def _():
                    pl.semaphore_signal(
                        barrier, inc=1, device_id=(2 * p + core, chip), device_id_type=pl.DeviceIdType.MESH
                    )
        others = [self.x_device(n) for n in range(1, nx)] + [self.y_device(n) for n in range(1, ny)]
        for device in others:
            pl.semaphore_signal(barrier, inc=1, device_id=device, device_id_type=pl.DeviceIdType.MESH)
        pl.semaphore_wait(barrier, 2 * STREAMS - 1 + len(others))


class Reducer:
    def __init__(self, at, rb, count, sources, refs, ahead=True):
        self.at, self.rb, self.count, self.sources, self.ahead = at, rb, count, sources, ahead
        (self.mine, self.rd, self.r2a, self.r2b, self.r3a, self.r3b, self.s3, self.r4, self.s4, self.r5, self.fin,
         self.lsem, self.ds, self.dr, self.as2, self.ar2, self.bs2, self.br2, self.as3, self.ar3, self.bs3, self.br3,
         self.s4s, self.s4r, self.s5s, self.s5r) = refs

    @staticmethod
    def scratch(n, nx, ny, rb):
        def v(*shape):
            return VM(shape, BF16)

        return [
            v(n, ny, nx, STREAMS, rb, D), v(n, ny, nx, STREAMS, rb, D),
            v(n, nx - 1, ny, STREAMS, rb, CUT), v(n, ny - 1, nx, STREAMS, rb, CUT),
            v(n, ny - 1, STREAMS, rb, CUT), v(n, nx - 1, STREAMS, rb, CUT),
            v(n, 2, 2, rb, D), v(n, 2, rb, D), v(n, 2, rb, D), v(n, rb, D), VM((n, rb, D), F32),
            dma(n), dma(n), dma(n),
            dma(n, nx - 1), dma(n, nx - 1), dma(n, ny - 1), dma(n, ny - 1),
            dma(n, ny - 1), dma(n, ny - 1), dma(n, nx - 1), dma(n, nx - 1),
            dma(n), dma(n), dma(n), dma(n),
        ]

    def issue(self, k):
        c = self.at.c
        begin = 0
        for size, get in self.sources:
            start = begin
            begin += size

            @pl.when((k >= start) & (k < start + size))
            def _():
                t = k - start
                remote(get(t, 1 - c), self.rd.at[k], self.ds.at[k], self.dr.at[k], self.at.near).start()
                pltpu.make_async_copy(get(t, c), self.mine.at[k], self.lsem.at[k]).start()

    def core(self, k):
        return remote(self.rd.at[k], self.rd.at[k], self.ds.at[k], self.dr.at[k], self.at.near)

    def a2(self, k, n):
        at = self.at
        src = self.mine.at[k, :, at.along_x(n), :, :, pl.ds(0, CUT)]
        return remote(src, self.r2a.at[k, n - 1], self.as2.at[k, n - 1], self.ar2.at[k, n - 1], at.x_device(n))

    def b2(self, k, n):
        at = self.at
        src = self.mine.at[k, at.along_y(n), :, :, :, pl.ds(CUT, CUT)]
        return remote(src, self.r2b.at[k, n - 1], self.bs2.at[k, n - 1], self.br2.at[k, n - 1], at.y_device(n))

    def a3(self, k, n):
        at = self.at
        src = self.r2a.at[k, 0, at.along_y(n)]
        return remote(src, self.r3a.at[k, n - 1], self.as3.at[k, n - 1], self.ar3.at[k, n - 1], at.y_device(n))

    def b3(self, k, n):
        at = self.at
        src = self.r2b.at[k, 0, at.along_x(n)]
        return remote(src, self.r3b.at[k, n - 1], self.bs3.at[k, n - 1], self.br3.at[k, n - 1], at.x_device(n))

    def c4(self, k):
        return remote(self.s3.at[k, :, 1 - self.at.lo], self.r4.at[k], self.s4s.at[k], self.s4r.at[k], self.at.z_one)

    def c5(self, k):
        return remote(self.s4.at[k, 1 - self.at.hi], self.r5.at[k], self.s5s.at[k], self.s5r.at[k], self.at.z_two)

    def tick(self, t, carry=0):
        self.run(t, t - 2, t - 4, t - 5, t - 6)
        return carry

    def run(self, *turns):
        at, rb, count = self.at, self.rb, self.count
        nx, ny, x, y = at.nx, at.ny, at.x, at.y

        def on(turn, body):
            k = turns[turn]
            if k is not None:
                pl.when((k >= 0) & (k < count))(lambda: body(k))

        def first(k):
            pltpu.make_async_copy(self.rd.at[k], self.mine.at[k], self.lsem.at[k]).wait()
            self.core(k).wait_recv()
            if self.ahead:
                self.issue(k + 2)
            for b in range(ny):
                for e in range(nx):
                    self.mine[k, b, e] = add_up(self.mine[k, b, e], self.rd[k, b, e]).astype(BF16)
            for n in range(1, nx):
                self.a2(k, n).start()
            for n in range(1, ny):
                self.b2(k, n).start()

        def second(k):
            for n in range(1, nx):
                self.a2(k, n).wait_recv()
            for b in range(ny):
                self.r2a[k, 0, b] = add_up(
                    self.mine[k, b, x, :, :, 0:CUT], *[self.r2a[k, n, b] for n in range(nx - 1)]
                ).astype(BF16)
            for n in range(1, ny):
                self.a3(k, n).start()
            for n in range(1, ny):
                self.b2(k, n).wait_recv()
            for b in range(nx):
                self.r2b[k, 0, b] = add_up(
                    self.mine[k, y, b, :, :, CUT:], *[self.r2b[k, n, b] for n in range(ny - 1)]
                ).astype(BF16)
            for n in range(1, nx):
                self.b3(k, n).start()

        def third(k):
            for n in range(1, ny):
                self.a3(k, n).wait_recv()
            for n in range(1, nx):
                self.b3(k, n).wait_recv()
            left = add_up(self.r2a[k, 0, y], *[self.r3a[k, n] for n in range(ny - 1)]).astype(BF16)
            right = add_up(self.r2b[k, 0, x], *[self.r3b[k, n] for n in range(nx - 1)]).astype(BF16)
            self.s3[k, :, :, :, 0:CUT] = left.reshape(2, 2, rb, CUT)
            self.s3[k, :, :, :, CUT:] = right.reshape(2, 2, rb, CUT)
            self.c4(k).start()

        def fourth(k):
            self.c4(k).wait_recv()
            self.s4[k] = add_up(self.s3[k, :, at.lo], self.r4[k]).astype(BF16)
            self.c5(k).start()

        def fifth(k):
            self.c5(k).wait_recv()
            self.fin[k] = add_up(self.s4[k, at.hi], self.r5[k])

        for turn, body in enumerate((first, second, third, fourth, fifth)):
            on(turn, body)

    def start(self):
        self.issue(0)
        self.issue(1)

    def drain(self):
        def one(k, carry):
            self.core(k).wait_send()
            for n in range(1, self.at.nx):
                self.a2(k, n).wait_send()
                self.b3(k, n).wait_send()
            for n in range(1, self.at.ny):
                self.b2(k, n).wait_send()
                self.a3(k, n).wait_send()
            self.c4(k).wait_send()
            self.c5(k).wait_send()
            return carry

        lax.fori_loop(0, self.count, one, 0)


def backward_kernel(
    nx, ny, rb,
    go_ref, d_ref, q_hbm, k_hbm, v_hbm, o_hbm,
    qc_ref, kc_ref, vc_ref, lse_ref, lsec_ref, cg_ref, sg_ref, ct_ref, st_ref, meta_ref,
    oo_ref, g_out,
    q_ref, k_ref, v_ref, o_ref, do_ref, g_ref, acc, accc, kt_ref, right, dqc,
    osem, isem, *refs,
):
    at = Place(nx, ny)
    p, c, q, r, z = at.p, at.c, at.hi, at.lo, at.z
    at.greet()
    reducer = Reducer(
        at, rb, LATE,
        (
            (LATE, lambda t, core: go_ref.at[:, :, core, :, t]),
        ),
        refs,
    )

    reducer.start()
    loads = [(q_hbm, q_ref), (k_hbm, k_ref), (v_hbm, v_ref), (o_hbm, o_ref), (d_ref, do_ref)]
    loads = [pltpu.make_async_copy(src, dst, isem.at[n]) for n, (src, dst) in enumerate(loads)]
    for copy in loads:
        copy.start()

    reducer.tick(0)
    cs_col, cs_row, _ = read_meta(meta_ref)
    acc[...] = jnp.zeros_like(acc)
    accc[...] = jnp.zeros_like(accc)
    kct = jnp.transpose(unpad_heads(kc_ref[...].astype(F32))).astype(BF16)
    for copy in loads:
        copy.wait()
    doc = do_ref[:, VIS:, :].reshape(PART, GW)
    oc = o_ref[:, VIS:, :].reshape(PART, GW)
    docp = pad_right(doc)
    lane = lax.broadcasted_iota(jnp.int32, (PART, WIDE), 1) % 128
    qcl = jnp.where(lane < HEAD_DIM, qc_ref[...].astype(F32), 0.0).astype(BF16)
    prod = doc.astype(F32) * oc.astype(F32)
    lo_col = first_slot(cs_col)
    near = (cs_row >= lo_col) & (cs_row <= cs_col)
    deltas = [
        jnp.sum(prod[:, h * HEAD_DIM : (h + 1) * HEAD_DIM], axis=1, keepdims=True) for h in range(GROUP)
    ]
    lses = [lsec_ref[:, h : h + 1] for h in range(GROUP)]
    dqs = []
    for h in range(GROUP):
        cols = slice(h * 128, (h + 1) * 128)
        s = jnp.where(near, nt(qc_ref[:, cols], kc_ref[:, cols]), NEG)
        pt = jnp.exp(s - lses[h])
        dst = pt * (nt(docp[:, cols], vc_ref[:, cols]) - deltas[h])
        accc[:, cols] += nn(jnp.transpose(pt).astype(BF16), docp[:, cols]) + nn(
            jnp.transpose(dst).astype(BF16), qcl[:, cols]
        )
        dqs.append(nn(dst.astype(BF16), kc_ref[:, cols]))

    def cond_step(j, dqs):
        near = (lo_col <= j) & (cs_col >= j)
        new = []
        for h in range(GROUP):
            cols = slice(h * 128, (h + 1) * 128)
            s = jnp.where(near, nt(qc_ref[:, cols], k_ref[j, :, cols]), NEG)
            pt = jnp.exp(s - lses[h])
            dst = pt * (nt(docp[:, cols], v_ref[j, :, cols]) - deltas[h])
            acc[j, :, cols] += nn(jnp.transpose(pt).astype(BF16), docp[:, cols]) + nn(
                jnp.transpose(dst).astype(BF16), qcl[:, cols]
            )
            new.append(dqs[h] + nn(dst.astype(BF16), k_ref[j, :, cols]))
        return new

    dqs = lax.fori_loop(0, FRAMES, cond_step, dqs)
    dqc[...] = jnp.concatenate([t[:, :HEAD_DIM] for t in dqs], axis=1) * 0.125

    def slot(i):
        start = pl.multiple_of(i * PART, PART)
        do = do_ref[:, pl.ds(start, PART), :].reshape(PATCHES, GW)
        o = o_ref[:, pl.ds(start, PART), :].reshape(PATCHES, GW)
        prod = jnp.transpose(do.astype(F32) * o.astype(F32))
        deltas = [
            jnp.sum(prod[h * HEAD_DIM : (h + 1) * HEAD_DIM], axis=0, keepdims=True) for h in range(GROUP)
        ]
        right[0:PATCHES] = pad_right(do)
        lane = lax.broadcasted_iota(jnp.int32, (PATCHES, WIDE), 1) % 128
        right[PATCHES:] = jnp.where(lane < HEAD_DIM, q_ref[i].astype(F32), 0.0).astype(BF16)
        kt_ref[i] = jnp.transpose(unpad_heads(k_ref[i].astype(F32))).astype(BF16)
        low = first_slot(i)
        near = (cs_col >= low) & (cs_col <= i)
        dqs = []
        for h in range(GROUP):
            cols = slice(h * 128, (h + 1) * 128)
            s = jnp.where(near, nt(kc_ref[:, cols], q_ref[i, :, cols]), NEG)
            pt = jnp.exp(s - lse_ref[i, h : h + 1, :])
            dst = (pt * (nt(vc_ref[:, cols], right[0:PATCHES, cols]) - deltas[h])).astype(BF16)
            accc[:, cols] += nn(jnp.concatenate([pt.astype(BF16), dst], axis=1), right[:, cols])
            dqs.append(nn(kct[h * HEAD_DIM : (h + 1) * HEAD_DIM], dst))

        def step(j, dqs):
            cols = [slice(h * 128, (h + 1) * 128) for h in range(GROUP)]
            scores = [nt(k_ref[j, :, w], q_ref[i, :, w]) for w in cols]
            grads = [nt(v_ref[j, :, w], right[0:PATCHES, w]) for w in cols]
            pts = [jnp.exp(scores[h] - lse_ref[i, h : h + 1, :]) for h in range(GROUP)]
            dsts = [(pts[h] * (grads[h] - deltas[h])).astype(BF16) for h in range(GROUP)]
            both = [jnp.concatenate([pts[h].astype(BF16), dsts[h]], axis=1) for h in range(GROUP)]
            for h in range(GROUP):
                acc[j, :, cols[h]] += nn(both[h], right[:, cols[h]])
            return [dqs[h] + nn(kt_ref[j, h * HEAD_DIM : (h + 1) * HEAD_DIM, :], dsts[h]) for h in range(GROUP)]

        dqs = lax.fori_loop(low, i + 1, step, dqs)
        dq = jnp.transpose(jnp.concatenate(dqs, axis=0)) * 0.125
        cosine = cg_ref[...] + ct_ref[pl.ds(i, 1), :]
        sine = sg_ref[...] + st_ref[pl.ds(i, 1), :]
        dq = turn(dq, cosine, -sine).astype(BF16).reshape(STREAMS, PART, GW)
        g_ref[:, pl.ds(start, PART), 0:GW] = dq

    def sweep(i, carry):
        slot(i)
        reducer.tick(i + 1)
        return carry

    lax.fori_loop(0, FRAMES, sweep, 0)

    cosine, sine = cond_tables(cs_col, ct_ref[...], st_ref[...])
    valid = cs_col < FRAMES
    dq = dqc[...]
    both = accc[...]
    parts = (turn(dq, cosine, -sine), turn(unpad_heads(both), cosine, -sine), unpad_right(both))
    for part, t in enumerate(parts):
        t = jnp.where(valid, t, 0.0).astype(BF16)
        g_ref[:, VIS:, part * GW : (part + 1) * GW] = t.reshape(STREAMS, CROWS, GW)

    def finish(i, carry):
        start = pl.multiple_of(i * PART, PART)
        cosine = cg_ref[...] + ct_ref[pl.ds(i, 1), :]
        sine = sg_ref[...] + st_ref[pl.ds(i, 1), :]
        both = acc[i]
        dk = turn(unpad_heads(both), cosine, -sine)
        g_ref[:, pl.ds(start, PART), GW : 2 * GW] = dk.astype(BF16).reshape(STREAMS, PART, GW)
        g_ref[:, pl.ds(start, PART), 2 * GW :] = unpad_right(both).astype(BF16).reshape(STREAMS, PART, GW)
        return carry

    lax.fori_loop(0, FRAMES, finish, 0)
    save = pltpu.make_async_copy(g_ref, g_out, isem.at[5])
    save.start()
    reducer.tick(LATE + 5)
    fin = reducer.fin
    outs = [pltpu.make_async_copy(fin.at[k], oo_ref.at[k], osem.at[k]) for k in range(4)]
    for copy in outs:
        copy.start()

    reducer.drain()
    save.wait()
    for copy in outs:
        copy.wait()


def unpad_right(t):
    return jnp.concatenate([t[:, h * 128 + HEAD_DIM : (h + 1) * 128] for h in range(GROUP)], axis=1)


def attend_backward(g_out, grad_o, saved, o, tables, meta):
    nx, ny, rb = grid_shape()
    q, k, v, *rest = saved

    def v16(*shape):
        return VM(shape, BF16)

    scratch = [
        v16(*q.shape), v16(*k.shape), v16(*v.shape), v16(*o.shape), v16(*o.shape), v16(STREAMS, ROWS, 3 * GW),
        VM((FRAMES, PATCHES, WIDE), F32), VM((PART, WIDE), F32), v16(FRAMES, GW, PATCHES), v16(2 * PATCHES, WIDE),
        VM((PART, GW), F32),
        dma(LATE), dma(6),
    ] + Reducer.scratch(LATE, nx, ny, rb)
    outs = (((4, rb, D), F32), ((STREAMS, ROWS, 3 * GW), BF16))
    ops = (g_out.reshape(ny, nx, 2, STREAMS, 4, rb, D), grad_o, q, k, v, o)
    return comm_call(
        functools.partial(backward_kernel, nx, ny, rb), "attend_backward", 3, outs, scratch, ops,
        tuple(rest) + tables + (meta,),
    )


def finish_kernel(
    nx, ny, rb,
    f_hbm, xa_hbm, gq_ref, w_hbm, x_hbm, h_hbm, gi_ref, gp_ref, ri_hbm, v_ref, gain_ref,
    gx_ref, oq_ref, ov_ref, oi_ref, op_ref,
    f, xa, w, x_own, h_own, big, near_in, near_out, own, land, tail, tail_out, total,
    q1, rq1a, rq1b, sq1a, sq1b, rq2a, rq2b, sq2, rq3, sq3, vm, vd, vx, vy, vz1, vz2, hold,
    isem, dsend, drecv, send, recv, csend, crecv, lsem,
    qs1a, qr1a, qs1b, qr1b, qs2a, qr2a, qs2b, qr2b, qs3, qr3, qs4, qr4, vs, vr, vsx, vrx, vsy, vry, relay, rsend, rrecv, cols_sum, osem, kept, ksem,
    *refs,
):
    at = Place(nx, ny)
    p, c, q, r, z, x, y, hi, lo = at.p, at.c, at.hi, at.lo, at.z, at.x, at.y, at.hi, at.lo
    group = 2 * r + c
    in_pair, inner = q == c, z == 1 + q
    reducer = Reducer(
        at, rb, LAST,
        ((LAST - 1, lambda t, core: gi_ref.at[:, :, core]), (1, lambda t, core: gp_ref.at[:, :, core])),
        refs, ahead=False,
    )
    loads = []
    for part in range(3):
        cols = pl.ds(pl.multiple_of(part * D + group * GW, GW), GW)
        loads.append(pltpu.make_async_copy(w_hbm.at[:, cols], w.at[:, pl.ds(part * GW, GW)], isem.at[part]))
    loads.append(pltpu.make_async_copy(f_hbm, f, isem.at[3]))
    loads.append(pltpu.make_async_copy(xa_hbm, xa, isem.at[4]))
    late = [
        pltpu.make_async_copy(gq_ref, q1, isem.at[5]),
        pltpu.make_async_copy(x_hbm, x_own, isem.at[6]),
        pltpu.make_async_copy(h_hbm, h_own, isem.at[7]),
    ]
    keep = pltpu.make_async_copy(ri_hbm, kept, ksem.at[0])
    for copy in loads + late + [keep]:
        copy.start()
    at.greet()
    rows = pl.ds(pl.multiple_of(c * HALF, HALF), HALF)
    rest = pl.ds(pl.multiple_of((1 - c) * HALF, HALF), HALF)
    last = pl.ds(VIS, CROWS)
    qa, qb = pl.ds(0, QCUT), pl.ds(QCUT, QCUT)

    def q1a(n):
        return remote(q1.at[:, at.along_x(n), :, :, qa], rq1a.at[n - 1], qs1a.at[n - 1], qr1a.at[n - 1], at.x_device(n))

    def q1b(n):
        return remote(q1.at[at.along_y(n), :, :, :, qb], rq1b.at[n - 1], qs1b.at[n - 1], qr1b.at[n - 1], at.y_device(n))

    def q2a(n):
        return remote(sq1a.at[at.along_y(n)], rq2a.at[n - 1], qs2a.at[n - 1], qr2a.at[n - 1], at.y_device(n))

    def q2b(n):
        return remote(sq1b.at[at.along_x(n)], rq2b.at[n - 1], qs2b.at[n - 1], qr2b.at[n - 1], at.x_device(n))

    def q3():
        return remote(sq2.at[:, 1 - hi], rq3, qs3, qr3, at.z_two)

    mates = [(at.near, 1, 0), (at.z_one, 0, 1), (at.slant, 1, 1)]

    def q4(n, part):
        device, core, side = mates[n]
        to_core = c + core - 2 * c * core
        to_side = lo + side - 2 * lo * side
        place = pl.ds(pl.multiple_of(part * D + group * GW, GW), GW)
        return remote(
            sq3.at[to_core, to_side, :, pl.ds(part * GW, GW)], oq_ref.at[:, place],
            qs4.at[n, part], qr4.at[n, part], device,
        )

    def q4_own(part):
        place = pl.ds(pl.multiple_of(part * D + group * GW, GW), GW)
        return pltpu.make_async_copy(sq3.at[c, lo, :, pl.ds(part * GW, GW)], oq_ref.at[:, place], lsem.at[2 + part])

    def v_core():
        return remote(vm.at[0], vd, vs.at[0], vr.at[0], at.near)

    def v_x(n):
        return remote(vm.at[1], vx.at[n - 1], vsx.at[n - 1], vrx.at[n - 1], at.x_device(n))

    def v_y(n):
        return remote(vm.at[2], vy.at[n - 1], vsy.at[n - 1], vry.at[n - 1], at.y_device(n))

    def v_z1():
        return remote(vm.at[3], vz1, vs.at[1], vr.at[1], at.z_one)

    def v_z2():
        return remote(vm.at[4], vz2, vs.at[2], vr.at[2], at.z_two)

    def near_copy(s):
        return remote(near_out.at[s], near_in.at[s], dsend.at[s], drecv.at[s], at.near)

    def row_copy(s):
        mark = jnp.where(s // 2 == q, r, 0)
        return remote(own.at[s], land.at[mark, rows], send.at[s], recv.at[mark, c], (2 * p + q, s))

    def row_own(s):
        return pltpu.make_async_copy(own.at[s], land.at[r, rows], lsem.at[0])

    def relay_copy(n, s):
        return remote(own.at[s], relay.at[n], rsend.at[n], rrecv.at[n], at.z_one)

    def tail_copy(s):
        return remote(tail_out.at[s], tail.at[group], csend.at[s], crecv.at[group], (2 * p + q, s))

    def tail_own(s):
        return pltpu.make_async_copy(tail_out.at[s], tail.at[group], lsem.at[1])

    def mine(s):
        return (q == c) & (s == z)

    def go(s, far, near):
        @pl.when(mine(s))
        def _():
            near(s)

        @pl.when(jnp.logical_not(mine(s)))
        def _():
            far(s)

    for k in range(LAST):
        reducer.issue(jnp.int32(k))
    late[0].wait()
    for n in range(1, nx):
        q1a(n).start()
    for n in range(1, ny):
        q1b(n).start()
    for copy in loads:
        copy.wait()
    hold[...] = jnp.zeros_like(hold)
    cols_sum[...] = jnp.zeros_like(cols_sum)

    far = (STREAMS - 1 - z, z + 2 - 4 * hi, z + 1 - 2 * lo, z)

    @pl.when(jnp.logical_not(in_pair))
    def _():
        land[1] = jnp.zeros_like(land[1])

    def combine(s):
        near_copy(s).wait_recv()
        for t in range(HALF // 64):
            part = pl.ds(t * 64, 64)
            own[s, part] = add_up(near_in[s, part], own[s, part]).astype(BF16)

    def pass_on(n):
        s = far[n]
        combine(s)
        if n >= 2:
            go(s, lambda s: row_copy(s).start(), lambda s: row_own(s).start())
        else:
            @pl.when(jnp.logical_not(inner))
            def _():
                relay_copy(n, s).start()

    def pass_far(n):
        s = far[1 - n]

        @pl.when(inner)
        def _():
            relay_copy(n, s).wait_recv()
            for t in range(HALF // 64):
                part = pl.ds(t * 64, 64)
                own[s, part] = add_up(relay[n, part], own[s, part]).astype(BF16)
            row_copy(s).start()

    def partial_rows(t, carry):
        s = jnp.where(t == 0, far[0], jnp.where(t == 1, far[1], jnp.where(t == 2, far[2], far[3])))
        big[...] = nt(f[s], w[...])
        near_out[s] = big[rest].astype(BF16)
        near_copy(s).start()
        own[s] = big[rows].astype(BF16)
        tail_out[s] = big[last].astype(BF16)
        go(s, lambda s: tail_copy(s).start(), lambda s: tail_own(s).start())
        for e in range(ROWS // 48):
            part = pl.ds(e * 48, 48)
            values = xa[s, part].astype(F32)
            centre = values - jnp.mean(values, axis=1, keepdims=True)
            scale = lax.rsqrt(jnp.mean(centre * centre, axis=1, keepdims=True) + EPS)
            g = big[part]
            gh = g * (centre * scale)
            flat = f[s, part].astype(F32)
            for m in range(6):
                cols_sum[...] += flat[m * 8 : m * 8 + 8]
                hold[0] += gh[m * 8 : m * 8 + 8]
                hold[1] += g[m * 8 : m * 8 + 8]

        for n in range(STREAMS - 1):
            @pl.when(t == n + 1)
            def _():
                pass_on(n)

        return carry

    lax.fori_loop(0, STREAMS, partial_rows, 0)
    pass_on(STREAMS - 1)

    def move(turn):
        def one(k, carry):
            reducer.run(*[k if n == turn else None for n in range(5)])
            return carry

        lax.fori_loop(0, LAST, one, 0)

    move(0)
    vm[0] = v_ref[...]
    vm[0, 0:1] = jnp.sum(hold[0], axis=0, keepdims=True)
    vm[0, 1:2] = jnp.sum(hold[1], axis=0, keepdims=True)
    for part in range(3):
        place = pl.ds(pl.multiple_of(group * GW, GW), GW)
        vm[0, 2 + part : 3 + part, place] = jnp.sum(cols_sum[:, part * GW : (part + 1) * GW], axis=0, keepdims=True)
    v_core().start()

    for n in range(1, nx):
        q1a(n).wait_recv()
    for n in range(1, ny):
        q1b(n).wait_recv()
    for b in range(ny):
        sq1a[b] = add_up(q1[b, x, :, :, 0:QCUT], *[rq1a[n, b] for n in range(nx - 1)]).astype(BF16)
    for n in range(1, ny):
        q2a(n).start()
    for b in range(nx):
        sq1b[b] = add_up(q1[y, b, :, :, QCUT:], *[rq1b[n, b] for n in range(ny - 1)]).astype(BF16)
    for n in range(1, nx):
        q2b(n).start()
    v_core().wait_recv()
    vm[1] = vm[0] + vd[...]
    for n in range(1, nx):
        v_x(n).start()
    pass_far(0)
    move(1)
    for n in range(1, ny):
        q2a(n).wait_recv()
    for n in range(1, nx):
        q2b(n).wait_recv()
    left = add_up(sq1a[y], *[rq2a[n] for n in range(ny - 1)]).astype(BF16)
    right = add_up(sq1b[x], *[rq2b[n] for n in range(nx - 1)]).astype(BF16)
    sq2[:, :, :, :, 0:QCUT] = left.reshape(2, 2, 2, rb, QCUT)
    sq2[:, :, :, :, QCUT:] = right.reshape(2, 2, 2, rb, QCUT)
    q3().start()
    for n in range(1, nx):
        v_x(n).wait_recv()
    vm[2] = add_up(vm[1], *[vx[n] for n in range(nx - 1)])
    for n in range(1, ny):
        v_y(n).start()
    for n in range(1, ny):
        v_y(n).wait_recv()
    vm[3] = add_up(vm[2], *[vy[n] for n in range(ny - 1)])
    v_z1().start()
    pass_far(1)
    move(2)
    q3().wait_recv()
    sq3[...] = add_up(sq2[:, hi], rq3[...])
    for part in range(3):
        for n in range(3):
            q4(n, part).start()
        q4_own(part).start()
    v_z1().wait_recv()
    vm[4] = vm[3] + vz1[...]
    v_z2().start()
    move(3)

    late[1].wait()
    late[2].wait()
    for side in range(2):
        for core in range(2):
            part = pl.ds(core * HALF, HALF)
            g = 2 * side + core
            self_made = (core == c) & (2 * c + side == z)

            @pl.when(jnp.logical_not(self_made))
            def _():
                remote(tail_out.at[0], tail.at[g], csend.at[0], crecv.at[g], at.near).wait_recv()

            @pl.when(jnp.logical_not(self_made) & (in_pair | (side == 0)))
            def _():
                remote(own.at[0], land.at[side, part], send.at[0], recv.at[side, core], at.near).wait_recv()

            @pl.when(self_made)
            def _():
                row_own(0).wait()
                tail_own(0).wait()

    gain = gain_ref[0:1]

    def back(dst, grad):
        values = x_own[dst].astype(F32)
        centre = values - jnp.mean(values, axis=1, keepdims=True)
        scale = lax.rsqrt(jnp.mean(centre * centre, axis=1, keepdims=True) + EPS)
        normed = centre * scale
        g = grad * gain
        total[dst] = h_own[dst] + scale * (
            g - jnp.mean(g, axis=1, keepdims=True) - normed * jnp.mean(g * normed, axis=1, keepdims=True)
        )

    def back_rows(t, carry):
        part = pl.ds(pl.multiple_of(t * 64, 64), 64)
        back(part, add_up(land[0, part], land[1, part]))
        return carry

    lax.fori_loop(0, VIS // 64, back_rows, 0)
    back(last, add_up(tail[0], tail[1], tail[2], tail[3]))
    done = pltpu.make_async_copy(total, gx_ref, lsem.at[5])
    done.start()
    move(4)
    outs = [
        pltpu.make_async_copy(reducer.fin.at[k], oi_ref.at[:, pl.ds((EARLY + k) * D, D)], osem.at[k])
        for k in range(LAST - 1)
    ]
    outs += [pltpu.make_async_copy(reducer.fin.at[LAST - 1], op_ref, osem.at[LAST - 1])]
    keep.wait()
    outs += [pltpu.make_async_copy(kept, oi_ref.at[:, pl.ds(0, EARLY * D)], ksem.at[1])]
    for copy in outs:
        copy.start()
    v_z2().wait_recv()
    vm[5] = vm[4] + vz2[...]
    v_done = pltpu.make_async_copy(vm.at[5], ov_ref, lsem.at[6])
    v_done.start()
    for n in range(1, nx):
        q1a(n).wait_send()
        q2b(n).wait_send()
        v_x(n).wait_send()
    for n in range(1, ny):
        q1b(n).wait_send()
        q2a(n).wait_send()
        v_y(n).wait_send()
    q3().wait_send()
    v_core().wait_send()
    v_z1().wait_send()
    v_z2().wait_send()
    for n in range(STREAMS):
        s = far[n]
        near_copy(s).wait_send()
        if n < 2:
            @pl.when(inner)
            def _():
                row_copy(s).wait_send()

            @pl.when(jnp.logical_not(inner))
            def _():
                relay_copy(n, s).wait_send()

            tail_copy(s).wait_send()
        else:
            @pl.when(jnp.logical_not(mine(s)))
            def _():
                row_copy(s).wait_send()
                tail_copy(s).wait_send()
    for part in range(3):
        q4_own(part).wait()
        for n in range(3):
            q4(n, part).wait_send()
            q4(n, part).wait_recv()
    reducer.drain()
    for copy in outs:
        copy.wait()
    done.wait()
    v_done.wait()


def finish_rows(flat, x_all, g_qkv, w_qkv, x, h, g_in, g_proj, red_in, vectors, gain):
    nx, ny, rb = grid_shape()

    def v(*shape):
        return VM(shape, BF16)

    def vf(*shape):
        return VM(shape, F32)

    scratch = [
        v(STREAMS, ROWS, 3 * GW), v(STREAMS, ROWS, D), v(D, 3 * GW), v(ROWS, D), vf(ROWS, D), vf(ROWS, D),
        v(STREAMS, HALF, D), v(STREAMS, HALF, D), v(STREAMS, HALF, D), v(2, VIS, D), v(4, CROWS, D), v(4, CROWS, D),
        vf(ROWS, D),
        v(ny, nx, 8, rb, 3 * GW), v(nx - 1, ny, 8, rb, QCUT), v(ny - 1, nx, 8, rb, QCUT),
        v(ny, 8, rb, QCUT), v(nx, 8, rb, QCUT), v(ny - 1, 8, rb, QCUT), v(nx - 1, 8, rb, QCUT),
        v(2, 2, 2, rb, 3 * GW), v(2, 2, rb, 3 * GW), vf(2, 2, rb, 3 * GW),
        vf(6, 16, D), vf(16, D), vf(nx - 1, 16, D), vf(ny - 1, 16, D), vf(16, D), vf(16, D), vf(2, 8, D),
        dma(8), dma(4), dma(4), dma(4), dma(2, 2), dma(4), dma(4), dma(7),
        dma(nx - 1), dma(nx - 1), dma(ny - 1), dma(ny - 1), dma(ny - 1), dma(ny - 1), dma(nx - 1), dma(nx - 1),
        pltpu.SemaphoreType.DMA, pltpu.SemaphoreType.DMA, dma(3, 3), dma(3, 3),
        dma(3), dma(3), dma(nx - 1), dma(nx - 1), dma(ny - 1), dma(ny - 1),
        v(2, HALF, D), dma(2), dma(2), vf(8, 3 * GW), dma(LAST), vf(rb, EARLY * D), dma(2),
    ] + Reducer.scratch(LAST, nx, ny, rb)
    outs = (
        ((ROWS, D), F32), ((rb, 3 * D), F32), ((16, D), F32), ((rb, 4 * D), F32), ((rb, D), F32),
    )
    ops = (
        flat, x_all, g_qkv.reshape(ny, nx, 8, rb, 3 * GW), w_qkv, x, h,
        g_in.reshape(ny, nx, 2, STREAMS, rb, (LAST - 1) * D), g_proj.reshape(ny, nx, 2, STREAMS, rb, D),
        red_in,
    )
    return comm_call(
        functools.partial(finish_kernel, nx, ny, rb), "finish_rows", 4, outs, scratch, ops, (vectors, gain)
    )


TILE = 48
TILES = ROWS // TILE


def tn(a, b):
    return lax.dot_general(a, b, (((0,), (0,)), ((), ())), preferred_element_type=F32)


def mlp_kernel(
    nx, ny, rb,
    win_hbm, wout_hbm, att_ref, x_ref, dy_ref, wp_ref, par_ref,
    do_out, gi_out, go_out, gp_out, oi_ref, y_ref, gh_ref, vec_ref,
    wi, wo, n_ref, h_ref, buf, dbuf, hid, du, yacc, dn, dhb, do_ref, stage, sums,
    gi, isem, ssem, hs, hr, hl, osem, *refs,
):
    at = Place(nx, ny)
    p, c, q, r, z = at.p, at.c, at.hi, at.lo, at.z
    reducer = Reducer(at, rb, EARLY, ((EARLY, lambda t, core: gi.at[t, :, :, core]),), refs, ahead=False)

    def fetch(t, slot):
        cols = pl.ds(pl.multiple_of(t * D, D), D)
        return (
            pltpu.make_async_copy(win_hbm.at[:, cols], wi.at[slot], isem.at[0, slot]),
            pltpu.make_async_copy(wout_hbm.at[cols, :], wo.at[slot], isem.at[1, slot]),
        )

    for copy in fetch(0, 0):
        copy.start()
    at.greet()
    sums[...] = jnp.zeros_like(sums)
    for j in range(2):
        cols = slice(j * CUT, (j + 1) * CUT)
        buf[:, cols] = nn(att_ref[...], wp_ref[:, cols])

    def tile(t):
        return pl.ds(pl.multiple_of(t * TILE, 16), TILE)

    def fold(row, values):
        total = values[0:8]
        for m in range(1, TILE // 8):
            total = total + values[m * 8 : m * 8 + 8]
        sums[row] += total

    def enter(t, carry):
        rows = tile(t)
        h = x_ref[rows].astype(F32) + buf[rows] + par_ref[9:10]
        h_ref[rows] = h
        centre = h - jnp.mean(h, axis=1, keepdims=True)
        scale = lax.rsqrt(jnp.mean(centre * centre, axis=1, keepdims=True) + EPS)
        n_ref[rows] = (centre * scale * par_ref[10:11] + par_ref[11:12]).astype(BF16)
        return carry

    lax.fori_loop(0, TILES, enter, 0)

    def block(t, carry):
        slot = t % 2
        for copy in fetch(t, slot):
            copy.wait()

        @pl.when(t < 3)
        def _():
            for copy in fetch(t + 1, 1 - slot):
                copy.start()

        reducer.run(t - 1, None, t - 2, None, t - 3)
        for j in range(2):
            cols = slice(j * CUT, (j + 1) * CUT)
            buf[:, cols] = nn(n_ref[...], wi[slot, :, cols])
            dbuf[:, cols] = nt(dy_ref[...], wo[slot, cols, :])
        place = pl.ds(pl.multiple_of(t * D, D), D)

        def act(e, carry):
            rows = tile(e)
            for j in range(4):
                cols = slice(j * 256, (j + 1) * 256)
                u = buf[rows, cols] + par_ref[pl.ds(5 + t, 1), cols]
                phi = 0.5 * (1.0 + lax.erf(u * (2.0**-0.5)))
                hid[rows, pl.ds(pl.multiple_of(t * D + j * 256, 256), 256)] = (u * phi).astype(BF16)
                slope = phi + u * (jnp.exp(-0.5 * u * u) * ((2.0 * math.pi) ** -0.5))
                g = (dbuf[rows, cols] * slope).astype(BF16)
                du[rows, cols] = g
                g = g.astype(F32)
                total = g[0:8]
                for m in range(1, TILE // 8):
                    total = total + g[m * 8 : m * 8 + 8]
                sums[t, :, cols] += total
            return carry

        lax.fori_loop(0, TILES, act, 0)

        @pl.when(t < EARLY)
        def _():
            for b in range(ny):
                block_rows = tn(n_ref[:, b * (D // ny) : (b + 1) * (D // ny)], du[...])
                gi[t, b] = block_rows.astype(BF16).reshape(nx, 2, STREAMS, rb, D)
            reducer.issue(t)

        reducer.run(None, t - 1, None, t - 2, None)
        for j in range(2):
            cols = slice(j * CUT, (j + 1) * CUT)
            more = nn(hid[:, place], wo[slot, :, cols])
            back = nt(du[...], wi[slot, cols, :])

            @pl.when(t == 0)
            def _():
                yacc[:, cols] = more
                dn[:, cols] = back

            @pl.when(t > 0)
            def _():
                yacc[:, cols] += more
                dn[:, cols] += back

        return carry

    lax.fori_loop(0, 4, block, 0)
    reducer.run(None, None, EARLY - 1, None, EARLY - 2)

    def leave(t, carry):
        rows = tile(t)
        h = h_ref[rows]
        y_ref[rows] = (h + yacc[rows] + par_ref[12:13]).astype(BF16)
        centre = h - jnp.mean(h, axis=1, keepdims=True)
        scale = lax.rsqrt(jnp.mean(centre * centre, axis=1, keepdims=True) + EPS)
        normed = centre * scale
        grad = dn[rows]
        dy = dy_ref[rows].astype(F32)
        fold(5, grad * normed)
        fold(6, grad)
        fold(7, dy)
        g = grad * par_ref[10:11]
        gh = dy + scale * (
            g - jnp.mean(g, axis=1, keepdims=True) - normed * jnp.mean(g * normed, axis=1, keepdims=True)
        )
        gh_ref[rows] = gh
        low = gh.astype(BF16)
        dhb[rows] = low
        fold(4, low.astype(F32))
        return carry

    lax.fori_loop(0, TILES, leave, 0)
    reducer.run(None, None, None, EARLY - 1, None)
    for j in range(2):
        rows = slice(j * CUT, (j + 1) * CUT)
        do_ref[:, rows] = nt(dhb[...], wp_ref[rows, :]).astype(BF16)

    def heads_copy(g):
        device = (2 * p + g % 2, 2 * c + g // 2)
        return remote(do_ref.at[:, pl.ds(g * GW, GW)], do_out.at[z], hs.at[g], hr.at[z], device)

    def heads_own(g):
        return pltpu.make_async_copy(do_ref.at[:, pl.ds(g * GW, GW)], do_out.at[z], hl)

    for g in range(4):
        self_made = (g % 2 == c) & (2 * c + g // 2 == z)

        @pl.when(self_made)
        def _():
            heads_own(g).start()

        @pl.when(jnp.logical_not(self_made))
        def _():
            heads_copy(g).start()

    vec_ref[...] = jnp.zeros_like(vec_ref)
    for n in range(8):
        vec_ref[5 + n : 6 + n] = jnp.sum(sums[n], axis=0, keepdims=True)

    def out_save(t, slot):
        return pltpu.make_async_copy(stage.at[slot], go_out.at[pl.ds(pl.multiple_of(t * D, D), D), :], ssem.at[slot])

    def weights(t, carry):
        slot = t % 2

        @pl.when(t > 1)
        def _():
            out_save(t - 2, slot).wait()

        for m in range(2):
            half = pl.ds(m * CUT, CUT)
            place = pl.ds(pl.multiple_of(t * D + m * CUT, CUT), CUT)
            stage[slot, half, :] = tn(hid[:, place], dy_ref[...]).astype(BF16)
        out_save(t, slot).start()
        return carry

    lax.fori_loop(0, 4, weights, 0)
    saves = []
    for slot, (lhs, rhs, out) in enumerate(((att_ref, dhb, gp_out), (n_ref, du, gi_out))):
        out_save(2 + slot, slot).wait()
        for m in range(2):
            half = pl.ds(m * CUT, CUT)
            stage[slot, half, :] = tn(lhs[:, half], rhs[...]).astype(BF16)
        saves.append(pltpu.make_async_copy(stage.at[slot], out, ssem.at[slot]))
        saves[-1].start()
    reducer.run(None, None, None, None, EARLY - 1)
    fin_saves = [
        pltpu.make_async_copy(reducer.fin.at[k], oi_ref.at[:, pl.ds(k * D, D)], osem.at[k]) for k in range(EARLY)
    ]
    for copy in fin_saves:
        copy.start()
    reducer.drain()
    for g in range(4):
        self_made = (g % 2 == c) & (2 * c + g // 2 == z)

        @pl.when(self_made)
        def _():
            heads_own(g).wait()

        @pl.when(jnp.logical_not(self_made))
        def _():
            heads_copy(g).wait_send()
    for s in range(STREAMS):
        @pl.when((q != c) | (s != z))
        def _():
            remote(do_ref.at[:, pl.ds(0, GW)], do_out.at[s], hs.at[0], hr.at[s], (2 * p + 1 - c, z)).wait_recv()
    for copy in saves + fin_saves:
        copy.wait()


def mlp(w_in, w_out, attended, x, dy, w_proj, params):
    nx, ny, rb = grid_shape()

    def v16(*shape):
        return VM(shape, BF16)

    def vf(*shape):
        return VM(shape, F32)

    scratch = [
        v16(2, D, D), v16(2, D, D), v16(ROWS, D), vf(ROWS, D), vf(ROWS, D), vf(ROWS, D),
        v16(ROWS, 4 * D), v16(ROWS, D), vf(ROWS, D), vf(ROWS, D), v16(ROWS, D), v16(ROWS, D),
        v16(2, D, D), vf(8, 8, D), v16(EARLY, ny, nx, 2, STREAMS, rb, D),
        dma(2, 2), dma(2), dma(4), dma(4), pltpu.SemaphoreType.DMA, dma(EARLY),
    ] + Reducer.scratch(EARLY, nx, ny, rb)
    outs = (
        ((STREAMS, ROWS, GW), BF16), ((D, (4 - EARLY) * D), BF16), ((4 * D, D), BF16), ((D, D), BF16),
        ((rb, EARLY * D), F32),
    )
    near_outs = (((ROWS, D), BF16), ((ROWS, D), F32), ((16, D), F32))
    return comm_call(
        functools.partial(mlp_kernel, nx, ny, rb), "mlp", 1, outs, scratch, (w_in, w_out), (attended, x, dy, w_proj, params), near_outs
    )


def own_meta(lengths, mask):
    frames = jnp.arange(FRAMES, dtype=jnp.int32)
    order = jnp.arange(lengths.shape[0])
    ends = jnp.sum(jnp.where(order[:, None] <= order[None, :], lengths[:, None], 0), axis=0)
    reached = ends[None, :] <= frames[:, None]
    begin = jnp.sum(jnp.where(reached, lengths[None, :], 0), axis=1)
    episode = jnp.sum(reached, axis=1)[:, None] == jnp.arange(lengths.shape[0])[None, :]
    length = jnp.sum(jnp.where(episode, lengths[None, :], 0), axis=1)
    base = jnp.where(length == MOST, 0, jnp.where(length == MIDDLE - MOST, MOST, MIDDLE))
    slot = base + frames - begin
    perm = jnp.sum(jnp.where(slot[:, None] == frames[None, :], frames[:, None], 0), axis=0)
    stream = jnp.arange(STREAMS)[:, None]
    row = jnp.arange(CROWS)[None, :]
    part = FRAMES // STREAMS
    frame = jnp.where(row < part * COND, part * stream + row // COND, FRAMES)
    cslot = jnp.sum(jnp.where(frame[..., None] == frames, slot[None, None, :], 0), axis=-1)
    cslot = jnp.where(frame < FRAMES, cslot, 99).reshape(1, PART)
    hidden = jnp.where(mask == 1, 0.0, NEG).astype(F32)
    bias = jnp.sum(jnp.where((perm[:, None] == frames[None, :])[:, :, None], hidden[None], 0.0), axis=1)
    line = jnp.pad(cslot.astype(F32), ((0, 7), (0, PATCHES - PART)))
    return perm.astype(jnp.int32), slot.astype(jnp.int32), jnp.concatenate([bias, line], axis=0)


def per_device(
    visual, conditioning, d_visual, d_conditioning, episode_frames, patch_mask,
    ln1_gain, ln1_bias, w_qkv, b_qkv, w_proj, b_proj, ln2_gain, ln2_bias, w_in, b_in, w_out, b_out,
):
    d, z = lax.axis_index("dp"), lax.axis_index("stream")
    perm, slot, own = own_meta(episode_frames[0], patch_mask[0])
    x, dy = place_rows(perm, visual, conditioning, d_visual, d_conditioning)
    params = jnp.concatenate(
        [ln1_gain, ln1_bias, b_qkv, b_in, b_proj, ln2_gain, ln2_bias, b_out, jnp.zeros((3 * D,), BF16)]
    ).astype(F32).reshape(16, D)
    tables = tuple(jnp.asarray(t) for t in rope_constants())
    attended, x_all, a, q, k, v, o, meta, *rest = attend_forward(x, w_qkv, own, params, tables)
    grad_heads, grad_w_in, grad_w_out, grad_w_proj, red_in, output, grad_h, vectors = mlp(
        w_in, w_out, attended, x, dy, w_proj, params
    )
    red_out, grad_qkv = attend_backward(grad_w_out, grad_heads, (q, k, v, *rest), o, tables, meta)
    role_grad = jnp.einsum(
        "rd,re->de", a.reshape(STREAMS * ROWS, D), grad_qkv.reshape(STREAMS * ROWS, 3 * GW), preferred_element_type=F32
    )
    grad_x, red_qkv, sums, red_in, red_proj = finish_rows(
        grad_qkv, x_all, role_grad.astype(BF16), w_qkv, x, grad_h, grad_w_in, grad_w_proj, red_in, vectors, params
    )
    out_visual, grad_visual, out_extra, grad_extra = restore_rows(slot, output, grad_x, conditioning.shape[1])
    owner = d * STREAMS + z
    owners = lax.axis_size("dp") * STREAMS

    def share(start, rows):
        size = rows * D // owners
        return lax.dynamic_slice_in_dim(sums[start : start + rows].reshape(-1), owner * size, size, 0)

    return (
        out_visual.reshape(visual.shape), out_extra.reshape(conditioning.shape),
        grad_visual.reshape(visual.shape), grad_extra.reshape(conditioning.shape),
        share(0, 1), share(1, 1), red_qkv, share(2, 2), share(4, 1), red_proj, share(9, 1), share(10, 1), share(11, 1),
        red_in, share(5, 4), red_out.reshape(-1, D), share(12, 1),
    )


def solution(mesh):
    rows = P("dp", None, "stream", None)
    extra = P("dp", "stream", None, None)
    vector = P(("dp", "stream"))
    matrix = P(("dp", "stream"), None)
    in_specs = (rows, extra, rows, extra, P("dp", None), P("dp", None, None)) + (P(),) * 12
    out_specs = (
        rows, extra, rows, extra, vector, vector, matrix, vector, vector, matrix, vector, vector, vector, matrix,
        vector, matrix, vector,
    )
    return jax.shard_map(per_device, mesh=mesh, in_specs=in_specs, out_specs=out_specs, check_vma=False)
```
